32 devices in a mesh: dp: 8 (over y, x, core), tp: 4 (over z).
Axes of the slice: x: 2, y: 2, z: 4, core: 2. Of those that a mesh axis runs over, the one named last changes fastest.
Arguments:
- hidden: bfloat16 [32, 512, 1024], P(('dp', 'tp')), may hold values from -6 to 6
- cell_ids: int32 [32, 512], P(('dp', 'tp')), may hold values from 0 to 63, never falling along the last dimension, each value on 1 to 60 neighbouring positions
- cell_boxes: int32 [32, 64, 4], P(('dp', 'tp')), may hold values from 0 to 1000
- cotangent: bfloat16 [32, 512, 1024], P(('dp', 'tp')), may hold values from -6 to 6
- weight_cols: bfloat16 [7, 1024, 1024], P(None, None, 'tp'), may hold values from -0.1875 to 0.1875
- weight_out: bfloat16 [1024, 1024], P('tp'), may hold values from -1.5 to 1.5
- weight_down: bfloat16 [4, 1024, 1024], P(None, 'tp'), may hold values from -0.09375 to 0.09375
- vectors: float32 [1024, 12], replicated
- vector_moment: float32 [1024, 12], P('dp')
- left_stat: float32 [16, 1024, 1024], P('dp', 'tp')
- right_stat: float32 [16, 1024, 1024], P('dp', 'tp')
- left_root: float32 [16, 1024, 1024], P('dp', 'tp')
- right_root: float32 [16, 1024, 1024], P('dp')
- master: float32 [16, 1024, 1024], P('dp', 'tp'), may hold values from -0.1875 to 0.1875
- averaged_weight: float32 [16, 1024, 1024], P('dp', 'tp'), may hold values from -0.1875 to 0.1875
Outputs:
- layer_out: float32 [32, 512, 1024], P(('dp', 'tp'))
- input_grad: float32 [32, 512, 1024], P(('dp', 'tp'))
- block_grad: float32 [16, 1024, 1024], P('dp', None, 'tp')
- left_new: float32 [16, 1024, 1024], P('dp', 'tp')
- right_new: float32 [16, 1024, 1024], P('dp', 'tp')
- master_new: float32 [16, 1024, 1024], P('dp', 'tp')
- weight_copy: bfloat16 [16, 1024, 1024], P('dp', 'tp')
- ema_new: float32 [16, 1024, 1024], P('dp', 'tp')
- vector_grad: float32 [1024, 12], P('dp')
- moment_new: float32 [1024, 12], P('dp')
- vector_new: float32 [1024, 12], P('dp')
- bias_grad: float32 [1024], P('dp')
The draws below stay inside these ranges and needn't reach their ends.
Inputs may be any that keep to these rules, and one draw needn't show every extreme that they name: `cell_ids`: on each page cell numbers never fall; each cell spans 1 to 60 consecutive tokens and some cell exactly 60.
All inputs are finite; a program needn't handle non-finite values.
Results may differ from the reference program's by a relative error of at most 0.022.
The reference program's roundings to bfloat16 on the way count: a program that leaves them out, or rounds other values in their place, can miss the bound.
Values may be sent and summed in bfloat16 or wider, within the bound.
A program may use at most 256 MiB of HBM per device.

```python
import math
import jax
import jax.numpy as jnp
import numpy as np
from jax import lax

MODEL_WIDTH = 1024
H = 16
HD = 64
FF = 4096
SEQ = 512
CELLS = 64
CELL_MOST = 60
PAGES = 32
TOKEN_TOTAL = 16384
BLOCK_SLOTS = 16


def shifted_identity(key, shape_all, lower, upper, spread):
    key_one, key_two = jax.random.split(key)
    diag_vals = jax.random.uniform(key_one, (shape_all[0], shape_all[1], 1), jnp.float32, lower, upper)
    jitter = jax.random.normal(key_two, shape_all, jnp.float32) * (spread / math.sqrt(shape_all[2]))
    eye_mask = jnp.arange(shape_all[1])[:, None] == jnp.arange(shape_all[2])[None, :]
    return jnp.where(eye_mask[None], diag_vals + jitter, jitter)


def draw_vectors(key, part):
    key_one, key_two = jax.random.split(key)
    column = jnp.arange(12)[None, :]
    offsets = 0.3 * jax.random.normal(key_one, (MODEL_WIDTH, 12), jnp.float32)
    gain_vals = 1.0 + 0.2 * jax.random.uniform(key_two, (MODEL_WIDTH, 12), jnp.float32, -1.0, 1.0)
    is_gain = (column == 2) | (column == 4)
    return jnp.where(is_gain, gain_vals, offsets)


def draw_vector_moment(key, part):
    return 0.5 * math.sqrt(TOKEN_TOTAL) * jax.random.normal(key, (MODEL_WIDTH, 12), jnp.float32)


def draw_left_stat(key, part):
    return 0.05 * TOKEN_TOTAL * MODEL_WIDTH * shifted_identity(jax.random.fold_in(key, 11), (BLOCK_SLOTS, MODEL_WIDTH, MODEL_WIDTH), 1.0, 4.0, 0.3)


def draw_right_stat(key, part):
    return 0.05 * TOKEN_TOTAL * MODEL_WIDTH * shifted_identity(jax.random.fold_in(key, 12), (BLOCK_SLOTS, MODEL_WIDTH, MODEL_WIDTH), 1.0, 4.0, 0.3)


def draw_left_root(key, part):
    return (0.05 * TOKEN_TOTAL * MODEL_WIDTH) ** (-0.25) * shifted_identity(jax.random.fold_in(key, 13), (BLOCK_SLOTS, MODEL_WIDTH, MODEL_WIDTH), 0.7, 2.0, 0.4)


def draw_right_root(key, part):
    return (0.05 * TOKEN_TOTAL * MODEL_WIDTH) ** (-0.25) * shifted_identity(jax.random.fold_in(key, 14), (BLOCK_SLOTS, MODEL_WIDTH, MODEL_WIDTH), 0.7, 2.0, 0.4)


def set_ends(values, stream_key, least, high):
    place = [jax.random.randint(jax.random.fold_in(stream_key, axis), (), 0, length) for axis, length in enumerate(values.shape)]
    widest = values.shape.index(max(values.shape))
    next_to = place[:widest] + [(place[widest] + 1) % values.shape[widest]] + place[widest + 1:]
    return values.at[tuple(place)].set(least).at[tuple(next_to)].set(high)


def block_scale(key, extent, shards, least, largest):
    factor_of, own = 1.0, jax.random.fold_in(key, 6)
    for position, parts in shards:
        heights = jnp.exp(jax.random.uniform(jax.random.fold_in(own, position), (parts,), jnp.float32, least / len(shards), largest / len(shards)))
        factor_of = factor_of * jnp.repeat(heights, extent[position] // parts).reshape([-1 if axis == position else 1 for axis in range(len(extent))])
    return factor_of


def split_up(count, total, reach, lean):
    weights = [(1 << 20) // math.isqrt(grade ** lean) + 1 for grade in range(2, count + 1)]
    surplus, given = total - reach - (count - 1), [1] * (count - 1)
    while surplus > 0:
        candidates = [i for i in range(count - 1) if given[i] < reach]
        whole, remaining = sum([weights[i] for i in candidates]), surplus
        for i in candidates:
            addition = min(reach - given[i], max(1, remaining * weights[i] // whole), surplus)
            given[i] = given[i] + addition
            surplus = surplus - addition
    return np.array([reach] + given)


def ragged_sizes(own_key, number_of, total, most, skew):
    if number_of == 2:
        one = jax.random.randint(own_key, (), max(1, total - most), min(most, total - 1) + 1)
        return jnp.stack([one, total - one])
    lengths = jnp.asarray(split_up(number_of, total, most, skew), jnp.int32)
    pairs = (number_of - 1) // 2
    donor, sink = lengths[1:1 + 2 * pairs:2], lengths[2:2 + 2 * pairs:2]
    room = jnp.minimum(donor - 1, most - sink)
    moved = jax.random.randint(jax.random.fold_in(own_key, 1), (pairs,), 0, 1 << 20) % (room + 1)
    lengths = lengths.at[1:1 + 2 * pairs:2].set(donor - moved).at[2:2 + 2 * pairs:2].set(sink + moved)
    return lengths[jax.random.permutation(jax.random.fold_in(own_key, 2), number_of)]


def gaussian(rng, extent, deviation, reach, shards=(), held_as=jnp.bfloat16):
    values = deviation * jax.random.normal(rng, extent, jnp.float32)
    if shards:
        values = values * block_scale(rng, extent, shards, -0.22, 0.18)
    return jnp.clip(values, -reach, reach).astype(held_as)


def setup_inputs(seed: int = 0) -> dict:
    key_of = jax.random.split(jax.random.key(seed), 16)
    return {
        "hidden": gaussian(key_of[0], (PAGES, SEQ, MODEL_WIDTH), 1.0, 6.0, ((0, 32),)),
        "cell_ids": jax.vmap(lambda own: jnp.searchsorted(jnp.cumsum(ragged_sizes(own, CELLS, SEQ, CELL_MOST, 1)), jnp.arange(SEQ), side="right"))(jax.random.split(key_of[1], PAGES)).reshape((PAGES, SEQ)).astype(jnp.int32),
        "cell_boxes": set_ends(jax.random.randint(key_of[2], (PAGES, CELLS, 4), 0, 1001), jax.random.fold_in(key_of[2], 1), 0, 1000).astype(jnp.int32),
        "cotangent": gaussian(key_of[3], (PAGES, SEQ, MODEL_WIDTH), 1.0, 6.0, ((0, 32),)),
        "weight_cols": gaussian(key_of[4], (7, MODEL_WIDTH, MODEL_WIDTH), MODEL_WIDTH ** -0.5, 0.1875, ((2, 4),)),
        "weight_out": gaussian(key_of[5], (MODEL_WIDTH, MODEL_WIDTH), (MODEL_WIDTH // 64) ** -0.5, 1.5, ((0, 4),)),
        "weight_down": gaussian(key_of[6], (4, MODEL_WIDTH, MODEL_WIDTH), FF ** -0.5, 0.09375, ((1, 4),)),
        "vectors": draw_vectors(jax.random.fold_in(key_of[15], 71), 0),
        "vector_moment": draw_vector_moment(jax.random.fold_in(key_of[15], 71), 0),
        "left_stat": draw_left_stat(jax.random.fold_in(key_of[15], 71), 0),
        "right_stat": draw_right_stat(jax.random.fold_in(key_of[15], 71), 0),
        "left_root": draw_left_root(jax.random.fold_in(key_of[15], 71), 0),
        "right_root": draw_right_root(jax.random.fold_in(key_of[15], 71), 0),
        "master": gaussian(key_of[13], (BLOCK_SLOTS, MODEL_WIDTH, MODEL_WIDTH), MODEL_WIDTH ** -0.5, 0.1875, ((0, 8), (1, 4)), jnp.float32),
        "averaged_weight": gaussian(key_of[14], (BLOCK_SLOTS, MODEL_WIDTH, MODEL_WIDTH), MODEL_WIDTH ** -0.5, 0.1875, ((0, 8), (1, 4)), jnp.float32),
    }


@jax.custom_vjp
def low(v):
    return lax.optimization_barrier(v.astype(jnp.bfloat16)).astype(jnp.float32)

@jax.custom_vjp
def low_back(v):
    return v

def low_keep(v):
    return (low(v), None)

def low_pass(kept, grad):
    return (grad,)

def back_keep(v):
    return (v, None)

def back_low(kept, grad):
    return (low(grad),)
low.defvjp(low_keep, low_pass)
low_back.defvjp(back_keep, back_low)
PRECISE = lax.Precision.HIGHEST
EPS_NORM = 1e-06
STAT_DECAY = 0.5
BLOCK_RATE = 0.7
EMA_DECAY = 0.9
MOMENTUM = 0.9
VEC_RATE = 0.2

def layout_embed(cell_boxes, cell_ids):
    cell_count = cell_boxes.shape[1]
    onehot = (cell_ids[:, :, None] == jnp.arange(cell_count, dtype=jnp.int32)[None, None, :]).astype(jnp.float32)
    corners = jnp.einsum('psc,pck->psk', onehot, cell_boxes.astype(jnp.float32), precision=PRECISE)
    quarter = MODEL_WIDTH // 4
    half_width = quarter // 2
    frequency = jnp.exp(-jnp.arange(half_width, dtype=jnp.float32) * (math.log(1000.0) / half_width))
    angle_grid = corners[..., None] * frequency
    wave_table = jnp.concatenate([jnp.sin(angle_grid), jnp.cos(angle_grid)], -1)
    return 0.5 * wave_table.reshape(corners.shape[0], corners.shape[1], MODEL_WIDTH)

def norm_apply(values, gain, shift):
    center = values - lax.optimization_barrier(jnp.mean(values, -1, keepdims=True))
    spread = lax.optimization_barrier(jnp.mean(center * center, -1, keepdims=True))
    return center * lax.rsqrt(spread + EPS_NORM) * gain + shift

def layer(x_in, col_mats, out_mat, down_mats, vectors):
    groups, seq_len = (x_in.shape[0], x_in.shape[1])
    x_low = low(x_in)
    projected = jnp.einsum('gtd,kdc->kgtc', x_low, col_mats[0:3], precision=PRECISE)
    query_low = low(low_back(projected[0] + vectors[:, 6]))
    key_low = low(low_back(projected[1]))
    value_low = low(low_back(projected[2] + vectors[:, 7]))
    shape_heads = (groups, seq_len, H, HD)
    scores = jnp.einsum('gqhe,gkhe->ghqk', query_low.reshape(shape_heads), key_low.reshape(shape_heads), precision=PRECISE) * HD ** (-0.5)
    scores = low_back(scores)
    weights = jax.nn.softmax(scores, axis=-1)
    context = jnp.einsum('ghqk,gkhe->gqhe', low(weights), value_low.reshape(shape_heads), precision=PRECISE)
    context = low(low_back(context.reshape(groups, seq_len, MODEL_WIDTH)))
    attn_out = low_back(jnp.einsum('gtc,cd->gtd', context, out_mat, precision=PRECISE))
    mid_out = norm_apply(x_in + attn_out + vectors[:, 0], vectors[:, 2], vectors[:, 3])
    up_pre = jnp.einsum('gtd,kdc->kgtc', low(mid_out), col_mats[3:7], precision=PRECISE)
    up_pre = up_pre + jnp.transpose(vectors[:, 8:12])[:, None, None, :]
    activation = low(jax.nn.gelu(low_back(up_pre), approximate=False))
    ffn_out = low_back(jnp.einsum('kgtc,kcd->gtd', activation, down_mats, precision=PRECISE))
    return norm_apply(mid_out + ffn_out + vectors[:, 1], vectors[:, 4], vectors[:, 5])

def reference(hidden, cell_ids, cell_boxes, cotangent, weight_cols, weight_out, weight_down, vectors, vector_moment, left_stat, right_stat, left_root, right_root, master, averaged_weight):
    x_all = hidden.astype(jnp.float32) + layout_embed(cell_boxes, cell_ids)
    cot_all = cotangent.astype(jnp.float32)
    col_mats = weight_cols.astype(jnp.float32)
    out_mat = weight_out.astype(jnp.float32)
    down_mats = weight_down.astype(jnp.float32)
    group_pages = 4 if PAGES % 4 == 0 else 1
    group_count = PAGES // group_pages
    x_groups = x_all.reshape(group_count, group_pages, SEQ, MODEL_WIDTH)
    cot_groups = cot_all.reshape(group_count, group_pages, SEQ, MODEL_WIDTH)

    def step_group(carry, item):
        x_part, cot_part = item
        result, puller = jax.vjp(layer, x_part, col_mats, out_mat, down_mats, vectors)
        grad_x, gradient_columns, output_gradient, down_gradient, grad_vec = puller(cot_part)
        carry = jax.tree.map(lambda left_val, right_val: left_val + right_val, carry, (gradient_columns, output_gradient, down_gradient, grad_vec))
        return (carry, (result, grad_x))
    start_sums = (jnp.zeros_like(col_mats), jnp.zeros_like(out_mat), jnp.zeros_like(down_mats), jnp.zeros_like(vectors))
    (gradient_columns, output_gradient, down_gradient, grad_vec), (outs_all, grads_all) = lax.scan(step_group, start_sums, (x_groups, cot_groups))
    layer_out = outs_all.reshape(PAGES, SEQ, MODEL_WIDTH)
    input_grad = grads_all.reshape(PAGES, SEQ, MODEL_WIDTH)
    block_list = jnp.concatenate([gradient_columns, jnp.transpose(output_gradient)[None], jnp.transpose(down_gradient, (0, 2, 1)), jnp.zeros((BLOCK_SLOTS - 12, MODEL_WIDTH, MODEL_WIDTH), jnp.float32)], 0)
    left_new = STAT_DECAY * left_stat + (1.0 - STAT_DECAY) * jnp.einsum('sic,sjc->sij', block_list, block_list, precision=PRECISE)
    right_new = STAT_DECAY * right_stat + (1.0 - STAT_DECAY) * jnp.einsum('sic,sij->scj', block_list, block_list, precision=PRECISE)
    precond = jnp.einsum('sij,sjc->sic', left_root, block_list, precision=PRECISE)
    precond = jnp.einsum('sic,scj->sij', precond, right_root, precision=PRECISE)
    master_new = master - BLOCK_RATE * precond
    weight_copy = master_new.astype(jnp.bfloat16)
    ema_new = EMA_DECAY * averaged_weight + (1.0 - EMA_DECAY) * master_new
    moment_new = MOMENTUM * vector_moment + grad_vec
    vector_new = vectors - VEC_RATE * lax.rsqrt(jnp.float32(TOKEN_TOTAL)) * moment_new
    bias_grad = grad_vec[:, 0]
    return (layer_out, input_grad, block_list, left_new, right_new, master_new, weight_copy, ema_new, grad_vec, moment_new, vector_new, bias_grad)
```

```python
import math

import jax
import jax.numpy as jnp
from jax import lax
from jax.experimental import pallas as pl
from jax.experimental.pallas import tpu as pltpu
from jax.sharding import PartitionSpec as P

MODEL_WIDTH = 1024
H = 16
HD = 64

PRECISE = lax.Precision.HIGHEST
EPS_NORM = 1e-06
STAT_DECAY = 0.5
BLOCK_RATE = 0.7
EMA_DECAY = 0.9
MOMENTUM = 0.9
VEC_RATE = 0.2

MESH = pl.DeviceIdType.MESH


def position():
    d, z = lax.axis_index("dp"), lax.axis_index("tp")
    core, x, y = d % 2, (d // 2) % 2, d // 4
    near = {
        "x": (d + 2 - 4 * x, z),
        "y": (d + 4 - 8 * y, z),
        "c": (d + 1 - 2 * core, z),
        "u": (d, z + 1),
        "v": (d, z - 1),
    }
    return z, core, x, y, near


def meet(z, near, extra=()):
    barrier = pltpu.get_barrier_semaphore()
    always = [near[name] for name in "xyc"] + list(extra)
    for device in always:
        pl.semaphore_signal(barrier, 1, device_id=device, device_id_type=MESH)

    @pl.when(z < 3)
    def _():
        pl.semaphore_signal(barrier, 1, device_id=near["u"], device_id_type=MESH)

    @pl.when(z > 0)
    def _():
        pl.semaphore_signal(barrier, 1, device_id=near["v"], device_id_type=MESH)

    pl.semaphore_wait(barrier, len(always) + (z + 2) // 3 + (5 - z) // 3)


ORDER = (0, 1, 2, 7, 3, 4, 5, 6, 8, 9, 10, 11)


def gather_kernel(
    cols, outw, down, full, bounce_cols, bounce_rows, load, store, along, onward, arrived, beside
):
    z, core, x, y, near = position()
    p = 2 * y + x
    meet(z, near)

    def own(k, h):
        if k < 7:
            return cols.at[k, pl.ds(h * 512, 512), :]
        if k == 7:
            return outw.at[pl.ds(h * 128, 128), :]
        return down.at[k - 8, pl.ds(h * 128, 128), :]

    def spot(s, k, h):
        if k < 7:
            return full.at[k, pl.ds(h * 512, 512), pl.ds(pl.multiple_of(s * 256, 256), 256)]
        return full.at[k, pl.ds(pl.multiple_of(s * 256 + h * 128, 128), 128), :]

    def spot_whole(s, k):
        if k < 7:
            return full.at[k, :, pl.ds(pl.multiple_of(s * 256, 256), 256)]
        return full.at[k, pl.ds(pl.multiple_of(s * 256, 256), 256), :]

    def to(source, s, k, send_sem, recv_sem, name):
        return pltpu.make_async_remote_copy(
            src_ref=source,
            dst_ref=spot(s, k, core),
            send_sem=send_sem,
            recv_sem=recv_sem.at[s, k],
            device_id=near[name],
            device_id_type=MESH,
        )

    def first(g, act):
        for t in range(3):
            k = ORDER[3 * g + t]
            mine = (p == t) | (p == 3) if t == 0 else p == t

            @pl.when(mine & (z < 3))
            def _(k=k):
                act(to(own(k, core), z, k, along.at[k], arrived, "u"))

            @pl.when(mine & (z > 0))
            def _(k=k):
                act(to(own(k, core), z, k, onward.at[0, z, k], arrived, "v"))

    far = 3 * (1 - z // 2)
    nearest = z + 1 - 2 * (z // 3)
    strips = (nearest, 6 - nearest - far - z, far)

    def item(n, t):
        return strips[n % 3], ORDER[3 * (n // 3) + t]

    first(0, lambda copy: copy.start())
    first(1, lambda copy: copy.start())
    for k in ORDER:
        if k < 7:
            pltpu.make_async_copy(cols.at[k], bounce_cols.at[k], load.at[k]).start()
        else:
            source = outw if k == 7 else down.at[k - 8]
            pltpu.make_async_copy(source, bounce_rows.at[k - 7], load.at[k]).start()

    def bounce(k, act):
        if k < 7:
            act(pltpu.make_async_copy(bounce_cols.at[k], spot_whole(z, k), store.at[k]))
        else:
            act(pltpu.make_async_copy(bounce_rows.at[k - 7], spot_whole(z, k), store.at[k]))

    def go(s, k, kind, name, sems):
        return to(spot(s, k, core), s, k, onward.at[kind, s, k], sems, name)

    def stage(n, hop, begin):
        for t in range(3):
            s, k = item(n, t)
            who = {
                (0, 0): (p == 0) | (p == 3),
                (0, 1): p == 1,
                (0, 2): p == 2,
                (1, 0): (p == 1) | (p == 2),
                (1, 1): (p == 0) | (p == 3),
                (1, 2): (p == 0) | (p == 3),
                (2, 0): None,
                (2, 1): p == 2,
                (2, 2): p == 1,
            }[hop, t]
            if who is None:
                continue

            @pl.when(who)
            def _(s=s, k=k, t=t):
                if begin:
                    go(s, k, 0, "x", arrived).wait_recv()

                def act(copy):
                    if begin:
                        copy.start()
                    else:
                        copy.wait_send()

                if hop == 0:

                    @pl.when((s > z) & (z > 0))
                    def _():
                        act(go(s, k, 0, "v", arrived))

                    @pl.when((s < z) & (z < 3))
                    def _():
                        act(go(s, k, 0, "u", arrived))

                    if t == 0:

                        @pl.when(p == 0)
                        def _():
                            act(go(s, k, 1, "x", arrived))
                            act(go(s, k, 2, "y", arrived))
                    else:
                        act(go(s, k, 1, "x", arrived))
                        act(go(s, k, 2, "y", arrived))
                if hop == 1 and t == 1:

                    @pl.when(p == 3)
                    def _():
                        act(go(s, k, 1, "x", arrived))

                if hop == 1 and t == 2:

                    @pl.when(p == 3)
                    def _():
                        act(go(s, k, 2, "y", arrived))

                act(go(s, k, 3, "c", beside))

    for n in range(14):
        if n in (3, 6):
            first(n // 3 + 1, lambda copy: copy.start())
        if n == 2:
            for k in ORDER:
                if k < 7:
                    pltpu.make_async_copy(cols.at[k], bounce_cols.at[k], load.at[k]).wait()
                else:
                    source = outw if k == 7 else down.at[k - 8]
                    pltpu.make_async_copy(source, bounce_rows.at[k - 7], load.at[k]).wait()
                bounce(k, lambda copy: copy.start())
        for hop in range(3):
            if 0 <= n - hop < 12:
                stage(n - hop, hop, True)
    for n in range(12):
        for hop in range(3):
            stage(n, hop, False)
        for t in range(3):
            s, k = item(n, t)
            pltpu.make_async_remote_copy(
                src_ref=spot(s, k, 1 - core),
                dst_ref=spot(s, k, 1 - core),
                send_sem=onward.at[3, s, k],
                recv_sem=beside.at[s, k],
                device_id=near["c"],
                device_id_type=MESH,
            ).wait_recv()
    for g in range(4):
        first(g, lambda copy: copy.wait_send())
    for k in ORDER:
        bounce(k, lambda copy: copy.wait())


def gather_weights(cols, outw, down):
    anywhere = pl.BlockSpec(memory_space=pl.ANY)
    dma = pltpu.SemaphoreType.DMA
    return pl.pallas_call(
        gather_kernel,
        name="gather_weights",
        out_shape=jax.ShapeDtypeStruct((12, MODEL_WIDTH, MODEL_WIDTH), jnp.bfloat16),
        in_specs=[anywhere] * 3,
        out_specs=anywhere,
        scratch_shapes=[
            pltpu.VMEM((7, 1024, 256), jnp.bfloat16),
            pltpu.VMEM((5, 256, 1024), jnp.bfloat16),
            dma((12,)),
            dma((12,)),
            dma((12,)),
            dma((4, 4, 12)),
            dma((4, 12)),
            dma((4, 12)),
        ],
        compiler_params=pltpu.CompilerParams(
            collective_id=1, has_side_effects=True, vmem_limit_bytes=16 << 20
        ),
    )(cols, outw, down)


CHUNK = 64
STEPS = 2 * (MODEL_WIDTH // CHUNK)
PER_SLOT = MODEL_WIDTH // CHUNK


def reduce_kernel(
    qkv, up, outb, down, vec, total, vec_sum,
    mine, sibling, merged, side, chain, vec_in,
    load, cross_send, cross_recv, send, merge_recv, side_recv, chain_send, chain_recv, vec_send, vec_recv,
):
    z, core, x, y, near = position()
    p = 2 * y + x
    d = 2 * p + core
    z_one = (d, z + 1 - 2 * (z % 2))
    z_two = (d, z + 2 - 4 * (z // 2))
    meet(z, near, (z_two,))

    def block(slot):
        if slot < 3:
            return qkv.at[slot]
        if slot < 7:
            return up.at[slot - 3]
        if slot == 7:
            return outb.at[0]
        return down.at[slot - 8]

    order = [(i, j) for i in range(2) for j in (2, 1, 0)]

    def fetch(j, i, c):
        return pltpu.make_async_copy(block((2 * j + c) * 2 + i), mine.at[2 * j + i], load.at[2 * j + i])

    def give(j, i, c, q):
        return pltpu.make_async_remote_copy(
            src_ref=block((2 * j + c) * 2 + i).at[pl.ds(q * 256, 256), :],
            dst_ref=sibling.at[2 * j + i, pl.ds(q * 256, 256), :],
            send_sem=cross_send.at[2 * j + i, q],
            recv_sem=cross_recv.at[2 * j + i, q],
            device_id=near["c"],
            device_id_type=MESH,
        )

    for c in range(2):

        @pl.when(core == c)
        def _(c=c):
            for i, j in order:
                fetch(j, i, c).start()
                for q in range(4):
                    give(j, i, 1 - c, q).start()

    def vec_hop(h):
        device = (near["c"], near["x"], near["y"], z_one, z_two)[h]
        return pltpu.make_async_remote_copy(
            src_ref=vec_sum,
            dst_ref=vec_in.at[h],
            send_sem=vec_send.at[h],
            recv_sem=vec_recv.at[h],
            device_id=device,
            device_id_type=MESH,
        )

    vec_sum[...] = vec[...]
    vec_hop(0).start()

    @pl.when(p == 3)
    def _():
        total[...] = jnp.zeros_like(total)

    def rows(r):
        return pl.ds(pl.multiple_of(r * CHUNK, CHUNK), CHUNK)

    def remote(source, dest, send_sem, recv_sem, device):
        return pltpu.make_async_remote_copy(
            src_ref=source, dst_ref=dest, send_sem=send_sem, recv_sem=recv_sem,
            device_id=device, device_id_type=MESH,
        )

    def forward(s, i, r, place, name, act):
        act(remote(mine.at[s, rows(r), :], side.at[place, i, rows(r), :], send.at[s, r], side_recv.at[place, i * PER_SLOT + r], near[name]))

    def to_merge(s, r, name, act):
        act(remote(mine.at[s, rows(r), :], merged.at[s, rows(r), :], send.at[s, r], merge_recv.at[s, r], near[name]))

    def roles(j):
        rx = x if j % 2 == 0 else 1 - x
        ry = y if j // 2 == 0 else 1 - y
        return rx, ry

    def add(ref_a, ref_b):
        return ref_a[...].astype(jnp.float32) + ref_b[...].astype(jnp.float32)

    def sends(j, i, r, act, direct):
        s = 2 * j + i
        rx, ry = roles(j)
        if direct:

            @pl.when((rx == 1) & (ry == 1) & (r % 2 == 0))
            def _():
                to_merge(s, r, "x", act)

            @pl.when((rx == 1) & (ry == 1) & (r % 2 == 1))
            def _():
                to_merge(s, r, "y", act)

            @pl.when((rx == 1) & (ry == 0) & (r % 2 == 0))
            def _():
                forward(s, i, r, 0, "x", act)

            @pl.when((rx == 0) & (ry == 1) & (r % 2 == 1))
            def _():
                forward(s, i, r, 1, "y", act)
        else:

            @pl.when((rx == 1) & (ry == 0) & (r % 2 == 1))
            def _():
                forward(s, i, r, 0, "x", act)

            @pl.when((rx == 0) & (ry == 1) & (r % 2 == 0))
            def _():
                forward(s, i, r, 1, "y", act)

    begin = lambda copy: copy.start()

    def stage_one(m):
        i, r = m // PER_SLOT, m % PER_SLOT
        for j in (2, 1, 0):
            s = 2 * j + i

            @pl.when(r == 0)
            def _(s=s):
                pltpu.make_async_copy(down.at[0], mine.at[s], load.at[s]).wait()

            @pl.when(r % 4 == 0)
            def _(s=s):
                q = r // 4
                remote(
                    sibling.at[s, pl.ds(pl.multiple_of(q * 256, 256), 256), :],
                    sibling.at[s, pl.ds(pl.multiple_of(q * 256, 256), 256), :],
                    cross_send.at[s, q], cross_recv.at[s, q], near["c"],
                ).wait_recv()

            mine[s, rows(r), :] = add(mine.at[s, rows(r), :], sibling.at[s, rows(r), :]).astype(jnp.bfloat16)
            sends(j, i, r, begin, True)

    def stage_two(m):
        i, r = m // PER_SLOT, m % PER_SLOT
        for j in (2, 1, 0):
            s = 2 * j + i
            rx, ry = roles(j)

            @pl.when(((rx == 1) & (ry == 0) & (r % 2 == 1)) | ((rx == 0) & (ry == 1) & (r % 2 == 0)))
            def _(s=s):
                remote(merged.at[s, rows(r), :], merged.at[s, rows(r), :], send.at[s, r], merge_recv.at[s, r], near["x"]).wait_recv()
                mine[s, rows(r), :] = add(mine.at[s, rows(r), :], merged.at[s, rows(r), :]).astype(jnp.bfloat16)

            sends(j, i, r, begin, False)

    def pass_on(m, way, act):
        i, r = m // PER_SLOT, m % PER_SLOT
        def copy(source, name):
            return remote(source, chain.at[way, i, rows(r), :], chain_send.at[way, m], chain_recv.at[way, m], near[name])
        name = "u" if way == 0 else "v"
        end = 0 if way == 0 else 3

        @pl.when(z == end)
        def _():
            act(copy(mine.at[2 * p + i, rows(r), :], name))

        @pl.when((z == 1) | (z == 2))
        def _():
            act(copy(side.at[way, i, rows(r), :], name))

    def stage_three(m):
        i, r = m // PER_SLOT, m % PER_SLOT
        s = 2 * p + i
        for place in range(2):
            remote(side.at[place, i, rows(r), :], side.at[place, i, rows(r), :], send.at[s, r], side_recv.at[place, m], near["x"]).wait_recv()
        value = add(mine.at[s, rows(r), :], side.at[0, i, rows(r), :]) + side[1, i, rows(r), :].astype(jnp.float32)
        mine[s, rows(r), :] = value.astype(jnp.bfloat16)

        @pl.when(z == 0)
        def _():
            pass_on(m, 0, begin)

        @pl.when(z == 3)
        def _():
            pass_on(m, 1, begin)

    def chain_in(m, way):
        i, r = m // PER_SLOT, m % PER_SLOT
        remote(chain.at[way, i, rows(r), :], chain.at[way, i, rows(r), :], chain_send.at[way, m], chain_recv.at[way, m], near["x"]).wait_recv()

    def link(m, way, last):
        i, r = m // PER_SLOT, m % PER_SLOT
        s = 2 * p + i
        chain_in(m, way)
        side[way, i, rows(r), :] = add(mine.at[s, rows(r), :], chain.at[way, i, rows(r), :]).astype(jnp.bfloat16)
        pass_on(m, way, begin)
        if last:
            total[i, rows(r), :] = add(side.at[1 - way, i, rows(r), :], chain.at[way, i, rows(r), :]).astype(jnp.bfloat16)

    def stage_four(m):
        @pl.when(z == 1)
        def _():
            link(m, 0, False)

        @pl.when(z == 2)
        def _():
            link(m, 1, False)

    def stage_five(m):
        @pl.when(z == 1)
        def _():
            link(m, 1, True)

        @pl.when(z == 2)
        def _():
            link(m, 0, True)

    def stage_six(m):
        i, r = m // PER_SLOT, m % PER_SLOT
        s = 2 * p + i
        for end, way in ((0, 1), (3, 0)):

            @pl.when(z == end)
            def _(way=way):
                chain_in(m, way)
                total[i, rows(r), :] = add(mine.at[s, rows(r), :], chain.at[way, i, rows(r), :]).astype(jnp.bfloat16)

    lags = LAGS

    def step(n, carry):
        @pl.when(n < STEPS)
        def _():
            stage_one(n)

        m2 = n - lags[0]

        @pl.when((m2 >= 0) & (m2 < STEPS))
        def _():
            stage_two(m2)

        for lag, stage in zip(lags[1:], (stage_three, stage_four, stage_five, stage_six)):
            m = n - lag

            @pl.when((m >= 0) & (m < STEPS) & (p < 3))
            def _(m=m, stage=stage):
                stage(m)

        for h in range(5):

            @pl.when(n == 2 + 3 * h)
            def _(h=h):
                vec_hop(h).wait()
                vec_sum[...] = vec_sum[...] + vec_in[h]
                if h < 4:
                    vec_hop(h + 1).start()

        return carry

    lax.fori_loop(0, STEPS + lags[4], step, 0)

    for c in range(2):

        @pl.when(core == c)
        def _(c=c):
            for i, j in order:
                for q in range(4):
                    give(j, i, 1 - c, q).wait_send()

    def finish(m, carry):
        i, r = m // PER_SLOT, m % PER_SLOT
        end = lambda copy: copy.wait_send()
        for j in range(3):
            sends(j, i, r, end, True)
            sends(j, i, r, end, False)

        @pl.when((p < 3) & (z < 3))
        def _():
            pass_on(m, 0, end)

        @pl.when((p < 3) & (z > 0))
        def _():
            pass_on(m, 1, end)

        return carry

    lax.fori_loop(0, STEPS, finish, 0)


LAGS = (2, 4, 6, 8, 10)


def reduce_blocks(qkv, up, outb, down, vec):
    anywhere = pl.BlockSpec(memory_space=pl.ANY)
    vmem = pl.BlockSpec(memory_space=pltpu.VMEM)
    dma = pltpu.SemaphoreType.DMA
    wide = MODEL_WIDTH
    return pl.pallas_call(
        reduce_kernel,
        name="reduce_blocks",
        out_shape=(
            jax.ShapeDtypeStruct((2, wide, wide), jnp.bfloat16),
            jax.ShapeDtypeStruct(vec.shape, jnp.float32),
        ),
        in_specs=[anywhere] * 4 + [vmem],
        out_specs=(vmem, vmem),
        scratch_shapes=[
            pltpu.VMEM((6, wide, wide), jnp.bfloat16),
            pltpu.VMEM((6, wide, wide), jnp.bfloat16),
            pltpu.VMEM((6, wide, wide), jnp.bfloat16),
            pltpu.VMEM((2, 2, wide, wide), jnp.bfloat16),
            pltpu.VMEM((2, 2, wide, wide), jnp.bfloat16),
            pltpu.VMEM((5,) + vec.shape, jnp.float32),
            dma((6,)),
            dma((6, 4)),
            dma((6, 4)),
            dma((6, PER_SLOT)),
            dma((6, PER_SLOT)),
            dma((2, STEPS)),
            dma((2, STEPS)),
            dma((2, STEPS)),
            dma((5,)),
            dma((5,)),
        ],
        compiler_params=pltpu.CompilerParams(
            collective_id=2, has_side_effects=True, vmem_limit_bytes=62 << 20
        ),
    )(qkv, up, outb, down, vec)


def layout_embed(cell_boxes, cell_ids):
    cell_count = cell_boxes.shape[1]
    onehot = (
        cell_ids[:, :, None] == jnp.arange(cell_count, dtype=jnp.int32)[None, None, :]
    ).astype(jnp.float32)
    corners = jnp.einsum("psc,pck->psk", onehot, cell_boxes.astype(jnp.float32), precision=PRECISE)
    quarter = MODEL_WIDTH // 4
    half_width = quarter // 2
    frequency = jnp.exp(
        -jnp.arange(half_width, dtype=jnp.float32) * (math.log(1000.0) / half_width)
    )
    angle_grid = corners[..., None] * frequency
    wave_table = jnp.concatenate([jnp.sin(angle_grid), jnp.cos(angle_grid)], -1)
    return 0.5 * wave_table.reshape(corners.shape[0], corners.shape[1], MODEL_WIDTH)


def gelu_exact(values):
    return jax.nn.gelu(values, approximate=False)


def norm_forward(values, gain, shift):
    center = values - jnp.mean(values, -1, keepdims=True)
    inv_std = lax.rsqrt(jnp.mean(center * center, -1, keepdims=True) + EPS_NORM)
    normed = center * inv_std
    return (normed * gain + shift, normed, inv_std)


def norm_backward(grad_in, normed, inv_std, gain):
    scaled = grad_in * gain
    grad_arg = inv_std * (
        scaled
        - jnp.mean(scaled, -1, keepdims=True)
        - normed * jnp.mean(scaled * normed, -1, keepdims=True)
    )
    return (grad_arg, jnp.sum(grad_in * normed, (0, 1)), jnp.sum(grad_in, (0, 1)))


def attend(query_low, key_low, value_low, head_count):
    groups, seq_len = (query_low.shape[0], query_low.shape[1])
    shape_heads = (groups, seq_len, head_count, HD)
    scores = jnp.einsum(
        "gqhe,gkhe->ghqk",
        query_low.reshape(shape_heads),
        key_low.reshape(shape_heads),
        preferred_element_type=jnp.float32,
    ) * HD ** (-0.5)
    row_max = jnp.max(scores, -1, keepdims=True)
    log_total = row_max + jnp.log(jnp.sum(jnp.exp(scores - row_max), -1, keepdims=True))
    probs = jnp.exp(scores - log_total).astype(jnp.bfloat16)
    context = jnp.einsum(
        "ghqk,gkhe->gqhe", probs, value_low.reshape(shape_heads), preferred_element_type=jnp.float32
    )
    return (context.reshape(groups, seq_len, head_count * HD).astype(jnp.bfloat16), log_total)


def attend_back(query_low, key_low, value_low, log_total, ctx_grad, head_count):
    groups, seq_len = (query_low.shape[0], query_low.shape[1])
    shape_heads = (groups, seq_len, head_count, HD)
    query_heads = query_low.reshape(shape_heads)
    key_heads = key_low.reshape(shape_heads)
    value_heads = value_low.reshape(shape_heads)
    grad_heads = ctx_grad.reshape(shape_heads)
    scale = HD ** (-0.5)
    scores = (
        jnp.einsum("gqhe,gkhe->ghqk", query_heads, key_heads, preferred_element_type=jnp.float32)
        * scale
    )
    probs = jnp.exp(scores - log_total)
    value_grad = jnp.einsum(
        "ghqk,gqhe->gkhe",
        probs.astype(jnp.bfloat16),
        grad_heads,
        preferred_element_type=jnp.float32,
    )
    prob_grad = jnp.einsum(
        "gqhe,gkhe->ghqk", grad_heads, value_heads, preferred_element_type=jnp.float32
    )
    score_grad = (probs * (prob_grad - jnp.sum(probs * prob_grad, -1, keepdims=True))).astype(
        jnp.bfloat16
    )
    query_grad = (
        jnp.einsum("ghqk,gkhe->gqhe", score_grad, key_heads, preferred_element_type=jnp.float32)
        * scale
    )
    key_grad = (
        jnp.einsum("ghqk,gqhe->gkhe", score_grad, query_heads, preferred_element_type=jnp.float32)
        * scale
    )
    width = head_count * HD
    return (
        query_grad.reshape(groups, seq_len, width).astype(jnp.bfloat16),
        key_grad.reshape(groups, seq_len, width).astype(jnp.bfloat16),
        value_grad.reshape(groups, seq_len, width).astype(jnp.bfloat16),
    )


def local(
    hidden,
    cell_ids,
    cell_boxes,
    cotangent,
    weight_cols,
    weight_out,
    weight_down,
    vectors,
    vector_moment,
    left_stat,
    right_stat,
    left_root,
    right_root,
    master,
    averaged_weight,
):
    tp_count = lax.axis_size("tp")
    dp_count = lax.axis_size("dp")
    tp_index = lax.axis_index("tp")
    dp_index = lax.axis_index("dp")
    strip_width = weight_cols.shape[2]
    page_rows, seq_len = (hidden.shape[0], hidden.shape[1])
    near_plan = dp_count == 8 and tp_count == 4
    if near_plan:
        full = gather_weights(weight_cols, weight_out, weight_down)
        col_mats, out_mat, down_mats = full[0:7], full[7], full[8:12]
    else:
        col_mats = lax.all_gather(weight_cols, "tp", axis=2, tiled=True)
        out_mat = lax.all_gather(weight_out, "tp", axis=0, tiled=True)
        down_mats = lax.all_gather(weight_down, "tp", axis=1, tiled=True)
    x_own = hidden.astype(jnp.float32) + layout_embed(cell_boxes, cell_ids)
    x_low = x_own.astype(jnp.bfloat16)
    projected = jnp.einsum(
        "gtd,kdc->kgtc", x_low, col_mats[0:3], preferred_element_type=jnp.float32
    )
    query_low = (projected[0] + vectors[:, 6]).astype(jnp.bfloat16)
    key_low = projected[1].astype(jnp.bfloat16)
    value_low = (projected[2] + vectors[:, 7]).astype(jnp.bfloat16)
    context, log_total = attend(query_low, key_low, value_low, H)
    attn_out = jnp.einsum("gtc,cd->gtd", context, out_mat, preferred_element_type=jnp.float32)
    mid_out, mid_hat, mid_inv = norm_forward(
        x_own + attn_out + vectors[:, 0], vectors[:, 2], vectors[:, 3]
    )
    mid_low = mid_out.astype(jnp.bfloat16)
    up_pre = jnp.einsum(
        "gtd,kdc->kgtc", mid_low, col_mats[3:7], preferred_element_type=jnp.float32
    )
    up_pre = up_pre + jnp.transpose(vectors[:, 8:12])[:, None, None, :]
    act_low = gelu_exact(up_pre).astype(jnp.bfloat16)
    ffn_out = jnp.einsum("kgtc,kcd->gtd", act_low, down_mats, preferred_element_type=jnp.float32)
    layer_out, out_hat, out_inv = norm_forward(
        mid_out + ffn_out + vectors[:, 1], vectors[:, 4], vectors[:, 5]
    )
    output_gradient = cotangent.astype(jnp.float32)
    grad_two, gain_two, shift_two = norm_backward(output_gradient, out_hat, out_inv, vectors[:, 4])
    two_low = grad_two.astype(jnp.bfloat16)
    act_grad = jnp.einsum("gtd,kcd->kgtc", two_low, down_mats, preferred_element_type=jnp.float32)
    gelu_pull = jax.vjp(gelu_exact, up_pre)[1]
    up_low = gelu_pull(act_grad)[0].astype(jnp.bfloat16)
    mid_back = jnp.einsum(
        "kgtc,kdc->gtd", up_low, col_mats[3:7], preferred_element_type=jnp.float32
    )
    grad_one, gain_one, shift_one = norm_backward(
        mid_back + grad_two, mid_hat, mid_inv, vectors[:, 2]
    )
    one_low = grad_one.astype(jnp.bfloat16)
    ctx_grad = jnp.einsum(
        "gtd,cd->gtc", one_low, out_mat, preferred_element_type=jnp.float32
    ).astype(jnp.bfloat16)
    query_grad, key_grad, value_grad = attend_back(
        query_low, key_low, value_low, log_total, ctx_grad, H
    )
    qkv_grad = jnp.stack([query_grad, key_grad, value_grad], 0)
    input_grad = grad_one + jnp.einsum(
        "kgtc,kdc->gtd", qkv_grad, col_mats[0:3], preferred_element_type=jnp.float32
    )

    def block(text, left, right):
        return jnp.einsum(text, left, right, preferred_element_type=jnp.float32).astype(
            jnp.bfloat16
        )

    qkv_blocks = block("gtd,kgtc->kdc", x_low, qkv_grad)
    up_blocks = block("gtd,kgtc->kdc", mid_low, up_low)
    out_block = block("gtd,gtc->dc", one_low, context)[None]
    down_blocks = block("gtd,kgtc->kdc", two_low, act_low)
    vector_part = jnp.stack(
        [
            jnp.sum(grad_one, (0, 1)),
            jnp.sum(grad_two, (0, 1)),
            gain_one,
            shift_one,
            gain_two,
            shift_two,
            jnp.sum(query_grad, (0, 1), dtype=jnp.float32),
            jnp.sum(value_grad, (0, 1), dtype=jnp.float32),
        ],
        0,
    )
    vector_part = jnp.concatenate(
        [vector_part, jnp.sum(up_low, (1, 2), dtype=jnp.float32)], 0
    )
    owned_rows = vector_moment.shape[0]
    slot_dev = left_stat.shape[0]
    if near_plan:
        padded = jnp.concatenate([vector_part, jnp.zeros((4, MODEL_WIDTH), jnp.float32)], 0)
        full_grad, vector_sum = reduce_blocks(qkv_blocks, up_blocks, out_block, down_blocks, padded)
        vector_all = vector_sum[0:12]
    else:
        block_part = jnp.concatenate(
            [
                qkv_blocks,
                up_blocks,
                out_block,
                down_blocks,
                jnp.zeros((slot_dev * dp_count - 12, MODEL_WIDTH, MODEL_WIDTH), jnp.bfloat16),
            ],
            0,
        )
        block_owned = lax.psum_scatter(block_part, "dp", scatter_dimension=0, tiled=True)
        full_grad = lax.psum(block_owned, "tp")
        vector_all = lax.psum(vector_part, ("dp", "tp"))
    vector_grad = jnp.transpose(
        lax.dynamic_slice_in_dim(vector_all, dp_index * owned_rows, owned_rows, 1)
    )
    own_rows = lax.dynamic_slice_in_dim(full_grad, tp_index * strip_width, strip_width, 1)
    own_cols = lax.dynamic_slice_in_dim(full_grad, tp_index * strip_width, strip_width, 2)
    block_grad = own_cols.astype(jnp.float32)
    left_new = STAT_DECAY * left_stat + (1.0 - STAT_DECAY) * jnp.einsum(
        "sic,sjc->sij", own_rows, full_grad, preferred_element_type=jnp.float32
    )
    right_new = STAT_DECAY * right_stat + (1.0 - STAT_DECAY) * jnp.einsum(
        "sic,sij->scj", own_cols, full_grad, preferred_element_type=jnp.float32
    )

    def parts(array):
        high = array.astype(jnp.bfloat16)
        return high, (array - high.astype(jnp.float32)).astype(jnp.bfloat16)

    def product(left, right):
        return jnp.einsum("sij,sjc->sic", left, right, preferred_element_type=jnp.float32)

    left_high, left_rest = parts(left_root)
    right_high, right_rest = parts(right_root)
    precond = product(left_high, full_grad) + product(left_rest, full_grad)
    pre_high, pre_rest = parts(precond)
    precond = (
        product(pre_high, right_high) + product(pre_rest, right_high) + product(pre_high, right_rest)
    )
    master_new = master - BLOCK_RATE * precond
    weight_copy = master_new.astype(jnp.bfloat16)
    ema_new = EMA_DECAY * averaged_weight + (1.0 - EMA_DECAY) * master_new
    vector_rows = lax.dynamic_slice_in_dim(vectors, dp_index * owned_rows, owned_rows, 0)
    moment_new = MOMENTUM * vector_moment + vector_grad
    total_tokens = page_rows * seq_len * dp_count * tp_count
    vector_new = vector_rows - VEC_RATE * lax.rsqrt(jnp.float32(total_tokens)) * moment_new
    bias_grad = vector_grad[:, 0]
    return (
        layer_out,
        input_grad,
        block_grad,
        left_new,
        right_new,
        master_new,
        weight_copy,
        ema_new,
        vector_grad,
        moment_new,
        vector_new,
        bias_grad,
    )


def solution(mesh):
    return jax.shard_map(
        local,
        mesh=mesh,
        in_specs=(
            P(("dp", "tp"), None, None),
            P(("dp", "tp"), None),
            P(("dp", "tp"), None, None),
            P(("dp", "tp"), None, None),
            P(None, None, "tp"),
            P("tp", None),
            P(None, "tp", None),
            P(),
            P("dp", None),
            P("dp", "tp", None),
            P("dp", "tp", None),
            P("dp", "tp", None),
            P("dp", None, None),
            P("dp", "tp", None),
            P("dp", "tp", None),
        ),
        out_specs=(
            P(("dp", "tp"), None, None),
            P(("dp", "tp"), None, None),
            P("dp", None, "tp"),
            P("dp", "tp", None),
            P("dp", "tp", None),
            P("dp", "tp", None),
            P("dp", "tp", None),
            P("dp", "tp", None),
            P("dp", None),
            P("dp", None),
            P("dp", None),
            P("dp"),
        ),
        check_vma=False,
    )
```

```python
import math

import jax
import jax.numpy as jnp
from jax import lax
from jax.experimental import pallas as pl
from jax.experimental.pallas import tpu as pltpu
from jax.sharding import PartitionSpec as P

MODEL_WIDTH = 1024
H = 16
HD = 64

PRECISE = lax.Precision.HIGHEST
EPS_NORM = 1e-06
STAT_DECAY = 0.5
BLOCK_RATE = 0.7
EMA_DECAY = 0.9
MOMENTUM = 0.9
VEC_RATE = 0.2

MESH = pl.DeviceIdType.MESH


def position():
    d, z = lax.axis_index("dp"), lax.axis_index("tp")
    core, x, y = d % 2, (d // 2) % 2, d // 4
    near = {
        "x": (d + 2 - 4 * x, z),
        "y": (d + 4 - 8 * y, z),
        "c": (d + 1 - 2 * core, z),
        "u": (d, z + 1),
        "v": (d, z - 1),
    }
    return z, core, x, y, near


def meet(z, near, extra=()):
    barrier = pltpu.get_barrier_semaphore()
    always = [near[name] for name in "xyc"] + list(extra)
    for device in always:
        pl.semaphore_signal(barrier, 1, device_id=device, device_id_type=MESH)

    @pl.when(z < 3)
    def _():
        pl.semaphore_signal(barrier, 1, device_id=near["u"], device_id_type=MESH)

    @pl.when(z > 0)
    def _():
        pl.semaphore_signal(barrier, 1, device_id=near["v"], device_id_type=MESH)

    pl.semaphore_wait(barrier, len(always) + (z + 2) // 3 + (5 - z) // 3)


ORDER = (0, 1, 2, 7, 3, 4, 5, 6, 8, 9, 10, 11)


NT = (((1,), (1,)), ((), ()))
TOKENS = 512
WIDE = MODEL_WIDTH


def dot(a, b):
    return jnp.dot(a, b, preferred_element_type=jnp.float32)


def dot_nt(a, b):
    return lax.dot_general(a, b, NT, preferred_element_type=jnp.float32)


def columns(i, width=256):
    return pl.ds(pl.multiple_of(i * width, width), width)


def loop(count, body):
    def step(i, carry):
        body(i)
        return carry

    lax.fori_loop(0, count, step, 0)


def mean_of(rows):
    return jnp.sum(rows, -1, keepdims=True) * (1.0 / WIDE)


def transpose_into(dest, source):
    def body(i):
        dest[columns(i), :] = source[:, columns(i)].T

    loop(WIDE // 256, body)


def transpose_back(dest, source):
    def body(i):
        dest[:, columns(i)] = source[columns(i), :].T

    loop(WIDE // 256, body)


def embed_tokens(hidden, ids, boxes, x_ref, x_low):
    cells = boxes.shape[0]
    half = WIDE // 8
    place = lax.broadcasted_iota(jnp.int32, (1, half), 1).astype(jnp.float32)
    rate = jnp.exp(place * (-math.log(1000.0) / half))
    marks = lax.broadcasted_iota(jnp.int32, (cells, TOKENS), 0) == ids[...]
    chosen = jnp.where(marks, 1.0, 0.0).T.astype(jnp.bfloat16)
    for c in range(4):
        angle = boxes[:, c : c + 1].astype(jnp.float32) * rate
        for kind, wave in enumerate((jnp.sin(angle), jnp.cos(angle))):
            wave = 0.5 * wave
            high = wave.astype(jnp.bfloat16)
            rest = wave - high.astype(jnp.float32)
            middle = rest.astype(jnp.bfloat16)
            low = (rest - middle.astype(jnp.float32)).astype(jnp.bfloat16)
            emb = dot(chosen, high) + (dot(chosen, middle) + dot(chosen, low))
            at = pl.ds(c * 2 * half + kind * half, half)
            value = hidden[:, at].astype(jnp.float32) + emb
            x_ref[:, at] = value
            x_low[:, at] = value.astype(jnp.bfloat16)


def project(x_low, weight, dest, bias, scale):
    def body(i):
        value = dot(x_low[...], weight[:, columns(i)])
        if bias is not None:
            value = value + bias[:, columns(i)]
        value = value.astype(jnp.bfloat16)
        if scale:
            value = value * jnp.asarray(HD ** (-0.5), jnp.bfloat16)
        dest[:, columns(i)] = value

    loop(WIDE // 256, body)


def half_mask(e, shape):
    lane = lax.broadcasted_iota(jnp.int32, shape, 1)
    return (lane < HD) if e == 0 else (lane >= HD)


def attend_pair(t, q8, k, v_t, ctx_t, stat):
    at = columns(t, 128)
    keys, queries = k[:, at], q8[:, at]
    for e in range(2):
        own = jnp.where(half_mask(e, queries.shape), queries, jnp.zeros_like(queries))
        scores = dot_nt(keys, own)
        top = jnp.max(scores, 0, keepdims=True)
        power = jnp.exp(scores - top)
        total = jnp.sum(power, 0, keepdims=True)
        probs = (power * (1.0 / total)).astype(jnp.bfloat16)
        rows = pl.ds(pl.multiple_of(t * 128 + e * 64, 64), 64)
        ctx_t[rows, :] = dot(v_t[rows, :], probs).astype(jnp.bfloat16)
        stat[2 * t + e, :, :] = top + jnp.log(total)


def norm_rows(values, gain, shift):
    center = values - mean_of(values)
    inv = lax.rsqrt(mean_of(center * center) + EPS_NORM)
    normed = center * inv
    return normed * gain + shift, normed, inv


SLICE = 64


def row_loop(body):
    loop(TOKENS // SLICE, lambda i: body(pl.ds(pl.multiple_of(i * SLICE, SLICE), SLICE)))


def gelu_both(value):
    phi = 0.5 * (1.0 + lax.erf(value * math.sqrt(0.5)))
    density = jnp.exp(-0.5 * value * value) * (1.0 / math.sqrt(2.0 * math.pi))
    return value * phi, phi + value * density


def forward_kernel(
    cols, outw, down, hidden, ids, boxes, cotangent, vec,
    full_out, layer_out, x_out, q_out, k_out, v_out, ctx_out, stat_out, mid_out, hat_out, inv_out, act_out, slope_out,
    two_out, sums_out,
    w, bounce_unused, x_ref, x_low, q8, k, v, v_t, ctx_t, ctx, stat, acc, mid, mid_low, hat, inv, act, slope, y_out, two, sums,
    load, along, onward, arrived, beside, store, spill,
):
    z, core, x, y, near = position()
    p = 2 * y + x
    meet(z, near)

    def own(kk, h):
        if kk < 7:
            return cols.at[kk, pl.ds(h * 512, 512), :]
        if kk == 7:
            return outw.at[pl.ds(h * 128, 128), :]
        return down.at[kk - 8, pl.ds(h * 128, 128), :]

    def spot(s, kk, h):
        if kk < 7:
            return w.at[kk, pl.ds(h * 512, 512), pl.ds(pl.multiple_of(s * 256, 256), 256)]
        return w.at[kk, pl.ds(pl.multiple_of(s * 256 + h * 128, 128), 128), :]

    def spot_whole(s, kk):
        if kk < 7:
            return w.at[kk, :, pl.ds(pl.multiple_of(s * 256, 256), 256)]
        return w.at[kk, pl.ds(pl.multiple_of(s * 256, 256), 256), :]

    def whole_own(kk):
        if kk < 7:
            return cols.at[kk]
        return outw if kk == 7 else down.at[kk - 8]

    def to(source, s, kk, send_sem, recv_sem, name):
        return pltpu.make_async_remote_copy(
            src_ref=source,
            dst_ref=spot(s, kk, core),
            send_sem=send_sem,
            recv_sem=recv_sem.at[s, kk],
            device_id=near[name],
            device_id_type=MESH,
        )

    def first(g, act_on):
        for t in range(3):
            kk = ORDER[3 * g + t]
            mine = (p == t) | (p == 3) if t == 0 else p == t

            @pl.when(mine & (z < 3))
            def _(kk=kk):
                act_on(to(own(kk, core), z, kk, along.at[kk], arrived, "u"))

            @pl.when(mine & (z > 0))
            def _(kk=kk):
                act_on(to(own(kk, core), z, kk, onward.at[0, z, kk], arrived, "v"))

    far = 3 * (1 - z // 2)
    nearest = z + 1 - 2 * (z // 3)
    strips = (nearest, 6 - nearest - far - z, far)

    def item(n, t):
        return strips[n % 3], ORDER[3 * (n // 3) + t]

    def go(s, kk, kind, name, sems):
        return to(spot(s, kk, core), s, kk, onward.at[kind, s, kk], sems, name)

    def stage(n, hop, begin):
        for t in range(3):
            s, kk = item(n, t)
            who = {
                (0, 0): (p == 0) | (p == 3),
                (0, 1): p == 1,
                (0, 2): p == 2,
                (1, 0): (p == 1) | (p == 2),
                (1, 1): (p == 0) | (p == 3),
                (1, 2): (p == 0) | (p == 3),
                (2, 0): None,
                (2, 1): p == 2,
                (2, 2): p == 1,
            }[hop, t]
            if who is None:
                continue

            @pl.when(who)
            def _(s=s, kk=kk, t=t):
                if begin:
                    go(s, kk, 0, "x", arrived).wait_recv()

                def act_on(copy):
                    if begin:
                        copy.start()
                    else:
                        copy.wait_send()

                if hop == 0:

                    @pl.when((s > z) & (z > 0))
                    def _():
                        act_on(go(s, kk, 0, "v", arrived))

                    @pl.when((s < z) & (z < 3))
                    def _():
                        act_on(go(s, kk, 0, "u", arrived))

                    if t == 0:

                        @pl.when(p == 0)
                        def _():
                            act_on(go(s, kk, 1, "x", arrived))
                            act_on(go(s, kk, 2, "y", arrived))
                    else:
                        act_on(go(s, kk, 1, "x", arrived))
                        act_on(go(s, kk, 2, "y", arrived))
                if hop == 1 and t == 1:

                    @pl.when(p == 3)
                    def _():
                        act_on(go(s, kk, 1, "x", arrived))

                if hop == 1 and t == 2:

                    @pl.when(p == 3)
                    def _():
                        act_on(go(s, kk, 2, "y", arrived))

                act_on(go(s, kk, 3, "c", beside))

    copies = []

    def keep(source, dest):
        copy = pltpu.make_async_copy(source, dest, spill.at[len(copies)])
        copy.start()
        copies.append(copy)

    def ready(kk):
        pltpu.make_async_copy(whole_own(kk), spot_whole(z, kk), load.at[kk]).wait()
        for s in strips:
            pltpu.make_async_remote_copy(
                src_ref=spot(s, kk, 1 - core),
                dst_ref=spot(s, kk, 1 - core),
                send_sem=onward.at[3, s, kk],
                recv_sem=beside.at[s, kk],
                device_id=near["c"],
                device_id_type=MESH,
            ).wait_recv()
        copy = pltpu.make_async_copy(w.at[kk], full_out.at[kk], store.at[kk])
        copy.start()

    def unit_embed():
        embed_tokens(hidden, ids, boxes, x_ref, x_low)
        keep(x_low, x_out)

    def unit_qkv():
        for kk in range(3):
            ready(kk)
        project(x_low, w.at[0], q8, vec.at[6:7], True)
        project(x_low, w.at[1], k, None, False)
        project(x_low, w.at[2], v, vec.at[7:8], False)
        transpose_into(v_t, v)
        keep(q8, q_out)
        keep(k, k_out)
        keep(v, v_out)

    def unit_attend(lo, hi):
        loop(hi - lo, lambda i: attend_pair(lo + i, q8, k, v_t, ctx_t, stat))

    def unit_context():
        transpose_back(ctx, ctx_t)
        keep(ctx, ctx_out)
        keep(stat, stat_out)

    def unit_mid():
        ready(7)

        def tile(i):
            acc[:, columns(i)] = dot(ctx[...], w[7, :, columns(i)])

        loop(WIDE // 256, tile)

        def rows(r):
            value = x_ref[r, :] + acc[r, :] + vec[0:1, :]
            out, normed, scale = norm_rows(value, vec[2:3, :], vec[3:4, :])
            mid[r, :] = out
            mid_low[r, :] = out.astype(jnp.bfloat16)
            hat[r, :] = normed
            inv[r, :] = jnp.broadcast_to(scale, (SLICE, 128))

        row_loop(rows)
        keep(mid_low, mid_out)
        keep(hat, hat_out)
        keep(inv, inv_out)

    def unit_up(u):
        ready(3 + u)
        def tile(i):
            at = columns(i)
            slot = i % 2

            @pl.when(i >= 2)
            def _():
                pltpu.make_async_copy(slope.at[slot], slope_out.at[u, :, at], store.at[12 + slot]).wait()

            for part in range(2):
                rows = pl.ds(part * 256, 256)
                value = dot(mid_low[rows, :], w[3 + u, :, at]) + vec[8 + u : 9 + u, at]
                out, grad = gelu_both(value)
                act[u, rows, at] = out.astype(jnp.bfloat16)
                slope[slot, rows, :] = grad
            pltpu.make_async_copy(slope.at[slot], slope_out.at[u, :, at], store.at[12 + slot]).start()

        loop(WIDE // 256, tile)
        for slot in range(2):
            pltpu.make_async_copy(slope.at[slot], slope_out.at[u, :, columns(slot)], store.at[12 + slot]).wait()
        keep(act.at[u], act_out.at[u])

    def unit_down(u):
        ready(8 + u)

        def tile(i):
            at = columns(i)
            value = dot(act[u], w[8 + u, :, at])
            acc[:, at] = value if u == 0 else acc[:, at] + value

        loop(WIDE // 256, tile)

    def unit_last():
        sums[...] = jnp.zeros_like(sums)

        def rows(r):
            value = mid[r, :] + acc[r, :] + vec[1:2, :]
            out, normed, scale = norm_rows(value, vec[4:5, :], vec[5:6, :])
            y_out[r, :] = out
            grad = cotangent[r, :].astype(jnp.float32)
            scaled = grad * vec[4:5, :]
            arg = scale * (scaled - mean_of(scaled) - normed * mean_of(scaled * normed))
            two[r, :] = arg
            sums[1:2, :] += jnp.sum(arg, 0, keepdims=True)
            sums[4:5, :] += jnp.sum(grad * normed, 0, keepdims=True)
            sums[5:6, :] += jnp.sum(grad, 0, keepdims=True)

        row_loop(rows)
        keep(y_out, layer_out)
        keep(two, two_out)
        keep(sums, sums_out)

    first(0, lambda copy: copy.start())
    first(1, lambda copy: copy.start())
    for kk in ORDER:
        pltpu.make_async_copy(whole_own(kk), spot_whole(z, kk), load.at[kk]).start()
    unit_embed()
    after = {
        4: unit_qkv,
        5: lambda: unit_attend(0, 4),
        6: lambda: (unit_attend(4, 8), unit_context()),
        7: unit_mid,
        8: lambda: unit_up(0),
        9: lambda: unit_up(1),
        10: lambda: unit_up(2),
        11: lambda: unit_up(3),
        12: lambda: unit_down(0),
        13: lambda: (unit_down(1), unit_down(2), unit_down(3), unit_last()),
    }
    for n in range(14):
        if n in (3, 6):
            first(n // 3 + 1, lambda copy: copy.start())
        for hop in range(3):
            if 0 <= n - hop < 12:
                stage(n - hop, hop, True)
        if n in after:
            after[n]()
    for n in range(12):
        for hop in range(3):
            stage(n, hop, False)
    for g in range(4):
        first(g, lambda copy: copy.wait_send())
    for kk in ORDER:
        pltpu.make_async_copy(w.at[kk], full_out.at[kk], store.at[kk]).wait()
    for copy in copies:
        copy.wait()


def forward(cols, outw, down, hidden, ids, boxes, cotangent, vec):
    anywhere = pl.BlockSpec(memory_space=pl.ANY)
    vmem = pl.BlockSpec(memory_space=pltpu.VMEM)
    dma = pltpu.SemaphoreType.DMA
    low, wide = jnp.bfloat16, jnp.float32
    page = (TOKENS, WIDE)
    outs = [
        ((12, WIDE, WIDE), low),
        (page, wide),
        (page, low),
        (page, low),
        (page, low),
        (page, low),
        (page, low),
        ((H, 1, TOKENS), wide),
        (page, low),
        (page, wide),
        ((TOKENS, 128), wide),
        ((4,) + page, low),
        ((4,) + page, wide),
        (page, wide),
        ((16, WIDE), wide),
    ]
    return pl.pallas_call(
        forward_kernel,
        name="forward",
        out_shape=[jax.ShapeDtypeStruct(*o) for o in outs],
        in_specs=[anywhere] * 3 + [vmem] * 5,
        out_specs=[anywhere] * len(outs),
        scratch_shapes=[
            pltpu.VMEM((12, WIDE, WIDE), low),
            pltpu.VMEM((8, 128), wide),
            pltpu.VMEM(page, wide),
            pltpu.VMEM(page, low),
            pltpu.VMEM(page, low),
            pltpu.VMEM(page, low),
            pltpu.VMEM(page, low),
            pltpu.VMEM((WIDE, TOKENS), low),
            pltpu.VMEM((WIDE, TOKENS), low),
            pltpu.VMEM(page, low),
            pltpu.VMEM((H, 1, TOKENS), wide),
            pltpu.VMEM(page, wide),
            pltpu.VMEM(page, wide),
            pltpu.VMEM(page, low),
            pltpu.VMEM(page, wide),
            pltpu.VMEM((TOKENS, 128), wide),
            pltpu.VMEM((4,) + page, low),
            pltpu.VMEM((2, TOKENS, 256), wide),
            pltpu.VMEM(page, wide),
            pltpu.VMEM(page, wide),
            pltpu.VMEM((16, WIDE), wide),
            dma((12,)),
            dma((12,)),
            dma((4, 4, 12)),
            dma((4, 12)),
            dma((4, 12)),
            dma((14,)),
            dma((20,)),
        ],
        compiler_params=pltpu.CompilerParams(
            collective_id=1, has_side_effects=True, vmem_limit_bytes=61 << 20
        ),
    )(cols, outw, down, hidden, ids, boxes, cotangent, vec)


USES = (8, 3, 9, 4, 10, 5, 11, 6, 7, 0, 1, 2)
RING = 4


def attend_pair_back(t, q8, k, v, ctx_grad, k_t, stat, dq_t, dk, dv):
    at = columns(t, 128)
    keys, queries, values, grads = k[:, at], q8[:, at], v[:, at], ctx_grad[:, at]
    none = jnp.zeros_like(queries)
    key_sum = value_sum = None
    for e in range(2):
        mask = half_mask(e, queries.shape)
        own_q = jnp.where(mask, queries, none)
        own_g = jnp.where(mask, grads, none)
        probs = jnp.exp(dot_nt(keys, own_q) - stat[2 * t + e])
        prob_grad = dot_nt(values, own_g)
        carried = jnp.sum(probs * prob_grad, 0, keepdims=True)
        score_grad = (probs * (prob_grad - carried)).astype(jnp.bfloat16)
        rows = pl.ds(pl.multiple_of(t * 128 + e * 64, 64), 64)
        dq_t[rows, :] = (dot(k_t[rows, :], score_grad) * HD ** (-0.5)).astype(jnp.bfloat16)
        key_part = dot(score_grad, own_q)
        value_part = dot(probs.astype(jnp.bfloat16), own_g)
        key_sum = key_part if e == 0 else key_sum + key_part
        value_sum = value_part if e == 0 else value_sum + value_part
    dk[:, at] = key_sum.astype(jnp.bfloat16)
    dv[:, at] = value_sum.astype(jnp.bfloat16)


def backward_kernel(
    full, x_in, q_in, k_in, v_in, ctx_in, stat_in, mid_in, hat_in, inv_in, act_in, slope_in, two_in, sums_in, vec,
    input_out, blocks_out, sums,
    w, x_low, q8, k, v, ctx, stat, mid_low, hat, inv, act, slope, two, two_low,
    two_t, mid_t, one_t, x_t, k_t, up_grad, back, one, one_low, ctx_grad, dq_t, dq, dk, dv, stage,
    wsem, asem, ssem, isem, osem, gsem,
):
    def weight(i):
        return pltpu.make_async_copy(full.at[USES[i]], w.at[i % RING], wsem.at[i % RING])

    def act_load(u):
        return pltpu.make_async_copy(act_in.at[u], act.at[u % 2], asem.at[u % 2])

    def slope_load(u):
        return pltpu.make_async_copy(slope_in.at[u], slope.at[u % 2], ssem.at[u % 2])

    loads = {}

    def fetch(name, source, dest):
        loads[name] = pltpu.make_async_copy(source, dest, isem.at[len(loads)])
        loads[name].start()

    fetch("two", two_in, two)
    weight(0).start()
    slope_load(0).start()
    act_load(0).start()
    fetch("mid", mid_in, mid_low)
    weight(1).start()
    fetch("sums", sums_in, sums)
    weight(2).start()
    slope_load(1).start()
    act_load(1).start()
    weight(3).start()
    for name, source, dest in (
        ("hat", hat_in, hat), ("inv", inv_in, inv), ("ctx", ctx_in, ctx), ("k", k_in, k), ("q", q_in, q8),
        ("v", v_in, v), ("stat", stat_in, stat), ("x", x_in, x_low),
    ):
        fetch(name, source, dest)

    def use(i):
        weight(i).wait()
        return w.at[i % RING]

    def done(i):
        if i + RING < 12:
            weight(i + RING).start()

    made = []

    def block(slot, left_t, right):
        n = len(made)
        out = pltpu.make_async_copy(stage.at[n % 2], blocks_out.at[slot], gsem.at[n % 2])
        if n >= 2:
            made[n - 2].wait()

        def tile(i):
            stage[n % 2, :, columns(i)] = dot(left_t[...], right[:, columns(i)]).astype(jnp.bfloat16)

        loop(WIDE // 256, tile)
        out.start()
        made.append(out)

    def token_sum(row, ref):
        def tile(i):
            at = columns(i)
            sums[row : row + 1, at] = jnp.sum(ref[:, at].astype(jnp.float32), 0, keepdims=True)

        loop(WIDE // 256, tile)

    loads["two"].wait()

    def to_low(r):
        two_low[r, :] = two[r, :].astype(jnp.bfloat16)

    row_loop(to_low)
    transpose_into(two_t, two_low)
    loads["mid"].wait()
    transpose_into(mid_t, mid_low)
    loads["sums"].wait()
    for u in range(4):
        weights = use(2 * u)
        slope_load(u).wait()
        act_load(u).wait()

        def tile(i):
            rows = columns(i)
            grad = dot_nt(two_low[...], weights[rows, :]) * slope[u % 2, :, rows]
            up_grad[:, rows] = grad.astype(jnp.bfloat16)

        loop(WIDE // 256, tile)
        done(2 * u)
        token_sum(8 + u, up_grad)
        block(8 + u, two_t, act.at[u % 2])
        weights = use(2 * u + 1)

        def tile_back(i):
            at = columns(i)
            value = dot_nt(up_grad[...], weights[at, :])
            back[:, at] = two[:, at] + value if u == 0 else back[:, at] + value

        loop(WIDE // 256, tile_back)
        done(2 * u + 1)
        block(3 + u, mid_t, up_grad)
        if u + 2 < 4:
            slope_load(u + 2).start()
            act_load(u + 2).start()
    for name in ("hat", "inv"):
        loads[name].wait()
    sums[0:1, :] = jnp.zeros((1, WIDE), jnp.float32)
    sums[2:4, :] = jnp.zeros((2, WIDE), jnp.float32)

    def rows(r):
        grad, normed = back[r, :], hat[r, :]
        scaled = grad * vec[2:3, :]
        arg = inv[r, 0:1] * (scaled - mean_of(scaled) - normed * mean_of(scaled * normed))
        one[r, :] = arg
        one_low[r, :] = arg.astype(jnp.bfloat16)
        sums[0:1, :] += jnp.sum(arg, 0, keepdims=True)
        sums[2:3, :] += jnp.sum(grad * normed, 0, keepdims=True)
        sums[3:4, :] += jnp.sum(grad, 0, keepdims=True)

    row_loop(rows)
    transpose_into(one_t, one_low)
    weights = use(8)

    def tile_ctx(i):
        at = columns(i)
        ctx_grad[:, at] = dot_nt(one_low[...], weights[at, :]).astype(jnp.bfloat16)

    loop(WIDE // 256, tile_ctx)
    done(8)
    loads["ctx"].wait()
    block(7, one_t, ctx)
    for name in ("k", "q", "v", "stat", "x"):
        loads[name].wait()
    transpose_into(k_t, k)
    loop(H // 2, lambda t: attend_pair_back(t, q8, k, v, ctx_grad, k_t, stat, dq_t, dk, dv))
    transpose_back(dq, dq_t)
    transpose_into(x_t, x_low)
    token_sum(6, dq)
    token_sum(7, dv)
    for kk, grad in enumerate((dq, dk, dv)):
        weights = use(9 + kk)

        def tile_in(i):
            at = columns(i)
            one[:, at] = one[:, at] + dot_nt(grad[...], weights[at, :])

        loop(WIDE // 256, tile_in)
    out = pltpu.make_async_copy(one, input_out, osem.at[0])
    out.start()
    for kk, grad in enumerate((dq, dk, dv)):
        block(kk, x_t, grad)
    made[-2].wait()
    made[-1].wait()
    out.wait()


def backward(full, x, q, k, v, ctx, stat, mid, hat, inv, act, slope, two, sums, vec):
    anywhere = pl.BlockSpec(memory_space=pl.ANY)
    vmem = pl.BlockSpec(memory_space=pltpu.VMEM)
    dma = pltpu.SemaphoreType.DMA
    low, wide = jnp.bfloat16, jnp.float32
    page = (TOKENS, WIDE)
    flipped = pltpu.VMEM((WIDE, TOKENS), low)
    return pl.pallas_call(
        backward_kernel,
        name="backward",
        out_shape=[
            jax.ShapeDtypeStruct(page, wide),
            jax.ShapeDtypeStruct((12, WIDE, WIDE), low),
            jax.ShapeDtypeStruct((16, WIDE), wide),
        ],
        in_specs=[anywhere] * 14 + [vmem],
        out_specs=[anywhere, anywhere, vmem],
        scratch_shapes=[
            pltpu.VMEM((RING, WIDE, WIDE), low),
            pltpu.VMEM(page, low),
            pltpu.VMEM(page, low),
            pltpu.VMEM(page, low),
            pltpu.VMEM(page, low),
            pltpu.VMEM(page, low),
            pltpu.VMEM((H, 1, TOKENS), wide),
            pltpu.VMEM(page, low),
            pltpu.VMEM(page, wide),
            pltpu.VMEM((TOKENS, 128), wide),
            pltpu.VMEM((2,) + page, low),
            pltpu.VMEM((2,) + page, wide),
            pltpu.VMEM(page, wide),
            pltpu.VMEM(page, low),
            flipped, flipped, flipped, flipped, flipped,
            pltpu.VMEM(page, low),
            pltpu.VMEM(page, wide),
            pltpu.VMEM(page, wide),
            pltpu.VMEM(page, low),
            pltpu.VMEM(page, low),
            flipped,
            pltpu.VMEM(page, low), pltpu.VMEM(page, low), pltpu.VMEM(page, low),
            pltpu.VMEM((2, WIDE, WIDE), low),
            dma((RING,)), dma((2,)), dma((2,)), dma((11,)), dma((1,)), dma((2,)),
        ],
        compiler_params=pltpu.CompilerParams(vmem_limit_bytes=61 << 20),
    )(full, x, q, k, v, ctx, stat, mid, hat, inv, act, slope, two, sums, vec)


CHUNK = 64
STEPS = 2 * (MODEL_WIDTH // CHUNK)
PER_SLOT = MODEL_WIDTH // CHUNK


def reduce_kernel(
    blocks, vec, total, vec_sum,
    mine, sibling, merged, side, chain, vec_in,
    load, cross_send, cross_recv, send, merge_recv, side_recv, chain_send, chain_recv, vec_send, vec_recv,
):
    z, core, x, y, near = position()
    p = 2 * y + x
    d = 2 * p + core
    z_one = (d, z + 1 - 2 * (z % 2))
    z_two = (d, z + 2 - 4 * (z // 2))
    meet(z, near, (z_two,))

    def block(slot):
        return blocks.at[slot]

    order = [(i, j) for i in range(2) for j in (2, 1, 0)]

    def fetch(j, i, c):
        return pltpu.make_async_copy(block((2 * j + c) * 2 + i), mine.at[2 * j + i], load.at[2 * j + i])

    def give(j, i, c, q):
        return pltpu.make_async_remote_copy(
            src_ref=block((2 * j + c) * 2 + i).at[pl.ds(q * 256, 256), :],
            dst_ref=sibling.at[2 * j + i, pl.ds(q * 256, 256), :],
            send_sem=cross_send.at[2 * j + i, q],
            recv_sem=cross_recv.at[2 * j + i, q],
            device_id=near["c"],
            device_id_type=MESH,
        )

    for c in range(2):

        @pl.when(core == c)
        def _(c=c):
            for i, j in order:
                fetch(j, i, c).start()
                for q in range(4):
                    give(j, i, 1 - c, q).start()

    def vec_hop(h):
        device = (near["c"], near["x"], near["y"], z_one, z_two)[h]
        return pltpu.make_async_remote_copy(
            src_ref=vec_sum,
            dst_ref=vec_in.at[h],
            send_sem=vec_send.at[h],
            recv_sem=vec_recv.at[h],
            device_id=device,
            device_id_type=MESH,
        )

    vec_sum[...] = vec[...]
    vec_hop(0).start()

    @pl.when(p == 3)
    def _():
        total[...] = jnp.zeros_like(total)

    def rows(r):
        return pl.ds(pl.multiple_of(r * CHUNK, CHUNK), CHUNK)

    def remote(source, dest, send_sem, recv_sem, device):
        return pltpu.make_async_remote_copy(
            src_ref=source, dst_ref=dest, send_sem=send_sem, recv_sem=recv_sem,
            device_id=device, device_id_type=MESH,
        )

    def forward(s, i, r, place, name, act):
        act(remote(mine.at[s, rows(r), :], side.at[place, i, rows(r), :], send.at[s, r], side_recv.at[place, i * PER_SLOT + r], near[name]))

    def to_merge(s, r, name, act):
        act(remote(mine.at[s, rows(r), :], merged.at[s, rows(r), :], send.at[s, r], merge_recv.at[s, r], near[name]))

    def roles(j):
        rx = x if j % 2 == 0 else 1 - x
        ry = y if j // 2 == 0 else 1 - y
        return rx, ry

    def add(ref_a, ref_b):
        return ref_a[...].astype(jnp.float32) + ref_b[...].astype(jnp.float32)

    def sends(j, i, r, act, direct):
        s = 2 * j + i
        rx, ry = roles(j)
        if direct:

            @pl.when((rx == 1) & (ry == 1) & (r % 2 == 0))
            def _():
                to_merge(s, r, "x", act)

            @pl.when((rx == 1) & (ry == 1) & (r % 2 == 1))
            def _():
                to_merge(s, r, "y", act)

            @pl.when((rx == 1) & (ry == 0) & (r % 2 == 0))
            def _():
                forward(s, i, r, 0, "x", act)

            @pl.when((rx == 0) & (ry == 1) & (r % 2 == 1))
            def _():
                forward(s, i, r, 1, "y", act)
        else:

            @pl.when((rx == 1) & (ry == 0) & (r % 2 == 1))
            def _():
                forward(s, i, r, 0, "x", act)

            @pl.when((rx == 0) & (ry == 1) & (r % 2 == 0))
            def _():
                forward(s, i, r, 1, "y", act)

    begin = lambda copy: copy.start()

    def stage_one(m):
        i, r = m // PER_SLOT, m % PER_SLOT
        for j in (2, 1, 0):
            s = 2 * j + i

            @pl.when(r == 0)
            def _(s=s):
                pltpu.make_async_copy(blocks.at[0], mine.at[s], load.at[s]).wait()

            @pl.when(r % 4 == 0)
            def _(s=s):
                q = r // 4
                remote(
                    sibling.at[s, pl.ds(pl.multiple_of(q * 256, 256), 256), :],
                    sibling.at[s, pl.ds(pl.multiple_of(q * 256, 256), 256), :],
                    cross_send.at[s, q], cross_recv.at[s, q], near["c"],
                ).wait_recv()

            mine[s, rows(r), :] = add(mine.at[s, rows(r), :], sibling.at[s, rows(r), :]).astype(jnp.bfloat16)
            sends(j, i, r, begin, True)

    def stage_two(m):
        i, r = m // PER_SLOT, m % PER_SLOT
        for j in (2, 1, 0):
            s = 2 * j + i
            rx, ry = roles(j)

            @pl.when(((rx == 1) & (ry == 0) & (r % 2 == 1)) | ((rx == 0) & (ry == 1) & (r % 2 == 0)))
            def _(s=s):
                remote(merged.at[s, rows(r), :], merged.at[s, rows(r), :], send.at[s, r], merge_recv.at[s, r], near["x"]).wait_recv()
                mine[s, rows(r), :] = add(mine.at[s, rows(r), :], merged.at[s, rows(r), :]).astype(jnp.bfloat16)

            sends(j, i, r, begin, False)

    def pass_on(m, way, act):
        i, r = m // PER_SLOT, m % PER_SLOT
        def copy(source, name):
            return remote(source, chain.at[way, i, rows(r), :], chain_send.at[way, m], chain_recv.at[way, m], near[name])
        name = "u" if way == 0 else "v"
        end = 0 if way == 0 else 3

        @pl.when(z == end)
        def _():
            act(copy(mine.at[2 * p + i, rows(r), :], name))

        @pl.when((z == 1) | (z == 2))
        def _():
            act(copy(side.at[way, i, rows(r), :], name))

    def stage_three(m):
        i, r = m // PER_SLOT, m % PER_SLOT
        s = 2 * p + i
        for place in range(2):
            remote(side.at[place, i, rows(r), :], side.at[place, i, rows(r), :], send.at[s, r], side_recv.at[place, m], near["x"]).wait_recv()
        value = add(mine.at[s, rows(r), :], side.at[0, i, rows(r), :]) + side[1, i, rows(r), :].astype(jnp.float32)
        mine[s, rows(r), :] = value.astype(jnp.bfloat16)

        @pl.when(z == 0)
        def _():
            pass_on(m, 0, begin)

        @pl.when(z == 3)
        def _():
            pass_on(m, 1, begin)

    def chain_in(m, way):
        i, r = m // PER_SLOT, m % PER_SLOT
        remote(chain.at[way, i, rows(r), :], chain.at[way, i, rows(r), :], chain_send.at[way, m], chain_recv.at[way, m], near["x"]).wait_recv()

    def link(m, way, last):
        i, r = m // PER_SLOT, m % PER_SLOT
        s = 2 * p + i
        chain_in(m, way)
        side[way, i, rows(r), :] = add(mine.at[s, rows(r), :], chain.at[way, i, rows(r), :]).astype(jnp.bfloat16)
        pass_on(m, way, begin)
        if last:
            total[i, rows(r), :] = add(side.at[1 - way, i, rows(r), :], chain.at[way, i, rows(r), :]).astype(jnp.bfloat16)

    def stage_four(m):
        @pl.when(z == 1)
        def _():
            link(m, 0, False)

        @pl.when(z == 2)
        def _():
            link(m, 1, False)

    def stage_five(m):
        @pl.when(z == 1)
        def _():
            link(m, 1, True)

        @pl.when(z == 2)
        def _():
            link(m, 0, True)

    def stage_six(m):
        i, r = m // PER_SLOT, m % PER_SLOT
        s = 2 * p + i
        for end, way in ((0, 1), (3, 0)):

            @pl.when(z == end)
            def _(way=way):
                chain_in(m, way)
                total[i, rows(r), :] = add(mine.at[s, rows(r), :], chain.at[way, i, rows(r), :]).astype(jnp.bfloat16)

    lags = LAGS

    def step(n, carry):
        @pl.when(n < STEPS)
        def _():
            stage_one(n)

        m2 = n - lags[0]

        @pl.when((m2 >= 0) & (m2 < STEPS))
        def _():
            stage_two(m2)

        for lag, stage in zip(lags[1:], (stage_three, stage_four, stage_five, stage_six)):
            m = n - lag

            @pl.when((m >= 0) & (m < STEPS) & (p < 3))
            def _(m=m, stage=stage):
                stage(m)

        for h in range(5):

            @pl.when(n == 2 + 3 * h)
            def _(h=h):
                vec_hop(h).wait()
                vec_sum[...] = vec_sum[...] + vec_in[h]
                if h < 4:
                    vec_hop(h + 1).start()

        return carry

    lax.fori_loop(0, STEPS + lags[4], step, 0)

    for c in range(2):

        @pl.when(core == c)
        def _(c=c):
            for i, j in order:
                for q in range(4):
                    give(j, i, 1 - c, q).wait_send()

    def finish(m, carry):
        i, r = m // PER_SLOT, m % PER_SLOT
        end = lambda copy: copy.wait_send()
        for j in range(3):
            sends(j, i, r, end, True)
            sends(j, i, r, end, False)

        @pl.when((p < 3) & (z < 3))
        def _():
            pass_on(m, 0, end)

        @pl.when((p < 3) & (z > 0))
        def _():
            pass_on(m, 1, end)

        return carry

    lax.fori_loop(0, STEPS, finish, 0)


LAGS = (2, 4, 6, 8, 10)


def reduce_blocks(blocks, vec):
    anywhere = pl.BlockSpec(memory_space=pl.ANY)
    vmem = pl.BlockSpec(memory_space=pltpu.VMEM)
    dma = pltpu.SemaphoreType.DMA
    wide = MODEL_WIDTH
    return pl.pallas_call(
        reduce_kernel,
        name="reduce_blocks",
        out_shape=(
            jax.ShapeDtypeStruct((2, wide, wide), jnp.bfloat16),
            jax.ShapeDtypeStruct(vec.shape, jnp.float32),
        ),
        in_specs=[anywhere, vmem],
        out_specs=(vmem, vmem),
        scratch_shapes=[
            pltpu.VMEM((6, wide, wide), jnp.bfloat16),
            pltpu.VMEM((6, wide, wide), jnp.bfloat16),
            pltpu.VMEM((6, wide, wide), jnp.bfloat16),
            pltpu.VMEM((2, 2, wide, wide), jnp.bfloat16),
            pltpu.VMEM((2, 2, wide, wide), jnp.bfloat16),
            pltpu.VMEM((5,) + vec.shape, jnp.float32),
            dma((6,)),
            dma((6, 4)),
            dma((6, 4)),
            dma((6, PER_SLOT)),
            dma((6, PER_SLOT)),
            dma((2, STEPS)),
            dma((2, STEPS)),
            dma((2, STEPS)),
            dma((5,)),
            dma((5,)),
        ],
        compiler_params=pltpu.CompilerParams(
            collective_id=2, has_side_effects=True, vmem_limit_bytes=62 << 20
        ),
    )(blocks, vec)


def layout_embed(cell_boxes, cell_ids):
    cell_count = cell_boxes.shape[1]
    onehot = (
        cell_ids[:, :, None] == jnp.arange(cell_count, dtype=jnp.int32)[None, None, :]
    ).astype(jnp.float32)
    corners = jnp.einsum("psc,pck->psk", onehot, cell_boxes.astype(jnp.float32), precision=PRECISE)
    quarter = MODEL_WIDTH // 4
    half_width = quarter // 2
    frequency = jnp.exp(
        -jnp.arange(half_width, dtype=jnp.float32) * (math.log(1000.0) / half_width)
    )
    angle_grid = corners[..., None] * frequency
    wave_table = jnp.concatenate([jnp.sin(angle_grid), jnp.cos(angle_grid)], -1)
    return 0.5 * wave_table.reshape(corners.shape[0], corners.shape[1], MODEL_WIDTH)


def gelu_exact(values):
    return jax.nn.gelu(values, approximate=False)


def norm_forward(values, gain, shift):
    center = values - jnp.mean(values, -1, keepdims=True)
    inv_std = lax.rsqrt(jnp.mean(center * center, -1, keepdims=True) + EPS_NORM)
    normed = center * inv_std
    return (normed * gain + shift, normed, inv_std)


def norm_backward(grad_in, normed, inv_std, gain):
    scaled = grad_in * gain
    grad_arg = inv_std * (
        scaled
        - jnp.mean(scaled, -1, keepdims=True)
        - normed * jnp.mean(scaled * normed, -1, keepdims=True)
    )
    return (grad_arg, jnp.sum(grad_in * normed, (0, 1)), jnp.sum(grad_in, (0, 1)))


def attend(query_low, key_low, value_low, head_count):
    groups, seq_len = (query_low.shape[0], query_low.shape[1])
    shape_heads = (groups, seq_len, head_count, HD)
    scores = jnp.einsum(
        "gqhe,gkhe->ghqk",
        query_low.reshape(shape_heads),
        key_low.reshape(shape_heads),
        preferred_element_type=jnp.float32,
    ) * HD ** (-0.5)
    row_max = jnp.max(scores, -1, keepdims=True)
    log_total = row_max + jnp.log(jnp.sum(jnp.exp(scores - row_max), -1, keepdims=True))
    probs = jnp.exp(scores - log_total).astype(jnp.bfloat16)
    context = jnp.einsum(
        "ghqk,gkhe->gqhe", probs, value_low.reshape(shape_heads), preferred_element_type=jnp.float32
    )
    return (context.reshape(groups, seq_len, head_count * HD).astype(jnp.bfloat16), log_total)


def attend_back(query_low, key_low, value_low, log_total, ctx_grad, head_count):
    groups, seq_len = (query_low.shape[0], query_low.shape[1])
    shape_heads = (groups, seq_len, head_count, HD)
    query_heads = query_low.reshape(shape_heads)
    key_heads = key_low.reshape(shape_heads)
    value_heads = value_low.reshape(shape_heads)
    grad_heads = ctx_grad.reshape(shape_heads)
    scale = HD ** (-0.5)
    scores = (
        jnp.einsum("gqhe,gkhe->ghqk", query_heads, key_heads, preferred_element_type=jnp.float32)
        * scale
    )
    probs = jnp.exp(scores - log_total)
    value_grad = jnp.einsum(
        "ghqk,gqhe->gkhe",
        probs.astype(jnp.bfloat16),
        grad_heads,
        preferred_element_type=jnp.float32,
    )
    prob_grad = jnp.einsum(
        "gqhe,gkhe->ghqk", grad_heads, value_heads, preferred_element_type=jnp.float32
    )
    score_grad = (probs * (prob_grad - jnp.sum(probs * prob_grad, -1, keepdims=True))).astype(
        jnp.bfloat16
    )
    query_grad = (
        jnp.einsum("ghqk,gkhe->gqhe", score_grad, key_heads, preferred_element_type=jnp.float32)
        * scale
    )
    key_grad = (
        jnp.einsum("ghqk,gqhe->gkhe", score_grad, query_heads, preferred_element_type=jnp.float32)
        * scale
    )
    width = head_count * HD
    return (
        query_grad.reshape(groups, seq_len, width).astype(jnp.bfloat16),
        key_grad.reshape(groups, seq_len, width).astype(jnp.bfloat16),
        value_grad.reshape(groups, seq_len, width).astype(jnp.bfloat16),
    )


def by_collectives(
    hidden, cell_ids, cell_boxes, cotangent, weight_cols, weight_out, weight_down, vectors, slot_dev
):
    dp_count = lax.axis_size("dp")
    col_mats = lax.all_gather(weight_cols, "tp", axis=2, tiled=True)
    out_mat = lax.all_gather(weight_out, "tp", axis=0, tiled=True)
    down_mats = lax.all_gather(weight_down, "tp", axis=1, tiled=True)
    x_own = hidden.astype(jnp.float32) + layout_embed(cell_boxes, cell_ids)
    x_low = x_own.astype(jnp.bfloat16)
    projected = jnp.einsum(
        "gtd,kdc->kgtc", x_low, col_mats[0:3], preferred_element_type=jnp.float32
    )
    query_low = (projected[0] + vectors[:, 6]).astype(jnp.bfloat16)
    key_low = projected[1].astype(jnp.bfloat16)
    value_low = (projected[2] + vectors[:, 7]).astype(jnp.bfloat16)
    context, log_total = attend(query_low, key_low, value_low, H)
    attn_out = jnp.einsum("gtc,cd->gtd", context, out_mat, preferred_element_type=jnp.float32)
    mid_out, mid_hat, mid_inv = norm_forward(
        x_own + attn_out + vectors[:, 0], vectors[:, 2], vectors[:, 3]
    )
    mid_low = mid_out.astype(jnp.bfloat16)
    up_pre = jnp.einsum(
        "gtd,kdc->kgtc", mid_low, col_mats[3:7], preferred_element_type=jnp.float32
    )
    up_pre = up_pre + jnp.transpose(vectors[:, 8:12])[:, None, None, :]
    act_low = gelu_exact(up_pre).astype(jnp.bfloat16)
    ffn_out = jnp.einsum("kgtc,kcd->gtd", act_low, down_mats, preferred_element_type=jnp.float32)
    layer_out, out_hat, out_inv = norm_forward(
        mid_out + ffn_out + vectors[:, 1], vectors[:, 4], vectors[:, 5]
    )
    output_gradient = cotangent.astype(jnp.float32)
    grad_two, gain_two, shift_two = norm_backward(output_gradient, out_hat, out_inv, vectors[:, 4])
    two_low = grad_two.astype(jnp.bfloat16)
    act_grad = jnp.einsum("gtd,kcd->kgtc", two_low, down_mats, preferred_element_type=jnp.float32)
    gelu_pull = jax.vjp(gelu_exact, up_pre)[1]
    up_low = gelu_pull(act_grad)[0].astype(jnp.bfloat16)
    mid_back = jnp.einsum(
        "kgtc,kdc->gtd", up_low, col_mats[3:7], preferred_element_type=jnp.float32
    )
    grad_one, gain_one, shift_one = norm_backward(
        mid_back + grad_two, mid_hat, mid_inv, vectors[:, 2]
    )
    one_low = grad_one.astype(jnp.bfloat16)
    ctx_grad = jnp.einsum(
        "gtd,cd->gtc", one_low, out_mat, preferred_element_type=jnp.float32
    ).astype(jnp.bfloat16)
    query_grad, key_grad, value_grad = attend_back(
        query_low, key_low, value_low, log_total, ctx_grad, H
    )
    qkv_grad = jnp.stack([query_grad, key_grad, value_grad], 0)
    input_grad = grad_one + jnp.einsum(
        "kgtc,kdc->gtd", qkv_grad, col_mats[0:3], preferred_element_type=jnp.float32
    )

    def block(text, left, right):
        return jnp.einsum(text, left, right, preferred_element_type=jnp.float32).astype(
            jnp.bfloat16
        )

    qkv_blocks = block("gtd,kgtc->kdc", x_low, qkv_grad)
    up_blocks = block("gtd,kgtc->kdc", mid_low, up_low)
    out_block = block("gtd,gtc->dc", one_low, context)[None]
    down_blocks = block("gtd,kgtc->kdc", two_low, act_low)
    vector_part = jnp.stack(
        [
            jnp.sum(grad_one, (0, 1)),
            jnp.sum(grad_two, (0, 1)),
            gain_one,
            shift_one,
            gain_two,
            shift_two,
            jnp.sum(query_grad, (0, 1), dtype=jnp.float32),
            jnp.sum(value_grad, (0, 1), dtype=jnp.float32),
        ],
        0,
    )
    vector_part = jnp.concatenate(
        [vector_part, jnp.sum(up_low, (1, 2), dtype=jnp.float32)], 0
    )
    block_part = jnp.concatenate(
        [
            qkv_blocks,
            up_blocks,
            out_block,
            down_blocks,
            jnp.zeros((slot_dev * dp_count - 12, MODEL_WIDTH, MODEL_WIDTH), jnp.bfloat16),
        ],
        0,
    )
    block_owned = lax.psum_scatter(block_part, "dp", scatter_dimension=0, tiled=True)
    full_grad = lax.psum(block_owned, "tp")
    vector_all = lax.psum(vector_part, ("dp", "tp"))
    return layer_out, input_grad, full_grad, vector_all


def local(
    hidden,
    cell_ids,
    cell_boxes,
    cotangent,
    weight_cols,
    weight_out,
    weight_down,
    vectors,
    vector_moment,
    left_stat,
    right_stat,
    left_root,
    right_root,
    master,
    averaged_weight,
):
    tp_count = lax.axis_size("tp")
    dp_count = lax.axis_size("dp")
    tp_index = lax.axis_index("tp")
    dp_index = lax.axis_index("dp")
    strip_width = weight_cols.shape[2]
    page_rows, seq_len = (hidden.shape[0], hidden.shape[1])
    owned_rows = vector_moment.shape[0]
    slot_dev = left_stat.shape[0]
    if dp_count == 8 and tp_count == 4:
        vec = jnp.transpose(vectors)
        full, layer_out, *kept, sums = forward(
            weight_cols, weight_out, weight_down, hidden[0], cell_ids, cell_boxes[0], cotangent[0], vec
        )
        input_grad, blocks, sums = backward(full, *kept, sums, vec)
        full_grad, vector_all = reduce_blocks(blocks, sums)
        layer_out, input_grad = layer_out[None], input_grad[None]
    else:
        layer_out, input_grad, full_grad, vector_all = by_collectives(
            hidden, cell_ids, cell_boxes, cotangent, weight_cols, weight_out, weight_down, vectors, slot_dev
        )
    vector_grad = jnp.transpose(
        lax.dynamic_slice_in_dim(vector_all[0:12], dp_index * owned_rows, owned_rows, 1)
    )
    own_rows = lax.dynamic_slice_in_dim(full_grad, tp_index * strip_width, strip_width, 1)
    own_cols = lax.dynamic_slice_in_dim(full_grad, tp_index * strip_width, strip_width, 2)
    block_grad = own_cols.astype(jnp.float32)
    left_new = STAT_DECAY * left_stat + (1.0 - STAT_DECAY) * jnp.einsum(
        "sic,sjc->sij", own_rows, full_grad, preferred_element_type=jnp.float32
    )
    right_new = STAT_DECAY * right_stat + (1.0 - STAT_DECAY) * jnp.einsum(
        "sic,sij->scj", own_cols, full_grad, preferred_element_type=jnp.float32
    )

    def parts(array):
        high = array.astype(jnp.bfloat16)
        return high, (array - high.astype(jnp.float32)).astype(jnp.bfloat16)

    def product(left, right):
        return jnp.einsum("sij,sjc->sic", left, right, preferred_element_type=jnp.float32)

    left_high, left_rest = parts(left_root)
    right_high, right_rest = parts(right_root)
    precond = product(left_high, full_grad) + product(left_rest, full_grad)
    pre_high, pre_rest = parts(precond)
    precond = (
        product(pre_high, right_high) + product(pre_rest, right_high) + product(pre_high, right_rest)
    )
    master_new = master - BLOCK_RATE * precond
    weight_copy = master_new.astype(jnp.bfloat16)
    ema_new = EMA_DECAY * averaged_weight + (1.0 - EMA_DECAY) * master_new
    vector_rows = lax.dynamic_slice_in_dim(vectors, dp_index * owned_rows, owned_rows, 0)
    moment_new = MOMENTUM * vector_moment + vector_grad
    total_tokens = page_rows * seq_len * dp_count * tp_count
    vector_new = vector_rows - VEC_RATE * lax.rsqrt(jnp.float32(total_tokens)) * moment_new
    bias_grad = vector_grad[:, 0]
    return (
        layer_out,
        input_grad,
        block_grad,
        left_new,
        right_new,
        master_new,
        weight_copy,
        ema_new,
        vector_grad,
        moment_new,
        vector_new,
        bias_grad,
    )


def solution(mesh):
    return jax.shard_map(
        local,
        mesh=mesh,
        in_specs=(
            P(("dp", "tp"), None, None),
            P(("dp", "tp"), None),
            P(("dp", "tp"), None, None),
            P(("dp", "tp"), None, None),
            P(None, None, "tp"),
            P("tp", None),
            P(None, "tp", None),
            P(),
            P("dp", None),
            P("dp", "tp", None),
            P("dp", "tp", None),
            P("dp", "tp", None),
            P("dp", None, None),
            P("dp", "tp", None),
            P("dp", "tp", None),
        ),
        out_specs=(
            P(("dp", "tp"), None, None),
            P(("dp", "tp"), None, None),
            P("dp", None, "tp"),
            P("dp", "tp", None),
            P("dp", "tp", None),
            P("dp", "tp", None),
            P("dp", "tp", None),
            P("dp", "tp", None),
            P("dp", None),
            P("dp", None),
            P("dp", None),
            P("dp"),
        ),
        check_vma=False,
    )
```

```python
import math

import jax
import jax.numpy as jnp
from jax import lax
from jax.experimental import pallas as pl
from jax.experimental.pallas import tpu as pltpu
from jax.sharding import PartitionSpec as P

MODEL_WIDTH = 1024
H = 16
HD = 64

PRECISE = lax.Precision.HIGHEST
EPS_NORM = 1e-06
STAT_DECAY = 0.5
BLOCK_RATE = 0.7
EMA_DECAY = 0.9
MOMENTUM = 0.9
VEC_RATE = 0.2

MESH = pl.DeviceIdType.MESH


def position():
    d, z = lax.axis_index("dp"), lax.axis_index("tp")
    core, x, y = d % 2, (d // 2) % 2, d // 4
    near = {
        "x": (d + 2 - 4 * x, z),
        "y": (d + 4 - 8 * y, z),
        "c": (d + 1 - 2 * core, z),
        "u": (d, z + 1),
        "v": (d, z - 1),
    }
    return z, core, x, y, near


def meet(z, near, extra=()):
    barrier = pltpu.get_barrier_semaphore()
    always = [near[name] for name in "xyc"] + list(extra)
    for device in always:
        pl.semaphore_signal(barrier, 1, device_id=device, device_id_type=MESH)

    @pl.when(z < 3)
    def _():
        pl.semaphore_signal(barrier, 1, device_id=near["u"], device_id_type=MESH)

    @pl.when(z > 0)
    def _():
        pl.semaphore_signal(barrier, 1, device_id=near["v"], device_id_type=MESH)

    pl.semaphore_wait(barrier, len(always) + (z + 2) // 3 + (5 - z) // 3)


ORDER = (0, 1, 2, 7, 3, 4, 5, 6, 8, 9, 10, 11)


NT = (((1,), (1,)), ((), ()))
TOKENS = 512
WIDE = MODEL_WIDTH


def dot(a, b):
    return jnp.dot(a, b, preferred_element_type=jnp.float32)


def dot_nt(a, b):
    return lax.dot_general(a, b, NT, preferred_element_type=jnp.float32)


def columns(i, width=256):
    return pl.ds(pl.multiple_of(i * width, width), width)


def loop(count, body):
    def step(i, carry):
        body(i)
        return carry

    lax.fori_loop(0, count, step, 0)


def mean_of(rows):
    return jnp.sum(rows, -1, keepdims=True) * (1.0 / WIDE)


def transpose_into(dest, source):
    def body(i):
        dest[columns(i), :] = source[:, columns(i)].T

    loop(WIDE // 256, body)


def transpose_back(dest, source):
    def body(i):
        dest[:, columns(i)] = source[columns(i), :].T

    loop(WIDE // 256, body)


def embed_tokens(hidden, ids, boxes, x_ref, x_low):
    cells = boxes.shape[0]
    half = WIDE // 8
    place = lax.broadcasted_iota(jnp.int32, (1, half), 1).astype(jnp.float32)
    rate = jnp.exp(place * (-math.log(1000.0) / half))
    marks = lax.broadcasted_iota(jnp.int32, (cells, TOKENS), 0) == ids[...]
    chosen = jnp.where(marks, 1.0, 0.0).T.astype(jnp.bfloat16)
    for c in range(4):
        angle = boxes[:, c : c + 1].astype(jnp.float32) * rate
        for kind, wave in enumerate((jnp.sin(angle), jnp.cos(angle))):
            wave = 0.5 * wave
            high = wave.astype(jnp.bfloat16)
            rest = wave - high.astype(jnp.float32)
            middle = rest.astype(jnp.bfloat16)
            low = (rest - middle.astype(jnp.float32)).astype(jnp.bfloat16)
            emb = dot(chosen, high) + (dot(chosen, middle) + dot(chosen, low))
            at = pl.ds(c * 2 * half + kind * half, half)
            value = hidden[:, at].astype(jnp.float32) + emb
            x_ref[:, at] = value
            x_low[:, at] = value.astype(jnp.bfloat16)


def project(x_low, weight, dest, bias, scale):
    def body(i):
        value = dot(x_low[...], weight[:, columns(i)])
        if bias is not None:
            value = value + bias[:, columns(i)]
        value = value.astype(jnp.bfloat16)
        if scale:
            value = value * jnp.asarray(HD ** (-0.5), jnp.bfloat16)
        dest[:, columns(i)] = value

    loop(WIDE // 256, body)


def half_mask(e, shape):
    lane = lax.broadcasted_iota(jnp.int32, shape, 1)
    return (lane < HD) if e == 0 else (lane >= HD)


def attend_pair(t, q8, k, v_t, ctx_t, stat):
    at = columns(t, 128)
    keys, queries = k[:, at], q8[:, at]
    for e in range(2):
        own = jnp.where(half_mask(e, queries.shape), queries, jnp.zeros_like(queries))
        scores = dot_nt(keys, own)
        top = jnp.max(scores, 0, keepdims=True)
        power = jnp.exp(scores - top)
        total = jnp.sum(power, 0, keepdims=True)
        probs = (power * (1.0 / total)).astype(jnp.bfloat16)
        rows = pl.ds(pl.multiple_of(t * 128 + e * 64, 64), 64)
        ctx_t[rows, :] = dot(v_t[rows, :], probs).astype(jnp.bfloat16)
        stat[2 * t + e, :, :] = top + jnp.log(total)


def norm_rows(values, gain, shift):
    center = values - mean_of(values)
    inv = lax.rsqrt(mean_of(center * center) + EPS_NORM)
    normed = center * inv
    return normed * gain + shift, normed, inv


SLICE = 64


def row_loop(body):
    loop(TOKENS // SLICE, lambda i: body(pl.ds(pl.multiple_of(i * SLICE, SLICE), SLICE)))


def gelu_both(value):
    phi = 0.5 * (1.0 + lax.erf(value * math.sqrt(0.5)))
    density = jnp.exp(-0.5 * value * value) * (1.0 / math.sqrt(2.0 * math.pi))
    return value * phi, phi + value * density


def forward_kernel(
    cols, outw, down, hidden, ids, boxes, cotangent, vec,
    full_out, layer_out, x_out, q_out, k_out, kt_out, v_out, ctx_out, stat_out, mid_out, hat_out, inv_out, act_out, slope_out,
    two_out, sums_out,
    w, x_t, mid_t, k_t, x_ref, x_low, q8, k, v, v_t, ctx_t, ctx, stat, acc, mid, mid_low, hat, inv, act, slope, y_out, two, sums,
    load, along, onward, arrived, beside, store, spill,
):
    z, core, x, y, near = position()
    p = 2 * y + x
    meet(z, near)

    def own(kk, h):
        if kk < 7:
            return cols.at[kk, pl.ds(h * 512, 512), :]
        if kk == 7:
            return outw.at[pl.ds(h * 128, 128), :]
        return down.at[kk - 8, pl.ds(h * 128, 128), :]

    def spot(s, kk, h):
        if kk < 7:
            return w.at[kk, pl.ds(h * 512, 512), pl.ds(pl.multiple_of(s * 256, 256), 256)]
        return w.at[kk, pl.ds(pl.multiple_of(s * 256 + h * 128, 128), 128), :]

    def spot_whole(s, kk):
        if kk < 7:
            return w.at[kk, :, pl.ds(pl.multiple_of(s * 256, 256), 256)]
        return w.at[kk, pl.ds(pl.multiple_of(s * 256, 256), 256), :]

    def whole_own(kk):
        if kk < 7:
            return cols.at[kk]
        return outw if kk == 7 else down.at[kk - 8]

    def to(source, s, kk, send_sem, recv_sem, name):
        return pltpu.make_async_remote_copy(
            src_ref=source,
            dst_ref=spot(s, kk, core),
            send_sem=send_sem,
            recv_sem=recv_sem.at[s, kk],
            device_id=near[name],
            device_id_type=MESH,
        )

    def first(g, act_on):
        for t in range(3):
            kk = ORDER[3 * g + t]
            mine = (p == t) | (p == 3) if t == 0 else p == t

            @pl.when(mine & (z < 3))
            def _(kk=kk):
                act_on(to(own(kk, core), z, kk, along.at[kk], arrived, "u"))

            @pl.when(mine & (z > 0))
            def _(kk=kk):
                act_on(to(own(kk, core), z, kk, onward.at[0, z, kk], arrived, "v"))

    far = 3 * (1 - z // 2)
    nearest = z + 1 - 2 * (z // 3)
    strips = (nearest, 6 - nearest - far - z, far)

    def item(n, t):
        return strips[n % 3], ORDER[3 * (n // 3) + t]

    def go(s, kk, kind, name, sems):
        return to(spot(s, kk, core), s, kk, onward.at[kind, s, kk], sems, name)

    def stage(n, hop, begin):
        for t in range(3):
            s, kk = item(n, t)
            who = {
                (0, 0): (p == 0) | (p == 3),
                (0, 1): p == 1,
                (0, 2): p == 2,
                (1, 0): (p == 1) | (p == 2),
                (1, 1): (p == 0) | (p == 3),
                (1, 2): (p == 0) | (p == 3),
                (2, 0): None,
                (2, 1): p == 2,
                (2, 2): p == 1,
            }[hop, t]
            if who is None:
                continue

            @pl.when(who)
            def _(s=s, kk=kk, t=t):
                if begin:
                    go(s, kk, 0, "x", arrived).wait_recv()

                def act_on(copy):
                    if begin:
                        copy.start()
                    else:
                        copy.wait_send()

                if hop == 0:

                    @pl.when((s > z) & (z > 0))
                    def _():
                        act_on(go(s, kk, 0, "v", arrived))

                    @pl.when((s < z) & (z < 3))
                    def _():
                        act_on(go(s, kk, 0, "u", arrived))

                    if t == 0:

                        @pl.when(p == 0)
                        def _():
                            act_on(go(s, kk, 1, "x", arrived))
                            act_on(go(s, kk, 2, "y", arrived))
                    else:
                        act_on(go(s, kk, 1, "x", arrived))
                        act_on(go(s, kk, 2, "y", arrived))
                if hop == 1 and t == 1:

                    @pl.when(p == 3)
                    def _():
                        act_on(go(s, kk, 1, "x", arrived))

                if hop == 1 and t == 2:

                    @pl.when(p == 3)
                    def _():
                        act_on(go(s, kk, 2, "y", arrived))

                act_on(go(s, kk, 3, "c", beside))

    copies = []

    def keep(source, dest):
        copy = pltpu.make_async_copy(source, dest, spill.at[len(copies)])
        copy.start()
        copies.append(copy)

    def ready(kk):
        pltpu.make_async_copy(whole_own(kk), spot_whole(z, kk), load.at[kk]).wait()
        for s in strips:
            pltpu.make_async_remote_copy(
                src_ref=spot(s, kk, 1 - core),
                dst_ref=spot(s, kk, 1 - core),
                send_sem=onward.at[3, s, kk],
                recv_sem=beside.at[s, kk],
                device_id=near["c"],
                device_id_type=MESH,
            ).wait_recv()
        copy = pltpu.make_async_copy(w.at[kk], full_out.at[kk], store.at[kk])
        copy.start()

    def unit_embed():
        embed_tokens(hidden, ids, boxes, x_ref, x_low)
        transpose_into(x_t, x_low)
        keep(x_t, x_out)

    def unit_qkv():
        for kk in range(3):
            ready(kk)
        project(x_low, w.at[0], q8, vec.at[6:7], True)
        project(x_low, w.at[1], k, None, False)
        project(x_low, w.at[2], v, vec.at[7:8], False)
        transpose_into(v_t, v)
        transpose_into(k_t, k)
        keep(q8, q_out)
        keep(k_t, kt_out)
        keep(k, k_out)
        keep(v, v_out)

    def unit_attend(lo, hi):
        loop(hi - lo, lambda i: attend_pair(lo + i, q8, k, v_t, ctx_t, stat))

    def unit_context():
        transpose_back(ctx, ctx_t)
        keep(ctx, ctx_out)
        keep(stat, stat_out)

    def unit_mid():
        ready(7)

        def tile(i):
            acc[:, columns(i)] = dot(ctx[...], w[7, :, columns(i)])

        loop(WIDE // 256, tile)

        def rows(r):
            value = x_ref[r, :] + acc[r, :] + vec[0:1, :]
            out, normed, scale = norm_rows(value, vec[2:3, :], vec[3:4, :])
            mid[r, :] = out
            mid_low[r, :] = out.astype(jnp.bfloat16)
            hat[r, :] = normed
            inv[r, :] = jnp.broadcast_to(scale, (SLICE, 128))

        row_loop(rows)
        transpose_into(mid_t, mid_low)
        keep(mid_t, mid_out)
        keep(hat, hat_out)
        keep(inv, inv_out)

    def unit_up(u):
        ready(3 + u)
        def tile(i):
            at = columns(i)
            slot = i % 2

            @pl.when(i >= 2)
            def _():
                pltpu.make_async_copy(slope.at[slot], slope_out.at[u, :, at], store.at[12 + slot]).wait()

            for part in range(2):
                rows = pl.ds(part * 256, 256)
                value = dot(mid_low[rows, :], w[3 + u, :, at]) + vec[8 + u : 9 + u, at]
                out, grad = gelu_both(value)
                act[u, rows, at] = out.astype(jnp.bfloat16)
                slope[slot, rows, :] = grad
            pltpu.make_async_copy(slope.at[slot], slope_out.at[u, :, at], store.at[12 + slot]).start()

        loop(WIDE // 256, tile)
        for slot in range(2):
            pltpu.make_async_copy(slope.at[slot], slope_out.at[u, :, columns(slot)], store.at[12 + slot]).wait()
        keep(act.at[u], act_out.at[u])

    def unit_down(u):
        ready(8 + u)

        def tile(i):
            at = columns(i)
            value = dot(act[u], w[8 + u, :, at])
            acc[:, at] = value if u == 0 else acc[:, at] + value

        loop(WIDE // 256, tile)

    def unit_last():
        sums[...] = jnp.zeros_like(sums)

        def rows(r):
            value = mid[r, :] + acc[r, :] + vec[1:2, :]
            out, normed, scale = norm_rows(value, vec[4:5, :], vec[5:6, :])
            y_out[r, :] = out
            grad = cotangent[r, :].astype(jnp.float32)
            scaled = grad * vec[4:5, :]
            arg = scale * (scaled - mean_of(scaled) - normed * mean_of(scaled * normed))
            two[r, :] = arg
            sums[1:2, :] += jnp.sum(arg, 0, keepdims=True)
            sums[4:5, :] += jnp.sum(grad * normed, 0, keepdims=True)
            sums[5:6, :] += jnp.sum(grad, 0, keepdims=True)

        row_loop(rows)
        keep(y_out, layer_out)
        keep(two, two_out)
        keep(sums, sums_out)

    first(0, lambda copy: copy.start())
    first(1, lambda copy: copy.start())
    for kk in ORDER:
        pltpu.make_async_copy(whole_own(kk), spot_whole(z, kk), load.at[kk]).start()
    unit_embed()
    after = {
        4: unit_qkv,
        5: lambda: unit_attend(0, 4),
        6: lambda: (unit_attend(4, 8), unit_context()),
        7: unit_mid,
        8: lambda: unit_up(0),
        9: lambda: unit_up(1),
        10: lambda: unit_up(2),
        11: lambda: unit_up(3),
        12: lambda: unit_down(0),
        13: lambda: (unit_down(1), unit_down(2), unit_down(3), unit_last()),
    }
    for n in range(14):
        if n in (3, 6):
            first(n // 3 + 1, lambda copy: copy.start())
        for hop in range(3):
            if 0 <= n - hop < 12:
                stage(n - hop, hop, True)
        if n in after:
            after[n]()
    for n in range(12):
        for hop in range(3):
            stage(n, hop, False)
    for g in range(4):
        first(g, lambda copy: copy.wait_send())
    for kk in ORDER:
        pltpu.make_async_copy(w.at[kk], full_out.at[kk], store.at[kk]).wait()
    for copy in copies:
        copy.wait()


def forward(cols, outw, down, hidden, ids, boxes, cotangent, vec):
    anywhere = pl.BlockSpec(memory_space=pl.ANY)
    vmem = pl.BlockSpec(memory_space=pltpu.VMEM)
    dma = pltpu.SemaphoreType.DMA
    low, wide = jnp.bfloat16, jnp.float32
    page = (TOKENS, WIDE)
    outs = [
        ((12, WIDE, WIDE), low),
        (page, wide),
        ((WIDE, TOKENS), low),
        (page, low),
        (page, low),
        ((WIDE, TOKENS), low),
        (page, low),
        (page, low),
        ((H, 1, TOKENS), wide),
        ((WIDE, TOKENS), low),
        (page, wide),
        ((TOKENS, 128), wide),
        ((4,) + page, low),
        ((4,) + page, wide),
        (page, wide),
        ((16, WIDE), wide),
    ]
    return pl.pallas_call(
        forward_kernel,
        name="forward",
        out_shape=[jax.ShapeDtypeStruct(*o) for o in outs],
        in_specs=[anywhere] * 3 + [vmem] * 5,
        out_specs=[anywhere] * len(outs),
        scratch_shapes=[
            pltpu.VMEM((12, WIDE, WIDE), low),
            pltpu.VMEM((WIDE, TOKENS), low),
            pltpu.VMEM((WIDE, TOKENS), low),
            pltpu.VMEM((WIDE, TOKENS), low),
            pltpu.VMEM(page, wide),
            pltpu.VMEM(page, low),
            pltpu.VMEM(page, low),
            pltpu.VMEM(page, low),
            pltpu.VMEM(page, low),
            pltpu.VMEM((WIDE, TOKENS), low),
            pltpu.VMEM((WIDE, TOKENS), low),
            pltpu.VMEM(page, low),
            pltpu.VMEM((H, 1, TOKENS), wide),
            pltpu.VMEM(page, wide),
            pltpu.VMEM(page, wide),
            pltpu.VMEM(page, low),
            pltpu.VMEM(page, wide),
            pltpu.VMEM((TOKENS, 128), wide),
            pltpu.VMEM((4,) + page, low),
            pltpu.VMEM((2, TOKENS, 256), wide),
            pltpu.VMEM(page, wide),
            pltpu.VMEM(page, wide),
            pltpu.VMEM((16, WIDE), wide),
            dma((12,)),
            dma((12,)),
            dma((4, 4, 12)),
            dma((4, 12)),
            dma((4, 12)),
            dma((14,)),
            dma((20,)),
        ],
        compiler_params=pltpu.CompilerParams(
            collective_id=1, has_side_effects=True, vmem_limit_bytes=61 << 20
        ),
    )(cols, outw, down, hidden, ids, boxes, cotangent, vec)


KEPT = ((8, 5, 9, 4, 0, 1), (3, 10, 11, 6, 7, 2))
EARLY = (((0, 8), (0, 3)), ((1, 5), (1, 10)), ((2, 9), (2, 11)), ((3, 4), (3, 6)), (None, (4, 7)))
LATE = (((4, 0), (5, 2)), ((5, 1), None))
UNIT_ORDER = (0, 2, 1, 3)
RING = 3


def pick(values, e):
    out = values[0]
    for at in range(1, len(values)):
        if values[at] != values[at - 1]:
            out = out + (values[at] - values[at - 1]) * lax.div(e + 8 - at, 8)
    return out


def attend_pair_back(t, q8, k, v, ctx_grad, k_t, stat, dq_t, dk, dv):
    at = columns(t, 128)
    keys, queries, values, grads = k[:, at], q8[:, at], v[:, at], ctx_grad[:, at]
    none = jnp.zeros_like(queries)
    key_sum = value_sum = None
    for e in range(2):
        mask = half_mask(e, queries.shape)
        own_q = jnp.where(mask, queries, none)
        own_g = jnp.where(mask, grads, none)
        probs = jnp.exp(dot_nt(keys, own_q) - stat[2 * t + e])
        prob_grad = dot_nt(values, own_g)
        carried = jnp.sum(probs * prob_grad, 0, keepdims=True)
        score_grad = (probs * (prob_grad - carried)).astype(jnp.bfloat16)
        rows = pl.ds(pl.multiple_of(t * 128 + e * 64, 64), 64)
        dq_t[rows, :] = (dot(k_t[rows, :], score_grad) * HD ** (-0.5)).astype(jnp.bfloat16)
        key_part = dot(score_grad, own_q)
        value_part = dot(probs.astype(jnp.bfloat16), own_g)
        key_sum = key_part if e == 0 else key_sum + key_part
        value_sum = value_part if e == 0 else value_sum + value_part
    dk[:, at] = key_sum.astype(jnp.bfloat16)
    dv[:, at] = value_sum.astype(jnp.bfloat16)


class Stream:
    def __init__(self, entries, chunk, lag, refs, ring, place):
        self.z, self.core, self.x, self.y, self.d = place
        self.p = 2 * self.y + self.x
        self.chunk, self.per, self.lag = chunk, WIDE // chunk, lag
        self.count = len(entries) * self.per
        self.entries, self.refs, self.ring = entries, refs, ring
        self.steps = self.count + 6 * lag + 5

    def where(self, m):
        e, r = lax.div(m, self.per), lax.rem(m, self.per)
        slots = [[(0, 0, -1) if item is None else (item[0], item[1], 1) for item in (pair[c] for pair in self.entries)] for c in range(2)]

        def both(function):
            a = pick([function(item) for item in slots[0]], e)
            b = pick([function(item) for item in slots[1]], e)
            return a + self.core * (b - a)

        q = both(lambda item: item[0])
        j = both(lambda item: item[1] // 4)
        i = both(lambda item: item[1] % 2)
        live = both(lambda item: item[2])
        return q, j, i, r, live

    def rows(self, r):
        return pl.ds(pl.multiple_of(r * self.chunk, self.chunk), self.chunk)

    def remote(self, source, dest, send_sem, recv_sem, device):
        return pltpu.make_async_remote_copy(
            src_ref=source, dst_ref=dest, send_sem=send_sem, recv_sem=recv_sem,
            device_id=device, device_id_type=MESH,
        )

    def role(self, j, r):
        jx, jy = lax.rem(j, 2), lax.div(j, 2)
        rx = self.x + jx - 2 * self.x * jx
        ry = self.y + jy - 2 * self.y * jy
        odd = lax.rem(r, 2)
        first = rx + odd - 2 * rx * odd
        second = ry + odd - 2 * ry * odd
        even_code = 3 - 3 * rx - ry + 2 * rx * ry
        odd_code = 3 - 3 * ry - rx + 2 * rx * ry
        return even_code + odd * (odd_code - even_code), odd

    def along(self, pos, odd):
        turn = odd if pos != 1 else 1 - odd
        return (self.d + turn * (2 - 4 * self.x) + (1 - turn) * (4 - 8 * self.y), self.z)

    def forward(self, q, r, pos, odd):
        R = self.refs
        at = self.rows(r)
        return self.remote(R["mine"].at[q, at, :], R["land"].at[q, at, :], R["send"].at[q, r], R["recv"].at[q, r], self.along(pos, odd))

    def landed(self, q, r):
        R = self.refs
        at = self.rows(r)
        return self.remote(R["land"].at[q, at, :], R["land"].at[q, at, :], R["send"].at[q, r], R["recv"].at[q, r], (self.d, self.z))

    def chained(self, i, r, way):
        R = self.refs
        at = self.rows(r)
        ref = R["chain"].at[way, i, at, :]
        return ref, R["chain_send"].at[way, i, r], R["chain_recv"].at[way, i, r]

    def pass_on(self, source, i, r, way):
        ref, ssem, rsem = self.chained(i, r, way)
        return self.remote(source, ref, ssem, rsem, (self.d, self.z + (1 if way == 0 else -1)))

    def total_out(self, source, i, r):
        R = self.refs
        return pltpu.make_async_copy(source, R["total"].at[i, self.rows(r), :], R["out"].at[i, r])

    def add_to_mine(self, q, r, ref):
        at = self.rows(r)
        mine = self.refs["mine"]
        mine[q, at, :] = (mine[q, at, :].astype(jnp.float32) + ref[...].astype(jnp.float32)).astype(jnp.bfloat16)

    def guarded(self, m, function):
        @pl.when((m >= 0) & (m < self.count))
        def _():
            q, j, i, r, live = self.where(m)

            @pl.when(live > 0)
            def _():
                function(m, q, j, i, r)


    def begin_pair(self, m, q, j, i, r):
        R = self.refs
        quarter = 256 // self.chunk

        @pl.when(lax.rem(r, quarter) == 0)
        def _():
            f = lax.div(r, quarter)
            at = pl.ds(pl.multiple_of(f * 256, 256), 256)
            self.remote(R["sib"].at[q, at, :], R["sib"].at[q, at, :], R["give_send"].at[q, f], R["give_recv"].at[q, f], (self.d, self.z)).wait_recv()

        slot = lax.rem(m, 2)
        pltpu.make_async_copy(R["sib"].at[q, self.rows(r), :], self.ring.at[0, slot], R["ring_sem"].at[0, slot]).start()

    def end_pair(self, m, q, j, i, r):
        R = self.refs
        slot = lax.rem(m, 2)
        pltpu.make_async_copy(R["sib"].at[q, self.rows(r), :], self.ring.at[0, slot], R["ring_sem"].at[0, slot]).wait()
        self.add_to_mine(q, r, self.ring.at[0, slot])
        pos, odd = self.role(j, r)

        @pl.when(pos == 0)
        def _():
            self.forward(q, r, 0, odd).start()

    def begin_path(self, step_pos):
        def run(m, q, j, i, r):
            pos, odd = self.role(j, r)
            R = self.refs

            @pl.when(pos == step_pos)
            def _():
                slot = lax.rem(m, 2)
                self.landed(q, r).wait_recv()
                pltpu.make_async_copy(R["land"].at[q, self.rows(r), :], self.ring.at[step_pos, slot], R["ring_sem"].at[step_pos, slot]).start()

        return run

    def end_path(self, step_pos):
        def run(m, q, j, i, r):
            pos, odd = self.role(j, r)
            R = self.refs

            @pl.when(pos == step_pos)
            def _():
                slot = lax.rem(m, 2)
                pltpu.make_async_copy(R["land"].at[q, self.rows(r), :], self.ring.at[step_pos, slot], R["ring_sem"].at[step_pos, slot]).wait()
                self.add_to_mine(q, r, self.ring.at[step_pos, slot])
                if step_pos < 3:
                    self.forward(q, r, step_pos, odd).start()
                else:
                    mine = R["mine"].at[q, self.rows(r), :]

                    @pl.when(self.z == 0)
                    def _():
                        self.pass_on(mine, i, r, 0).start()

                    @pl.when(self.z == 3)
                    def _():
                        self.pass_on(mine, i, r, 1).start()

        return run

    def link(self, q, i, r, way, last):
        R = self.refs
        at = self.rows(r)
        ref, ssem, rsem = self.chained(i, r, way)
        self.remote(ref, ref, ssem, rsem, (self.d, self.z)).wait_recv()
        came = ref[...].astype(jnp.float32)
        mine = R["mine"]
        ref[...] = (mine[q, at, :].astype(jnp.float32) + came).astype(jnp.bfloat16)
        self.pass_on(ref, i, r, way).start()
        if last:
            other = R["chain"][1 - way, i, at, :].astype(jnp.float32)
            mine[q, at, :] = (other + came).astype(jnp.bfloat16)
            self.total_out(mine.at[q, at, :], i, r).start()

    def links(self, last):
        def run(m, q, j, i, r):
            for z, way in ((1, 1 if last else 0), (2, 0 if last else 1)):

                @pl.when((self.p == j) & (self.z == z))
                def _(way=way):
                    self.link(q, i, r, way, last)

        return run

    def ends(self, m, q, j, i, r):
        R = self.refs
        at = self.rows(r)
        for z, way in ((0, 1), (3, 0)):

            @pl.when((self.p == j) & (self.z == z))
            def _(way=way):
                ref, ssem, rsem = self.chained(i, r, way)
                self.remote(ref, ref, ssem, rsem, (self.d, self.z)).wait_recv()
                ref[...] = (R["mine"][q, at, :].astype(jnp.float32) + ref[...].astype(jnp.float32)).astype(jnp.bfloat16)
                self.total_out(ref, i, r).start()

    def step(self, n):
        L = self.lag
        parts = [
            (0, self.begin_pair),
            (1, self.end_pair),
            (1 + L, self.begin_path(1)),
            (2 + L, self.end_path(1)),
            (2 + 2 * L, self.begin_path(2)),
            (3 + 2 * L, self.end_path(2)),
            (3 + 3 * L, self.begin_path(3)),
            (4 + 3 * L, self.end_path(3)),
            (4 + 4 * L, self.links(False)),
            (4 + 5 * L, self.links(True)),
            (4 + 6 * L, self.ends),
        ]
        for lag, part in reversed(parts):
            self.guarded(n - lag, part)

    def finish(self, m):
        def run(m, q, j, i, r):
            pos, odd = self.role(j, r)

            @pl.when(pos < 3)
            def _():
                self.forward(q, r, 0, odd).wait_send()

            mine = self.refs["mine"].at[q, self.rows(r), :]

            @pl.when((pos == 3) & (self.z < 3))
            def _():
                self.pass_on(mine, i, r, 0).wait_send()

            @pl.when((pos == 3) & (self.z > 0))
            def _():
                self.pass_on(mine, i, r, 1).wait_send()

            @pl.when(pos == 3)
            def _():
                self.total_out(mine, i, r).wait()

        self.guarded(m, run)


def backward_kernel(
    full, x_in, q_in, k_in, kt_in, v_in, ctx_in, stat_in, mid_in, hat_in, inv_in, act_in, slope_in, two_in, sums_in, vec,
    input_out, total, sums, sib, land,
    w, pb, pt, pf, stat, inv, stage, mine, chain, ring_a, ring_b, vec_in,
    wsem, asem, ssem, isem, osem,
    give_send, give_recv, send_a, recv_a, chain_send_a, chain_recv_a, out_a, ring_sem_a,
    send_b, recv_b, chain_send_b, chain_recv_b, out_b, ring_sem_b, vec_send, vec_recv,
):
    z, core, x, y, near = position()
    p = 2 * y + x
    d = 2 * p + core
    z_one = (d, z + 1 - 2 * (z % 2))
    z_two = (d, z + 2 - 4 * (z // 2))
    shared = {"mine": mine, "land": land, "chain": chain, "sib": sib, "total": total, "give_send": give_send, "give_recv": give_recv}
    place = (z, core, x, y, d)
    early = Stream(EARLY, CHUNK_EARLY, LAG_EARLY, dict(
        shared, send=send_a, recv=recv_a, chain_send=chain_send_a, chain_recv=chain_recv_a, out=out_a, ring_sem=ring_sem_a,
    ), ring_a, place)
    late = Stream(LATE, CHUNK_LATE, LAG_LATE, dict(
        shared, send=send_b, recv=recv_b, chain_send=chain_send_b, chain_recv=chain_recv_b, out=out_b, ring_sem=ring_sem_b,
    ), ring_b, place)

    two_low, act_ring, up_grad = pb.at[0], (pb.at[1], pb.at[2]), pb.at[3]
    k, q8, v = pb.at[4], pb.at[5], pb.at[6]
    one_low, ctx, ctx_grad, dq, dk, dv = pb.at[0], pb.at[1], pb.at[2], pb.at[0], pb.at[1], pb.at[3]
    two_t, mid_t, k_t = pt.at[0], pt.at[1], pt.at[2]
    one_t, x_t, dq_t = pt.at[0], pt.at[1], pt.at[0]
    two, back, slope_ring = pf.at[0], pf.at[1], (pf.at[2], pf.at[3])
    one, hat = pf.at[0], pf.at[2]
    uses = [slot for u in UNIT_ORDER for slot in (8 + u, 3 + u)] + [7, 0, 1, 2]

    def weight(n):
        return pltpu.make_async_copy(full.at[uses[n]], w.at[n % RING], wsem.at[n % RING])

    def act_load(n):
        return pltpu.make_async_copy(act_in.at[UNIT_ORDER[n]], act_ring[n % 2], asem.at[n % 2])

    def slope_load(n):
        return pltpu.make_async_copy(slope_in.at[UNIT_ORDER[n]], slope_ring[n % 2], ssem.at[n % 2])

    loads = {}

    def fetch(name, source, dest):
        loads[name] = pltpu.make_async_copy(source, dest, isem.at[len(loads)])
        loads[name].start()

    fetch("two", two_in, two)
    weight(0).start()
    slope_load(0).start()
    act_load(0).start()
    fetch("mid", mid_in, mid_t)
    weight(1).start()
    fetch("sums", sums_in, sums)
    weight(2).start()
    slope_load(1).start()
    act_load(1).start()
    for name, source, dest in (
        ("inv", inv_in, inv), ("k", k_in, k), ("q", q_in, q8), ("v", v_in, v), ("kt", kt_in, k_t), ("stat", stat_in, stat),
    ):
        fetch(name, source, dest)
    meet(z, near, (z_two,))

    counter = {"early": 0, "late": 0, "whole": 0}
    produced = set()

    def run(count, body, per=0, every=1, stream=early, name="early"):
        base = counter[name]
        total_steps = (count // every) * per

        def one_turn(i):
            body(i)
            if per:
                if every == 1:
                    for s in range(per):
                        stream.step(base + i * per + s)
                else:

                    @pl.when(lax.rem(i, every) == every - 1)
                    def _():
                        for s in range(per):
                            stream.step(base + lax.div(i, every) * per + s)

        if per:
            have = 0
            for pair in stream.entries:
                if all(item is None or item[1] in produced for item in pair):
                    have += 1
                else:
                    break
            limit = stream.steps if have == len(stream.entries) else have * stream.per
            assert base + total_steps <= limit, (name, base, total_steps, limit)
        loop(count, one_turn)
        counter[name] = base + total_steps

    def use(n):
        weight(n).wait()
        return w.at[n % RING]

    def done(n):
        if n + RING < 12:
            weight(n + RING).start()

    given = {0: [], 1: []}

    def give(slot, c, n, f):
        at = pl.ds(f * 256, 256)
        q = KEPT[1 - c].index(slot)
        return pltpu.make_async_remote_copy(
            src_ref=stage.at[n % 2, at, :], dst_ref=sib.at[q, at, :], send_sem=give_send.at[q, f],
            recv_sem=give_recv.at[q, f], device_id=near["c"], device_id_type=MESH,
        )

    def block(slot, left_t, right, **steps):
        owner = (slot // 2) % 2
        giver = 1 - owner
        q = KEPT[owner].index(slot)
        n = len(given[giver])
        if n >= 2:

            @pl.when(core == giver)
            def _():
                for f in range(4):
                    give(given[giver][n - 2], giver, n - 2, f).wait_send()

        def tile(i):
            value = dot(left_t[...], right[:, columns(i)]).astype(jnp.bfloat16)

            @pl.when(core == owner)
            def _():
                mine[q, :, columns(i)] = value

            @pl.when(core == giver)
            def _():
                stage[n % 2, :, columns(i)] = value

        run(WIDE // 256, tile, **steps)

        @pl.when(core == giver)
        def _():
            for f in range(4):
                give(slot, giver, n, f).start()

        given[giver].append(slot)
        produced.add(slot)

    def token_sum(row, ref):
        def tile(i):
            at = columns(i)
            sums[row : row + 1, at] = jnp.sum(ref[:, at].astype(jnp.float32), 0, keepdims=True)

        loop(WIDE // 256, tile)

    @pl.when(p == 3)
    def _():
        chain[0] = jnp.zeros(chain.shape[1:], chain.dtype)
        pltpu.make_async_copy(chain.at[0], total, osem.at[1]).start()

    loads["two"].wait()

    def to_low(r):
        two_low[r, :] = two[r, :].astype(jnp.bfloat16)

    row_loop(to_low)
    transpose_into(two_t, two_low)
    loads["mid"].wait()
    loads["sums"].wait()
    for n, u in enumerate(UNIT_ORDER):
        pace = PACE[n]
        weights = use(2 * n)
        slope_load(n).wait()
        act_load(n).wait()
        slope = slope_ring[n % 2]

        def tile(i):
            rows = columns(i)
            grad = dot_nt(two_low[...], weights[rows, :]) * slope[:, rows]
            up_grad[:, rows] = grad.astype(jnp.bfloat16)

        run(WIDE // 256, tile, **pace[0])
        done(2 * n)
        if n == 2:
            fetch("hat", hat_in, hat)
        token_sum(8 + u, up_grad)
        block(8 + u, two_t, act_ring[n % 2], **pace[1])
        if n == 2:
            fetch("ctx", ctx_in, ctx)
        weights = use(2 * n + 1)

        def tile_back(i):
            at = columns(i)
            value = dot_nt(up_grad[...], weights[at, :])
            back[:, at] = two[:, at] + value if n == 0 else back[:, at] + value

        run(WIDE // 256, tile_back, **pace[2])
        done(2 * n + 1)
        block(3 + u, mid_t, up_grad, **pace[3])
        if n + 2 < 4:
            slope_load(n + 2).start()
            act_load(n + 2).start()
    fetch("x", x_in, x_t)
    for name in ("hat", "inv"):
        loads[name].wait()
    sums[0:1, :] = jnp.zeros((1, WIDE), jnp.float32)
    sums[2:4, :] = jnp.zeros((2, WIDE), jnp.float32)

    def rows(i):
        r = pl.ds(pl.multiple_of(i * SLICE, SLICE), SLICE)
        grad, normed = back[r, :], hat[r, :]
        scaled = grad * vec[2:3, :]
        arg = inv[r, 0:1] * (scaled - mean_of(scaled) - normed * mean_of(scaled * normed))
        one[r, :] = arg
        one_low[r, :] = arg.astype(jnp.bfloat16)
        sums[0:1, :] += jnp.sum(arg, 0, keepdims=True)
        sums[2:3, :] += jnp.sum(grad * normed, 0, keepdims=True)
        sums[3:4, :] += jnp.sum(grad, 0, keepdims=True)

    run(TOKENS // SLICE, rows, **PACE[4])
    transpose_into(one_t, one_low)
    weights = use(8)

    def tile_ctx(i):
        at = columns(i)
        ctx_grad[:, at] = dot_nt(one_low[...], weights[at, :]).astype(jnp.bfloat16)

    run(WIDE // 256, tile_ctx, **PACE[5])
    done(8)
    loads["ctx"].wait()
    block(7, one_t, ctx, **PACE[6])
    for name in ("k", "q", "v", "kt", "stat"):
        loads[name].wait()
    run(H // 2, lambda t: attend_pair_back(t, q8, k, v, ctx_grad, k_t, stat, dq_t, dk, dv), **PACE[7])
    transpose_back(dq, dq_t)
    loads["x"].wait()
    block(0, x_t, dq, **PACE[8])
    block(2, x_t, dv, **PACE[8])
    block(1, x_t, dk, **PACE[8])

    def vec_hop(h):
        device = (near["c"], near["x"], near["y"], z_one, z_two)[h]
        return pltpu.make_async_remote_copy(
            src_ref=sums, dst_ref=vec_in.at[h], send_sem=vec_send.at[h], recv_sem=vec_recv.at[h],
            device_id=device, device_id_type=MESH,
        )

    token_sum(6, dq)
    token_sum(7, dv)
    vec_hop(0).start()
    hop = 0
    tail = {"early": counter["early"], "late": 0}

    def both(count, rate, body=None):
        base_late, base_early = tail["late"], tail["early"]

        def turn(i):
            if body is not None:
                body(i)

            for s in range(rate):
                early.step(base_early + i * rate + s)
            late.step(base_late + i)

        loop(count, turn)
        tail["late"] += count
        tail["early"] += count * rate

    for kk, grad in ((0, dq), (1, dk), (2, dv)):
        weights = use(9 + kk)

        def tile_in(i):
            at = columns(i)
            one[:, at] = one[:, at] + dot_nt(grad[...], weights[at, :])

        both(WIDE // 256, EARLY_RATE, tile_in)
    out = pltpu.make_async_copy(one, input_out, osem.at[0])
    out.start()
    for h in range(5):
        vec_hop(h).wait()
        sums[...] = sums[...] + vec_in[h]
        if h < 4:
            vec_hop(h + 1).start()
            both(4, EARLY_RATE)
    left = max(0, -(-(early.steps - tail["early"]) // EARLY_RATE))
    both(min(left, late.steps - tail["late"]), EARLY_RATE)
    loop(late.steps - tail["late"], lambda i, base=tail["late"]: late.step(base + i))
    assert tail["early"] >= early.steps

    for c in range(2):

        @pl.when(core == c)
        def _(c=c):
            n = len(given[c])
            for back_by in (2, 1):
                for f in range(4):
                    give(given[c][n - back_by], c, n - back_by, f).wait_send()

    loop(early.count, early.finish)
    loop(late.count, late.finish)
    out.wait()

    @pl.when(p == 3)
    def _():
        pltpu.make_async_copy(chain.at[0], total, osem.at[1]).wait()


CHUNK_EARLY, CHUNK_LATE = 128, 64
LAG_EARLY, LAG_LATE = 2, 3
EARLY_RATE = 1
NO = {}
SLOW = {"per": 1, "every": 2}
ONE = {"per": 1}
PACE = (
    (NO, NO, NO, NO),
    (SLOW, SLOW, SLOW, SLOW),
    (SLOW, SLOW, SLOW, SLOW),
    (NO, NO, SLOW, SLOW),
    {"per": 1, "every": 4},
    SLOW,
    SLOW,
    {"per": 1, "every": 2},
    SLOW,
)


def backward(full, x, q, k, kt, v, ctx, stat, mid, hat, inv, act, slope, two, sums, vec):
    anywhere = pl.BlockSpec(memory_space=pl.ANY)
    vmem = pl.BlockSpec(memory_space=pltpu.VMEM)
    dma = pltpu.SemaphoreType.DMA
    low, wide = jnp.bfloat16, jnp.float32
    page = (TOKENS, WIDE)
    many_a, many_b = WIDE // CHUNK_EARLY, WIDE // CHUNK_LATE

    def stream_sems(many):
        return [dma((6, many)), dma((6, many)), dma((2, 2, many)), dma((2, 2, many)), dma((2, many)), dma((4, 2))]

    return pl.pallas_call(
        backward_kernel,
        name="backward",
        out_shape=[
            jax.ShapeDtypeStruct(page, wide),
            jax.ShapeDtypeStruct((2, WIDE, WIDE), low),
            jax.ShapeDtypeStruct((16, WIDE), wide),
            jax.ShapeDtypeStruct((6, WIDE, WIDE), low),
            jax.ShapeDtypeStruct((6, WIDE, WIDE), low),
        ],
        in_specs=[anywhere] * 15 + [vmem],
        out_specs=[anywhere, anywhere, vmem, anywhere, anywhere],
        scratch_shapes=[
            pltpu.VMEM((RING, WIDE, WIDE), low),
            pltpu.VMEM((7,) + page, low),
            pltpu.VMEM((3, WIDE, TOKENS), low),
            pltpu.VMEM((4,) + page, wide),
            pltpu.VMEM((H, 1, TOKENS), wide),
            pltpu.VMEM((TOKENS, 128), wide),
            pltpu.VMEM((2, WIDE, WIDE), low),
            pltpu.VMEM((6, WIDE, WIDE), low),
            pltpu.VMEM((2, 2, WIDE, WIDE), low),
            pltpu.VMEM((4, 2, CHUNK_EARLY, WIDE), low),
            pltpu.VMEM((4, 2, CHUNK_LATE, WIDE), low),
            pltpu.VMEM((5, 16, WIDE), wide),
            dma((RING,)), dma((2,)), dma((2,)), dma((12,)), dma((2,)),
            dma((6, 4)), dma((6, 4)),
            *stream_sems(many_a),
            *stream_sems(many_b),
            dma((5,)), dma((5,)),
        ],
        compiler_params=pltpu.CompilerParams(
            collective_id=2, has_side_effects=True, vmem_limit_bytes=62 << 20
        ),
    )(full, x, q, k, kt, v, ctx, stat, mid, hat, inv, act, slope, two, sums, vec)


def layout_embed(cell_boxes, cell_ids):
    cell_count = cell_boxes.shape[1]
    onehot = (
        cell_ids[:, :, None] == jnp.arange(cell_count, dtype=jnp.int32)[None, None, :]
    ).astype(jnp.float32)
    corners = jnp.einsum("psc,pck->psk", onehot, cell_boxes.astype(jnp.float32), precision=PRECISE)
    quarter = MODEL_WIDTH // 4
    half_width = quarter // 2
    frequency = jnp.exp(
        -jnp.arange(half_width, dtype=jnp.float32) * (math.log(1000.0) / half_width)
    )
    angle_grid = corners[..., None] * frequency
    wave_table = jnp.concatenate([jnp.sin(angle_grid), jnp.cos(angle_grid)], -1)
    return 0.5 * wave_table.reshape(corners.shape[0], corners.shape[1], MODEL_WIDTH)


def gelu_exact(values):
    return jax.nn.gelu(values, approximate=False)


def norm_forward(values, gain, shift):
    center = values - jnp.mean(values, -1, keepdims=True)
    inv_std = lax.rsqrt(jnp.mean(center * center, -1, keepdims=True) + EPS_NORM)
    normed = center * inv_std
    return (normed * gain + shift, normed, inv_std)


def norm_backward(grad_in, normed, inv_std, gain):
    scaled = grad_in * gain
    grad_arg = inv_std * (
        scaled
        - jnp.mean(scaled, -1, keepdims=True)
        - normed * jnp.mean(scaled * normed, -1, keepdims=True)
    )
    return (grad_arg, jnp.sum(grad_in * normed, (0, 1)), jnp.sum(grad_in, (0, 1)))


def attend(query_low, key_low, value_low, head_count):
    groups, seq_len = (query_low.shape[0], query_low.shape[1])
    shape_heads = (groups, seq_len, head_count, HD)
    scores = jnp.einsum(
        "gqhe,gkhe->ghqk",
        query_low.reshape(shape_heads),
        key_low.reshape(shape_heads),
        preferred_element_type=jnp.float32,
    ) * HD ** (-0.5)
    row_max = jnp.max(scores, -1, keepdims=True)
    log_total = row_max + jnp.log(jnp.sum(jnp.exp(scores - row_max), -1, keepdims=True))
    probs = jnp.exp(scores - log_total).astype(jnp.bfloat16)
    context = jnp.einsum(
        "ghqk,gkhe->gqhe", probs, value_low.reshape(shape_heads), preferred_element_type=jnp.float32
    )
    return (context.reshape(groups, seq_len, head_count * HD).astype(jnp.bfloat16), log_total)


def attend_back(query_low, key_low, value_low, log_total, ctx_grad, head_count):
    groups, seq_len = (query_low.shape[0], query_low.shape[1])
    shape_heads = (groups, seq_len, head_count, HD)
    query_heads = query_low.reshape(shape_heads)
    key_heads = key_low.reshape(shape_heads)
    value_heads = value_low.reshape(shape_heads)
    grad_heads = ctx_grad.reshape(shape_heads)
    scale = HD ** (-0.5)
    scores = (
        jnp.einsum("gqhe,gkhe->ghqk", query_heads, key_heads, preferred_element_type=jnp.float32)
        * scale
    )
    probs = jnp.exp(scores - log_total)
    value_grad = jnp.einsum(
        "ghqk,gqhe->gkhe",
        probs.astype(jnp.bfloat16),
        grad_heads,
        preferred_element_type=jnp.float32,
    )
    prob_grad = jnp.einsum(
        "gqhe,gkhe->ghqk", grad_heads, value_heads, preferred_element_type=jnp.float32
    )
    score_grad = (probs * (prob_grad - jnp.sum(probs * prob_grad, -1, keepdims=True))).astype(
        jnp.bfloat16
    )
    query_grad = (
        jnp.einsum("ghqk,gkhe->gqhe", score_grad, key_heads, preferred_element_type=jnp.float32)
        * scale
    )
    key_grad = (
        jnp.einsum("ghqk,gqhe->gkhe", score_grad, query_heads, preferred_element_type=jnp.float32)
        * scale
    )
    width = head_count * HD
    return (
        query_grad.reshape(groups, seq_len, width).astype(jnp.bfloat16),
        key_grad.reshape(groups, seq_len, width).astype(jnp.bfloat16),
        value_grad.reshape(groups, seq_len, width).astype(jnp.bfloat16),
    )


def by_collectives(
    hidden, cell_ids, cell_boxes, cotangent, weight_cols, weight_out, weight_down, vectors, slot_dev
):
    dp_count = lax.axis_size("dp")
    col_mats = lax.all_gather(weight_cols, "tp", axis=2, tiled=True)
    out_mat = lax.all_gather(weight_out, "tp", axis=0, tiled=True)
    down_mats = lax.all_gather(weight_down, "tp", axis=1, tiled=True)
    x_own = hidden.astype(jnp.float32) + layout_embed(cell_boxes, cell_ids)
    x_low = x_own.astype(jnp.bfloat16)
    projected = jnp.einsum(
        "gtd,kdc->kgtc", x_low, col_mats[0:3], preferred_element_type=jnp.float32
    )
    query_low = (projected[0] + vectors[:, 6]).astype(jnp.bfloat16)
    key_low = projected[1].astype(jnp.bfloat16)
    value_low = (projected[2] + vectors[:, 7]).astype(jnp.bfloat16)
    context, log_total = attend(query_low, key_low, value_low, H)
    attn_out = jnp.einsum("gtc,cd->gtd", context, out_mat, preferred_element_type=jnp.float32)
    mid_out, mid_hat, mid_inv = norm_forward(
        x_own + attn_out + vectors[:, 0], vectors[:, 2], vectors[:, 3]
    )
    mid_low = mid_out.astype(jnp.bfloat16)
    up_pre = jnp.einsum(
        "gtd,kdc->kgtc", mid_low, col_mats[3:7], preferred_element_type=jnp.float32
    )
    up_pre = up_pre + jnp.transpose(vectors[:, 8:12])[:, None, None, :]
    act_low = gelu_exact(up_pre).astype(jnp.bfloat16)
    ffn_out = jnp.einsum("kgtc,kcd->gtd", act_low, down_mats, preferred_element_type=jnp.float32)
    layer_out, out_hat, out_inv = norm_forward(
        mid_out + ffn_out + vectors[:, 1], vectors[:, 4], vectors[:, 5]
    )
    output_gradient = cotangent.astype(jnp.float32)
    grad_two, gain_two, shift_two = norm_backward(output_gradient, out_hat, out_inv, vectors[:, 4])
    two_low = grad_two.astype(jnp.bfloat16)
    act_grad = jnp.einsum("gtd,kcd->kgtc", two_low, down_mats, preferred_element_type=jnp.float32)
    gelu_pull = jax.vjp(gelu_exact, up_pre)[1]
    up_low = gelu_pull(act_grad)[0].astype(jnp.bfloat16)
    mid_back = jnp.einsum(
        "kgtc,kdc->gtd", up_low, col_mats[3:7], preferred_element_type=jnp.float32
    )
    grad_one, gain_one, shift_one = norm_backward(
        mid_back + grad_two, mid_hat, mid_inv, vectors[:, 2]
    )
    one_low = grad_one.astype(jnp.bfloat16)
    ctx_grad = jnp.einsum(
        "gtd,cd->gtc", one_low, out_mat, preferred_element_type=jnp.float32
    ).astype(jnp.bfloat16)
    query_grad, key_grad, value_grad = attend_back(
        query_low, key_low, value_low, log_total, ctx_grad, H
    )
    qkv_grad = jnp.stack([query_grad, key_grad, value_grad], 0)
    input_grad = grad_one + jnp.einsum(
        "kgtc,kdc->gtd", qkv_grad, col_mats[0:3], preferred_element_type=jnp.float32
    )

    def block(text, left, right):
        return jnp.einsum(text, left, right, preferred_element_type=jnp.float32).astype(
            jnp.bfloat16
        )

    qkv_blocks = block("gtd,kgtc->kdc", x_low, qkv_grad)
    up_blocks = block("gtd,kgtc->kdc", mid_low, up_low)
    out_block = block("gtd,gtc->dc", one_low, context)[None]
    down_blocks = block("gtd,kgtc->kdc", two_low, act_low)
    vector_part = jnp.stack(
        [
            jnp.sum(grad_one, (0, 1)),
            jnp.sum(grad_two, (0, 1)),
            gain_one,
            shift_one,
            gain_two,
            shift_two,
            jnp.sum(query_grad, (0, 1), dtype=jnp.float32),
            jnp.sum(value_grad, (0, 1), dtype=jnp.float32),
        ],
        0,
    )
    vector_part = jnp.concatenate(
        [vector_part, jnp.sum(up_low, (1, 2), dtype=jnp.float32)], 0
    )
    block_part = jnp.concatenate(
        [
            qkv_blocks,
            up_blocks,
            out_block,
            down_blocks,
            jnp.zeros((slot_dev * dp_count - 12, MODEL_WIDTH, MODEL_WIDTH), jnp.bfloat16),
        ],
        0,
    )
    block_owned = lax.psum_scatter(block_part, "dp", scatter_dimension=0, tiled=True)
    full_grad = lax.psum(block_owned, "tp")
    vector_all = lax.psum(vector_part, ("dp", "tp"))
    return layer_out, input_grad, full_grad, vector_all


def local(
    hidden,
    cell_ids,
    cell_boxes,
    cotangent,
    weight_cols,
    weight_out,
    weight_down,
    vectors,
    vector_moment,
    left_stat,
    right_stat,
    left_root,
    right_root,
    master,
    averaged_weight,
):
    tp_count = lax.axis_size("tp")
    dp_count = lax.axis_size("dp")
    tp_index = lax.axis_index("tp")
    dp_index = lax.axis_index("dp")
    strip_width = weight_cols.shape[2]
    page_rows, seq_len = (hidden.shape[0], hidden.shape[1])
    owned_rows = vector_moment.shape[0]
    slot_dev = left_stat.shape[0]
    if dp_count == 8 and tp_count == 4:
        vec = jnp.transpose(vectors)
        full, layer_out, *kept, sums = forward(
            weight_cols, weight_out, weight_down, hidden[0], cell_ids, cell_boxes[0], cotangent[0], vec
        )
        input_grad, full_grad, vector_all, *_ = backward(full, *kept, sums, vec)
        layer_out, input_grad = layer_out[None], input_grad[None]
    else:
        layer_out, input_grad, full_grad, vector_all = by_collectives(
            hidden, cell_ids, cell_boxes, cotangent, weight_cols, weight_out, weight_down, vectors, slot_dev
        )
    vector_grad = jnp.transpose(
        lax.dynamic_slice_in_dim(vector_all[0:12], dp_index * owned_rows, owned_rows, 1)
    )
    own_rows = lax.dynamic_slice_in_dim(full_grad, tp_index * strip_width, strip_width, 1)
    own_cols = lax.dynamic_slice_in_dim(full_grad, tp_index * strip_width, strip_width, 2)
    block_grad = own_cols.astype(jnp.float32)
    left_new = STAT_DECAY * left_stat + (1.0 - STAT_DECAY) * jnp.einsum(
        "sic,sjc->sij", own_rows, full_grad, preferred_element_type=jnp.float32
    )
    right_new = STAT_DECAY * right_stat + (1.0 - STAT_DECAY) * jnp.einsum(
        "sic,sij->scj", own_cols, full_grad, preferred_element_type=jnp.float32
    )

    def parts(array):
        high = array.astype(jnp.bfloat16)
        return high, (array - high.astype(jnp.float32)).astype(jnp.bfloat16)

    def product(left, right):
        return jnp.einsum("sij,sjc->sic", left, right, preferred_element_type=jnp.float32)

    left_high, left_rest = parts(left_root)
    right_high, right_rest = parts(right_root)
    precond = product(left_high, full_grad) + product(left_rest, full_grad)
    pre_high, pre_rest = parts(precond)
    precond = (
        product(pre_high, right_high) + product(pre_rest, right_high) + product(pre_high, right_rest)
    )
    master_new = master - BLOCK_RATE * precond
    weight_copy = master_new.astype(jnp.bfloat16)
    ema_new = EMA_DECAY * averaged_weight + (1.0 - EMA_DECAY) * master_new
    vector_rows = lax.dynamic_slice_in_dim(vectors, dp_index * owned_rows, owned_rows, 0)
    moment_new = MOMENTUM * vector_moment + vector_grad
    total_tokens = page_rows * seq_len * dp_count * tp_count
    vector_new = vector_rows - VEC_RATE * lax.rsqrt(jnp.float32(total_tokens)) * moment_new
    bias_grad = vector_grad[:, 0]
    return (
        layer_out,
        input_grad,
        block_grad,
        left_new,
        right_new,
        master_new,
        weight_copy,
        ema_new,
        vector_grad,
        moment_new,
        vector_new,
        bias_grad,
    )


def solution(mesh):
    return jax.shard_map(
        local,
        mesh=mesh,
        in_specs=(
            P(("dp", "tp"), None, None),
            P(("dp", "tp"), None),
            P(("dp", "tp"), None, None),
            P(("dp", "tp"), None, None),
            P(None, None, "tp"),
            P("tp", None),
            P(None, "tp", None),
            P(),
            P("dp", None),
            P("dp", "tp", None),
            P("dp", "tp", None),
            P("dp", "tp", None),
            P("dp", None, None),
            P("dp", "tp", None),
            P("dp", "tp", None),
        ),
        out_specs=(
            P(("dp", "tp"), None, None),
            P(("dp", "tp"), None, None),
            P("dp", None, "tp"),
            P("dp", "tp", None),
            P("dp", "tp", None),
            P("dp", "tp", None),
            P("dp", "tp", None),
            P("dp", "tp", None),
            P("dp", None),
            P("dp", None),
            P("dp", None),
            P("dp"),
        ),
        check_vma=False,
    )
```

```python
import math

import jax
import jax.numpy as jnp
from jax import lax
from jax.experimental import pallas as pl
from jax.experimental.pallas import tpu as pltpu
from jax.sharding import PartitionSpec as P

MODEL_WIDTH = 1024
H = 16
HD = 64

PRECISE = lax.Precision.HIGHEST
EPS_NORM = 1e-06
STAT_DECAY = 0.5
BLOCK_RATE = 0.7
EMA_DECAY = 0.9
MOMENTUM = 0.9
VEC_RATE = 0.2

MESH = pl.DeviceIdType.MESH


def position():
    d, z = lax.axis_index("dp"), lax.axis_index("tp")
    core, x, y = d % 2, (d // 2) % 2, d // 4
    near = {
        "x": (d + 2 - 4 * x, z),
        "y": (d + 4 - 8 * y, z),
        "c": (d + 1 - 2 * core, z),
        "u": (d, z + 1),
        "v": (d, z - 1),
    }
    return z, core, x, y, near


def meet(z, near, extra=()):
    barrier = pltpu.get_barrier_semaphore()
    always = [near[name] for name in "xyc"] + list(extra)
    for device in always:
        pl.semaphore_signal(barrier, 1, device_id=device, device_id_type=MESH)

    @pl.when(z < 3)
    def _():
        pl.semaphore_signal(barrier, 1, device_id=near["u"], device_id_type=MESH)

    @pl.when(z > 0)
    def _():
        pl.semaphore_signal(barrier, 1, device_id=near["v"], device_id_type=MESH)

    pl.semaphore_wait(barrier, len(always) + (z + 2) // 3 + (5 - z) // 3)


ORDER = (0, 1, 2, 7, 3, 4, 5, 6, 8, 9, 10, 11)


NT = (((1,), (1,)), ((), ()))
TOKENS = 512
WIDE = MODEL_WIDTH


def dot(a, b):
    return jnp.dot(a, b, preferred_element_type=jnp.float32)


def dot_nt(a, b):
    return lax.dot_general(a, b, NT, preferred_element_type=jnp.float32)


def columns(i, width=256):
    return pl.ds(pl.multiple_of(i * width, width), width)


def loop(count, body):
    def step(i, carry):
        body(i)
        return carry

    lax.fori_loop(0, count, step, 0)


def mean_of(rows):
    return jnp.sum(rows, -1, keepdims=True) * (1.0 / WIDE)


def transpose_into(dest, source):
    def body(i):
        dest[columns(i), :] = source[:, columns(i)].T

    loop(WIDE // 256, body)


def transpose_back(dest, source):
    def body(i):
        dest[:, columns(i)] = source[columns(i), :].T

    loop(WIDE // 256, body)


def embed_tokens(hidden, ids, boxes, x_ref, x_low):
    cells = boxes.shape[0]
    half = WIDE // 8
    place = lax.broadcasted_iota(jnp.int32, (1, half), 1).astype(jnp.float32)
    rate = jnp.exp(place * (-math.log(1000.0) / half))
    marks = lax.broadcasted_iota(jnp.int32, (cells, TOKENS), 0) == ids[...]
    chosen = jnp.where(marks, 1.0, 0.0).T.astype(jnp.bfloat16)
    for c in range(4):
        angle = boxes[:, c : c + 1].astype(jnp.float32) * rate
        for kind, wave in enumerate((jnp.sin(angle), jnp.cos(angle))):
            wave = 0.5 * wave
            high = wave.astype(jnp.bfloat16)
            rest = wave - high.astype(jnp.float32)
            middle = rest.astype(jnp.bfloat16)
            low = (rest - middle.astype(jnp.float32)).astype(jnp.bfloat16)
            emb = dot(chosen, high) + (dot(chosen, middle) + dot(chosen, low))
            at = pl.ds(c * 2 * half + kind * half, half)
            value = hidden[:, at].astype(jnp.float32) + emb
            x_ref[:, at] = value
            x_low[:, at] = value.astype(jnp.bfloat16)


def project(x_low, weight, dest, bias, scale):
    def body(i):
        value = dot(x_low[...], weight[:, columns(i)])
        if bias is not None:
            value = value + bias[:, columns(i)]
        value = value.astype(jnp.bfloat16)
        if scale:
            value = value * jnp.asarray(HD ** (-0.5), jnp.bfloat16)
        dest[:, columns(i)] = value

    loop(WIDE // 256, body)


def half_mask(e, shape):
    lane = lax.broadcasted_iota(jnp.int32, shape, 1)
    return (lane < HD) if e == 0 else (lane >= HD)


def attend_pair(t, q8, k, v_t, ctx_t, stat):
    at = columns(t, 128)
    keys, queries = k[:, at], q8[:, at]
    for e in range(2):
        own = jnp.where(half_mask(e, queries.shape), queries, jnp.zeros_like(queries))
        scores = dot_nt(keys, own)
        top = jnp.max(scores, 0, keepdims=True)
        power = jnp.exp(scores - top)
        total = jnp.sum(power, 0, keepdims=True)
        probs = (power * (1.0 / total)).astype(jnp.bfloat16)
        rows = pl.ds(pl.multiple_of(t * 128 + e * 64, 64), 64)
        ctx_t[rows, :] = dot(v_t[rows, :], probs).astype(jnp.bfloat16)
        stat[2 * t + e, :, :] = top + jnp.log(total)


def norm_rows(values, gain, shift):
    center = values - mean_of(values)
    inv = lax.rsqrt(mean_of(center * center) + EPS_NORM)
    normed = center * inv
    return normed * gain + shift, normed, inv


SLICE = 64


def row_loop(body):
    loop(TOKENS // SLICE, lambda i: body(pl.ds(pl.multiple_of(i * SLICE, SLICE), SLICE)))


def gelu_both(value):
    phi = 0.5 * (1.0 + lax.erf(value * math.sqrt(0.5)))
    density = jnp.exp(-0.5 * value * value) * (1.0 / math.sqrt(2.0 * math.pi))
    return value * phi, phi + value * density


def forward_kernel(
    cols, outw, down, hidden, ids, boxes, cotangent, vec,
    full_out, layer_out, x_out, q_out, k_out, kt_out, v_out, ctx_out, stat_out, mid_out, hat_out, inv_out, act_out, slope_out,
    two_out, sums_out,
    w, x_t, mid_t, k_t, x_ref, x_low, q8, k, v, v_t, ctx_t, ctx, stat, acc, mid, mid_low, hat, inv, act, slope, y_out, two, sums,
    load, along, onward, arrived, beside, store, spill,
):
    z, core, x, y, near = position()
    p = 2 * y + x
    meet(z, near)

    def own(kk, h):
        if kk < 7:
            return cols.at[kk, pl.ds(h * 512, 512), :]
        if kk == 7:
            return outw.at[pl.ds(h * 128, 128), :]
        return down.at[kk - 8, pl.ds(h * 128, 128), :]

    def spot(s, kk, h):
        if kk < 7:
            return w.at[kk, pl.ds(h * 512, 512), pl.ds(pl.multiple_of(s * 256, 256), 256)]
        return w.at[kk, pl.ds(pl.multiple_of(s * 256 + h * 128, 128), 128), :]

    def spot_whole(s, kk):
        if kk < 7:
            return w.at[kk, :, pl.ds(pl.multiple_of(s * 256, 256), 256)]
        return w.at[kk, pl.ds(pl.multiple_of(s * 256, 256), 256), :]

    def whole_own(kk):
        if kk < 7:
            return cols.at[kk]
        return outw if kk == 7 else down.at[kk - 8]

    def to(source, s, kk, send_sem, recv_sem, name):
        return pltpu.make_async_remote_copy(
            src_ref=source,
            dst_ref=spot(s, kk, core),
            send_sem=send_sem,
            recv_sem=recv_sem.at[s, kk],
            device_id=near[name],
            device_id_type=MESH,
        )

    def first(g, act_on):
        for t in range(3):
            kk = ORDER[3 * g + t]
            mine = (p == t) | (p == 3) if t == 0 else p == t

            @pl.when(mine & (z < 3))
            def _(kk=kk):
                act_on(to(own(kk, core), z, kk, along.at[kk], arrived, "u"))

            @pl.when(mine & (z > 0))
            def _(kk=kk):
                act_on(to(own(kk, core), z, kk, onward.at[0, z, kk], arrived, "v"))

    far = 3 * (1 - z // 2)
    nearest = z + 1 - 2 * (z // 3)
    strips = (nearest, 6 - nearest - far - z, far)

    def item(n, t):
        return strips[n % 3], ORDER[3 * (n // 3) + t]

    def go(s, kk, kind, name, sems):
        return to(spot(s, kk, core), s, kk, onward.at[kind, s, kk], sems, name)

    def stage(n, hop, begin):
        for t in range(3):
            s, kk = item(n, t)
            who = {
                (0, 0): (p == 0) | (p == 3),
                (0, 1): p == 1,
                (0, 2): p == 2,
                (1, 0): (p == 1) | (p == 2),
                (1, 1): (p == 0) | (p == 3),
                (1, 2): (p == 0) | (p == 3),
                (2, 0): None,
                (2, 1): p == 2,
                (2, 2): p == 1,
            }[hop, t]
            if who is None:
                continue

            @pl.when(who)
            def _(s=s, kk=kk, t=t):
                if begin:
                    go(s, kk, 0, "x", arrived).wait_recv()

                def act_on(copy):
                    if begin:
                        copy.start()
                    else:
                        copy.wait_send()

                if hop == 0:

                    @pl.when((s > z) & (z > 0))
                    def _():
                        act_on(go(s, kk, 0, "v", arrived))

                    @pl.when((s < z) & (z < 3))
                    def _():
                        act_on(go(s, kk, 0, "u", arrived))

                    if t == 0:

                        @pl.when(p == 0)
                        def _():
                            act_on(go(s, kk, 1, "x", arrived))
                            act_on(go(s, kk, 2, "y", arrived))
                    else:
                        act_on(go(s, kk, 1, "x", arrived))
                        act_on(go(s, kk, 2, "y", arrived))
                if hop == 1 and t == 1:

                    @pl.when(p == 3)
                    def _():
                        act_on(go(s, kk, 1, "x", arrived))

                if hop == 1 and t == 2:

                    @pl.when(p == 3)
                    def _():
                        act_on(go(s, kk, 2, "y", arrived))

                act_on(go(s, kk, 3, "c", beside))

    copies = []

    def keep(source, dest):
        copy = pltpu.make_async_copy(source, dest, spill.at[len(copies)])
        copy.start()
        copies.append(copy)

    def ready(kk):
        pltpu.make_async_copy(whole_own(kk), spot_whole(z, kk), load.at[kk]).wait()
        for s in strips:
            pltpu.make_async_remote_copy(
                src_ref=spot(s, kk, 1 - core),
                dst_ref=spot(s, kk, 1 - core),
                send_sem=onward.at[3, s, kk],
                recv_sem=beside.at[s, kk],
                device_id=near["c"],
                device_id_type=MESH,
            ).wait_recv()
        copy = pltpu.make_async_copy(w.at[kk], full_out.at[kk], store.at[kk])
        copy.start()

    def unit_embed():
        embed_tokens(hidden, ids, boxes, x_ref, x_low)
        transpose_into(x_t, x_low)
        keep(x_t, x_out)

    def unit_qkv():
        for kk in range(3):
            ready(kk)
        project(x_low, w.at[0], q8, vec.at[6:7], True)
        project(x_low, w.at[1], k, None, False)
        project(x_low, w.at[2], v, vec.at[7:8], False)
        transpose_into(v_t, v)
        transpose_into(k_t, k)
        keep(q8, q_out)
        keep(k_t, kt_out)
        keep(k, k_out)
        keep(v, v_out)

    def unit_attend(lo, hi):
        loop(hi - lo, lambda i: attend_pair(lo + i, q8, k, v_t, ctx_t, stat))

    def unit_context():
        transpose_back(ctx, ctx_t)
        keep(ctx, ctx_out)
        keep(stat, stat_out)

    def unit_mid():
        ready(7)

        def tile(i):
            acc[:, columns(i)] = dot(ctx[...], w[7, :, columns(i)])

        loop(WIDE // 256, tile)

        def rows(r):
            value = x_ref[r, :] + acc[r, :] + vec[0:1, :]
            out, normed, scale = norm_rows(value, vec[2:3, :], vec[3:4, :])
            mid[r, :] = out
            mid_low[r, :] = out.astype(jnp.bfloat16)
            hat[r, :] = normed
            inv[r, :] = jnp.broadcast_to(scale, (SLICE, 128))

        row_loop(rows)
        transpose_into(mid_t, mid_low)
        keep(mid_t, mid_out)
        keep(hat, hat_out)
        keep(inv, inv_out)

    def unit_up(u):
        ready(3 + u)
        def tile(i):
            at = columns(i)
            slot = i % 2

            @pl.when(i >= 2)
            def _():
                pltpu.make_async_copy(slope.at[slot], slope_out.at[u, :, at], store.at[12 + slot]).wait()

            for part in range(2):
                rows = pl.ds(part * 256, 256)
                value = dot(mid_low[rows, :], w[3 + u, :, at]) + vec[8 + u : 9 + u, at]
                out, grad = gelu_both(value)
                act[u, rows, at] = out.astype(jnp.bfloat16)
                slope[slot, rows, :] = grad
            pltpu.make_async_copy(slope.at[slot], slope_out.at[u, :, at], store.at[12 + slot]).start()

        loop(WIDE // 256, tile)
        for slot in range(2):
            pltpu.make_async_copy(slope.at[slot], slope_out.at[u, :, columns(slot)], store.at[12 + slot]).wait()
        keep(act.at[u], act_out.at[u])

    def unit_down(u):
        ready(8 + u)

        def tile(i):
            at = columns(i)
            value = dot(act[u], w[8 + u, :, at])
            acc[:, at] = value if u == 0 else acc[:, at] + value

        loop(WIDE // 256, tile)

    def unit_last():
        sums[...] = jnp.zeros_like(sums)

        def rows(r):
            value = mid[r, :] + acc[r, :] + vec[1:2, :]
            out, normed, scale = norm_rows(value, vec[4:5, :], vec[5:6, :])
            y_out[r, :] = out
            grad = cotangent[r, :].astype(jnp.float32)
            scaled = grad * vec[4:5, :]
            arg = scale * (scaled - mean_of(scaled) - normed * mean_of(scaled * normed))
            two[r, :] = arg
            sums[1:2, :] += jnp.sum(arg, 0, keepdims=True)
            sums[4:5, :] += jnp.sum(grad * normed, 0, keepdims=True)
            sums[5:6, :] += jnp.sum(grad, 0, keepdims=True)

        row_loop(rows)
        keep(y_out, layer_out)
        keep(two, two_out)
        keep(sums, sums_out)

    first(0, lambda copy: copy.start())
    first(1, lambda copy: copy.start())
    for kk in ORDER:
        pltpu.make_async_copy(whole_own(kk), spot_whole(z, kk), load.at[kk]).start()
    unit_embed()
    after = {
        4: unit_qkv,
        5: lambda: unit_attend(0, 4),
        6: lambda: (unit_attend(4, 8), unit_context()),
        7: unit_mid,
        8: lambda: unit_up(0),
        9: lambda: unit_up(1),
        10: lambda: unit_up(2),
        11: lambda: unit_up(3),
        12: lambda: unit_down(0),
        13: lambda: (unit_down(1), unit_down(2), unit_down(3), unit_last()),
    }
    for n in range(14):
        if n in (3, 6):
            first(n // 3 + 1, lambda copy: copy.start())
        for hop in range(3):
            if 0 <= n - hop < 12:
                stage(n - hop, hop, True)
        if n in after:
            after[n]()
    for n in range(12):
        for hop in range(3):
            stage(n, hop, False)
    for g in range(4):
        first(g, lambda copy: copy.wait_send())
    for kk in ORDER:
        pltpu.make_async_copy(w.at[kk], full_out.at[kk], store.at[kk]).wait()
    for copy in copies:
        copy.wait()


def forward(cols, outw, down, hidden, ids, boxes, cotangent, vec):
    anywhere = pl.BlockSpec(memory_space=pl.ANY)
    vmem = pl.BlockSpec(memory_space=pltpu.VMEM)
    dma = pltpu.SemaphoreType.DMA
    low, wide = jnp.bfloat16, jnp.float32
    page = (TOKENS, WIDE)
    outs = [
        ((12, WIDE, WIDE), low),
        (page, wide),
        ((WIDE, TOKENS), low),
        (page, low),
        (page, low),
        ((WIDE, TOKENS), low),
        (page, low),
        (page, low),
        ((H, 1, TOKENS), wide),
        ((WIDE, TOKENS), low),
        (page, wide),
        ((TOKENS, 128), wide),
        ((4,) + page, low),
        ((4,) + page, wide),
        (page, wide),
        ((16, WIDE), wide),
    ]
    return pl.pallas_call(
        forward_kernel,
        name="forward",
        out_shape=[jax.ShapeDtypeStruct(*o) for o in outs],
        in_specs=[anywhere] * 3 + [vmem] * 5,
        out_specs=[anywhere] * len(outs),
        scratch_shapes=[
            pltpu.VMEM((12, WIDE, WIDE), low),
            pltpu.VMEM((WIDE, TOKENS), low),
            pltpu.VMEM((WIDE, TOKENS), low),
            pltpu.VMEM((WIDE, TOKENS), low),
            pltpu.VMEM(page, wide),
            pltpu.VMEM(page, low),
            pltpu.VMEM(page, low),
            pltpu.VMEM(page, low),
            pltpu.VMEM(page, low),
            pltpu.VMEM((WIDE, TOKENS), low),
            pltpu.VMEM((WIDE, TOKENS), low),
            pltpu.VMEM(page, low),
            pltpu.VMEM((H, 1, TOKENS), wide),
            pltpu.VMEM(page, wide),
            pltpu.VMEM(page, wide),
            pltpu.VMEM(page, low),
            pltpu.VMEM(page, wide),
            pltpu.VMEM((TOKENS, 128), wide),
            pltpu.VMEM((4,) + page, low),
            pltpu.VMEM((2, TOKENS, 256), wide),
            pltpu.VMEM(page, wide),
            pltpu.VMEM(page, wide),
            pltpu.VMEM((16, WIDE), wide),
            dma((12,)),
            dma((12,)),
            dma((4, 4, 12)),
            dma((4, 12)),
            dma((4, 12)),
            dma((14,)),
            dma((20,)),
        ],
        compiler_params=pltpu.CompilerParams(
            collective_id=1, has_side_effects=True, vmem_limit_bytes=61 << 20
        ),
    )(cols, outw, down, hidden, ids, boxes, cotangent, vec)


KEPT = ((8, 5, 9, 0, 1, 4), (10, 3, 11, 2, 6, 7))
EARLY = (((0, 8), (0, 10), 0), ((1, 5), None, 0), (None, (1, 3), 0), ((2, 9), (2, 11), 8))
LATE = (((3, 0), (3, 2), 0), ((4, 1), None, 0), ((5, 4), (4, 6), 0), (None, (5, 7), 0))
UNIT_ORDER = (0, 2, 1, 3)
RING = 3


def attend_pair_back(t, q8, k, v, ctx_grad, k_t, stat, dq_t, dk, dv):
    at = columns(t, 128)
    keys, queries, values, grads = k[:, at], q8[:, at], v[:, at], ctx_grad[:, at]
    none = jnp.zeros_like(queries)
    key_sum = value_sum = None
    for e in range(2):
        mask = half_mask(e, queries.shape)
        own_q = jnp.where(mask, queries, none)
        own_g = jnp.where(mask, grads, none)
        probs = jnp.exp(dot_nt(keys, own_q) - stat[2 * t + e])
        prob_grad = dot_nt(values, own_g)
        carried = jnp.sum(probs * prob_grad, 0, keepdims=True)
        score_grad = (probs * (prob_grad - carried)).astype(jnp.bfloat16)
        rows = pl.ds(pl.multiple_of(t * 128 + e * 64, 64), 64)
        dq_t[rows, :] = (dot(k_t[rows, :], score_grad) * HD ** (-0.5)).astype(jnp.bfloat16)
        key_part = dot(score_grad, own_q)
        value_part = dot(probs.astype(jnp.bfloat16), own_g)
        key_sum = key_part if e == 0 else key_sum + key_part
        value_sum = value_part if e == 0 else value_sum + value_part
    dk[:, at] = key_sum.astype(jnp.bfloat16)
    dv[:, at] = value_sum.astype(jnp.bfloat16)


class Stream:
    def __init__(self, entries, chunk, lag, refs, ring, place):
        self.z, self.core, self.x, self.y, self.d = place
        self.p = 2 * self.y + self.x
        self.chunk, self.per, self.lag = chunk, WIDE // chunk, lag
        self.entries, self.refs, self.ring = entries, refs, ring
        self.steps = max(entry[2] for entry in entries) + self.per + 6 * lag
        x, y = self.x, self.y
        self.corner = [(x if j % 2 == 0 else 1 - x, y if j // 2 == 0 else 1 - y) for j in range(3)]
        self.by_x, self.by_y = 2 - 4 * x, 4 - 8 * y

    def rows(self, r):
        return pl.ds(pl.multiple_of(r * self.chunk, self.chunk), self.chunk)

    def remote(self, source, dest, send_sem, recv_sem, device):
        return pltpu.make_async_remote_copy(
            src_ref=source, dst_ref=dest, send_sem=send_sem, recv_sem=recv_sem,
            device_id=device, device_id_type=MESH,
        )


    def forward(self, q, r, turn):
        R = self.refs
        at = self.rows(r)
        device = (self.d + self.by_y + turn * (self.by_x - self.by_y), self.z)
        return self.remote(R["mine"].at[q, at, :], R["land"].at[q, at, :], R["send"].at[q, r], R["recv"].at[q, r], device)

    def chained(self, i, r, way):
        R = self.refs
        at = self.rows(r)
        return R["chain"].at[way, i, at, :], R["chain_send"].at[way, i, r], R["chain_recv"].at[way, i, r]

    def pass_on(self, source, i, r, way):
        ref, ssem, rsem = self.chained(i, r, way)
        return self.remote(source, ref, ssem, rsem, (self.d, self.z + (1 if way == 0 else -1)))

    def total_out(self, source, i, r):
        R = self.refs
        return pltpu.make_async_copy(source, R["total"].at[i, self.rows(r), :], R["out"].at[i, r])

    def add_to_mine(self, q, r, ref):
        mine = self.refs["mine"]

        def part(g):
            at = pl.ds(pl.multiple_of(r * self.chunk + g * 32, 32), 32)
            here = pl.ds(pl.multiple_of(g * 32, 32), 32)
            mine[q, at, :] = (mine[q, at, :].astype(jnp.float32) + ref[here, :].astype(jnp.float32)).astype(jnp.bfloat16)

        loop(self.chunk // 32, part)

    def load(self, e, kind, q, r):
        source = self.refs["sib" if kind == 0 else "land"]
        return pltpu.make_async_copy(source.at[q, self.rows(r), :], self.ring.at[e, kind], self.refs["ring_sem"].at[e, kind])

    def begin_pair(self, e, q, j, i, r):
        R = self.refs
        quarter = 256 // self.chunk

        def arrival(f):
            at = pl.ds(pl.multiple_of(f * 256, 256), 256)
            ref = R["sib"].at[q, at, :]
            self.remote(ref, ref, R["give_send"].at[q, f], R["give_recv"].at[q, f], (self.d, self.z)).wait_recv()

        if quarter == 1:
            arrival(r)
        else:

            @pl.when(lax.rem(r, quarter) == 0)
            def _():
                arrival(lax.div(r, quarter))

        self.load(e, 0, q, r).start()

    def end_pair(self, e, q, j, i, r):
        self.load(e, 0, q, r).wait()
        self.add_to_mine(q, r, self.ring.at[e, 0])
        odd = lax.rem(r, 2)
        rx, ry = self.corner[j]

        @pl.when((rx + ry == 1) & (rx + odd == 1))
        def _():
            self.forward(q, r, odd).start()

    def path(self, hop, begin):
        def run(e, q, j, i, r):
            odd = lax.rem(r, 2)
            rx, ry = self.corner[j]
            here = {1: rx + ry == 2, 2: (rx + ry == 1) & (rx == odd), 3: rx + ry == 0}[hop]

            @pl.when(here)
            def _():
                copy = self.load(e, 1, q, r)
                if begin:
                    self.forward(q, r, odd).wait_recv()
                    copy.start()
                    return
                copy.wait()
                self.add_to_mine(q, r, self.ring.at[e, 1])
                if hop == 1:
                    self.forward(q, r, 1 - odd).start()
                if hop == 2:
                    self.forward(q, r, odd).start()
                if hop == 3:
                    mine = self.refs["mine"].at[q, self.rows(r), :]

                    @pl.when(self.z == 0)
                    def _():
                        self.pass_on(mine, i, r, 0).start()

                    @pl.when(self.z == 3)
                    def _():
                        self.pass_on(mine, i, r, 1).start()

        return run

    def link(self, q, i, r, way, last):
        R = self.refs
        at = self.rows(r)
        ref, ssem, rsem = self.chained(i, r, way)
        self.remote(ref, ref, ssem, rsem, (self.d, self.z)).wait_recv()
        mine, chain = R["mine"], R["chain"]

        def part(g):
            piece = pl.ds(pl.multiple_of(r * self.chunk + g * 32, 32), 32)
            came = chain[way, i, piece, :].astype(jnp.float32)
            chain[way, i, piece, :] = (mine[q, piece, :].astype(jnp.float32) + came).astype(jnp.bfloat16)
            if last:
                other = chain[1 - way, i, piece, :].astype(jnp.float32)
                mine[q, piece, :] = (other + came).astype(jnp.bfloat16)

        loop(self.chunk // 32, part)
        self.pass_on(ref, i, r, way).start()
        if last:
            self.total_out(mine.at[q, at, :], i, r).start()

    def links(self, last):
        def run(e, q, j, i, r):
            @pl.when(self.p == j)
            def _():
                for z, way in ((1, 1 if last else 0), (2, 0 if last else 1)):

                    @pl.when(self.z == z)
                    def _(way=way):
                        self.link(q, i, r, way, last)

        return run

    def ends(self, e, q, j, i, r):
        R = self.refs
        at = self.rows(r)

        @pl.when(self.p == j)
        def _():
            for z, way in ((0, 1), (3, 0)):

                @pl.when(self.z == z)
                def _(way=way):
                    ref, ssem, rsem = self.chained(i, r, way)
                    self.remote(ref, ref, ssem, rsem, (self.d, self.z)).wait_recv()
                    mine, chain = R["mine"], R["chain"]

                    def part(g):
                        piece = pl.ds(pl.multiple_of(r * self.chunk + g * 32, 32), 32)
                        chain[way, i, piece, :] = (
                            mine[q, piece, :].astype(jnp.float32) + chain[way, i, piece, :].astype(jnp.float32)
                        ).astype(jnp.bfloat16)

                    loop(self.chunk // 32, part)
                    self.total_out(ref, i, r).start()

    def each(self, function):
        for e, entry in enumerate(self.entries):
            here = [item for item in entry[:2] if item is not None]
            if len(here) == 2:
                (q, slot), (q_other, slot_other) = here
                assert slot // 4 == slot_other // 4
                if q != q_other:
                    q = q + self.core * (q_other - q)
                i = slot % 2
                if i != slot_other % 2:
                    i = i + self.core * (slot_other % 2 - i)
                function(e, entry[2], q, slot // 4, i)
            else:
                only = 0 if entry[1] is None else 1

                @pl.when(self.core == only)
                def _(e=e, entry=entry, item=here[0]):
                    function(e, entry[2], item[0], item[1] // 4, item[1] % 2)

    def step(self, n):
        L = self.lag
        begins = ((0, self.begin_pair), (L, self.path(1, True)), (2 * L, self.path(2, True)), (3 * L, self.path(3, True)))
        ends = (
            (6 * L, self.ends),
            (5 * L, self.links(True)),
            (4 * L, self.links(False)),
            (3 * L, self.path(3, False)),
            (2 * L, self.path(2, False)),
            (L, self.path(1, False)),
            (0, self.end_pair),
        )

        def visit(parts):
            def entry_parts(e, start, q, j, i):
                m = n - start

                @pl.when((m >= 0) & (m < self.per + 6 * L))
                def _():
                    for lag, part in parts:
                        r = m - lag

                        @pl.when((r >= 0) & (r < self.per))
                        def _(r=r, part=part):
                            part(e, q, j, i, r)

            self.each(entry_parts)

        visit(begins)
        visit(ends)

    def finish(self):
        def chunk(e, start, q, j, i):
            rx, ry = self.corner[j]

            def body(r):
                @pl.when(rx + ry > 0)
                def _():
                    self.forward(q, r, 0).wait_send()

                mine = self.refs["mine"].at[q, self.rows(r), :]

                @pl.when((rx + ry == 0) & (self.z < 3))
                def _():
                    self.pass_on(mine, i, r, 0).wait_send()

                @pl.when((rx + ry == 0) & (self.z > 0))
                def _():
                    self.pass_on(mine, i, r, 1).wait_send()

                @pl.when(rx + ry == 0)
                def _():
                    self.total_out(mine, i, r).wait()

            loop(self.per, body)

        self.each(chunk)


def backward_kernel(
    full, x_in, q_in, k_in, kt_in, v_in, ctx_in, stat_in, mid_in, hat_in, inv_in, act_in, slope_in, two_in, sums_in, vec,
    input_out, total, sums, sib, land,
    w, pb, pt, pf, stat, inv, stage, mine, chain, ring_a, ring_b, vec_in,
    wsem, asem, ssem, isem, osem,
    give_send, give_recv, send_a, recv_a, chain_send_a, chain_recv_a, out_a, ring_sem_a,
    send_b, recv_b, chain_send_b, chain_recv_b, out_b, ring_sem_b, vec_send, vec_recv,
):
    z, core, x, y, near = position()
    p = 2 * y + x
    d = 2 * p + core
    z_one = (d, z + 1 - 2 * (z % 2))
    z_two = (d, z + 2 - 4 * (z // 2))
    shared = {"mine": mine, "land": land, "chain": chain, "sib": sib, "total": total, "give_send": give_send, "give_recv": give_recv}
    place = (z, core, x, y, d)
    early = Stream(EARLY, CHUNK_EARLY, LAG_EARLY, dict(
        shared, send=send_a, recv=recv_a, chain_send=chain_send_a, chain_recv=chain_recv_a, out=out_a, ring_sem=ring_sem_a,
    ), ring_a, place)
    late = Stream(LATE, CHUNK_LATE, LAG_LATE, dict(
        shared, send=send_b, recv=recv_b, chain_send=chain_send_b, chain_recv=chain_recv_b, out=out_b, ring_sem=ring_sem_b,
    ), ring_b, place)

    two_low, act_ring = pb.at[0], (pb.at[1], pb.at[2])
    up_grads = {0: pb.at[3], 2: pb.at[3], 1: pb.at[7], 3: pb.at[8]}
    k, q8, v = pb.at[4], pb.at[5], pb.at[6]
    one_low, ctx, ctx_grad, dq, dk, dv = pb.at[0], pb.at[1], pb.at[2], pb.at[0], pb.at[9], pb.at[3]
    two_t, mid_t, k_t = pt.at[0], pt.at[1], pt.at[2]
    one_t, x_t, dq_t = pt.at[0], pt.at[3], pt.at[4]
    two, back, slope_ring = pf.at[0], pf.at[1], (pf.at[2], pf.at[3])
    one, hat = pf.at[0], pf.at[2]
    uses = [slot for u in UNIT_ORDER for slot in (8 + u, 3 + u)] + [7, 0, 1, 2]

    def weight(n):
        return pltpu.make_async_copy(full.at[uses[n]], w.at[n % RING], wsem.at[n % RING])

    def act_load(n):
        return pltpu.make_async_copy(act_in.at[UNIT_ORDER[n]], act_ring[n % 2], asem.at[n % 2])

    def slope_load(n):
        return pltpu.make_async_copy(slope_in.at[UNIT_ORDER[n]], slope_ring[n % 2], ssem.at[n % 2])

    loads = {}

    def fetch(name, source, dest):
        loads[name] = pltpu.make_async_copy(source, dest, isem.at[len(loads)])
        loads[name].start()

    fetch("two", two_in, two)
    weight(0).start()
    slope_load(0).start()
    act_load(0).start()
    fetch("mid", mid_in, mid_t)
    weight(1).start()
    fetch("sums", sums_in, sums)
    weight(2).start()
    slope_load(1).start()
    act_load(1).start()
    for name, source, dest in (
        ("inv", inv_in, inv), ("k", k_in, k), ("q", q_in, q8), ("v", v_in, v), ("kt", kt_in, k_t), ("stat", stat_in, stat), ("x", x_in, x_t),
    ):
        fetch(name, source, dest)
    meet(z, near, (z_two,))

    counter = {"early": 0}
    produced = set()

    def run(count, body, at=()):
        base = counter["early"]
        for one_entry in EARLY:
            if at and one_entry[2] < base + len(at):
                assert all(item is None or item[1] in produced for item in one_entry[:2])

        def one_turn(i):
            body(i)
            if at:
                first, stride = at[0], (at[1] - at[0] if len(at) > 1 else count)

                @pl.when((i >= first) & (lax.rem(i - first + stride, stride) == 0))
                def _():
                    early.step(base + lax.div(i - first, stride))

        loop(count, one_turn)
        counter["early"] += len(at)

    def use(n):
        weight(n).wait()
        return w.at[n % RING]

    def done(n):
        if n + RING < 12:
            weight(n + RING).start()

    given = {0: [], 1: []}

    def give(slot, c, n, f):
        at = pl.ds(f * 256, 256)
        q = KEPT[1 - c].index(slot)
        return pltpu.make_async_remote_copy(
            src_ref=stage.at[n % 2, at, :], dst_ref=sib.at[q, at, :], send_sem=give_send.at[q, f],
            recv_sem=give_recv.at[q, f], device_id=near["c"], device_id_type=MESH,
        )

    def block(slot, left_t, right, at=()):
        owner = (slot // 2) % 2
        giver = 1 - owner
        q = KEPT[owner].index(slot)
        n = len(given[giver])
        if n >= 2:

            @pl.when(core == giver)
            def _():
                for f in range(4):
                    give(given[giver][n - 2], giver, n - 2, f).wait_send()

        def tile(i):
            value = dot(left_t[...], right[:, columns(i)]).astype(jnp.bfloat16)

            @pl.when(core == owner)
            def _():
                mine[q, :, columns(i)] = value

            @pl.when(core == giver)
            def _():
                stage[n % 2, :, columns(i)] = value

        run(WIDE // 256, tile, at)

        @pl.when(core == giver)
        def _():
            for f in range(4):
                give(slot, giver, n, f).start()

        given[giver].append(slot)
        produced.add(slot)

    def token_sum(row, ref):
        def tile(i):
            at = columns(i)
            sums[row : row + 1, at] = jnp.sum(ref[:, at].astype(jnp.float32), 0, keepdims=True)

        loop(WIDE // 256, tile)

    @pl.when(p == 3)
    def _():
        chain[0] = jnp.zeros(chain.shape[1:], chain.dtype)
        pltpu.make_async_copy(chain.at[0], total, osem.at[1]).start()

    loads["two"].wait()

    def to_low(r):
        two_low[r, :] = two[r, :].astype(jnp.bfloat16)

    row_loop(to_low)
    transpose_into(two_t, two_low)
    loads["mid"].wait()
    loads["sums"].wait()
    for n, u in enumerate(UNIT_ORDER):
        pace = PACE[n]
        weights = use(2 * n)
        slope_load(n).wait()
        act_load(n).wait()
        slope, up_grad = slope_ring[n % 2], up_grads[u]

        def tile(i):
            rows = columns(i)
            grad = dot_nt(two_low[...], weights[rows, :]) * slope[:, rows]
            up_grad[:, rows] = grad.astype(jnp.bfloat16)

        run(WIDE // 256, tile, pace[0])
        done(2 * n)
        if n == 2:
            fetch("hat", hat_in, hat)
        token_sum(8 + u, up_grad)
        block(8 + u, two_t, act_ring[n % 2], pace[1])
        if n == 2:
            fetch("ctx", ctx_in, ctx)
        weights = use(2 * n + 1)

        def tile_back(i):
            at = columns(i)
            value = dot_nt(up_grad[...], weights[at, :])
            back[:, at] = two[:, at] + value if n == 0 else back[:, at] + value

        run(WIDE // 256, tile_back, pace[2])
        done(2 * n + 1)
        if n < 2:
            block(3 + u, mid_t, up_grad, pace[3])
        if n + 2 < 4:
            slope_load(n + 2).start()
            act_load(n + 2).start()
    for name in ("hat", "inv"):
        loads[name].wait()
    sums[0:1, :] = jnp.zeros((1, WIDE), jnp.float32)
    sums[2:4, :] = jnp.zeros((2, WIDE), jnp.float32)

    def rows(i):
        r = pl.ds(pl.multiple_of(i * SLICE, SLICE), SLICE)
        grad, normed = back[r, :], hat[r, :]
        scaled = grad * vec[2:3, :]
        arg = inv[r, 0:1] * (scaled - mean_of(scaled) - normed * mean_of(scaled * normed))
        one[r, :] = arg
        one_low[r, :] = arg.astype(jnp.bfloat16)
        sums[0:1, :] += jnp.sum(arg, 0, keepdims=True)
        sums[2:3, :] += jnp.sum(grad * normed, 0, keepdims=True)
        sums[3:4, :] += jnp.sum(grad, 0, keepdims=True)

    run(TOKENS // SLICE, rows, PACE[4])
    transpose_into(one_t, one_low)
    weights = use(8)

    def tile_ctx(i):
        at = columns(i)
        ctx_grad[:, at] = dot_nt(one_low[...], weights[at, :]).astype(jnp.bfloat16)

    run(WIDE // 256, tile_ctx, PACE[5])
    done(8)
    for name in ("k", "q", "v", "kt", "stat"):
        loads[name].wait()
    run(H // 2, lambda t: attend_pair_back(t, q8, k, v, ctx_grad, k_t, stat, dq_t, dk, dv), PACE[7])
    transpose_back(dq, dq_t)
    loads["x"].wait()
    block(0, x_t, dq, PACE[8])
    block(2, x_t, dv)
    block(1, x_t, dk)
    block(4, mid_t, up_grads[1], PACE[8])
    block(6, mid_t, up_grads[3])
    loads["ctx"].wait()
    block(7, one_t, ctx, PACE[8])

    def vec_hop(h):
        device = (near["c"], near["x"], near["y"], z_one, z_two)[h]
        return pltpu.make_async_remote_copy(
            src_ref=sums, dst_ref=vec_in.at[h], send_sem=vec_send.at[h], recv_sem=vec_recv.at[h],
            device_id=device, device_id_type=MESH,
        )

    token_sum(6, dq)
    token_sum(7, dv)
    vec_hop(0).start()
    hop = 0
    tail = {"early": counter["early"], "late": 0}

    def both(count, body=None, hops=False):
        base_late, base_early = tail["late"], tail["early"]

        def turn(i):
            if body is not None:
                body(i)
            late.step(base_late + i)
            if hops:
                for h in range(5):

                    @pl.when(i == 1 + 2 * h)
                    def _(h=h):
                        vec_hop(h).wait()
                        sums[...] = sums[...] + vec_in[h]
                        if h < 4:
                            vec_hop(h + 1).start()

            @pl.when(lax.rem(i, LATE_TURNS) == LATE_TURNS - 1)
            def _():
                early.step(base_early + lax.div(i, LATE_TURNS))

        loop(count, turn)
        tail["late"] += count
        tail["early"] += count // LATE_TURNS

    for kk, grad in ((0, dq), (1, dk), (2, dv)):
        weights = use(9 + kk)

        def tile_in(i):
            at = columns(i)
            one[:, at] = one[:, at] + dot_nt(grad[...], weights[at, :])

        both(WIDE // 256, tile_in)
    out = pltpu.make_async_copy(one, input_out, osem.at[0])
    out.start()
    turns = max(late.steps - tail["late"], LATE_TURNS * (early.steps - tail["early"]))
    both(-(-turns // LATE_TURNS) * LATE_TURNS, hops=True)

    for c in range(2):

        @pl.when(core == c)
        def _(c=c):
            n = len(given[c])
            for back_by in (2, 1):
                for f in range(4):
                    give(given[c][n - back_by], c, n - back_by, f).wait_send()

    early.finish()
    late.finish()
    out.wait()

    @pl.when(p == 3)
    def _():
        pltpu.make_async_copy(chain.at[0], total, osem.at[1]).wait()


CHUNK_EARLY, CHUNK_LATE = 128, 64
LAG_EARLY, LAG_LATE = 2, 2
LATE_TURNS = 1
NO = ()
PACE = (
    (NO, NO, NO, NO),
    (NO, NO, NO, NO),
    (NO, (3,), NO, NO),
    ((3,), NO, (3,), NO),
    NO,
    (3,),
    (3,),
    (1, 3, 5, 7),
    (3,),
)


def backward(full, x, q, k, kt, v, ctx, stat, mid, hat, inv, act, slope, two, sums, vec):
    anywhere = pl.BlockSpec(memory_space=pl.ANY)
    vmem = pl.BlockSpec(memory_space=pltpu.VMEM)
    dma = pltpu.SemaphoreType.DMA
    low, wide = jnp.bfloat16, jnp.float32
    page = (TOKENS, WIDE)
    many_a, many_b = WIDE // CHUNK_EARLY, WIDE // CHUNK_LATE

    def stream_sems(many, entries):
        return [dma((6, many)), dma((6, many)), dma((2, 2, many)), dma((2, 2, many)), dma((2, many)), dma((entries, 2))]

    return pl.pallas_call(
        backward_kernel,
        name="backward",
        out_shape=[
            jax.ShapeDtypeStruct(page, wide),
            jax.ShapeDtypeStruct((2, WIDE, WIDE), low),
            jax.ShapeDtypeStruct((16, WIDE), wide),
            jax.ShapeDtypeStruct((6, WIDE, WIDE), low),
            jax.ShapeDtypeStruct((6, WIDE, WIDE), low),
        ],
        in_specs=[anywhere] * 15 + [vmem],
        out_specs=[anywhere, anywhere, vmem, anywhere, anywhere],
        scratch_shapes=[
            pltpu.VMEM((RING, WIDE, WIDE), low),
            pltpu.VMEM((10,) + page, low),
            pltpu.VMEM((5, WIDE, TOKENS), low),
            pltpu.VMEM((4,) + page, wide),
            pltpu.VMEM((H, 1, TOKENS), wide),
            pltpu.VMEM((TOKENS, 128), wide),
            pltpu.VMEM((2, WIDE, WIDE), low),
            pltpu.VMEM((6, WIDE, WIDE), low),
            pltpu.VMEM((2, 2, WIDE, WIDE), low),
            pltpu.VMEM((len(EARLY), 2, CHUNK_EARLY, WIDE), low),
            pltpu.VMEM((len(LATE), 2, CHUNK_LATE, WIDE), low),
            pltpu.VMEM((5, 16, WIDE), wide),
            dma((RING,)), dma((2,)), dma((2,)), dma((12,)), dma((2,)),
            dma((6, 4)), dma((6, 4)),
            *stream_sems(many_a, len(EARLY)),
            *stream_sems(many_b, len(LATE)),
            dma((5,)), dma((5,)),
        ],
        compiler_params=pltpu.CompilerParams(
            collective_id=2, has_side_effects=True, vmem_limit_bytes=62 << 20
        ),
    )(full, x, q, k, kt, v, ctx, stat, mid, hat, inv, act, slope, two, sums, vec)


def layout_embed(cell_boxes, cell_ids):
    cell_count = cell_boxes.shape[1]
    onehot = (
        cell_ids[:, :, None] == jnp.arange(cell_count, dtype=jnp.int32)[None, None, :]
    ).astype(jnp.float32)
    corners = jnp.einsum("psc,pck->psk", onehot, cell_boxes.astype(jnp.float32), precision=PRECISE)
    quarter = MODEL_WIDTH // 4
    half_width = quarter // 2
    frequency = jnp.exp(
        -jnp.arange(half_width, dtype=jnp.float32) * (math.log(1000.0) / half_width)
    )
    angle_grid = corners[..., None] * frequency
    wave_table = jnp.concatenate([jnp.sin(angle_grid), jnp.cos(angle_grid)], -1)
    return 0.5 * wave_table.reshape(corners.shape[0], corners.shape[1], MODEL_WIDTH)


def gelu_exact(values):
    return jax.nn.gelu(values, approximate=False)


def norm_forward(values, gain, shift):
    center = values - jnp.mean(values, -1, keepdims=True)
    inv_std = lax.rsqrt(jnp.mean(center * center, -1, keepdims=True) + EPS_NORM)
    normed = center * inv_std
    return (normed * gain + shift, normed, inv_std)


def norm_backward(grad_in, normed, inv_std, gain):
    scaled = grad_in * gain
    grad_arg = inv_std * (
        scaled
        - jnp.mean(scaled, -1, keepdims=True)
        - normed * jnp.mean(scaled * normed, -1, keepdims=True)
    )
    return (grad_arg, jnp.sum(grad_in * normed, (0, 1)), jnp.sum(grad_in, (0, 1)))


def attend(query_low, key_low, value_low, head_count):
    groups, seq_len = (query_low.shape[0], query_low.shape[1])
    shape_heads = (groups, seq_len, head_count, HD)
    scores = jnp.einsum(
        "gqhe,gkhe->ghqk",
        query_low.reshape(shape_heads),
        key_low.reshape(shape_heads),
        preferred_element_type=jnp.float32,
    ) * HD ** (-0.5)
    row_max = jnp.max(scores, -1, keepdims=True)
    log_total = row_max + jnp.log(jnp.sum(jnp.exp(scores - row_max), -1, keepdims=True))
    probs = jnp.exp(scores - log_total).astype(jnp.bfloat16)
    context = jnp.einsum(
        "ghqk,gkhe->gqhe", probs, value_low.reshape(shape_heads), preferred_element_type=jnp.float32
    )
    return (context.reshape(groups, seq_len, head_count * HD).astype(jnp.bfloat16), log_total)


def attend_back(query_low, key_low, value_low, log_total, ctx_grad, head_count):
    groups, seq_len = (query_low.shape[0], query_low.shape[1])
    shape_heads = (groups, seq_len, head_count, HD)
    query_heads = query_low.reshape(shape_heads)
    key_heads = key_low.reshape(shape_heads)
    value_heads = value_low.reshape(shape_heads)
    grad_heads = ctx_grad.reshape(shape_heads)
    scale = HD ** (-0.5)
    scores = (
        jnp.einsum("gqhe,gkhe->ghqk", query_heads, key_heads, preferred_element_type=jnp.float32)
        * scale
    )
    probs = jnp.exp(scores - log_total)
    value_grad = jnp.einsum(
        "ghqk,gqhe->gkhe",
        probs.astype(jnp.bfloat16),
        grad_heads,
        preferred_element_type=jnp.float32,
    )
    prob_grad = jnp.einsum(
        "gqhe,gkhe->ghqk", grad_heads, value_heads, preferred_element_type=jnp.float32
    )
    score_grad = (probs * (prob_grad - jnp.sum(probs * prob_grad, -1, keepdims=True))).astype(
        jnp.bfloat16
    )
    query_grad = (
        jnp.einsum("ghqk,gkhe->gqhe", score_grad, key_heads, preferred_element_type=jnp.float32)
        * scale
    )
    key_grad = (
        jnp.einsum("ghqk,gqhe->gkhe", score_grad, query_heads, preferred_element_type=jnp.float32)
        * scale
    )
    width = head_count * HD
    return (
        query_grad.reshape(groups, seq_len, width).astype(jnp.bfloat16),
        key_grad.reshape(groups, seq_len, width).astype(jnp.bfloat16),
        value_grad.reshape(groups, seq_len, width).astype(jnp.bfloat16),
    )


def by_collectives(
    hidden, cell_ids, cell_boxes, cotangent, weight_cols, weight_out, weight_down, vectors, slot_dev
):
    dp_count = lax.axis_size("dp")
    col_mats = lax.all_gather(weight_cols, "tp", axis=2, tiled=True)
    out_mat = lax.all_gather(weight_out, "tp", axis=0, tiled=True)
    down_mats = lax.all_gather(weight_down, "tp", axis=1, tiled=True)
    x_own = hidden.astype(jnp.float32) + layout_embed(cell_boxes, cell_ids)
    x_low = x_own.astype(jnp.bfloat16)
    projected = jnp.einsum(
        "gtd,kdc->kgtc", x_low, col_mats[0:3], preferred_element_type=jnp.float32
    )
    query_low = (projected[0] + vectors[:, 6]).astype(jnp.bfloat16)
    key_low = projected[1].astype(jnp.bfloat16)
    value_low = (projected[2] + vectors[:, 7]).astype(jnp.bfloat16)
    context, log_total = attend(query_low, key_low, value_low, H)
    attn_out = jnp.einsum("gtc,cd->gtd", context, out_mat, preferred_element_type=jnp.float32)
    mid_out, mid_hat, mid_inv = norm_forward(
        x_own + attn_out + vectors[:, 0], vectors[:, 2], vectors[:, 3]
    )
    mid_low = mid_out.astype(jnp.bfloat16)
    up_pre = jnp.einsum(
        "gtd,kdc->kgtc", mid_low, col_mats[3:7], preferred_element_type=jnp.float32
    )
    up_pre = up_pre + jnp.transpose(vectors[:, 8:12])[:, None, None, :]
    act_low = gelu_exact(up_pre).astype(jnp.bfloat16)
    ffn_out = jnp.einsum("kgtc,kcd->gtd", act_low, down_mats, preferred_element_type=jnp.float32)
    layer_out, out_hat, out_inv = norm_forward(
        mid_out + ffn_out + vectors[:, 1], vectors[:, 4], vectors[:, 5]
    )
    output_gradient = cotangent.astype(jnp.float32)
    grad_two, gain_two, shift_two = norm_backward(output_gradient, out_hat, out_inv, vectors[:, 4])
    two_low = grad_two.astype(jnp.bfloat16)
    act_grad = jnp.einsum("gtd,kcd->kgtc", two_low, down_mats, preferred_element_type=jnp.float32)
    gelu_pull = jax.vjp(gelu_exact, up_pre)[1]
    up_low = gelu_pull(act_grad)[0].astype(jnp.bfloat16)
    mid_back = jnp.einsum(
        "kgtc,kdc->gtd", up_low, col_mats[3:7], preferred_element_type=jnp.float32
    )
    grad_one, gain_one, shift_one = norm_backward(
        mid_back + grad_two, mid_hat, mid_inv, vectors[:, 2]
    )
    one_low = grad_one.astype(jnp.bfloat16)
    ctx_grad = jnp.einsum(
        "gtd,cd->gtc", one_low, out_mat, preferred_element_type=jnp.float32
    ).astype(jnp.bfloat16)
    query_grad, key_grad, value_grad = attend_back(
        query_low, key_low, value_low, log_total, ctx_grad, H
    )
    qkv_grad = jnp.stack([query_grad, key_grad, value_grad], 0)
    input_grad = grad_one + jnp.einsum(
        "kgtc,kdc->gtd", qkv_grad, col_mats[0:3], preferred_element_type=jnp.float32
    )

    def block(text, left, right):
        return jnp.einsum(text, left, right, preferred_element_type=jnp.float32).astype(
            jnp.bfloat16
        )

    qkv_blocks = block("gtd,kgtc->kdc", x_low, qkv_grad)
    up_blocks = block("gtd,kgtc->kdc", mid_low, up_low)
    out_block = block("gtd,gtc->dc", one_low, context)[None]
    down_blocks = block("gtd,kgtc->kdc", two_low, act_low)
    vector_part = jnp.stack(
        [
            jnp.sum(grad_one, (0, 1)),
            jnp.sum(grad_two, (0, 1)),
            gain_one,
            shift_one,
            gain_two,
            shift_two,
            jnp.sum(query_grad, (0, 1), dtype=jnp.float32),
            jnp.sum(value_grad, (0, 1), dtype=jnp.float32),
        ],
        0,
    )
    vector_part = jnp.concatenate(
        [vector_part, jnp.sum(up_low, (1, 2), dtype=jnp.float32)], 0
    )
    block_part = jnp.concatenate(
        [
            qkv_blocks,
            up_blocks,
            out_block,
            down_blocks,
            jnp.zeros((slot_dev * dp_count - 12, MODEL_WIDTH, MODEL_WIDTH), jnp.bfloat16),
        ],
        0,
    )
    block_owned = lax.psum_scatter(block_part, "dp", scatter_dimension=0, tiled=True)
    full_grad = lax.psum(block_owned, "tp")
    vector_all = lax.psum(vector_part, ("dp", "tp"))
    return layer_out, input_grad, full_grad, vector_all


def local(
    hidden,
    cell_ids,
    cell_boxes,
    cotangent,
    weight_cols,
    weight_out,
    weight_down,
    vectors,
    vector_moment,
    left_stat,
    right_stat,
    left_root,
    right_root,
    master,
    averaged_weight,
):
    tp_count = lax.axis_size("tp")
    dp_count = lax.axis_size("dp")
    tp_index = lax.axis_index("tp")
    dp_index = lax.axis_index("dp")
    strip_width = weight_cols.shape[2]
    page_rows, seq_len = (hidden.shape[0], hidden.shape[1])
    owned_rows = vector_moment.shape[0]
    slot_dev = left_stat.shape[0]
    if dp_count == 8 and tp_count == 4:
        vec = jnp.transpose(vectors)
        full, layer_out, *kept, sums = forward(
            weight_cols, weight_out, weight_down, hidden[0], cell_ids, cell_boxes[0], cotangent[0], vec
        )
        input_grad, full_grad, vector_all, *_ = backward(full, *kept, sums, vec)
        layer_out, input_grad = layer_out[None], input_grad[None]
    else:
        layer_out, input_grad, full_grad, vector_all = by_collectives(
            hidden, cell_ids, cell_boxes, cotangent, weight_cols, weight_out, weight_down, vectors, slot_dev
        )
    vector_grad = jnp.transpose(
        lax.dynamic_slice_in_dim(vector_all[0:12], dp_index * owned_rows, owned_rows, 1)
    )
    own_rows = lax.dynamic_slice_in_dim(full_grad, tp_index * strip_width, strip_width, 1)
    own_cols = lax.dynamic_slice_in_dim(full_grad, tp_index * strip_width, strip_width, 2)
    block_grad = own_cols.astype(jnp.float32)
    left_new = STAT_DECAY * left_stat + (1.0 - STAT_DECAY) * jnp.einsum(
        "sic,sjc->sij", own_rows, full_grad, preferred_element_type=jnp.float32
    )
    right_new = STAT_DECAY * right_stat + (1.0 - STAT_DECAY) * jnp.einsum(
        "sic,sij->scj", own_cols, full_grad, preferred_element_type=jnp.float32
    )

    def parts(array):
        high = array.astype(jnp.bfloat16)
        return high, (array - high.astype(jnp.float32)).astype(jnp.bfloat16)

    def product(left, right):
        return jnp.einsum("sij,sjc->sic", left, right, preferred_element_type=jnp.float32)

    left_high, left_rest = parts(left_root)
    right_high, right_rest = parts(right_root)
    precond = product(left_high, full_grad) + product(left_rest, full_grad)
    pre_high, pre_rest = parts(precond)
    precond = (
        product(pre_high, right_high) + product(pre_rest, right_high) + product(pre_high, right_rest)
    )
    master_new = master - BLOCK_RATE * precond
    weight_copy = master_new.astype(jnp.bfloat16)
    ema_new = EMA_DECAY * averaged_weight + (1.0 - EMA_DECAY) * master_new
    vector_rows = lax.dynamic_slice_in_dim(vectors, dp_index * owned_rows, owned_rows, 0)
    moment_new = MOMENTUM * vector_moment + vector_grad
    total_tokens = page_rows * seq_len * dp_count * tp_count
    vector_new = vector_rows - VEC_RATE * lax.rsqrt(jnp.float32(total_tokens)) * moment_new
    bias_grad = vector_grad[:, 0]
    return (
        layer_out,
        input_grad,
        block_grad,
        left_new,
        right_new,
        master_new,
        weight_copy,
        ema_new,
        vector_grad,
        moment_new,
        vector_new,
        bias_grad,
    )


def solution(mesh):
    return jax.shard_map(
        local,
        mesh=mesh,
        in_specs=(
            P(("dp", "tp"), None, None),
            P(("dp", "tp"), None),
            P(("dp", "tp"), None, None),
            P(("dp", "tp"), None, None),
            P(None, None, "tp"),
            P("tp", None),
            P(None, "tp", None),
            P(),
            P("dp", None),
            P("dp", "tp", None),
            P("dp", "tp", None),
            P("dp", "tp", None),
            P("dp", None, None),
            P("dp", "tp", None),
            P("dp", "tp", None),
        ),
        out_specs=(
            P(("dp", "tp"), None, None),
            P(("dp", "tp"), None, None),
            P("dp", None, "tp"),
            P("dp", "tp", None),
            P("dp", "tp", None),
            P("dp", "tp", None),
            P("dp", "tp", None),
            P("dp", "tp", None),
            P("dp", None),
            P("dp", None),
            P("dp", None),
            P("dp"),
        ),
        check_vma=False,
    )
```

```python
import math

import jax
import jax.numpy as jnp
from jax import lax
from jax.experimental import pallas as pl
from jax.experimental.pallas import tpu as pltpu
from jax.sharding import PartitionSpec as P

MODEL_WIDTH = 1024
H = 16
HD = 64

PRECISE = lax.Precision.HIGHEST
EPS_NORM = 1e-06
STAT_DECAY = 0.5
BLOCK_RATE = 0.7
EMA_DECAY = 0.9
MOMENTUM = 0.9
VEC_RATE = 0.2

MESH = pl.DeviceIdType.MESH


def position():
    d, z = lax.axis_index("dp"), lax.axis_index("tp")
    core, x, y = d % 2, (d // 2) % 2, d // 4
    near = {
        "x": (d + 2 - 4 * x, z),
        "y": (d + 4 - 8 * y, z),
        "c": (d + 1 - 2 * core, z),
        "u": (d, z + 1),
        "v": (d, z - 1),
    }
    return z, core, x, y, near


def meet(z, near, extra=()):
    barrier = pltpu.get_barrier_semaphore()
    always = [near[name] for name in "xyc"] + list(extra)
    for device in always:
        pl.semaphore_signal(barrier, 1, device_id=device, device_id_type=MESH)

    @pl.when(z < 3)
    def _():
        pl.semaphore_signal(barrier, 1, device_id=near["u"], device_id_type=MESH)

    @pl.when(z > 0)
    def _():
        pl.semaphore_signal(barrier, 1, device_id=near["v"], device_id_type=MESH)

    pl.semaphore_wait(barrier, len(always) + (z + 2) // 3 + (5 - z) // 3)


ORDER = (0, 1, 2, 7, 3, 4, 5, 6, 8, 9, 10, 11)


NT = (((1,), (1,)), ((), ()))
TOKENS = 512
WIDE = MODEL_WIDTH


def dot(a, b):
    return jnp.dot(a, b, preferred_element_type=jnp.float32)


def dot_nt(a, b):
    return lax.dot_general(a, b, NT, preferred_element_type=jnp.float32)


def columns(i, width=256):
    return pl.ds(pl.multiple_of(i * width, width), width)


def loop(count, body):
    def step(i, carry):
        body(i)
        return carry

    lax.fori_loop(0, count, step, 0)


def mean_of(rows):
    return jnp.sum(rows, -1, keepdims=True) * (1.0 / WIDE)


def transpose_into(dest, source):
    def body(i):
        dest[columns(i), :] = source[:, columns(i)].T

    loop(WIDE // 256, body)


def transpose_back(dest, source):
    def body(i):
        dest[:, columns(i)] = source[columns(i), :].T

    loop(WIDE // 256, body)


def embed_tokens(hidden, ids, boxes, x_ref, x_low):
    cells = boxes.shape[1]
    corners = boxes[...].astype(jnp.float32).T
    half = WIDE // 8
    place = lax.broadcasted_iota(jnp.int32, (1, half), 1).astype(jnp.float32)
    rate = jnp.exp(place * (-math.log(1000.0) / half))
    marks = lax.broadcasted_iota(jnp.int32, (cells, TOKENS), 0) == ids[...]
    chosen = jnp.where(marks, 1.0, 0.0).T.astype(jnp.bfloat16)
    for c in range(4):
        angle = corners[:, c : c + 1] * rate
        for kind, wave in enumerate((jnp.sin(angle), jnp.cos(angle))):
            wave = 0.5 * wave
            high = wave.astype(jnp.bfloat16)
            rest = wave - high.astype(jnp.float32)
            middle = rest.astype(jnp.bfloat16)
            low = (rest - middle.astype(jnp.float32)).astype(jnp.bfloat16)
            emb = dot(chosen, high) + (dot(chosen, middle) + dot(chosen, low))
            at = pl.ds(c * 2 * half + kind * half, half)
            value = hidden[:, at].astype(jnp.float32) + emb
            x_ref[:, at] = value
            x_low[:, at] = value.astype(jnp.bfloat16)


def project(x_low, weight, dest, bias, scale):
    def body(i):
        value = dot(x_low[...], weight[:, columns(i)])
        if bias is not None:
            value = value + bias[:, columns(i)]
        value = value.astype(jnp.bfloat16)
        if scale:
            value = value * jnp.asarray(HD ** (-0.5), jnp.bfloat16)
        dest[:, columns(i)] = value

    loop(WIDE // 256, body)


def half_mask(e, shape):
    lane = lax.broadcasted_iota(jnp.int32, shape, 1)
    return (lane < HD) if e == 0 else (lane >= HD)


def attend_pair(t, q8, k, v_t, ctx_t, stat):
    at = columns(t, 128)
    keys, queries = k[:, at], q8[:, at]
    for e in range(2):
        own = jnp.where(half_mask(e, queries.shape), queries, jnp.zeros_like(queries))
        scores = dot_nt(keys, own)
        top = jnp.max(scores, 0, keepdims=True)
        power = jnp.exp(scores - top)
        total = jnp.sum(power, 0, keepdims=True)
        probs = (power * (1.0 / total)).astype(jnp.bfloat16)
        rows = pl.ds(pl.multiple_of(t * 128 + e * 64, 64), 64)
        ctx_t[rows, :] = dot(v_t[rows, :], probs).astype(jnp.bfloat16)
        stat[2 * t + e, :, :] = top + jnp.log(total)


def norm_rows(values, gain, shift):
    center = values - mean_of(values)
    inv = lax.rsqrt(mean_of(center * center) + EPS_NORM)
    normed = center * inv
    return normed * gain + shift, normed, inv


SLICE = 64


def row_loop(body):
    loop(TOKENS // SLICE, lambda i: body(pl.ds(pl.multiple_of(i * SLICE, SLICE), SLICE)))


def gelu_both(value):
    phi = 0.5 * (1.0 + lax.erf(value * math.sqrt(0.5)))
    density = jnp.exp(-0.5 * value * value) * (1.0 / math.sqrt(2.0 * math.pi))
    return value * phi, phi + value * density


def forward_kernel(
    cols, outw, down, hidden, ids, boxes, cotangent, vec,
    full_out, layer_out, x_out, q_out, k_out, kt_out, v_out, ctx_out, stat_out, mid_out, hat_out, inv_out, act_out, slope_out,
    two_out, sums_out,
    w, x_t, mid_t, k_t, x_ref, x_low, q8, k, v, v_t, ctx_t, ctx, stat, acc, mid, mid_low, hat, inv, act, slope, y_out, two, sums,
    load, along, onward, arrived, beside, store, spill,
):
    z, core, x, y, near = position()
    p = 2 * y + x
    meet(z, near)

    def own(kk, h):
        if kk < 7:
            return cols.at[kk, pl.ds(h * 512, 512), :]
        if kk == 7:
            return outw.at[pl.ds(h * 128, 128), :]
        return down.at[kk - 8, pl.ds(h * 128, 128), :]

    def spot(s, kk, h):
        if kk < 7:
            return w.at[kk, pl.ds(h * 512, 512), pl.ds(pl.multiple_of(s * 256, 256), 256)]
        return w.at[kk, pl.ds(pl.multiple_of(s * 256 + h * 128, 128), 128), :]

    def spot_whole(s, kk):
        if kk < 7:
            return w.at[kk, :, pl.ds(pl.multiple_of(s * 256, 256), 256)]
        return w.at[kk, pl.ds(pl.multiple_of(s * 256, 256), 256), :]

    def whole_own(kk):
        if kk < 7:
            return cols.at[kk]
        return outw if kk == 7 else down.at[kk - 8]

    def to(source, s, kk, send_sem, recv_sem, name):
        return pltpu.make_async_remote_copy(
            src_ref=source,
            dst_ref=spot(s, kk, core),
            send_sem=send_sem,
            recv_sem=recv_sem.at[s, kk],
            device_id=near[name],
            device_id_type=MESH,
        )

    def first(g, act_on):
        for t in range(3):
            kk = ORDER[3 * g + t]
            mine = (p == t) | (p == 3) if t == 0 else p == t

            @pl.when(mine & (z < 3))
            def _(kk=kk):
                act_on(to(own(kk, core), z, kk, along.at[kk], arrived, "u"))

            @pl.when(mine & (z > 0))
            def _(kk=kk):
                act_on(to(own(kk, core), z, kk, onward.at[0, z, kk], arrived, "v"))

    far = 3 * (1 - z // 2)
    nearest = z + 1 - 2 * (z // 3)
    strips = (nearest, 6 - nearest - far - z, far)

    def item(n, t):
        return strips[n % 3], ORDER[3 * (n // 3) + t]

    def go(s, kk, kind, name, sems):
        return to(spot(s, kk, core), s, kk, onward.at[kind, s, kk], sems, name)

    def stage(n, hop, begin):
        for t in range(3):
            s, kk = item(n, t)
            who = {
                (0, 0): (p == 0) | (p == 3),
                (0, 1): p == 1,
                (0, 2): p == 2,
                (1, 0): (p == 1) | (p == 2),
                (1, 1): (p == 0) | (p == 3),
                (1, 2): (p == 0) | (p == 3),
                (2, 0): None,
                (2, 1): p == 2,
                (2, 2): p == 1,
            }[hop, t]
            if who is None:
                continue

            @pl.when(who)
            def _(s=s, kk=kk, t=t):
                if begin:
                    go(s, kk, 0, "x", arrived).wait_recv()

                def act_on(copy):
                    if begin:
                        copy.start()
                    else:
                        copy.wait_send()

                if hop == 0:

                    @pl.when((s > z) & (z > 0))
                    def _():
                        act_on(go(s, kk, 0, "v", arrived))

                    @pl.when((s < z) & (z < 3))
                    def _():
                        act_on(go(s, kk, 0, "u", arrived))

                    if t == 0:

                        @pl.when(p == 0)
                        def _():
                            act_on(go(s, kk, 1, "x", arrived))
                            act_on(go(s, kk, 2, "y", arrived))
                    else:
                        act_on(go(s, kk, 1, "x", arrived))
                        act_on(go(s, kk, 2, "y", arrived))
                if hop == 1 and t == 1:

                    @pl.when(p == 3)
                    def _():
                        act_on(go(s, kk, 1, "x", arrived))

                if hop == 1 and t == 2:

                    @pl.when(p == 3)
                    def _():
                        act_on(go(s, kk, 2, "y", arrived))

                act_on(go(s, kk, 3, "c", beside))

    copies = []

    def keep(source, dest):
        copy = pltpu.make_async_copy(source, dest, spill.at[len(copies)])
        copy.start()
        copies.append(copy)

    def ready(kk):
        pltpu.make_async_copy(whole_own(kk), spot_whole(z, kk), load.at[kk]).wait()
        for s in strips:
            pltpu.make_async_remote_copy(
                src_ref=spot(s, kk, 1 - core),
                dst_ref=spot(s, kk, 1 - core),
                send_sem=onward.at[3, s, kk],
                recv_sem=beside.at[s, kk],
                device_id=near["c"],
                device_id_type=MESH,
            ).wait_recv()
        copy = pltpu.make_async_copy(w.at[kk], full_out.at[kk], store.at[kk])
        copy.start()

    def unit_embed():
        embed_tokens(hidden, ids, boxes, x_ref, x_low)
        transpose_into(x_t, x_low)
        keep(x_t, x_out)

    def unit_qkv():
        for kk in range(3):
            ready(kk)
        project(x_low, w.at[0], q8, vec.at[6:7], True)
        project(x_low, w.at[1], k, None, False)
        project(x_low, w.at[2], v, vec.at[7:8], False)
        transpose_into(v_t, v)
        transpose_into(k_t, k)
        keep(q8, q_out)
        keep(k_t, kt_out)
        keep(k, k_out)
        keep(v, v_out)

    def unit_attend(lo, hi):
        loop(hi - lo, lambda i: attend_pair(lo + i, q8, k, v_t, ctx_t, stat))

    def unit_context():
        transpose_back(ctx, ctx_t)
        keep(ctx, ctx_out)
        keep(stat, stat_out)

    def unit_mid():
        ready(7)

        def tile(i):
            acc[:, columns(i)] = dot(ctx[...], w[7, :, columns(i)])

        loop(WIDE // 256, tile)

        def rows(r):
            value = x_ref[r, :] + acc[r, :] + vec[0:1, :]
            out, normed, scale = norm_rows(value, vec[2:3, :], vec[3:4, :])
            mid[r, :] = out
            mid_low[r, :] = out.astype(jnp.bfloat16)
            hat[r, :] = normed
            inv[r, :] = jnp.broadcast_to(scale, (SLICE, 128))

        row_loop(rows)
        transpose_into(mid_t, mid_low)
        keep(mid_t, mid_out)
        keep(hat, hat_out)
        keep(inv, inv_out)

    def unit_up(u):
        ready(3 + u)
        def tile(i):
            at = columns(i)
            slot = i % 2

            @pl.when(i >= 2)
            def _():
                pltpu.make_async_copy(slope.at[slot], slope_out.at[u, :, at], store.at[12 + slot]).wait()

            for part in range(2):
                rows = pl.ds(part * 256, 256)
                value = dot(mid_low[rows, :], w[3 + u, :, at]) + vec[8 + u : 9 + u, at]
                out, grad = gelu_both(value)
                act[u, rows, at] = out.astype(jnp.bfloat16)
                slope[slot, rows, :] = grad
            pltpu.make_async_copy(slope.at[slot], slope_out.at[u, :, at], store.at[12 + slot]).start()

        loop(WIDE // 256, tile)
        for slot in range(2):
            pltpu.make_async_copy(slope.at[slot], slope_out.at[u, :, columns(slot)], store.at[12 + slot]).wait()
        keep(act.at[u], act_out.at[u])

    def unit_down(u):
        ready(8 + u)

        def tile(i):
            at = columns(i)
            value = dot(act[u], w[8 + u, :, at])
            acc[:, at] = value if u == 0 else acc[:, at] + value

        loop(WIDE // 256, tile)

    def unit_last():
        sums[...] = jnp.zeros_like(sums)

        def rows(r):
            value = mid[r, :] + acc[r, :] + vec[1:2, :]
            out, normed, scale = norm_rows(value, vec[4:5, :], vec[5:6, :])
            y_out[r, :] = out
            grad = cotangent[r, :].astype(jnp.float32)
            scaled = grad * vec[4:5, :]
            arg = scale * (scaled - mean_of(scaled) - normed * mean_of(scaled * normed))
            two[r, :] = arg
            sums[1:2, :] += jnp.sum(arg, 0, keepdims=True)
            sums[4:5, :] += jnp.sum(grad * normed, 0, keepdims=True)
            sums[5:6, :] += jnp.sum(grad, 0, keepdims=True)

        row_loop(rows)
        keep(y_out, layer_out)
        keep(two, two_out)
        keep(sums, sums_out)

    first(0, lambda copy: copy.start())
    first(1, lambda copy: copy.start())
    for kk in ORDER:
        pltpu.make_async_copy(whole_own(kk), spot_whole(z, kk), load.at[kk]).start()
    unit_embed()
    after = {
        4: unit_qkv,
        5: lambda: unit_attend(0, 4),
        6: lambda: (unit_attend(4, 8), unit_context()),
        7: unit_mid,
        8: lambda: unit_up(0),
        9: lambda: unit_up(1),
        10: lambda: unit_up(2),
        11: lambda: unit_up(3),
        12: lambda: unit_down(0),
        13: lambda: (unit_down(1), unit_down(2), unit_down(3), unit_last()),
    }
    for n in range(14):
        if n in (3, 6):
            first(n // 3 + 1, lambda copy: copy.start())
        for hop in range(3):
            if 0 <= n - hop < 12:
                stage(n - hop, hop, True)
        if n in after:
            after[n]()
    for n in range(12):
        for hop in range(3):
            stage(n, hop, False)
    for g in range(4):
        first(g, lambda copy: copy.wait_send())
    for kk in ORDER:
        pltpu.make_async_copy(w.at[kk], full_out.at[kk], store.at[kk]).wait()
    for copy in copies:
        copy.wait()


def forward(cols, outw, down, hidden, ids, boxes, cotangent, vec):
    anywhere = pl.BlockSpec(memory_space=pl.ANY)
    vmem = pl.BlockSpec(memory_space=pltpu.VMEM)
    dma = pltpu.SemaphoreType.DMA
    low, wide = jnp.bfloat16, jnp.float32
    page = (TOKENS, WIDE)
    outs = [
        ((12, WIDE, WIDE), low),
        (page, wide),
        ((WIDE, TOKENS), low),
        (page, low),
        (page, low),
        ((WIDE, TOKENS), low),
        (page, low),
        (page, low),
        ((H, 1, TOKENS), wide),
        ((WIDE, TOKENS), low),
        (page, wide),
        ((TOKENS, 128), wide),
        ((4,) + page, low),
        ((4,) + page, wide),
        (page, wide),
        ((16, WIDE), wide),
    ]
    return pl.pallas_call(
        forward_kernel,
        name="forward",
        out_shape=[jax.ShapeDtypeStruct(*o) for o in outs],
        in_specs=[anywhere] * 3 + [vmem] * 5,
        out_specs=[anywhere] * len(outs),
        scratch_shapes=[
            pltpu.VMEM((12, WIDE, WIDE), low),
            pltpu.VMEM((WIDE, TOKENS), low),
            pltpu.VMEM((WIDE, TOKENS), low),
            pltpu.VMEM((WIDE, TOKENS), low),
            pltpu.VMEM(page, wide),
            pltpu.VMEM(page, low),
            pltpu.VMEM(page, low),
            pltpu.VMEM(page, low),
            pltpu.VMEM(page, low),
            pltpu.VMEM((WIDE, TOKENS), low),
            pltpu.VMEM((WIDE, TOKENS), low),
            pltpu.VMEM(page, low),
            pltpu.VMEM((H, 1, TOKENS), wide),
            pltpu.VMEM(page, wide),
            pltpu.VMEM(page, wide),
            pltpu.VMEM(page, low),
            pltpu.VMEM(page, wide),
            pltpu.VMEM((TOKENS, 128), wide),
            pltpu.VMEM((4,) + page, low),
            pltpu.VMEM((2, TOKENS, 256), wide),
            pltpu.VMEM(page, wide),
            pltpu.VMEM(page, wide),
            pltpu.VMEM((16, WIDE), wide),
            dma((12,)),
            dma((12,)),
            dma((4, 4, 12)),
            dma((4, 12)),
            dma((4, 12)),
            dma((14,)),
            dma((20,)),
        ],
        compiler_params=pltpu.CompilerParams(
            collective_id=1, has_side_effects=True, vmem_limit_bytes=61 << 20
        ),
    )(cols, outw, down, hidden, ids, boxes, cotangent, vec)


KEPT = ((8, 5, 9, 0, 1, 4), (10, 3, 11, 2, 6, 7))
EARLY = (((0, 8), (0, 10), 0), ((1, 5), None, 0), (None, (1, 3), 0), ((2, 9), (2, 11), 8))
LATE = (((3, 0), (3, 2), 0), ((4, 1), None, 0), ((5, 4), (4, 6), 0), (None, (5, 7), 0))
UNIT_ORDER = (0, 2, 1, 3)
RING = 3


def attend_pair_back(t, q8, k, v, ctx_grad, k_t, stat, dq_t, dk, dv):
    at = columns(t, 128)
    keys, queries, values, grads = k[:, at], q8[:, at], v[:, at], ctx_grad[:, at]
    none = jnp.zeros_like(queries)
    key_sum = value_sum = None
    for e in range(2):
        mask = half_mask(e, queries.shape)
        own_q = jnp.where(mask, queries, none)
        own_g = jnp.where(mask, grads, none)
        probs = jnp.exp(dot_nt(keys, own_q) - stat[2 * t + e])
        prob_grad = dot_nt(values, own_g)
        carried = jnp.sum(probs * prob_grad, 0, keepdims=True)
        score_grad = (probs * (prob_grad - carried)).astype(jnp.bfloat16)
        rows = pl.ds(pl.multiple_of(t * 128 + e * 64, 64), 64)
        dq_t[rows, :] = (dot(k_t[rows, :], score_grad) * HD ** (-0.5)).astype(jnp.bfloat16)
        key_part = dot(score_grad, own_q)
        value_part = dot(probs.astype(jnp.bfloat16), own_g)
        key_sum = key_part if e == 0 else key_sum + key_part
        value_sum = value_part if e == 0 else value_sum + value_part
    dk[:, at] = key_sum.astype(jnp.bfloat16)
    dv[:, at] = value_sum.astype(jnp.bfloat16)


class Stream:
    def __init__(self, entries, chunk, lag, refs, ring, place):
        self.z, self.core, self.x, self.y, self.d = place
        self.p = 2 * self.y + self.x
        self.chunk, self.per, self.lag = chunk, WIDE // chunk, lag
        self.entries, self.refs, self.ring = entries, refs, ring
        self.base = min(item[0] for entry in entries for item in entry[:2] if item is not None)
        self.steps = max(entry[2] for entry in entries) + self.per + 6 * lag
        x, y = self.x, self.y
        self.corner = [(x if j % 2 == 0 else 1 - x, y if j // 2 == 0 else 1 - y) for j in range(3)]
        self.by_x, self.by_y = 2 - 4 * x, 4 - 8 * y

    def rows(self, r):
        return pl.ds(pl.multiple_of(r * self.chunk, self.chunk), self.chunk)

    def remote(self, source, dest, send_sem, recv_sem, device):
        return pltpu.make_async_remote_copy(
            src_ref=source, dst_ref=dest, send_sem=send_sem, recv_sem=recv_sem,
            device_id=device, device_id_type=MESH,
        )


    def forward(self, q, r, turn):
        R = self.refs
        at = self.rows(r)
        device = (self.d + self.by_y + turn * (self.by_x - self.by_y), self.z)
        return self.remote(R["mine"].at[q, at, :], R["land"].at[q, at, :], R["send"].at[q, r], R["recv"].at[q, r], device)

    def chained(self, i, r, way):
        R = self.refs
        at = self.rows(r)
        return R["chain"].at[way, i, at, :], R["chain_send"].at[way, i, r], R["chain_recv"].at[way, i, r]

    def pass_on(self, source, i, r, way):
        ref, ssem, rsem = self.chained(i, r, way)
        return self.remote(source, ref, ssem, rsem, (self.d, self.z + (1 if way == 0 else -1)))

    def total_out(self, source, i, r):
        R = self.refs
        return pltpu.make_async_copy(source, R["total"].at[i, self.rows(r), :], R["out"].at[i, r])

    def add_to_mine(self, q, r, ref):
        mine = self.refs["mine"]

        def part(g):
            at = pl.ds(pl.multiple_of(r * self.chunk + g * 32, 32), 32)
            here = pl.ds(pl.multiple_of(g * 32, 32), 32)
            mine[q, at, :] = (mine[q, at, :].astype(jnp.float32) + ref[here, :].astype(jnp.float32)).astype(jnp.bfloat16)

        loop(self.chunk // 32, part)

    def load(self, e, kind, q, r):
        source = self.refs["sib" if kind == 0 else "land"]
        return pltpu.make_async_copy(source.at[q, self.rows(r), :], self.ring.at[q - self.base, kind], self.refs["ring_sem"].at[q - self.base, kind])

    def begin_pair(self, e, q, j, i, r):
        R = self.refs
        quarter = 256 // self.chunk

        def arrival(f):
            at = pl.ds(pl.multiple_of(f * 256, 256), 256)
            ref = R["sib"].at[q, at, :]
            self.remote(ref, ref, R["give_send"].at[q, f], R["give_recv"].at[q, f], (self.d, self.z)).wait_recv()

        if quarter == 1:
            arrival(r)
        else:

            @pl.when(lax.rem(r, quarter) == 0)
            def _():
                arrival(lax.div(r, quarter))

        self.load(e, 0, q, r).start()

    def end_pair(self, e, q, j, i, r):
        self.load(e, 0, q, r).wait()
        self.add_to_mine(q, r, self.ring.at[q - self.base, 0])
        odd = lax.rem(r, 2)
        rx, ry = self.corner[j]

        @pl.when((rx + ry == 1) & (rx + odd == 1))
        def _():
            self.forward(q, r, odd).start()

    def path(self, hop, begin):
        def run(e, q, j, i, r):
            odd = lax.rem(r, 2)
            rx, ry = self.corner[j]
            here = {1: rx + ry == 2, 2: (rx + ry == 1) & (rx == odd), 3: rx + ry == 0}[hop]

            @pl.when(here)
            def _():
                copy = self.load(e, 1, q, r)
                if begin:
                    self.forward(q, r, odd).wait_recv()
                    copy.start()
                    return
                copy.wait()
                self.add_to_mine(q, r, self.ring.at[q - self.base, 1])
                if hop == 1:
                    self.forward(q, r, 1 - odd).start()
                if hop == 2:
                    self.forward(q, r, odd).start()
                if hop == 3:
                    mine = self.refs["mine"].at[q, self.rows(r), :]

                    @pl.when(self.z == 0)
                    def _():
                        self.pass_on(mine, i, r, 0).start()

                    @pl.when(self.z == 3)
                    def _():
                        self.pass_on(mine, i, r, 1).start()

        return run

    def link(self, q, i, r, way, last):
        R = self.refs
        at = self.rows(r)
        ref, ssem, rsem = self.chained(i, r, way)
        self.remote(ref, ref, ssem, rsem, (self.d, self.z)).wait_recv()
        mine, chain = R["mine"], R["chain"]

        def part(g):
            piece = pl.ds(pl.multiple_of(r * self.chunk + g * 32, 32), 32)
            came = chain[way, i, piece, :].astype(jnp.float32)
            chain[way, i, piece, :] = (mine[q, piece, :].astype(jnp.float32) + came).astype(jnp.bfloat16)
            if last:
                other = chain[1 - way, i, piece, :].astype(jnp.float32)
                mine[q, piece, :] = (other + came).astype(jnp.bfloat16)

        loop(self.chunk // 32, part)
        self.pass_on(ref, i, r, way).start()
        if last:
            self.total_out(mine.at[q, at, :], i, r).start()

    def links(self, last):
        def run(e, q, j, i, r):
            @pl.when(self.p == j)
            def _():
                for z, way in ((1, 1 if last else 0), (2, 0 if last else 1)):

                    @pl.when(self.z == z)
                    def _(way=way):
                        self.link(q, i, r, way, last)

        return run

    def ends(self, e, q, j, i, r):
        R = self.refs
        at = self.rows(r)

        @pl.when(self.p == j)
        def _():
            for z, way in ((0, 1), (3, 0)):

                @pl.when(self.z == z)
                def _(way=way):
                    ref, ssem, rsem = self.chained(i, r, way)
                    self.remote(ref, ref, ssem, rsem, (self.d, self.z)).wait_recv()
                    mine, chain = R["mine"], R["chain"]

                    def part(g):
                        piece = pl.ds(pl.multiple_of(r * self.chunk + g * 32, 32), 32)
                        chain[way, i, piece, :] = (
                            mine[q, piece, :].astype(jnp.float32) + chain[way, i, piece, :].astype(jnp.float32)
                        ).astype(jnp.bfloat16)

                    loop(self.chunk // 32, part)
                    self.total_out(ref, i, r).start()

    def each(self, function):
        for e, entry in enumerate(self.entries):
            here = [item for item in entry[:2] if item is not None]
            if len(here) == 2:
                (q, slot), (q_other, slot_other) = here
                assert slot // 4 == slot_other // 4
                if q != q_other:
                    q = q + self.core * (q_other - q)
                i = slot % 2
                if i != slot_other % 2:
                    i = i + self.core * (slot_other % 2 - i)
                function(e, entry[2], q, slot // 4, i)
            else:
                only = 0 if entry[1] is None else 1

                @pl.when(self.core == only)
                def _(e=e, entry=entry, item=here[0]):
                    function(e, entry[2], item[0], item[1] // 4, item[1] % 2)

    def step(self, n):
        L = self.lag
        begins = ((0, self.begin_pair), (L, self.path(1, True)), (2 * L, self.path(2, True)), (3 * L, self.path(3, True)))
        ends = (
            (6 * L, self.ends),
            (5 * L, self.links(True)),
            (4 * L, self.links(False)),
            (3 * L, self.path(3, False)),
            (2 * L, self.path(2, False)),
            (L, self.path(1, False)),
            (0, self.end_pair),
        )

        def visit(parts):
            def entry_parts(e, start, q, j, i):
                m = n - start

                @pl.when((m >= 0) & (m < self.per + 6 * L))
                def _():
                    for lag, part in parts:
                        r = m - lag

                        @pl.when((r >= 0) & (r < self.per))
                        def _(r=r, part=part):
                            part(e, q, j, i, r)

            self.each(entry_parts)

        visit(begins)
        visit(ends)

    def finish(self):
        def chunk(e, start, q, j, i):
            rx, ry = self.corner[j]

            def body(r):
                @pl.when(rx + ry > 0)
                def _():
                    self.forward(q, r, 0).wait_send()

                mine = self.refs["mine"].at[q, self.rows(r), :]

                @pl.when((rx + ry == 0) & (self.z < 3))
                def _():
                    self.pass_on(mine, i, r, 0).wait_send()

                @pl.when((rx + ry == 0) & (self.z > 0))
                def _():
                    self.pass_on(mine, i, r, 1).wait_send()

                @pl.when(rx + ry == 0)
                def _():
                    self.total_out(mine, i, r).wait()

            loop(self.per, body)

        self.each(chunk)


def backward_kernel(
    full, x_in, q_in, k_in, kt_in, v_in, ctx_in, stat_in, mid_in, hat_in, inv_in, act_in, slope_in, two_in, sums_in, vec,
    input_out, total, sums, sib, land,
    w, pb, pt, pf, stat, inv, stage, mine, chain, ring_a, ring_b, vec_in,
    wsem, asem, ssem, isem, osem,
    give_send, give_recv, send_a, recv_a, chain_send_a, chain_recv_a, out_a, ring_sem_a,
    send_b, recv_b, chain_send_b, chain_recv_b, out_b, ring_sem_b, vec_send, vec_recv,
):
    z, core, x, y, near = position()
    p = 2 * y + x
    d = 2 * p + core
    z_one = (d, z + 1 - 2 * (z % 2))
    z_two = (d, z + 2 - 4 * (z // 2))
    shared = {"mine": mine, "land": land, "chain": chain, "sib": sib, "total": total, "give_send": give_send, "give_recv": give_recv}
    place = (z, core, x, y, d)
    early = Stream(EARLY, CHUNK_EARLY, LAG_EARLY, dict(
        shared, send=send_a, recv=recv_a, chain_send=chain_send_a, chain_recv=chain_recv_a, out=out_a, ring_sem=ring_sem_a,
    ), ring_a, place)
    late = Stream(LATE, CHUNK_LATE, LAG_LATE, dict(
        shared, send=send_b, recv=recv_b, chain_send=chain_send_b, chain_recv=chain_recv_b, out=out_b, ring_sem=ring_sem_b,
    ), ring_b, place)

    two_low, act_ring = pb.at[0], (pb.at[1], pb.at[2])
    up_grads = {0: pb.at[3], 2: pb.at[3], 1: pb.at[7], 3: pb.at[8]}
    k, q8, v = pb.at[4], pb.at[5], pb.at[6]
    one_low, ctx, ctx_grad, dq, dk, dv = pb.at[0], pb.at[1], pb.at[2], pb.at[0], pb.at[9], pb.at[3]
    two_t, mid_t, k_t = pt.at[0], pt.at[1], pt.at[2]
    one_t, x_t, dq_t = pt.at[0], pt.at[3], pt.at[4]
    two, back, slope_ring = pf.at[0], pf.at[1], (pf.at[2], pf.at[3])
    one, hat = pf.at[0], pf.at[2]
    uses = [slot for u in UNIT_ORDER for slot in (8 + u, 3 + u)] + [7, 0, 1, 2]

    def weight(n):
        return pltpu.make_async_copy(full.at[uses[n]], w.at[n % RING], wsem.at[n % RING])

    def act_load(n):
        return pltpu.make_async_copy(act_in.at[UNIT_ORDER[n]], act_ring[n % 2], asem.at[n % 2])

    def slope_load(n):
        return pltpu.make_async_copy(slope_in.at[UNIT_ORDER[n]], slope_ring[n % 2], ssem.at[n % 2])

    loads = {}

    def fetch(name, source, dest):
        loads[name] = pltpu.make_async_copy(source, dest, isem.at[len(loads)])
        loads[name].start()

    fetch("two", two_in, two)
    weight(0).start()
    slope_load(0).start()
    act_load(0).start()
    fetch("mid", mid_in, mid_t)
    weight(1).start()
    fetch("sums", sums_in, sums)
    weight(2).start()
    slope_load(1).start()
    act_load(1).start()
    for name, source, dest in (
        ("inv", inv_in, inv), ("k", k_in, k), ("q", q_in, q8), ("v", v_in, v), ("kt", kt_in, k_t), ("stat", stat_in, stat), ("x", x_in, x_t),
    ):
        fetch(name, source, dest)
    meet(z, near, (z_two,))

    counter = {"early": 0}
    produced = set()

    def run(count, body, at=()):
        base = counter["early"]
        for one_entry in EARLY:
            if at and one_entry[2] < base + len(at):
                assert all(item is None or item[1] in produced for item in one_entry[:2])

        def one_turn(i):
            body(i)
            if at:
                first, stride = at[0], (at[1] - at[0] if len(at) > 1 else count)

                @pl.when((i >= first) & (lax.rem(i - first + stride, stride) == 0))
                def _():
                    early.step(base + lax.div(i - first, stride))

        loop(count, one_turn)
        counter["early"] += len(at)

    def use(n):
        weight(n).wait()
        return w.at[n % RING]

    def done(n):
        if n + RING < 12:
            weight(n + RING).start()

    given = {0: [], 1: []}

    def give(slot, c, n, f):
        at = pl.ds(f * 256, 256)
        q = KEPT[1 - c].index(slot)
        return pltpu.make_async_remote_copy(
            src_ref=stage.at[n % 2, at, :], dst_ref=sib.at[q, at, :], send_sem=give_send.at[q, f],
            recv_sem=give_recv.at[q, f], device_id=near["c"], device_id_type=MESH,
        )

    def block(slot, left_t, right, at=()):
        owner = (slot // 2) % 2
        giver = 1 - owner
        q = KEPT[owner].index(slot)
        n = len(given[giver])
        if n >= 2:

            @pl.when(core == giver)
            def _():
                for f in range(4):
                    give(given[giver][n - 2], giver, n - 2, f).wait_send()

        def tile(i):
            value = dot(left_t[...], right[:, columns(i)]).astype(jnp.bfloat16)

            @pl.when(core == owner)
            def _():
                mine[q, :, columns(i)] = value

            @pl.when(core == giver)
            def _():
                stage[n % 2, :, columns(i)] = value

        run(WIDE // 256, tile, at)

        @pl.when(core == giver)
        def _():
            for f in range(4):
                give(slot, giver, n, f).start()

        given[giver].append(slot)
        produced.add(slot)

    def token_sum(row, ref):
        def tile(i):
            at = columns(i)
            sums[row : row + 1, at] = jnp.sum(ref[:, at].astype(jnp.float32), 0, keepdims=True)

        loop(WIDE // 256, tile)

    @pl.when(p == 3)
    def _():
        chain[0] = jnp.zeros(chain.shape[1:], chain.dtype)
        pltpu.make_async_copy(chain.at[0], total, osem.at[1]).start()

    loads["two"].wait()

    def to_low(r):
        two_low[r, :] = two[r, :].astype(jnp.bfloat16)

    row_loop(to_low)
    transpose_into(two_t, two_low)
    loads["mid"].wait()
    loads["sums"].wait()
    for n, u in enumerate(UNIT_ORDER):
        pace = PACE[n]
        weights = use(2 * n)
        slope_load(n).wait()
        act_load(n).wait()
        slope, up_grad = slope_ring[n % 2], up_grads[u]

        def tile(i):
            rows = columns(i)
            grad = dot_nt(two_low[...], weights[rows, :]) * slope[:, rows]
            up_grad[:, rows] = grad.astype(jnp.bfloat16)

        run(WIDE // 256, tile, pace[0])
        done(2 * n)
        if n == 2:
            fetch("hat", hat_in, hat)
        token_sum(8 + u, up_grad)
        block(8 + u, two_t, act_ring[n % 2], pace[1])
        if n == 2:
            fetch("ctx", ctx_in, ctx)
        weights = use(2 * n + 1)

        def tile_back(i):
            at = columns(i)
            value = dot_nt(up_grad[...], weights[at, :])
            back[:, at] = two[:, at] + value if n == 0 else back[:, at] + value

        run(WIDE // 256, tile_back, pace[2])
        done(2 * n + 1)
        if n < 2:
            block(3 + u, mid_t, up_grad, pace[3])
        if n + 2 < 4:
            slope_load(n + 2).start()
            act_load(n + 2).start()
    for name in ("hat", "inv"):
        loads[name].wait()
    sums[0:1, :] = jnp.zeros((1, WIDE), jnp.float32)
    sums[2:4, :] = jnp.zeros((2, WIDE), jnp.float32)

    def rows(i):
        r = pl.ds(pl.multiple_of(i * SLICE, SLICE), SLICE)
        grad, normed = back[r, :], hat[r, :]
        scaled = grad * vec[2:3, :]
        arg = inv[r, 0:1] * (scaled - mean_of(scaled) - normed * mean_of(scaled * normed))
        one[r, :] = arg
        one_low[r, :] = arg.astype(jnp.bfloat16)
        sums[0:1, :] += jnp.sum(arg, 0, keepdims=True)
        sums[2:3, :] += jnp.sum(grad * normed, 0, keepdims=True)
        sums[3:4, :] += jnp.sum(grad, 0, keepdims=True)

    run(TOKENS // SLICE, rows, PACE[4])
    transpose_into(one_t, one_low)
    weights = use(8)

    def tile_ctx(i):
        at = columns(i)
        ctx_grad[:, at] = dot_nt(one_low[...], weights[at, :]).astype(jnp.bfloat16)

    run(WIDE // 256, tile_ctx, PACE[5])
    done(8)
    for name in ("k", "q", "v", "kt", "stat"):
        loads[name].wait()
    run(H // 2, lambda t: attend_pair_back(t, q8, k, v, ctx_grad, k_t, stat, dq_t, dk, dv), PACE[7])
    transpose_back(dq, dq_t)
    loads["x"].wait()
    block(0, x_t, dq, PACE[8])
    block(2, x_t, dv)
    block(1, x_t, dk)
    block(4, mid_t, up_grads[1], PACE[8])
    block(6, mid_t, up_grads[3])
    loads["ctx"].wait()
    block(7, one_t, ctx, PACE[8])

    def vec_hop(h):
        device = (near["c"], near["x"], near["y"], z_one, z_two)[h]
        return pltpu.make_async_remote_copy(
            src_ref=sums, dst_ref=vec_in.at[h], send_sem=vec_send.at[h], recv_sem=vec_recv.at[h],
            device_id=device, device_id_type=MESH,
        )

    token_sum(6, dq)
    token_sum(7, dv)
    vec_hop(0).start()
    hop = 0
    tail = {"early": counter["early"], "late": 0}

    def both(count, body=None, hops=False):
        base_late, base_early = tail["late"], tail["early"]

        def turn(i):
            if body is not None:
                body(i)
            late.step(base_late + i)
            if hops:
                for h in range(5):

                    @pl.when(i == 1 + 2 * h)
                    def _(h=h):
                        vec_hop(h).wait()
                        sums[...] = sums[...] + vec_in[h]
                        if h < 4:
                            vec_hop(h + 1).start()

            @pl.when(lax.rem(i, LATE_TURNS) == LATE_TURNS - 1)
            def _():
                early.step(base_early + lax.div(i, LATE_TURNS))

        loop(count, turn)
        tail["late"] += count
        tail["early"] += count // LATE_TURNS

    for kk, grad in ((0, dq), (1, dk), (2, dv)):
        weights = use(9 + kk)

        def tile_in(i):
            at = columns(i)
            one[:, at] = one[:, at] + dot_nt(grad[...], weights[at, :])

        both(WIDE // 256, tile_in)
    out = pltpu.make_async_copy(one, input_out, osem.at[0])
    out.start()
    turns = max(late.steps - tail["late"], LATE_TURNS * (early.steps - tail["early"]))
    both(-(-turns // LATE_TURNS) * LATE_TURNS, hops=True)

    for c in range(2):

        @pl.when(core == c)
        def _(c=c):
            n = len(given[c])
            for back_by in (2, 1):
                for f in range(4):
                    give(given[c][n - back_by], c, n - back_by, f).wait_send()

    early.finish()
    late.finish()
    out.wait()

    @pl.when(p == 3)
    def _():
        pltpu.make_async_copy(chain.at[0], total, osem.at[1]).wait()


CHUNK_EARLY, CHUNK_LATE = 128, 32
LAG_EARLY, LAG_LATE = 2, 3
LATE_TURNS = 2
NO = ()
PACE = (
    (NO, NO, NO, NO),
    (NO, NO, NO, NO),
    (NO, (3,), NO, NO),
    ((3,), NO, (3,), NO),
    NO,
    (3,),
    (3,),
    (1, 3, 5, 7),
    (3,),
)


def backward(full, x, q, k, kt, v, ctx, stat, mid, hat, inv, act, slope, two, sums, vec):
    anywhere = pl.BlockSpec(memory_space=pl.ANY)
    vmem = pl.BlockSpec(memory_space=pltpu.VMEM)
    dma = pltpu.SemaphoreType.DMA
    low, wide = jnp.bfloat16, jnp.float32
    page = (TOKENS, WIDE)
    many_a, many_b = WIDE // CHUNK_EARLY, WIDE // CHUNK_LATE

    def stream_sems(many):
        return [dma((6, many)), dma((6, many)), dma((2, 2, many)), dma((2, 2, many)), dma((2, many)), dma((3, 2))]

    return pl.pallas_call(
        backward_kernel,
        name="backward",
        out_shape=[
            jax.ShapeDtypeStruct(page, wide),
            jax.ShapeDtypeStruct((2, WIDE, WIDE), low),
            jax.ShapeDtypeStruct((16, WIDE), wide),
            jax.ShapeDtypeStruct((6, WIDE, WIDE), low),
            jax.ShapeDtypeStruct((6, WIDE, WIDE), low),
        ],
        in_specs=[anywhere] * 15 + [vmem],
        out_specs=[anywhere, anywhere, vmem, anywhere, anywhere],
        scratch_shapes=[
            pltpu.VMEM((RING, WIDE, WIDE), low),
            pltpu.VMEM((10,) + page, low),
            pltpu.VMEM((5, WIDE, TOKENS), low),
            pltpu.VMEM((4,) + page, wide),
            pltpu.VMEM((H, 1, TOKENS), wide),
            pltpu.VMEM((TOKENS, 128), wide),
            pltpu.VMEM((2, WIDE, WIDE), low),
            pltpu.VMEM((6, WIDE, WIDE), low),
            pltpu.VMEM((2, 2, WIDE, WIDE), low),
            pltpu.VMEM((3, 2, CHUNK_EARLY, WIDE), low),
            pltpu.VMEM((3, 2, CHUNK_LATE, WIDE), low),
            pltpu.VMEM((5, 16, WIDE), wide),
            dma((RING,)), dma((2,)), dma((2,)), dma((12,)), dma((2,)),
            dma((6, 4)), dma((6, 4)),
            *stream_sems(many_a),
            *stream_sems(many_b),
            dma((5,)), dma((5,)),
        ],
        compiler_params=pltpu.CompilerParams(
            collective_id=2, has_side_effects=True, vmem_limit_bytes=62 << 20
        ),
    )(full, x, q, k, kt, v, ctx, stat, mid, hat, inv, act, slope, two, sums, vec)


STRIP = 256


def update_kernel(
    grads, left_stat, right_stat, left_root, right_root, master, averaged, sums, vectors, moment, page_one, page_two,
    block_out, left_out, right_out, master_out, copy_out, ema_out, vgrad_out, moment_out, vector_out, bias_out, one_out, two_out,
    b, ls, rs, lr, rr, ms, av, bt, pre, bo, cp, pages, isem, osem, psem,
):
    z, dp = lax.axis_index("tp"), lax.axis_index("dp")
    sources = (grads, left_root, right_root, left_stat, right_stat, master, averaged)
    places = (b, lr, rr, ls, rs, ms, av)

    def load(n, s):
        return pltpu.make_async_copy(sources[n].at[s], places[n].at[s], isem.at[n, s])

    for s in range(2):
        for n in range(7):
            load(n, s).start()

    def page(n, way):
        if way == 0:
            return pltpu.make_async_copy((page_one, page_two)[n], pages.at[n], psem.at[n, 0])
        return pltpu.make_async_copy(pages.at[n], (one_out, two_out)[n], psem.at[n, 1])

    page(0, 0).start()
    page(1, 0).start()
    own = pl.ds(pl.multiple_of(dp * 128, 128), 128)
    grad = sums[0:12, own]
    bias_out[...] = sums[0:1, own]
    vgrad_out[...] = grad
    fresh = MOMENTUM * moment[...] + grad
    moment_out[...] = fresh
    tokens = TOKENS * 32
    vector_out[...] = vectors[:, own] - (VEC_RATE / math.sqrt(tokens)) * fresh

    def store(n, s):
        dest = (block_out, left_out, right_out, master_out, copy_out, ema_out)[n].at[s]
        source = (bo, ls, rs, ms, cp, av)[n].at[s]
        return pltpu.make_async_copy(source, dest, osem.at[n, s])

    strip = pl.ds(pl.multiple_of(z * STRIP, STRIP), STRIP)
    for s in range(2):
        load(0, s).wait()
        load(1, s).wait()
        root_low = lr[s].astype(jnp.bfloat16)

        def first(i):
            at = columns(i)
            pre[:, at] = dot(root_low, b[s, :, at]).astype(jnp.bfloat16)
            turned = b[s, columns(i), strip]
            bo[s, columns(i), :] = turned.astype(jnp.float32)
            bt[:, at] = turned.T

        loop(WIDE // 256, first)
        store(0, s).start()
        load(3, s).wait()
        load(4, s).wait()

        def stats(i):
            at = columns(i)
            ls[s, :, at] = STAT_DECAY * ls[s, :, at] + (1.0 - STAT_DECAY) * dot_nt(b[s, strip, :], b[s, at, :])
            rs[s, :, at] = STAT_DECAY * rs[s, :, at] + (1.0 - STAT_DECAY) * dot(bt[...], b[s, :, at])

        loop(WIDE // 256, stats)
        page(s, 0).wait()
        page(s, 1).start()
        store(1, s).start()
        store(2, s).start()
        load(2, s).wait()
        load(5, s).wait()
        load(6, s).wait()

        def second(i):
            at = columns(i)
            change = dot(pre[...], rr[s, :, at].astype(jnp.bfloat16))
            value = ms[s, :, at] - BLOCK_RATE * change
            ms[s, :, at] = value
            cp[s, :, at] = value.astype(jnp.bfloat16)
            av[s, :, at] = EMA_DECAY * av[s, :, at] + (1.0 - EMA_DECAY) * value

        loop(WIDE // 256, second)
        for n in (3, 4, 5):
            store(n, s).start()
    for s in range(2):
        page(s, 1).wait()
        for n in range(6):
            store(n, s).wait()


def update(grads, left_stat, right_stat, left_root, right_root, master, averaged, sums, vectors, moment, page_one, page_two):
    anywhere = pl.BlockSpec(memory_space=pl.ANY)
    vmem = pl.BlockSpec(memory_space=pltpu.VMEM)
    dma = pltpu.SemaphoreType.DMA
    low, wide = jnp.bfloat16, jnp.float32
    rows = (2, STRIP, WIDE)
    shapes = [
        ((2, WIDE, STRIP), wide), (rows, wide), (rows, wide), (rows, wide), (rows, low), (rows, wide),
        ((12, 128), wide), ((12, 128), wide), ((12, 128), wide), ((1, 128), wide),
        ((TOKENS, WIDE), wide), ((TOKENS, WIDE), wide),
    ]
    return pl.pallas_call(
        update_kernel,
        name="update",
        out_shape=[jax.ShapeDtypeStruct(*shape) for shape in shapes],
        in_specs=[anywhere] * 7 + [vmem] * 3 + [anywhere] * 2,
        out_specs=[anywhere] * 6 + [vmem] * 4 + [anywhere] * 2,
        scratch_shapes=[
            pltpu.VMEM((2, WIDE, WIDE), low),
            pltpu.VMEM(rows, wide), pltpu.VMEM(rows, wide), pltpu.VMEM(rows, wide),
            pltpu.VMEM((2, WIDE, WIDE), wide),
            pltpu.VMEM(rows, wide), pltpu.VMEM(rows, wide),
            pltpu.VMEM((WIDE // 4, WIDE), low), pltpu.VMEM((STRIP, WIDE), low),
            pltpu.VMEM((2, WIDE, STRIP), wide),
            pltpu.VMEM(rows, low),
            pltpu.VMEM((2, TOKENS, WIDE), wide),
            dma((7, 2)), dma((6, 2)), dma((2, 2)),
        ],
        compiler_params=pltpu.CompilerParams(vmem_limit_bytes=56 << 20),
    )(grads, left_stat, right_stat, left_root, right_root, master, averaged, sums, vectors, moment, page_one, page_two)


def layout_embed(cell_boxes, cell_ids):
    cell_count = cell_boxes.shape[1]
    onehot = (
        cell_ids[:, :, None] == jnp.arange(cell_count, dtype=jnp.int32)[None, None, :]
    ).astype(jnp.float32)
    corners = jnp.einsum("psc,pck->psk", onehot, cell_boxes.astype(jnp.float32), precision=PRECISE)
    quarter = MODEL_WIDTH // 4
    half_width = quarter // 2
    frequency = jnp.exp(
        -jnp.arange(half_width, dtype=jnp.float32) * (math.log(1000.0) / half_width)
    )
    angle_grid = corners[..., None] * frequency
    wave_table = jnp.concatenate([jnp.sin(angle_grid), jnp.cos(angle_grid)], -1)
    return 0.5 * wave_table.reshape(corners.shape[0], corners.shape[1], MODEL_WIDTH)


def gelu_exact(values):
    return jax.nn.gelu(values, approximate=False)


def norm_forward(values, gain, shift):
    center = values - jnp.mean(values, -1, keepdims=True)
    inv_std = lax.rsqrt(jnp.mean(center * center, -1, keepdims=True) + EPS_NORM)
    normed = center * inv_std
    return (normed * gain + shift, normed, inv_std)


def norm_backward(grad_in, normed, inv_std, gain):
    scaled = grad_in * gain
    grad_arg = inv_std * (
        scaled
        - jnp.mean(scaled, -1, keepdims=True)
        - normed * jnp.mean(scaled * normed, -1, keepdims=True)
    )
    return (grad_arg, jnp.sum(grad_in * normed, (0, 1)), jnp.sum(grad_in, (0, 1)))


def attend(query_low, key_low, value_low, head_count):
    groups, seq_len = (query_low.shape[0], query_low.shape[1])
    shape_heads = (groups, seq_len, head_count, HD)
    scores = jnp.einsum(
        "gqhe,gkhe->ghqk",
        query_low.reshape(shape_heads),
        key_low.reshape(shape_heads),
        preferred_element_type=jnp.float32,
    ) * HD ** (-0.5)
    row_max = jnp.max(scores, -1, keepdims=True)
    log_total = row_max + jnp.log(jnp.sum(jnp.exp(scores - row_max), -1, keepdims=True))
    probs = jnp.exp(scores - log_total).astype(jnp.bfloat16)
    context = jnp.einsum(
        "ghqk,gkhe->gqhe", probs, value_low.reshape(shape_heads), preferred_element_type=jnp.float32
    )
    return (context.reshape(groups, seq_len, head_count * HD).astype(jnp.bfloat16), log_total)


def attend_back(query_low, key_low, value_low, log_total, ctx_grad, head_count):
    groups, seq_len = (query_low.shape[0], query_low.shape[1])
    shape_heads = (groups, seq_len, head_count, HD)
    query_heads = query_low.reshape(shape_heads)
    key_heads = key_low.reshape(shape_heads)
    value_heads = value_low.reshape(shape_heads)
    grad_heads = ctx_grad.reshape(shape_heads)
    scale = HD ** (-0.5)
    scores = (
        jnp.einsum("gqhe,gkhe->ghqk", query_heads, key_heads, preferred_element_type=jnp.float32)
        * scale
    )
    probs = jnp.exp(scores - log_total)
    value_grad = jnp.einsum(
        "ghqk,gqhe->gkhe",
        probs.astype(jnp.bfloat16),
        grad_heads,
        preferred_element_type=jnp.float32,
    )
    prob_grad = jnp.einsum(
        "gqhe,gkhe->ghqk", grad_heads, value_heads, preferred_element_type=jnp.float32
    )
    score_grad = (probs * (prob_grad - jnp.sum(probs * prob_grad, -1, keepdims=True))).astype(
        jnp.bfloat16
    )
    query_grad = (
        jnp.einsum("ghqk,gkhe->gqhe", score_grad, key_heads, preferred_element_type=jnp.float32)
        * scale
    )
    key_grad = (
        jnp.einsum("ghqk,gqhe->gkhe", score_grad, query_heads, preferred_element_type=jnp.float32)
        * scale
    )
    width = head_count * HD
    return (
        query_grad.reshape(groups, seq_len, width).astype(jnp.bfloat16),
        key_grad.reshape(groups, seq_len, width).astype(jnp.bfloat16),
        value_grad.reshape(groups, seq_len, width).astype(jnp.bfloat16),
    )


def by_collectives(
    hidden, cell_ids, cell_boxes, cotangent, weight_cols, weight_out, weight_down, vectors, slot_dev
):
    dp_count = lax.axis_size("dp")
    col_mats = lax.all_gather(weight_cols, "tp", axis=2, tiled=True)
    out_mat = lax.all_gather(weight_out, "tp", axis=0, tiled=True)
    down_mats = lax.all_gather(weight_down, "tp", axis=1, tiled=True)
    x_own = hidden.astype(jnp.float32) + layout_embed(cell_boxes, cell_ids)
    x_low = x_own.astype(jnp.bfloat16)
    projected = jnp.einsum(
        "gtd,kdc->kgtc", x_low, col_mats[0:3], preferred_element_type=jnp.float32
    )
    query_low = (projected[0] + vectors[:, 6]).astype(jnp.bfloat16)
    key_low = projected[1].astype(jnp.bfloat16)
    value_low = (projected[2] + vectors[:, 7]).astype(jnp.bfloat16)
    context, log_total = attend(query_low, key_low, value_low, H)
    attn_out = jnp.einsum("gtc,cd->gtd", context, out_mat, preferred_element_type=jnp.float32)
    mid_out, mid_hat, mid_inv = norm_forward(
        x_own + attn_out + vectors[:, 0], vectors[:, 2], vectors[:, 3]
    )
    mid_low = mid_out.astype(jnp.bfloat16)
    up_pre = jnp.einsum(
        "gtd,kdc->kgtc", mid_low, col_mats[3:7], preferred_element_type=jnp.float32
    )
    up_pre = up_pre + jnp.transpose(vectors[:, 8:12])[:, None, None, :]
    act_low = gelu_exact(up_pre).astype(jnp.bfloat16)
    ffn_out = jnp.einsum("kgtc,kcd->gtd", act_low, down_mats, preferred_element_type=jnp.float32)
    layer_out, out_hat, out_inv = norm_forward(
        mid_out + ffn_out + vectors[:, 1], vectors[:, 4], vectors[:, 5]
    )
    output_gradient = cotangent.astype(jnp.float32)
    grad_two, gain_two, shift_two = norm_backward(output_gradient, out_hat, out_inv, vectors[:, 4])
    two_low = grad_two.astype(jnp.bfloat16)
    act_grad = jnp.einsum("gtd,kcd->kgtc", two_low, down_mats, preferred_element_type=jnp.float32)
    gelu_pull = jax.vjp(gelu_exact, up_pre)[1]
    up_low = gelu_pull(act_grad)[0].astype(jnp.bfloat16)
    mid_back = jnp.einsum(
        "kgtc,kdc->gtd", up_low, col_mats[3:7], preferred_element_type=jnp.float32
    )
    grad_one, gain_one, shift_one = norm_backward(
        mid_back + grad_two, mid_hat, mid_inv, vectors[:, 2]
    )
    one_low = grad_one.astype(jnp.bfloat16)
    ctx_grad = jnp.einsum(
        "gtd,cd->gtc", one_low, out_mat, preferred_element_type=jnp.float32
    ).astype(jnp.bfloat16)
    query_grad, key_grad, value_grad = attend_back(
        query_low, key_low, value_low, log_total, ctx_grad, H
    )
    qkv_grad = jnp.stack([query_grad, key_grad, value_grad], 0)
    input_grad = grad_one + jnp.einsum(
        "kgtc,kdc->gtd", qkv_grad, col_mats[0:3], preferred_element_type=jnp.float32
    )

    def block(text, left, right):
        return jnp.einsum(text, left, right, preferred_element_type=jnp.float32).astype(
            jnp.bfloat16
        )

    qkv_blocks = block("gtd,kgtc->kdc", x_low, qkv_grad)
    up_blocks = block("gtd,kgtc->kdc", mid_low, up_low)
    out_block = block("gtd,gtc->dc", one_low, context)[None]
    down_blocks = block("gtd,kgtc->kdc", two_low, act_low)
    vector_part = jnp.stack(
        [
            jnp.sum(grad_one, (0, 1)),
            jnp.sum(grad_two, (0, 1)),
            gain_one,
            shift_one,
            gain_two,
            shift_two,
            jnp.sum(query_grad, (0, 1), dtype=jnp.float32),
            jnp.sum(value_grad, (0, 1), dtype=jnp.float32),
        ],
        0,
    )
    vector_part = jnp.concatenate(
        [vector_part, jnp.sum(up_low, (1, 2), dtype=jnp.float32)], 0
    )
    block_part = jnp.concatenate(
        [
            qkv_blocks,
            up_blocks,
            out_block,
            down_blocks,
            jnp.zeros((slot_dev * dp_count - 12, MODEL_WIDTH, MODEL_WIDTH), jnp.bfloat16),
        ],
        0,
    )
    block_owned = lax.psum_scatter(block_part, "dp", scatter_dimension=0, tiled=True)
    full_grad = lax.psum(block_owned, "tp")
    vector_all = lax.psum(vector_part, ("dp", "tp"))
    return layer_out, input_grad, full_grad, vector_all


def local(
    hidden,
    cell_ids,
    cell_boxes,
    cotangent,
    weight_cols,
    weight_out,
    weight_down,
    vectors,
    vector_moment,
    left_stat,
    right_stat,
    left_root,
    right_root,
    master,
    averaged_weight,
):
    tp_count = lax.axis_size("tp")
    dp_count = lax.axis_size("dp")
    tp_index = lax.axis_index("tp")
    dp_index = lax.axis_index("dp")
    strip_width = weight_cols.shape[2]
    page_rows, seq_len = (hidden.shape[0], hidden.shape[1])
    owned_rows = vector_moment.shape[0]
    slot_dev = left_stat.shape[0]
    if dp_count == 8 and tp_count == 4:
        vec = jnp.transpose(vectors)
        full, layer_out, *kept, sums = forward(
            weight_cols, weight_out, weight_down, hidden[0], cell_ids, jnp.transpose(cell_boxes[0]), cotangent[0], vec
        )
        input_grad, full_grad, vector_all, *_ = backward(full, *kept, sums, vec)
        outs = update(
            full_grad, left_stat, right_stat, left_root, right_root, master, averaged_weight, vector_all, vec,
            jnp.transpose(vector_moment), layer_out, input_grad
        )
        *blocks, vector_grad, moment_new, vector_new, bias_grad, layer_out, input_grad = outs
        thin = [jnp.transpose(array) for array in (vector_grad, moment_new, vector_new)]
        return (layer_out[None], input_grad[None], *blocks, *thin, bias_grad[0])
    else:
        layer_out, input_grad, full_grad, vector_all = by_collectives(
            hidden, cell_ids, cell_boxes, cotangent, weight_cols, weight_out, weight_down, vectors, slot_dev
        )
    vector_grad = jnp.transpose(
        lax.dynamic_slice_in_dim(vector_all[0:12], dp_index * owned_rows, owned_rows, 1)
    )
    own_rows = lax.dynamic_slice_in_dim(full_grad, tp_index * strip_width, strip_width, 1)
    own_cols = lax.dynamic_slice_in_dim(full_grad, tp_index * strip_width, strip_width, 2)
    block_grad = own_cols.astype(jnp.float32)
    left_new = STAT_DECAY * left_stat + (1.0 - STAT_DECAY) * jnp.einsum(
        "sic,sjc->sij", own_rows, full_grad, preferred_element_type=jnp.float32
    )
    right_new = STAT_DECAY * right_stat + (1.0 - STAT_DECAY) * jnp.einsum(
        "sic,sij->scj", own_cols, full_grad, preferred_element_type=jnp.float32
    )

    def parts(array):
        high = array.astype(jnp.bfloat16)
        return high, (array - high.astype(jnp.float32)).astype(jnp.bfloat16)

    def product(left, right):
        return jnp.einsum("sij,sjc->sic", left, right, preferred_element_type=jnp.float32)

    left_high, left_rest = parts(left_root)
    right_high, right_rest = parts(right_root)
    precond = product(left_high, full_grad) + product(left_rest, full_grad)
    pre_high, pre_rest = parts(precond)
    precond = (
        product(pre_high, right_high) + product(pre_rest, right_high) + product(pre_high, right_rest)
    )
    master_new = master - BLOCK_RATE * precond
    weight_copy = master_new.astype(jnp.bfloat16)
    ema_new = EMA_DECAY * averaged_weight + (1.0 - EMA_DECAY) * master_new
    vector_rows = lax.dynamic_slice_in_dim(vectors, dp_index * owned_rows, owned_rows, 0)
    moment_new = MOMENTUM * vector_moment + vector_grad
    total_tokens = page_rows * seq_len * dp_count * tp_count
    vector_new = vector_rows - VEC_RATE * lax.rsqrt(jnp.float32(total_tokens)) * moment_new
    bias_grad = vector_grad[:, 0]
    return (
        layer_out,
        input_grad,
        block_grad,
        left_new,
        right_new,
        master_new,
        weight_copy,
        ema_new,
        vector_grad,
        moment_new,
        vector_new,
        bias_grad,
    )


def solution(mesh):
    return jax.shard_map(
        local,
        mesh=mesh,
        in_specs=(
            P(("dp", "tp"), None, None),
            P(("dp", "tp"), None),
            P(("dp", "tp"), None, None),
            P(("dp", "tp"), None, None),
            P(None, None, "tp"),
            P("tp", None),
            P(None, "tp", None),
            P(),
            P("dp", None),
            P("dp", "tp", None),
            P("dp", "tp", None),
            P("dp", "tp", None),
            P("dp", None, None),
            P("dp", "tp", None),
            P("dp", "tp", None),
        ),
        out_specs=(
            P(("dp", "tp"), None, None),
            P(("dp", "tp"), None, None),
            P("dp", None, "tp"),
            P("dp", "tp", None),
            P("dp", "tp", None),
            P("dp", "tp", None),
            P("dp", "tp", None),
            P("dp", "tp", None),
            P("dp", None),
            P("dp", None),
            P("dp", None),
            P("dp"),
        ),
        check_vma=False,
    )
```

```python
import math

import jax
import jax.numpy as jnp
from jax import lax
from jax.experimental import pallas as pl
from jax.experimental.pallas import tpu as pltpu
from jax.sharding import PartitionSpec as P

MODEL_WIDTH = 1024
H = 16
HD = 64

PRECISE = lax.Precision.HIGHEST
EPS_NORM = 1e-06
STAT_DECAY = 0.5
BLOCK_RATE = 0.7
EMA_DECAY = 0.9
MOMENTUM = 0.9
VEC_RATE = 0.2

MESH = pl.DeviceIdType.MESH


def position():
    d, z = lax.axis_index("dp"), lax.axis_index("tp")
    core, x, y = d % 2, (d // 2) % 2, d // 4
    near = {
        "x": (d + 2 - 4 * x, z),
        "y": (d + 4 - 8 * y, z),
        "c": (d + 1 - 2 * core, z),
        "u": (d, z + 1),
        "v": (d, z - 1),
    }
    return z, core, x, y, near


def meet(z, near, extra=()):
    barrier = pltpu.get_barrier_semaphore()
    always = [near[name] for name in "xyc"] + list(extra)
    for device in always:
        pl.semaphore_signal(barrier, 1, device_id=device, device_id_type=MESH)

    @pl.when(z < 3)
    def _():
        pl.semaphore_signal(barrier, 1, device_id=near["u"], device_id_type=MESH)

    @pl.when(z > 0)
    def _():
        pl.semaphore_signal(barrier, 1, device_id=near["v"], device_id_type=MESH)

    pl.semaphore_wait(barrier, len(always) + (z + 2) // 3 + (5 - z) // 3)


ORDER = (0, 1, 2, 7, 3, 4, 5, 6, 8, 9, 10, 11)


NT = (((1,), (1,)), ((), ()))
TOKENS = 512
WIDE = MODEL_WIDTH


def dot(a, b):
    return jnp.dot(a, b, preferred_element_type=jnp.float32)


def dot_nt(a, b):
    return lax.dot_general(a, b, NT, preferred_element_type=jnp.float32)


def columns(i, width=256):
    return pl.ds(pl.multiple_of(i * width, width), width)


def loop(count, body):
    def step(i, carry):
        body(i)
        return carry

    lax.fori_loop(0, count, step, 0)


def mean_of(rows):
    return jnp.sum(rows, -1, keepdims=True) * (1.0 / WIDE)


def transpose_into(dest, source):
    def body(i):
        dest[columns(i), :] = source[:, columns(i)].T

    loop(WIDE // 256, body)


def transpose_back(dest, source):
    def body(i):
        dest[:, columns(i)] = source[columns(i), :].T

    loop(WIDE // 256, body)


def embed_tokens(hidden, ids, boxes, x_ref, x_low):
    cells = boxes.shape[1]
    corners = boxes[...].astype(jnp.float32).T
    half = WIDE // 8
    place = lax.broadcasted_iota(jnp.int32, (1, half), 1).astype(jnp.float32)
    rate = jnp.exp(place * (-math.log(1000.0) / half))
    marks = lax.broadcasted_iota(jnp.int32, (cells, TOKENS), 0) == ids[...]
    chosen = jnp.where(marks, 1.0, 0.0).T.astype(jnp.bfloat16)
    for c in range(4):
        angle = corners[:, c : c + 1] * rate
        for kind, wave in enumerate((jnp.sin(angle), jnp.cos(angle))):
            wave = 0.5 * wave
            high = wave.astype(jnp.bfloat16)
            rest = wave - high.astype(jnp.float32)
            middle = rest.astype(jnp.bfloat16)
            low = (rest - middle.astype(jnp.float32)).astype(jnp.bfloat16)
            emb = dot(chosen, high) + (dot(chosen, middle) + dot(chosen, low))
            at = pl.ds(c * 2 * half + kind * half, half)
            value = hidden[:, at].astype(jnp.float32) + emb
            x_ref[:, at] = value
            x_low[:, at] = value.astype(jnp.bfloat16)


def project(x_low, weight, dest, bias, scale):
    def body(i):
        at = columns(i, 512)
        value = dot(x_low[...], weight[:, at])
        if bias is not None:
            value = value + bias[:, at]
        value = value.astype(jnp.bfloat16)
        if scale:
            value = value * jnp.asarray(HD ** (-0.5), jnp.bfloat16)
        dest[:, at] = value

    loop(WIDE // 512, body)


def half_mask(e, shape):
    lane = lax.broadcasted_iota(jnp.int32, shape, 1)
    return (lane < HD) if e == 0 else (lane >= HD)


def attend_pair(t, q8, k, v_t, ctx_t, stat):
    at = columns(t, 128)
    keys, queries = k[:, at], q8[:, at]
    for e in range(2):
        own = jnp.where(half_mask(e, queries.shape), queries, jnp.zeros_like(queries))
        scores = dot_nt(keys, own)
        top = jnp.max(scores, 0, keepdims=True)
        power = jnp.exp(scores - top)
        total = jnp.sum(power, 0, keepdims=True)
        probs = (power * (1.0 / total)).astype(jnp.bfloat16)
        rows = pl.ds(pl.multiple_of(t * 128 + e * 64, 64), 64)
        ctx_t[rows, :] = dot(v_t[rows, :], probs).astype(jnp.bfloat16)
        stat[2 * t + e, :, :] = top + jnp.log(total)


def norm_rows(values, gain, shift):
    center = values - mean_of(values)
    inv = lax.rsqrt(mean_of(center * center) + EPS_NORM)
    normed = center * inv
    return normed * gain + shift, normed, inv


SLICE = 64


def row_loop(body):
    loop(TOKENS // SLICE, lambda i: body(pl.ds(pl.multiple_of(i * SLICE, SLICE), SLICE)))


def gelu_both(value):
    phi = 0.5 * (1.0 + lax.erf(value * math.sqrt(0.5)))
    density = jnp.exp(-0.5 * value * value) * (1.0 / math.sqrt(2.0 * math.pi))
    return value * phi, phi + value * density


def forward_kernel(
    cols, outw, down, hidden, ids, boxes, cotangent, vec,
    full_out, layer_out, x_out, q_out, k_out, kt_out, v_out, ctx_out, stat_out, mid_out, hat_out, inv_out, act_out, slope_out,
    two_out, sums_out,
    w, x_t, mid_t, k_t, x_ref, x_low, q8, k, v, v_t, ctx_t, ctx, stat, acc, mid, mid_low, hat, inv, act, slope, y_out, two, sums,
    load, along, onward, arrived, beside, store, spill,
):
    z, core, x, y, near = position()
    p = 2 * y + x
    meet(z, near)

    def own(kk, h):
        if kk < 7:
            return cols.at[kk, pl.ds(h * 512, 512), :]
        if kk == 7:
            return outw.at[pl.ds(h * 128, 128), :]
        return down.at[kk - 8, pl.ds(h * 128, 128), :]

    def spot(s, kk, h):
        if kk < 7:
            return w.at[kk, pl.ds(h * 512, 512), pl.ds(pl.multiple_of(s * 256, 256), 256)]
        return w.at[kk, pl.ds(pl.multiple_of(s * 256 + h * 128, 128), 128), :]

    def spot_whole(s, kk):
        if kk < 7:
            return w.at[kk, :, pl.ds(pl.multiple_of(s * 256, 256), 256)]
        return w.at[kk, pl.ds(pl.multiple_of(s * 256, 256), 256), :]

    def whole_own(kk):
        if kk < 7:
            return cols.at[kk]
        return outw if kk == 7 else down.at[kk - 8]

    def to(source, s, kk, send_sem, recv_sem, name):
        return pltpu.make_async_remote_copy(
            src_ref=source,
            dst_ref=spot(s, kk, core),
            send_sem=send_sem,
            recv_sem=recv_sem.at[s, kk],
            device_id=near[name],
            device_id_type=MESH,
        )

    def first(g, act_on):
        for t in range(3):
            kk = ORDER[3 * g + t]
            mine = (p == t) | (p == 3) if t == 0 else p == t

            @pl.when(mine & (z < 3))
            def _(kk=kk):
                act_on(to(own(kk, core), z, kk, along.at[kk], arrived, "u"))

            @pl.when(mine & (z > 0))
            def _(kk=kk):
                act_on(to(own(kk, core), z, kk, onward.at[0, z, kk], arrived, "v"))

    far = 3 * (1 - z // 2)
    nearest = z + 1 - 2 * (z // 3)
    strips = (nearest, 6 - nearest - far - z, far)

    def item(n, t):
        return strips[n % 3], ORDER[3 * (n // 3) + t]

    def go(s, kk, kind, name, sems):
        return to(spot(s, kk, core), s, kk, onward.at[kind, s, kk], sems, name)

    def stage(n, hop, begin):
        for t in range(3):
            s, kk = item(n, t)
            who = {
                (0, 0): (p == 0) | (p == 3),
                (0, 1): p == 1,
                (0, 2): p == 2,
                (1, 0): (p == 1) | (p == 2),
                (1, 1): (p == 0) | (p == 3),
                (1, 2): (p == 0) | (p == 3),
                (2, 0): None,
                (2, 1): p == 2,
                (2, 2): p == 1,
            }[hop, t]
            if who is None:
                continue

            @pl.when(who)
            def _(s=s, kk=kk, t=t):
                if begin:
                    go(s, kk, 0, "x", arrived).wait_recv()

                def act_on(copy):
                    if begin:
                        copy.start()
                    else:
                        copy.wait_send()

                if hop == 0:

                    @pl.when((s > z) & (z > 0))
                    def _():
                        act_on(go(s, kk, 0, "v", arrived))

                    @pl.when((s < z) & (z < 3))
                    def _():
                        act_on(go(s, kk, 0, "u", arrived))

                    if t == 0:

                        @pl.when(p == 0)
                        def _():
                            act_on(go(s, kk, 1, "x", arrived))
                            act_on(go(s, kk, 2, "y", arrived))
                    else:
                        act_on(go(s, kk, 1, "x", arrived))
                        act_on(go(s, kk, 2, "y", arrived))
                if hop == 1 and t == 1:

                    @pl.when(p == 3)
                    def _():
                        act_on(go(s, kk, 1, "x", arrived))

                if hop == 1 and t == 2:

                    @pl.when(p == 3)
                    def _():
                        act_on(go(s, kk, 2, "y", arrived))

                act_on(go(s, kk, 3, "c", beside))

    copies = []

    def keep(source, dest):
        copy = pltpu.make_async_copy(source, dest, spill.at[len(copies)])
        copy.start()
        copies.append(copy)

    def ready(kk):
        pltpu.make_async_copy(whole_own(kk), spot_whole(z, kk), load.at[kk]).wait()
        for s in strips:
            pltpu.make_async_remote_copy(
                src_ref=spot(s, kk, 1 - core),
                dst_ref=spot(s, kk, 1 - core),
                send_sem=onward.at[3, s, kk],
                recv_sem=beside.at[s, kk],
                device_id=near["c"],
                device_id_type=MESH,
            ).wait_recv()
        copy = pltpu.make_async_copy(w.at[kk], full_out.at[kk], store.at[kk])
        copy.start()

    def unit_embed():
        embed_tokens(hidden, ids, boxes, x_ref, x_low)
        transpose_into(x_t, x_low)
        keep(x_t, x_out)

    def unit_qk():
        ready(0)
        project(x_low, w.at[0], q8, vec.at[6:7], True)
        keep(q8, q_out)
        ready(1)
        project(x_low, w.at[1], k, None, False)
        keep(k, k_out)

    def unit_v():
        ready(2)
        project(x_low, w.at[2], v, vec.at[7:8], False)
        transpose_into(v_t, v)
        keep(v, v_out)

    def unit_k_t():
        transpose_into(k_t, k)
        keep(k_t, kt_out)

    def unit_attend(lo, hi):
        loop(hi - lo, lambda i: attend_pair(lo + i, q8, k, v_t, ctx_t, stat))

    def unit_context():
        transpose_back(ctx, ctx_t)
        keep(ctx, ctx_out)
        keep(stat, stat_out)

    def unit_mid():
        ready(7)

        def tile(i):
            at = columns(i, 512)
            acc[:, at] = dot(ctx[...], w[7, :, at])

        loop(WIDE // 512, tile)

        def rows(r):
            value = x_ref[r, :] + acc[r, :] + vec[0:1, :]
            out, normed, scale = norm_rows(value, vec[2:3, :], vec[3:4, :])
            mid[r, :] = out
            mid_low[r, :] = out.astype(jnp.bfloat16)
            hat[r, :] = normed
            inv[r, :] = jnp.broadcast_to(scale, (SLICE, 128))

        row_loop(rows)
        transpose_into(mid_t, mid_low)
        keep(mid_t, mid_out)
        keep(hat, hat_out)
        keep(inv, inv_out)

    def unit_up(u):
        ready(3 + u)
        def tile(i):
            at = columns(i)
            slot = i % 2

            @pl.when(i >= 2)
            def _():
                pltpu.make_async_copy(slope.at[slot], slope_out.at[u, :, at], store.at[12 + slot]).wait()

            value = dot(mid_low[...], w[3 + u, :, at]) + vec[8 + u : 9 + u, at]
            out, grad = gelu_both(value)
            act[u, :, at] = out.astype(jnp.bfloat16)
            slope[slot] = grad
            pltpu.make_async_copy(slope.at[slot], slope_out.at[u, :, at], store.at[12 + slot]).start()

        loop(WIDE // 256, tile)
        for slot in range(2):
            pltpu.make_async_copy(slope.at[slot], slope_out.at[u, :, columns(slot)], store.at[12 + slot]).wait()
        keep(act.at[u], act_out.at[u])

    def unit_down(u):
        ready(8 + u)

        def tile(i):
            at = columns(i, 512)
            value = dot(act[u], w[8 + u, :, at])
            acc[:, at] = value if u == 0 else acc[:, at] + value

        loop(WIDE // 512, tile)

    def unit_last():
        sums[...] = jnp.zeros_like(sums)

        def rows(r):
            value = mid[r, :] + acc[r, :] + vec[1:2, :]
            out, normed, scale = norm_rows(value, vec[4:5, :], vec[5:6, :])
            y_out[r, :] = out
            grad = cotangent[r, :].astype(jnp.float32)
            scaled = grad * vec[4:5, :]
            arg = scale * (scaled - mean_of(scaled) - normed * mean_of(scaled * normed))
            two[r, :] = arg
            sums[1:2, :] += jnp.sum(arg, 0, keepdims=True)
            sums[4:5, :] += jnp.sum(grad * normed, 0, keepdims=True)
            sums[5:6, :] += jnp.sum(grad, 0, keepdims=True)

        row_loop(rows)
        keep(y_out, layer_out)
        keep(two, two_out)
        keep(sums, sums_out)

    first(0, lambda copy: copy.start())
    first(1, lambda copy: copy.start())
    for kk in ORDER:
        pltpu.make_async_copy(whole_own(kk), spot_whole(z, kk), load.at[kk]).start()
    unit_embed()
    after = {
        4: lambda: (unit_qk(), unit_v()),
        5: lambda: unit_attend(0, 4),
        6: lambda: (unit_attend(4, 8), unit_context()),
        7: unit_mid,
        8: lambda: unit_up(0),
        9: lambda: (unit_up(1), unit_k_t()),
        10: lambda: unit_up(2),
        11: lambda: unit_up(3),
        12: lambda: unit_down(0),
        13: lambda: (unit_down(1), unit_down(2), unit_down(3), unit_last()),
    }
    for n in range(14):
        if n in (3, 6):
            first(n // 3 + 1, lambda copy: copy.start())
        for hop in range(3):
            if 0 <= n - hop < 12:
                stage(n - hop, hop, True)
        if n in after:
            after[n]()
    for n in range(12):
        for hop in range(3):
            stage(n, hop, False)
    for g in range(4):
        first(g, lambda copy: copy.wait_send())
    for kk in ORDER:
        pltpu.make_async_copy(w.at[kk], full_out.at[kk], store.at[kk]).wait()
    for copy in copies:
        copy.wait()


def forward(cols, outw, down, hidden, ids, boxes, cotangent, vec):
    anywhere = pl.BlockSpec(memory_space=pl.ANY)
    vmem = pl.BlockSpec(memory_space=pltpu.VMEM)
    dma = pltpu.SemaphoreType.DMA
    low, wide = jnp.bfloat16, jnp.float32
    page = (TOKENS, WIDE)
    outs = [
        ((12, WIDE, WIDE), low),
        (page, wide),
        ((WIDE, TOKENS), low),
        (page, low),
        (page, low),
        ((WIDE, TOKENS), low),
        (page, low),
        (page, low),
        ((H, 1, TOKENS), wide),
        ((WIDE, TOKENS), low),
        (page, wide),
        ((TOKENS, 128), wide),
        ((4,) + page, low),
        ((4,) + page, wide),
        (page, wide),
        ((16, WIDE), wide),
    ]
    return pl.pallas_call(
        forward_kernel,
        name="forward",
        out_shape=[jax.ShapeDtypeStruct(*o) for o in outs],
        in_specs=[anywhere] * 3 + [vmem] * 5,
        out_specs=[anywhere] * len(outs),
        scratch_shapes=[
            pltpu.VMEM((12, WIDE, WIDE), low),
            pltpu.VMEM((WIDE, TOKENS), low),
            pltpu.VMEM((WIDE, TOKENS), low),
            pltpu.VMEM((WIDE, TOKENS), low),
            pltpu.VMEM(page, wide),
            pltpu.VMEM(page, low),
            pltpu.VMEM(page, low),
            pltpu.VMEM(page, low),
            pltpu.VMEM(page, low),
            pltpu.VMEM((WIDE, TOKENS), low),
            pltpu.VMEM((WIDE, TOKENS), low),
            pltpu.VMEM(page, low),
            pltpu.VMEM((H, 1, TOKENS), wide),
            pltpu.VMEM(page, wide),
            pltpu.VMEM(page, wide),
            pltpu.VMEM(page, low),
            pltpu.VMEM(page, wide),
            pltpu.VMEM((TOKENS, 128), wide),
            pltpu.VMEM((4,) + page, low),
            pltpu.VMEM((2, TOKENS, 256), wide),
            pltpu.VMEM(page, wide),
            pltpu.VMEM(page, wide),
            pltpu.VMEM((16, WIDE), wide),
            dma((12,)),
            dma((12,)),
            dma((4, 4, 12)),
            dma((4, 12)),
            dma((4, 12)),
            dma((14,)),
            dma((20,)),
        ],
        compiler_params=pltpu.CompilerParams(
            collective_id=1, has_side_effects=True, vmem_limit_bytes=61 << 20
        ),
    )(cols, outw, down, hidden, ids, boxes, cotangent, vec)


KEPT = ((8, 5, 9, 0, 1, 4), (10, 3, 11, 2, 6, 7))
EARLY = (((0, 8), (0, 10), 0), ((1, 5), None, 0), (None, (1, 3), 0), ((2, 9), (2, 11), 8))
LATE = (((3, 0), (3, 2), 0), ((4, 1), None, 0), ((5, 4), (4, 6), 0), (None, (5, 7), 0))
UNIT_ORDER = (0, 2, 1, 3)
RING = 3


def attend_pair_back(t, q8, k, v, ctx_grad, k_t, stat, dq_t, dk, dv):
    at = columns(t, 128)
    keys, queries, values, grads = k[:, at], q8[:, at], v[:, at], ctx_grad[:, at]
    none = jnp.zeros_like(queries)
    key_sum = value_sum = None
    for e in range(2):
        mask = half_mask(e, queries.shape)
        own_q = jnp.where(mask, queries, none)
        own_g = jnp.where(mask, grads, none)
        probs = jnp.exp(dot_nt(keys, own_q) - stat[2 * t + e])
        prob_grad = dot_nt(values, own_g)
        carried = jnp.sum(probs * prob_grad, 0, keepdims=True)
        score_grad = (probs * (prob_grad - carried)).astype(jnp.bfloat16)
        rows = pl.ds(pl.multiple_of(t * 128 + e * 64, 64), 64)
        dq_t[rows, :] = (dot(k_t[rows, :], score_grad) * HD ** (-0.5)).astype(jnp.bfloat16)
        key_part = dot(score_grad, own_q)
        value_part = dot(probs.astype(jnp.bfloat16), own_g)
        key_sum = key_part if e == 0 else key_sum + key_part
        value_sum = value_part if e == 0 else value_sum + value_part
    dk[:, at] = key_sum.astype(jnp.bfloat16)
    dv[:, at] = value_sum.astype(jnp.bfloat16)


class Stream:
    def __init__(self, entries, chunk, lag, refs, ring, place):
        self.z, self.core, self.x, self.y, self.d = place
        self.p = 2 * self.y + self.x
        self.chunk, self.per, self.lag = chunk, WIDE // chunk, lag
        self.entries, self.refs, self.ring = entries, refs, ring
        self.base = min(item[0] for entry in entries for item in entry[:2] if item is not None)
        self.steps = max(entry[2] for entry in entries) + self.per + 6 * lag
        x, y = self.x, self.y
        self.corner = [(x if j % 2 == 0 else 1 - x, y if j // 2 == 0 else 1 - y) for j in range(3)]
        self.by_x, self.by_y = 2 - 4 * x, 4 - 8 * y

    def rows(self, r):
        return pl.ds(pl.multiple_of(r * self.chunk, self.chunk), self.chunk)

    def remote(self, source, dest, send_sem, recv_sem, device):
        return pltpu.make_async_remote_copy(
            src_ref=source, dst_ref=dest, send_sem=send_sem, recv_sem=recv_sem,
            device_id=device, device_id_type=MESH,
        )


    def forward(self, q, r, turn):
        R = self.refs
        at = self.rows(r)
        device = (self.d + self.by_y + turn * (self.by_x - self.by_y), self.z)
        return self.remote(R["mine"].at[q, at, :], R["land"].at[q, at, :], R["send"].at[q, r], R["recv"].at[q, r], device)

    def chained(self, i, r, way):
        R = self.refs
        at = self.rows(r)
        return R["chain"].at[way, i, at, :], R["chain_send"].at[way, i, r], R["chain_recv"].at[way, i, r]

    def pass_on(self, source, i, r, way):
        ref, ssem, rsem = self.chained(i, r, way)
        return self.remote(source, ref, ssem, rsem, (self.d, self.z + (1 if way == 0 else -1)))

    def total_out(self, source, i, r):
        R = self.refs
        return pltpu.make_async_copy(source, R["total"].at[i, self.rows(r), :], R["out"].at[i, r])

    def add_to_mine(self, q, r, ref):
        mine = self.refs["mine"]

        def part(g):
            at = pl.ds(pl.multiple_of(r * self.chunk + g * 32, 32), 32)
            here = pl.ds(pl.multiple_of(g * 32, 32), 32)
            mine[q, at, :] = (mine[q, at, :].astype(jnp.float32) + ref[here, :].astype(jnp.float32)).astype(jnp.bfloat16)

        loop(self.chunk // 32, part)

    def load(self, e, kind, q, r):
        source = self.refs["sib" if kind == 0 else "land"]
        return pltpu.make_async_copy(source.at[q, self.rows(r), :], self.ring.at[q - self.base, kind], self.refs["ring_sem"].at[q - self.base, kind])

    def begin_pair(self, e, q, j, i, r):
        R = self.refs
        quarter = 256 // self.chunk

        def arrival(f):
            at = pl.ds(pl.multiple_of(f * 256, 256), 256)
            ref = R["sib"].at[q, at, :]
            self.remote(ref, ref, R["give_send"].at[q, f], R["give_recv"].at[q, f], (self.d, self.z)).wait_recv()

        if quarter == 1:
            arrival(r)
        else:

            @pl.when(lax.rem(r, quarter) == 0)
            def _():
                arrival(lax.div(r, quarter))

        self.load(e, 0, q, r).start()

    def end_pair(self, e, q, j, i, r):
        self.load(e, 0, q, r).wait()
        self.add_to_mine(q, r, self.ring.at[q - self.base, 0])
        odd = lax.rem(r, 2)
        rx, ry = self.corner[j]

        @pl.when((rx + ry == 1) & (rx + odd == 1))
        def _():
            self.forward(q, r, odd).start()

    def path(self, hop, begin):
        def run(e, q, j, i, r):
            odd = lax.rem(r, 2)
            rx, ry = self.corner[j]
            here = {1: rx + ry == 2, 2: (rx + ry == 1) & (rx == odd), 3: rx + ry == 0}[hop]

            @pl.when(here)
            def _():
                copy = self.load(e, 1, q, r)
                if begin:
                    self.forward(q, r, odd).wait_recv()
                    copy.start()
                    return
                copy.wait()
                self.add_to_mine(q, r, self.ring.at[q - self.base, 1])
                if hop == 1:
                    self.forward(q, r, 1 - odd).start()
                if hop == 2:
                    self.forward(q, r, odd).start()
                if hop == 3:
                    mine = self.refs["mine"].at[q, self.rows(r), :]

                    @pl.when(self.z == 0)
                    def _():
                        self.pass_on(mine, i, r, 0).start()

                    @pl.when(self.z == 3)
                    def _():
                        self.pass_on(mine, i, r, 1).start()

        return run

    def link(self, q, i, r, way, last):
        R = self.refs
        at = self.rows(r)
        ref, ssem, rsem = self.chained(i, r, way)
        self.remote(ref, ref, ssem, rsem, (self.d, self.z)).wait_recv()
        mine, chain = R["mine"], R["chain"]

        def part(g):
            piece = pl.ds(pl.multiple_of(r * self.chunk + g * 32, 32), 32)
            came = chain[way, i, piece, :].astype(jnp.float32)
            chain[way, i, piece, :] = (mine[q, piece, :].astype(jnp.float32) + came).astype(jnp.bfloat16)
            if last:
                other = chain[1 - way, i, piece, :].astype(jnp.float32)
                mine[q, piece, :] = (other + came).astype(jnp.bfloat16)

        loop(self.chunk // 32, part)
        self.pass_on(ref, i, r, way).start()
        if last:
            self.total_out(mine.at[q, at, :], i, r).start()

    def links(self, last):
        def run(e, q, j, i, r):
            @pl.when(self.p == j)
            def _():
                for z, way in ((1, 1 if last else 0), (2, 0 if last else 1)):

                    @pl.when(self.z == z)
                    def _(way=way):
                        self.link(q, i, r, way, last)

        return run

    def ends(self, e, q, j, i, r):
        R = self.refs
        at = self.rows(r)

        @pl.when(self.p == j)
        def _():
            for z, way in ((0, 1), (3, 0)):

                @pl.when(self.z == z)
                def _(way=way):
                    ref, ssem, rsem = self.chained(i, r, way)
                    self.remote(ref, ref, ssem, rsem, (self.d, self.z)).wait_recv()
                    mine, chain = R["mine"], R["chain"]

                    def part(g):
                        piece = pl.ds(pl.multiple_of(r * self.chunk + g * 32, 32), 32)
                        chain[way, i, piece, :] = (
                            mine[q, piece, :].astype(jnp.float32) + chain[way, i, piece, :].astype(jnp.float32)
                        ).astype(jnp.bfloat16)

                    loop(self.chunk // 32, part)
                    self.total_out(ref, i, r).start()

    def each(self, function):
        for e, entry in enumerate(self.entries):
            here = [item for item in entry[:2] if item is not None]
            if len(here) == 2:
                (q, slot), (q_other, slot_other) = here
                assert slot // 4 == slot_other // 4
                if q != q_other:
                    q = q + self.core * (q_other - q)
                i = slot % 2
                if i != slot_other % 2:
                    i = i + self.core * (slot_other % 2 - i)
                function(e, entry[2], q, slot // 4, i)
            else:
                only = 0 if entry[1] is None else 1

                @pl.when(self.core == only)
                def _(e=e, entry=entry, item=here[0]):
                    function(e, entry[2], item[0], item[1] // 4, item[1] % 2)

    def step(self, n):
        L = self.lag
        begins = ((0, self.begin_pair), (L, self.path(1, True)), (2 * L, self.path(2, True)), (3 * L, self.path(3, True)))
        ends = (
            (6 * L, self.ends),
            (5 * L, self.links(True)),
            (4 * L, self.links(False)),
            (3 * L, self.path(3, False)),
            (2 * L, self.path(2, False)),
            (L, self.path(1, False)),
            (0, self.end_pair),
        )

        def visit(parts):
            def entry_parts(e, start, q, j, i):
                m = n - start

                @pl.when((m >= 0) & (m < self.per + 6 * L))
                def _():
                    for lag, part in parts:
                        r = m - lag

                        @pl.when((r >= 0) & (r < self.per))
                        def _(r=r, part=part):
                            part(e, q, j, i, r)

            self.each(entry_parts)

        visit(begins)
        visit(ends)

    def finish(self):
        def chunk(e, start, q, j, i):
            rx, ry = self.corner[j]

            def body(r):
                @pl.when(rx + ry > 0)
                def _():
                    self.forward(q, r, 0).wait_send()

                mine = self.refs["mine"].at[q, self.rows(r), :]

                @pl.when((rx + ry == 0) & (self.z < 3))
                def _():
                    self.pass_on(mine, i, r, 0).wait_send()

                @pl.when((rx + ry == 0) & (self.z > 0))
                def _():
                    self.pass_on(mine, i, r, 1).wait_send()

                @pl.when(rx + ry == 0)
                def _():
                    self.total_out(mine, i, r).wait()

            loop(self.per, body)

        self.each(chunk)


def backward_kernel(
    full, x_in, q_in, k_in, kt_in, v_in, ctx_in, stat_in, mid_in, hat_in, inv_in, act_in, slope_in, two_in, sums_in, vec,
    input_out, total, sums, sib, land,
    w, pb, pt, pf, stat, inv, stage, mine, chain, ring_a, ring_b, vec_in,
    wsem, asem, ssem, isem, osem,
    give_send, give_recv, send_a, recv_a, chain_send_a, chain_recv_a, out_a, ring_sem_a,
    send_b, recv_b, chain_send_b, chain_recv_b, out_b, ring_sem_b, vec_send, vec_recv,
):
    z, core, x, y, near = position()
    p = 2 * y + x
    d = 2 * p + core
    z_one = (d, z + 1 - 2 * (z % 2))
    z_two = (d, z + 2 - 4 * (z // 2))
    shared = {"mine": mine, "land": land, "chain": chain, "sib": sib, "total": total, "give_send": give_send, "give_recv": give_recv}
    place = (z, core, x, y, d)
    early = Stream(EARLY, CHUNK_EARLY, LAG_EARLY, dict(
        shared, send=send_a, recv=recv_a, chain_send=chain_send_a, chain_recv=chain_recv_a, out=out_a, ring_sem=ring_sem_a,
    ), ring_a, place)
    late = Stream(LATE, CHUNK_LATE, LAG_LATE, dict(
        shared, send=send_b, recv=recv_b, chain_send=chain_send_b, chain_recv=chain_recv_b, out=out_b, ring_sem=ring_sem_b,
    ), ring_b, place)

    two_low, act_ring = pb.at[0], (pb.at[1], pb.at[2])
    up_grads = {0: pb.at[3], 2: pb.at[3], 1: pb.at[7], 3: pb.at[8]}
    k, q8, v = pb.at[4], pb.at[5], pb.at[6]
    one_low, ctx, ctx_grad, dq, dk, dv = pb.at[0], pb.at[1], pb.at[2], pb.at[0], pb.at[9], pb.at[3]
    two_t, mid_t, k_t = pt.at[0], pt.at[1], pt.at[2]
    one_t, x_t, dq_t = pt.at[0], pt.at[3], pt.at[4]
    two, back, slope_ring = pf.at[0], pf.at[1], (pf.at[2], pf.at[3])
    one, hat = pf.at[0], pf.at[2]
    uses = [slot for u in UNIT_ORDER for slot in (8 + u, 3 + u)] + [7, 0, 1, 2]

    def weight(n):
        return pltpu.make_async_copy(full.at[uses[n]], w.at[n % RING], wsem.at[n % RING])

    def act_load(n):
        return pltpu.make_async_copy(act_in.at[UNIT_ORDER[n]], act_ring[n % 2], asem.at[n % 2])

    def slope_load(n):
        return pltpu.make_async_copy(slope_in.at[UNIT_ORDER[n]], slope_ring[n % 2], ssem.at[n % 2])

    loads = {}

    def fetch(name, source, dest):
        loads[name] = pltpu.make_async_copy(source, dest, isem.at[len(loads)])
        loads[name].start()

    fetch("two", two_in, two)
    weight(0).start()
    slope_load(0).start()
    act_load(0).start()
    fetch("mid", mid_in, mid_t)
    weight(1).start()
    fetch("sums", sums_in, sums)
    weight(2).start()
    slope_load(1).start()
    act_load(1).start()
    for name, source, dest in (
        ("inv", inv_in, inv), ("k", k_in, k), ("q", q_in, q8), ("v", v_in, v), ("kt", kt_in, k_t), ("stat", stat_in, stat), ("x", x_in, x_t),
    ):
        fetch(name, source, dest)
    meet(z, near, (z_two,))

    counter = {"early": 0}
    produced = set()

    def run(count, body, at=()):
        base = counter["early"]
        for one_entry in EARLY:
            if at and one_entry[2] < base + len(at):
                assert all(item is None or item[1] in produced for item in one_entry[:2])

        def one_turn(i):
            body(i)
            if at:
                first, stride = at[0], (at[1] - at[0] if len(at) > 1 else count)

                @pl.when((i >= first) & (lax.rem(i - first + stride, stride) == 0))
                def _():
                    early.step(base + lax.div(i - first, stride))

        loop(count, one_turn)
        counter["early"] += len(at)

    def use(n):
        weight(n).wait()
        return w.at[n % RING]

    def done(n):
        if n + RING < 12:
            weight(n + RING).start()

    given = {0: [], 1: []}

    def give(slot, c, n, f):
        at = pl.ds(f * 256, 256)
        q = KEPT[1 - c].index(slot)
        return pltpu.make_async_remote_copy(
            src_ref=stage.at[n % 2, at, :], dst_ref=sib.at[q, at, :], send_sem=give_send.at[q, f],
            recv_sem=give_recv.at[q, f], device_id=near["c"], device_id_type=MESH,
        )

    def block(slot, left_t, right, after=()):
        owner = (slot // 2) % 2
        giver = 1 - owner
        q = KEPT[owner].index(slot)
        n = len(given[giver])
        if n >= 2:

            @pl.when(core == giver)
            def _():
                for f in range(4):
                    give(given[giver][n - 2], giver, n - 2, f).wait_send()

        def tile(i):
            at = columns(i, 512)
            value = dot(left_t[...], right[:, at]).astype(jnp.bfloat16)

            @pl.when(core == owner)
            def _():
                mine[q, :, at] = value

            @pl.when(core == giver)
            def _():
                stage[n % 2, :, at] = value

        run(WIDE // 512, tile, after)

        @pl.when(core == giver)
        def _():
            for f in range(4):
                give(slot, giver, n, f).start()

        given[giver].append(slot)
        produced.add(slot)

    def token_sum(row, ref):
        def tile(i):
            at = columns(i)
            sums[row : row + 1, at] = jnp.sum(ref[:, at].astype(jnp.float32), 0, keepdims=True)

        loop(WIDE // 256, tile)

    @pl.when(p == 3)
    def _():
        chain[0] = jnp.zeros(chain.shape[1:], chain.dtype)
        pltpu.make_async_copy(chain.at[0], total, osem.at[1]).start()

    loads["two"].wait()

    def to_low(r):
        two_low[r, :] = two[r, :].astype(jnp.bfloat16)

    row_loop(to_low)
    transpose_into(two_t, two_low)
    loads["mid"].wait()
    loads["sums"].wait()
    for n, u in enumerate(UNIT_ORDER):
        pace = PACE[n]
        weights = use(2 * n)
        slope_load(n).wait()
        act_load(n).wait()
        slope, up_grad = slope_ring[n % 2], up_grads[u]

        def tile(i):
            rows = columns(i, MOST)
            grad = dot_nt(two_low[...], weights[rows, :]) * slope[:, rows]
            up_grad[:, rows] = grad.astype(jnp.bfloat16)

        run(WIDE // MOST, tile, pace[0])
        done(2 * n)
        if n == 2:
            fetch("hat", hat_in, hat)
        token_sum(8 + u, up_grad)
        block(8 + u, two_t, act_ring[n % 2], pace[1])
        if n == 2:
            fetch("ctx", ctx_in, ctx)
        weights = use(2 * n + 1)

        def tile_back(i):
            at = columns(i, MOST)
            value = dot_nt(up_grad[...], weights[at, :])
            back[:, at] = two[:, at] + value if n == 0 else back[:, at] + value

        run(WIDE // MOST, tile_back, pace[2])
        done(2 * n + 1)
        if n < 2:
            block(3 + u, mid_t, up_grad, pace[3])
        if n + 2 < 4:
            slope_load(n + 2).start()
            act_load(n + 2).start()
    for name in ("hat", "inv"):
        loads[name].wait()
    sums[0:1, :] = jnp.zeros((1, WIDE), jnp.float32)
    sums[2:4, :] = jnp.zeros((2, WIDE), jnp.float32)

    def rows(i):
        r = pl.ds(pl.multiple_of(i * SLICE, SLICE), SLICE)
        grad, normed = back[r, :], hat[r, :]
        scaled = grad * vec[2:3, :]
        arg = inv[r, 0:1] * (scaled - mean_of(scaled) - normed * mean_of(scaled * normed))
        one[r, :] = arg
        one_low[r, :] = arg.astype(jnp.bfloat16)
        sums[0:1, :] += jnp.sum(arg, 0, keepdims=True)
        sums[2:3, :] += jnp.sum(grad * normed, 0, keepdims=True)
        sums[3:4, :] += jnp.sum(grad, 0, keepdims=True)

    run(TOKENS // SLICE, rows, PACE[4])
    transpose_into(one_t, one_low)
    weights = use(8)

    def tile_ctx(i):
        at = columns(i, MOST)
        ctx_grad[:, at] = dot_nt(one_low[...], weights[at, :]).astype(jnp.bfloat16)

    run(WIDE // MOST, tile_ctx, PACE[5])
    done(8)
    for name in ("k", "q", "v", "kt", "stat"):
        loads[name].wait()
    run(H // 2, lambda t: attend_pair_back(t, q8, k, v, ctx_grad, k_t, stat, dq_t, dk, dv), PACE[7])
    transpose_back(dq, dq_t)
    loads["x"].wait()
    block(0, x_t, dq, PACE[8])
    block(2, x_t, dv)
    block(1, x_t, dk)
    block(4, mid_t, up_grads[1], PACE[8])
    block(6, mid_t, up_grads[3])
    loads["ctx"].wait()
    block(7, one_t, ctx, PACE[8])

    def vec_hop(h):
        device = (near["c"], near["x"], near["y"], z_one, z_two)[h]
        return pltpu.make_async_remote_copy(
            src_ref=sums, dst_ref=vec_in.at[h], send_sem=vec_send.at[h], recv_sem=vec_recv.at[h],
            device_id=device, device_id_type=MESH,
        )

    token_sum(6, dq)
    token_sum(7, dv)
    vec_hop(0).start()
    hop = 0
    tail = {"early": counter["early"], "late": 0}

    def both(count, body=None, hops=False):
        base_late, base_early = tail["late"], tail["early"]

        def turn(i):
            if body is not None:
                body(i)
            late.step(base_late + i)
            if hops:
                for h in range(5):

                    @pl.when(i == 1 + 2 * h)
                    def _(h=h):
                        vec_hop(h).wait()
                        sums[...] = sums[...] + vec_in[h]
                        if h < 4:
                            vec_hop(h + 1).start()

            @pl.when(lax.rem(i, LATE_TURNS) == LATE_TURNS - 1)
            def _():
                early.step(base_early + lax.div(i, LATE_TURNS))

        loop(count, turn)
        tail["late"] += count
        tail["early"] += count // LATE_TURNS

    for kk, grad in ((0, dq), (1, dk), (2, dv)):
        weights = use(9 + kk)

        def tile_in(i):
            at = columns(i, 512)
            one[:, at] = one[:, at] + dot_nt(grad[...], weights[at, :])

        both(WIDE // 512, tile_in)
    out = pltpu.make_async_copy(one, input_out, osem.at[0])
    out.start()
    turns = max(late.steps - tail["late"], LATE_TURNS * (early.steps - tail["early"]))
    both(-(-turns // LATE_TURNS) * LATE_TURNS, hops=True)

    for c in range(2):

        @pl.when(core == c)
        def _(c=c):
            n = len(given[c])
            for back_by in (2, 1):
                for f in range(4):
                    give(given[c][n - back_by], c, n - back_by, f).wait_send()

    early.finish()
    late.finish()
    out.wait()

    @pl.when(p == 3)
    def _():
        pltpu.make_async_copy(chain.at[0], total, osem.at[1]).wait()


CHUNK_EARLY, CHUNK_LATE = 128, 32
LAG_EARLY, LAG_LATE = 2, 3
LATE_TURNS = 2
NO = ()
MOST = 512
PACE = (
    (NO, NO, NO, NO),
    (NO, NO, NO, NO),
    (NO, (1,), NO, NO),
    ((1,), NO, (1,), NO),
    NO,
    (1,),
    NO,
    (1, 3, 5, 7),
    (1,),
)


def backward(full, x, q, k, kt, v, ctx, stat, mid, hat, inv, act, slope, two, sums, vec):
    anywhere = pl.BlockSpec(memory_space=pl.ANY)
    vmem = pl.BlockSpec(memory_space=pltpu.VMEM)
    dma = pltpu.SemaphoreType.DMA
    low, wide = jnp.bfloat16, jnp.float32
    page = (TOKENS, WIDE)
    many_a, many_b = WIDE // CHUNK_EARLY, WIDE // CHUNK_LATE

    def stream_sems(many):
        return [dma((6, many)), dma((6, many)), dma((2, 2, many)), dma((2, 2, many)), dma((2, many)), dma((3, 2))]

    return pl.pallas_call(
        backward_kernel,
        name="backward",
        out_shape=[
            jax.ShapeDtypeStruct(page, wide),
            jax.ShapeDtypeStruct((2, WIDE, WIDE), low),
            jax.ShapeDtypeStruct((16, WIDE), wide),
            jax.ShapeDtypeStruct((6, WIDE, WIDE), low),
            jax.ShapeDtypeStruct((6, WIDE, WIDE), low),
        ],
        in_specs=[anywhere] * 15 + [vmem],
        out_specs=[anywhere, anywhere, vmem, anywhere, anywhere],
        scratch_shapes=[
            pltpu.VMEM((RING, WIDE, WIDE), low),
            pltpu.VMEM((10,) + page, low),
            pltpu.VMEM((5, WIDE, TOKENS), low),
            pltpu.VMEM((4,) + page, wide),
            pltpu.VMEM((H, 1, TOKENS), wide),
            pltpu.VMEM((TOKENS, 128), wide),
            pltpu.VMEM((2, WIDE, WIDE), low),
            pltpu.VMEM((6, WIDE, WIDE), low),
            pltpu.VMEM((2, 2, WIDE, WIDE), low),
            pltpu.VMEM((3, 2, CHUNK_EARLY, WIDE), low),
            pltpu.VMEM((3, 2, CHUNK_LATE, WIDE), low),
            pltpu.VMEM((5, 16, WIDE), wide),
            dma((RING,)), dma((2,)), dma((2,)), dma((12,)), dma((2,)),
            dma((6, 4)), dma((6, 4)),
            *stream_sems(many_a),
            *stream_sems(many_b),
            dma((5,)), dma((5,)),
        ],
        compiler_params=pltpu.CompilerParams(
            collective_id=2, has_side_effects=True, vmem_limit_bytes=62 << 20
        ),
    )(full, x, q, k, kt, v, ctx, stat, mid, hat, inv, act, slope, two, sums, vec)


STRIP = 256


def update_kernel(
    grads, left_stat, right_stat, left_root, right_root, master, averaged, sums, vectors, moment, page_one, page_two,
    block_out, left_out, right_out, master_out, copy_out, ema_out, vgrad_out, moment_out, vector_out, bias_out, one_out, two_out,
    b, ls, rs, lr, rr, ms, av, bt, pre, bo, cp, pages, isem, osem, psem,
):
    z, dp = lax.axis_index("tp"), lax.axis_index("dp")
    sources = (grads, left_root, right_root, left_stat, right_stat, master, averaged)
    places = (b, lr, rr, ls, rs, ms, av)

    def load(n, s):
        return pltpu.make_async_copy(sources[n].at[s], places[n].at[s], isem.at[n, s])

    for s in range(2):
        for n in range(7):
            load(n, s).start()

    def page(n, way):
        if way == 0:
            return pltpu.make_async_copy((page_one, page_two)[n], pages.at[n], psem.at[n, 0])
        return pltpu.make_async_copy(pages.at[n], (one_out, two_out)[n], psem.at[n, 1])

    page(0, 0).start()
    page(1, 0).start()
    own = pl.ds(pl.multiple_of(dp * 128, 128), 128)
    grad = sums[0:12, own]
    bias_out[...] = sums[0:1, own]
    vgrad_out[...] = grad
    fresh = MOMENTUM * moment[...] + grad
    moment_out[...] = fresh
    tokens = TOKENS * 32
    vector_out[...] = vectors[:, own] - (VEC_RATE / math.sqrt(tokens)) * fresh

    def store(n, s):
        dest = (block_out, left_out, right_out, master_out, copy_out, ema_out)[n].at[s]
        source = (bo, ls, rs, ms, cp, av)[n].at[s]
        return pltpu.make_async_copy(source, dest, osem.at[n, s])

    strip = pl.ds(pl.multiple_of(z * STRIP, STRIP), STRIP)
    for s in range(2):
        load(0, s).wait()
        load(1, s).wait()
        root_low = lr[s].astype(jnp.bfloat16)

        def first(i):
            at = columns(i)
            turned = b[s, columns(i), strip]
            bo[s, columns(i), :] = turned.astype(jnp.float32)
            bt[:, at] = turned.T

        pre[...] = dot(root_low, b[s]).astype(jnp.bfloat16)
        loop(WIDE // 256, first)
        store(0, s).start()
        load(3, s).wait()
        load(4, s).wait()

        def stats(i):
            at = columns(i, 512)
            ls[s, :, at] = STAT_DECAY * ls[s, :, at] + (1.0 - STAT_DECAY) * dot_nt(b[s, strip, :], b[s, at, :])
            rs[s, :, at] = STAT_DECAY * rs[s, :, at] + (1.0 - STAT_DECAY) * dot(bt[...], b[s, :, at])

        loop(WIDE // 512, stats)
        page(s, 0).wait()
        page(s, 1).start()
        store(1, s).start()
        store(2, s).start()
        load(2, s).wait()
        load(5, s).wait()
        load(6, s).wait()

        def second(i):
            at = columns(i, 512)
            change = dot(pre[...], rr[s, :, at].astype(jnp.bfloat16))
            value = ms[s, :, at] - BLOCK_RATE * change
            ms[s, :, at] = value
            cp[s, :, at] = value.astype(jnp.bfloat16)
            av[s, :, at] = EMA_DECAY * av[s, :, at] + (1.0 - EMA_DECAY) * value

        loop(WIDE // 512, second)
        for n in (3, 4, 5):
            store(n, s).start()
    for s in range(2):
        page(s, 1).wait()
        for n in range(6):
            store(n, s).wait()


def update(grads, left_stat, right_stat, left_root, right_root, master, averaged, sums, vectors, moment, page_one, page_two):
    anywhere = pl.BlockSpec(memory_space=pl.ANY)
    vmem = pl.BlockSpec(memory_space=pltpu.VMEM)
    dma = pltpu.SemaphoreType.DMA
    low, wide = jnp.bfloat16, jnp.float32
    rows = (2, STRIP, WIDE)
    shapes = [
        ((2, WIDE, STRIP), wide), (rows, wide), (rows, wide), (rows, wide), (rows, low), (rows, wide),
        ((12, 128), wide), ((12, 128), wide), ((12, 128), wide), ((1, 128), wide),
        ((TOKENS, WIDE), wide), ((TOKENS, WIDE), wide),
    ]
    return pl.pallas_call(
        update_kernel,
        name="update",
        out_shape=[jax.ShapeDtypeStruct(*shape) for shape in shapes],
        in_specs=[anywhere] * 7 + [vmem] * 3 + [anywhere] * 2,
        out_specs=[anywhere] * 6 + [vmem] * 4 + [anywhere] * 2,
        scratch_shapes=[
            pltpu.VMEM((2, WIDE, WIDE), low),
            pltpu.VMEM(rows, wide), pltpu.VMEM(rows, wide), pltpu.VMEM(rows, wide),
            pltpu.VMEM((2, WIDE, WIDE), wide),
            pltpu.VMEM(rows, wide), pltpu.VMEM(rows, wide),
            pltpu.VMEM((WIDE // 4, WIDE), low), pltpu.VMEM((STRIP, WIDE), low),
            pltpu.VMEM((2, WIDE, STRIP), wide),
            pltpu.VMEM(rows, low),
            pltpu.VMEM((2, TOKENS, WIDE), wide),
            dma((7, 2)), dma((6, 2)), dma((2, 2)),
        ],
        compiler_params=pltpu.CompilerParams(vmem_limit_bytes=56 << 20),
    )(grads, left_stat, right_stat, left_root, right_root, master, averaged, sums, vectors, moment, page_one, page_two)


def layout_embed(cell_boxes, cell_ids):
    cell_count = cell_boxes.shape[1]
    onehot = (
        cell_ids[:, :, None] == jnp.arange(cell_count, dtype=jnp.int32)[None, None, :]
    ).astype(jnp.float32)
    corners = jnp.einsum("psc,pck->psk", onehot, cell_boxes.astype(jnp.float32), precision=PRECISE)
    quarter = MODEL_WIDTH // 4
    half_width = quarter // 2
    frequency = jnp.exp(
        -jnp.arange(half_width, dtype=jnp.float32) * (math.log(1000.0) / half_width)
    )
    angle_grid = corners[..., None] * frequency
    wave_table = jnp.concatenate([jnp.sin(angle_grid), jnp.cos(angle_grid)], -1)
    return 0.5 * wave_table.reshape(corners.shape[0], corners.shape[1], MODEL_WIDTH)


def gelu_exact(values):
    return jax.nn.gelu(values, approximate=False)


def norm_forward(values, gain, shift):
    center = values - jnp.mean(values, -1, keepdims=True)
    inv_std = lax.rsqrt(jnp.mean(center * center, -1, keepdims=True) + EPS_NORM)
    normed = center * inv_std
    return (normed * gain + shift, normed, inv_std)


def norm_backward(grad_in, normed, inv_std, gain):
    scaled = grad_in * gain
    grad_arg = inv_std * (
        scaled
        - jnp.mean(scaled, -1, keepdims=True)
        - normed * jnp.mean(scaled * normed, -1, keepdims=True)
    )
    return (grad_arg, jnp.sum(grad_in * normed, (0, 1)), jnp.sum(grad_in, (0, 1)))


def attend(query_low, key_low, value_low, head_count):
    groups, seq_len = (query_low.shape[0], query_low.shape[1])
    shape_heads = (groups, seq_len, head_count, HD)
    scores = jnp.einsum(
        "gqhe,gkhe->ghqk",
        query_low.reshape(shape_heads),
        key_low.reshape(shape_heads),
        preferred_element_type=jnp.float32,
    ) * HD ** (-0.5)
    row_max = jnp.max(scores, -1, keepdims=True)
    log_total = row_max + jnp.log(jnp.sum(jnp.exp(scores - row_max), -1, keepdims=True))
    probs = jnp.exp(scores - log_total).astype(jnp.bfloat16)
    context = jnp.einsum(
        "ghqk,gkhe->gqhe", probs, value_low.reshape(shape_heads), preferred_element_type=jnp.float32
    )
    return (context.reshape(groups, seq_len, head_count * HD).astype(jnp.bfloat16), log_total)


def attend_back(query_low, key_low, value_low, log_total, ctx_grad, head_count):
    groups, seq_len = (query_low.shape[0], query_low.shape[1])
    shape_heads = (groups, seq_len, head_count, HD)
    query_heads = query_low.reshape(shape_heads)
    key_heads = key_low.reshape(shape_heads)
    value_heads = value_low.reshape(shape_heads)
    grad_heads = ctx_grad.reshape(shape_heads)
    scale = HD ** (-0.5)
    scores = (
        jnp.einsum("gqhe,gkhe->ghqk", query_heads, key_heads, preferred_element_type=jnp.float32)
        * scale
    )
    probs = jnp.exp(scores - log_total)
    value_grad = jnp.einsum(
        "ghqk,gqhe->gkhe",
        probs.astype(jnp.bfloat16),
        grad_heads,
        preferred_element_type=jnp.float32,
    )
    prob_grad = jnp.einsum(
        "gqhe,gkhe->ghqk", grad_heads, value_heads, preferred_element_type=jnp.float32
    )
    score_grad = (probs * (prob_grad - jnp.sum(probs * prob_grad, -1, keepdims=True))).astype(
        jnp.bfloat16
    )
    query_grad = (
        jnp.einsum("ghqk,gkhe->gqhe", score_grad, key_heads, preferred_element_type=jnp.float32)
        * scale
    )
    key_grad = (
        jnp.einsum("ghqk,gqhe->gkhe", score_grad, query_heads, preferred_element_type=jnp.float32)
        * scale
    )
    width = head_count * HD
    return (
        query_grad.reshape(groups, seq_len, width).astype(jnp.bfloat16),
        key_grad.reshape(groups, seq_len, width).astype(jnp.bfloat16),
        value_grad.reshape(groups, seq_len, width).astype(jnp.bfloat16),
    )


def by_collectives(
    hidden, cell_ids, cell_boxes, cotangent, weight_cols, weight_out, weight_down, vectors, slot_dev
):
    dp_count = lax.axis_size("dp")
    col_mats = lax.all_gather(weight_cols, "tp", axis=2, tiled=True)
    out_mat = lax.all_gather(weight_out, "tp", axis=0, tiled=True)
    down_mats = lax.all_gather(weight_down, "tp", axis=1, tiled=True)
    x_own = hidden.astype(jnp.float32) + layout_embed(cell_boxes, cell_ids)
    x_low = x_own.astype(jnp.bfloat16)
    projected = jnp.einsum(
        "gtd,kdc->kgtc", x_low, col_mats[0:3], preferred_element_type=jnp.float32
    )
    query_low = (projected[0] + vectors[:, 6]).astype(jnp.bfloat16)
    key_low = projected[1].astype(jnp.bfloat16)
    value_low = (projected[2] + vectors[:, 7]).astype(jnp.bfloat16)
    context, log_total = attend(query_low, key_low, value_low, H)
    attn_out = jnp.einsum("gtc,cd->gtd", context, out_mat, preferred_element_type=jnp.float32)
    mid_out, mid_hat, mid_inv = norm_forward(
        x_own + attn_out + vectors[:, 0], vectors[:, 2], vectors[:, 3]
    )
    mid_low = mid_out.astype(jnp.bfloat16)
    up_pre = jnp.einsum(
        "gtd,kdc->kgtc", mid_low, col_mats[3:7], preferred_element_type=jnp.float32
    )
    up_pre = up_pre + jnp.transpose(vectors[:, 8:12])[:, None, None, :]
    act_low = gelu_exact(up_pre).astype(jnp.bfloat16)
    ffn_out = jnp.einsum("kgtc,kcd->gtd", act_low, down_mats, preferred_element_type=jnp.float32)
    layer_out, out_hat, out_inv = norm_forward(
        mid_out + ffn_out + vectors[:, 1], vectors[:, 4], vectors[:, 5]
    )
    output_gradient = cotangent.astype(jnp.float32)
    grad_two, gain_two, shift_two = norm_backward(output_gradient, out_hat, out_inv, vectors[:, 4])
    two_low = grad_two.astype(jnp.bfloat16)
    act_grad = jnp.einsum("gtd,kcd->kgtc", two_low, down_mats, preferred_element_type=jnp.float32)
    gelu_pull = jax.vjp(gelu_exact, up_pre)[1]
    up_low = gelu_pull(act_grad)[0].astype(jnp.bfloat16)
    mid_back = jnp.einsum(
        "kgtc,kdc->gtd", up_low, col_mats[3:7], preferred_element_type=jnp.float32
    )
    grad_one, gain_one, shift_one = norm_backward(
        mid_back + grad_two, mid_hat, mid_inv, vectors[:, 2]
    )
    one_low = grad_one.astype(jnp.bfloat16)
    ctx_grad = jnp.einsum(
        "gtd,cd->gtc", one_low, out_mat, preferred_element_type=jnp.float32
    ).astype(jnp.bfloat16)
    query_grad, key_grad, value_grad = attend_back(
        query_low, key_low, value_low, log_total, ctx_grad, H
    )
    qkv_grad = jnp.stack([query_grad, key_grad, value_grad], 0)
    input_grad = grad_one + jnp.einsum(
        "kgtc,kdc->gtd", qkv_grad, col_mats[0:3], preferred_element_type=jnp.float32
    )

    def block(text, left, right):
        return jnp.einsum(text, left, right, preferred_element_type=jnp.float32).astype(
            jnp.bfloat16
        )

    qkv_blocks = block("gtd,kgtc->kdc", x_low, qkv_grad)
    up_blocks = block("gtd,kgtc->kdc", mid_low, up_low)
    out_block = block("gtd,gtc->dc", one_low, context)[None]
    down_blocks = block("gtd,kgtc->kdc", two_low, act_low)
    vector_part = jnp.stack(
        [
            jnp.sum(grad_one, (0, 1)),
            jnp.sum(grad_two, (0, 1)),
            gain_one,
            shift_one,
            gain_two,
            shift_two,
            jnp.sum(query_grad, (0, 1), dtype=jnp.float32),
            jnp.sum(value_grad, (0, 1), dtype=jnp.float32),
        ],
        0,
    )
    vector_part = jnp.concatenate(
        [vector_part, jnp.sum(up_low, (1, 2), dtype=jnp.float32)], 0
    )
    block_part = jnp.concatenate(
        [
            qkv_blocks,
            up_blocks,
            out_block,
            down_blocks,
            jnp.zeros((slot_dev * dp_count - 12, MODEL_WIDTH, MODEL_WIDTH), jnp.bfloat16),
        ],
        0,
    )
    block_owned = lax.psum_scatter(block_part, "dp", scatter_dimension=0, tiled=True)
    full_grad = lax.psum(block_owned, "tp")
    vector_all = lax.psum(vector_part, ("dp", "tp"))
    return layer_out, input_grad, full_grad, vector_all


def local(
    hidden,
    cell_ids,
    cell_boxes,
    cotangent,
    weight_cols,
    weight_out,
    weight_down,
    vectors,
    vector_moment,
    left_stat,
    right_stat,
    left_root,
    right_root,
    master,
    averaged_weight,
):
    tp_count = lax.axis_size("tp")
    dp_count = lax.axis_size("dp")
    tp_index = lax.axis_index("tp")
    dp_index = lax.axis_index("dp")
    strip_width = weight_cols.shape[2]
    page_rows, seq_len = (hidden.shape[0], hidden.shape[1])
    owned_rows = vector_moment.shape[0]
    slot_dev = left_stat.shape[0]
    if dp_count == 8 and tp_count == 4:
        vec = jnp.transpose(vectors)
        full, layer_out, *kept, sums = forward(
            weight_cols, weight_out, weight_down, hidden[0], cell_ids, jnp.transpose(cell_boxes[0]), cotangent[0], vec
        )
        input_grad, full_grad, vector_all, *_ = backward(full, *kept, sums, vec)
        outs = update(
            full_grad, left_stat, right_stat, left_root, right_root, master, averaged_weight, vector_all, vec,
            jnp.transpose(vector_moment), layer_out, input_grad
        )
        *blocks, vector_grad, moment_new, vector_new, bias_grad, layer_out, input_grad = outs
        thin = [jnp.transpose(array) for array in (vector_grad, moment_new, vector_new)]
        return (layer_out[None], input_grad[None], *blocks, *thin, bias_grad[0])
    else:
        layer_out, input_grad, full_grad, vector_all = by_collectives(
            hidden, cell_ids, cell_boxes, cotangent, weight_cols, weight_out, weight_down, vectors, slot_dev
        )
    vector_grad = jnp.transpose(
        lax.dynamic_slice_in_dim(vector_all[0:12], dp_index * owned_rows, owned_rows, 1)
    )
    own_rows = lax.dynamic_slice_in_dim(full_grad, tp_index * strip_width, strip_width, 1)
    own_cols = lax.dynamic_slice_in_dim(full_grad, tp_index * strip_width, strip_width, 2)
    block_grad = own_cols.astype(jnp.float32)
    left_new = STAT_DECAY * left_stat + (1.0 - STAT_DECAY) * jnp.einsum(
        "sic,sjc->sij", own_rows, full_grad, preferred_element_type=jnp.float32
    )
    right_new = STAT_DECAY * right_stat + (1.0 - STAT_DECAY) * jnp.einsum(
        "sic,sij->scj", own_cols, full_grad, preferred_element_type=jnp.float32
    )

    def parts(array):
        high = array.astype(jnp.bfloat16)
        return high, (array - high.astype(jnp.float32)).astype(jnp.bfloat16)

    def product(left, right):
        return jnp.einsum("sij,sjc->sic", left, right, preferred_element_type=jnp.float32)

    left_high, left_rest = parts(left_root)
    right_high, right_rest = parts(right_root)
    precond = product(left_high, full_grad) + product(left_rest, full_grad)
    pre_high, pre_rest = parts(precond)
    precond = (
        product(pre_high, right_high) + product(pre_rest, right_high) + product(pre_high, right_rest)
    )
    master_new = master - BLOCK_RATE * precond
    weight_copy = master_new.astype(jnp.bfloat16)
    ema_new = EMA_DECAY * averaged_weight + (1.0 - EMA_DECAY) * master_new
    vector_rows = lax.dynamic_slice_in_dim(vectors, dp_index * owned_rows, owned_rows, 0)
    moment_new = MOMENTUM * vector_moment + vector_grad
    total_tokens = page_rows * seq_len * dp_count * tp_count
    vector_new = vector_rows - VEC_RATE * lax.rsqrt(jnp.float32(total_tokens)) * moment_new
    bias_grad = vector_grad[:, 0]
    return (
        layer_out,
        input_grad,
        block_grad,
        left_new,
        right_new,
        master_new,
        weight_copy,
        ema_new,
        vector_grad,
        moment_new,
        vector_new,
        bias_grad,
    )


def solution(mesh):
    return jax.shard_map(
        local,
        mesh=mesh,
        in_specs=(
            P(("dp", "tp"), None, None),
            P(("dp", "tp"), None),
            P(("dp", "tp"), None, None),
            P(("dp", "tp"), None, None),
            P(None, None, "tp"),
            P("tp", None),
            P(None, "tp", None),
            P(),
            P("dp", None),
            P("dp", "tp", None),
            P("dp", "tp", None),
            P("dp", "tp", None),
            P("dp", None, None),
            P("dp", "tp", None),
            P("dp", "tp", None),
        ),
        out_specs=(
            P(("dp", "tp"), None, None),
            P(("dp", "tp"), None, None),
            P("dp", None, "tp"),
            P("dp", "tp", None),
            P("dp", "tp", None),
            P("dp", "tp", None),
            P("dp", "tp", None),
            P("dp", "tp", None),
            P("dp", None),
            P("dp", None),
            P("dp", None),
            P("dp"),
        ),
        check_vma=False,
    )
```

```python
import math

import jax
import jax.numpy as jnp
from jax import lax
from jax.experimental import pallas as pl
from jax.experimental.pallas import tpu as pltpu
from jax.sharding import PartitionSpec as P

MODEL_WIDTH = 1024
H = 16
HD = 64

PRECISE = lax.Precision.HIGHEST
EPS_NORM = 1e-06
STAT_DECAY = 0.5
BLOCK_RATE = 0.7
EMA_DECAY = 0.9
MOMENTUM = 0.9
VEC_RATE = 0.2

MESH = pl.DeviceIdType.MESH


def position():
    d, z = lax.axis_index("dp"), lax.axis_index("tp")
    core, x, y = d % 2, (d // 2) % 2, d // 4
    near = {
        "x": (d + 2 - 4 * x, z),
        "y": (d + 4 - 8 * y, z),
        "c": (d + 1 - 2 * core, z),
        "u": (d, z + 1),
        "v": (d, z - 1),
    }
    return z, core, x, y, near


def meet(z, near, extra=()):
    barrier = pltpu.get_barrier_semaphore()
    always = [near[name] for name in "xyc"] + list(extra)
    for device in always:
        pl.semaphore_signal(barrier, 1, device_id=device, device_id_type=MESH)

    @pl.when(z < 3)
    def _():
        pl.semaphore_signal(barrier, 1, device_id=near["u"], device_id_type=MESH)

    @pl.when(z > 0)
    def _():
        pl.semaphore_signal(barrier, 1, device_id=near["v"], device_id_type=MESH)

    pl.semaphore_wait(barrier, len(always) + (z + 2) // 3 + (5 - z) // 3)


ORDER = (0, 1, 2, 7, 3, 4, 5, 6, 8, 9, 10, 11)


NT = (((1,), (1,)), ((), ()))
TOKENS = 512
WIDE = MODEL_WIDTH


def dot(a, b):
    return jnp.dot(a, b, preferred_element_type=jnp.float32)


def dot_nt(a, b):
    return lax.dot_general(a, b, NT, preferred_element_type=jnp.float32)


def columns(i, width=256):
    return pl.ds(pl.multiple_of(i * width, width), width)


def loop(count, body):
    if count == 1:
        body(0)
        return

    def step(i, carry):
        body(i)
        return carry

    lax.fori_loop(0, count, step, 0)


def mean_of(rows):
    return jnp.sum(rows, -1, keepdims=True) * (1.0 / WIDE)


def transpose_into(dest, source):
    def body(i):
        dest[columns(i), :] = source[:, columns(i)].T

    loop(WIDE // 256, body)


def transpose_back(dest, source):
    def body(i):
        dest[:, columns(i)] = source[columns(i), :].T

    loop(WIDE // 256, body)


def embed_tokens(hidden, ids, boxes, x_ref, x_low):
    cells = boxes.shape[1]
    corners = boxes[...].astype(jnp.float32).T
    half = WIDE // 8
    place = lax.broadcasted_iota(jnp.int32, (1, half), 1).astype(jnp.float32)
    rate = jnp.exp(place * (-math.log(1000.0) / half))
    marks = lax.broadcasted_iota(jnp.int32, (cells, TOKENS), 0) == ids[...]
    chosen = jnp.where(marks, 1.0, 0.0).T.astype(jnp.bfloat16)
    for c in range(4):
        angle = corners[:, c : c + 1] * rate
        for kind, wave in enumerate((jnp.sin(angle), jnp.cos(angle))):
            wave = 0.5 * wave
            high = wave.astype(jnp.bfloat16)
            rest = wave - high.astype(jnp.float32)
            middle = rest.astype(jnp.bfloat16)
            low = (rest - middle.astype(jnp.float32)).astype(jnp.bfloat16)
            emb = dot(chosen, high) + (dot(chosen, middle) + dot(chosen, low))
            at = pl.ds(c * 2 * half + kind * half, half)
            value = hidden[:, at].astype(jnp.float32) + emb
            x_ref[:, at] = value
            x_low[:, at] = value.astype(jnp.bfloat16)


def project(x_low, weight, dest, bias, scale):
    def body(i):
        at = columns(i, 1024)
        value = dot(x_low[...], weight[:, at])
        if bias is not None:
            value = value + bias[:, at]
        value = value.astype(jnp.bfloat16)
        if scale:
            value = value * jnp.asarray(HD ** (-0.5), jnp.bfloat16)
        dest[:, at] = value

    loop(WIDE // 1024, body)


def half_mask(e, shape):
    lane = lax.broadcasted_iota(jnp.int32, shape, 1)
    return (lane < HD) if e == 0 else (lane >= HD)


def attend_pair(t, q8, k, v_t, ctx_t, stat):
    at = columns(t, 128)
    keys, queries = k[:, at], q8[:, at]
    for e in range(2):
        own = jnp.where(half_mask(e, queries.shape), queries, jnp.zeros_like(queries))
        scores = dot_nt(keys, own)
        top = jnp.max(scores, 0, keepdims=True)
        power = jnp.exp(scores - top)
        total = jnp.sum(power, 0, keepdims=True)
        probs = (power * (1.0 / total)).astype(jnp.bfloat16)
        rows = pl.ds(pl.multiple_of(t * 128 + e * 64, 64), 64)
        ctx_t[rows, :] = dot(v_t[rows, :], probs).astype(jnp.bfloat16)
        stat[2 * t + e, :, :] = top + jnp.log(total)


def norm_rows(values, gain, shift):
    center = values - mean_of(values)
    inv = lax.rsqrt(mean_of(center * center) + EPS_NORM)
    normed = center * inv
    return normed * gain + shift, normed, inv


SLICE = 64


def row_loop(body):
    loop(TOKENS // SLICE, lambda i: body(pl.ds(pl.multiple_of(i * SLICE, SLICE), SLICE)))


def gelu_both(value):
    phi = 0.5 * (1.0 + lax.erf(value * math.sqrt(0.5)))
    density = jnp.exp(-0.5 * value * value) * (1.0 / math.sqrt(2.0 * math.pi))
    return value * phi, phi + value * density


def forward_kernel(
    cols, outw, down, hidden, ids, boxes, cotangent, vec,
    full_out, layer_out, x_out, q_out, k_out, kt_out, v_out, ctx_out, stat_out, mid_out, hat_out, inv_out, act_out, slope_out,
    two_out, sums_out,
    w, x_t, mid_t, k_t, x_ref, x_low, q8, k, v, v_t, ctx_t, ctx, stat, acc, mid, mid_low, hat, inv, act, slope, y_out, two, sums,
    load, along, onward, arrived, beside, store, spill,
):
    z, core, x, y, near = position()
    p = 2 * y + x
    meet(z, near)

    def own(kk, h):
        if kk < 7:
            return cols.at[kk, pl.ds(h * 512, 512), :]
        if kk == 7:
            return outw.at[pl.ds(h * 128, 128), :]
        return down.at[kk - 8, pl.ds(h * 128, 128), :]

    def spot(s, kk, h):
        if kk < 7:
            return w.at[kk, pl.ds(h * 512, 512), pl.ds(pl.multiple_of(s * 256, 256), 256)]
        return w.at[kk, pl.ds(pl.multiple_of(s * 256 + h * 128, 128), 128), :]

    def spot_whole(s, kk):
        if kk < 7:
            return w.at[kk, :, pl.ds(pl.multiple_of(s * 256, 256), 256)]
        return w.at[kk, pl.ds(pl.multiple_of(s * 256, 256), 256), :]

    def whole_own(kk):
        if kk < 7:
            return cols.at[kk]
        return outw if kk == 7 else down.at[kk - 8]

    def to(source, s, kk, send_sem, recv_sem, name):
        return pltpu.make_async_remote_copy(
            src_ref=source,
            dst_ref=spot(s, kk, core),
            send_sem=send_sem,
            recv_sem=recv_sem.at[s, kk],
            device_id=near[name],
            device_id_type=MESH,
        )

    def first(g, act_on):
        for t in range(3):
            kk = ORDER[3 * g + t]
            mine = (p == t) | (p == 3) if t == 0 else p == t

            @pl.when(mine & (z < 3))
            def _(kk=kk):
                act_on(to(own(kk, core), z, kk, along.at[kk], arrived, "u"))

            @pl.when(mine & (z > 0))
            def _(kk=kk):
                act_on(to(own(kk, core), z, kk, onward.at[0, z, kk], arrived, "v"))

    far = 3 * (1 - z // 2)
    nearest = z + 1 - 2 * (z // 3)
    strips = (nearest, 6 - nearest - far - z, far)

    def item(n, t):
        return strips[n % 3], ORDER[3 * (n // 3) + t]

    def go(s, kk, kind, name, sems):
        return to(spot(s, kk, core), s, kk, onward.at[kind, s, kk], sems, name)

    def stage(n, hop, begin):
        for t in range(3):
            s, kk = item(n, t)
            who = {
                (0, 0): (p == 0) | (p == 3),
                (0, 1): p == 1,
                (0, 2): p == 2,
                (1, 0): (p == 1) | (p == 2),
                (1, 1): (p == 0) | (p == 3),
                (1, 2): (p == 0) | (p == 3),
                (2, 0): None,
                (2, 1): p == 2,
                (2, 2): p == 1,
            }[hop, t]
            if who is None:
                continue

            @pl.when(who)
            def _(s=s, kk=kk, t=t):
                if begin:
                    go(s, kk, 0, "x", arrived).wait_recv()

                def act_on(copy):
                    if begin:
                        copy.start()
                    else:
                        copy.wait_send()

                if hop == 0:

                    @pl.when((s > z) & (z > 0))
                    def _():
                        act_on(go(s, kk, 0, "v", arrived))

                    @pl.when((s < z) & (z < 3))
                    def _():
                        act_on(go(s, kk, 0, "u", arrived))

                    if t == 0:

                        @pl.when(p == 0)
                        def _():
                            act_on(go(s, kk, 1, "x", arrived))
                            act_on(go(s, kk, 2, "y", arrived))
                    else:
                        act_on(go(s, kk, 1, "x", arrived))
                        act_on(go(s, kk, 2, "y", arrived))
                if hop == 1 and t == 1:

                    @pl.when(p == 3)
                    def _():
                        act_on(go(s, kk, 1, "x", arrived))

                if hop == 1 and t == 2:

                    @pl.when(p == 3)
                    def _():
                        act_on(go(s, kk, 2, "y", arrived))

                act_on(go(s, kk, 3, "c", beside))

    copies = []

    def keep(source, dest):
        copy = pltpu.make_async_copy(source, dest, spill.at[len(copies)])
        copy.start()
        copies.append(copy)

    def ready(kk):
        pltpu.make_async_copy(whole_own(kk), spot_whole(z, kk), load.at[kk]).wait()
        for s in strips:
            pltpu.make_async_remote_copy(
                src_ref=spot(s, kk, 1 - core),
                dst_ref=spot(s, kk, 1 - core),
                send_sem=onward.at[3, s, kk],
                recv_sem=beside.at[s, kk],
                device_id=near["c"],
                device_id_type=MESH,
            ).wait_recv()
        copy = pltpu.make_async_copy(w.at[kk], full_out.at[kk], store.at[kk])
        copy.start()

    def unit_embed():
        embed_tokens(hidden, ids, boxes, x_ref, x_low)
        transpose_into(x_t, x_low)
        keep(x_t, x_out)

    def unit_qk():
        ready(0)
        project(x_low, w.at[0], q8, vec.at[6:7], True)
        keep(q8, q_out)
        ready(1)
        project(x_low, w.at[1], k, None, False)
        keep(k, k_out)

    def unit_v():
        ready(2)
        project(x_low, w.at[2], v, vec.at[7:8], False)
        transpose_into(v_t, v)
        keep(v, v_out)

    def unit_k_t():
        transpose_into(k_t, k)
        keep(k_t, kt_out)

    def unit_attend(lo, hi):
        loop(hi - lo, lambda i: attend_pair(lo + i, q8, k, v_t, ctx_t, stat))

    def unit_context():
        transpose_back(ctx, ctx_t)
        keep(ctx, ctx_out)
        keep(stat, stat_out)

    def unit_mid():
        ready(7)

        def tile(i):
            at = columns(i, 1024)
            acc[:, at] = dot(ctx[...], w[7, :, at])

        loop(WIDE // 1024, tile)

        def rows(r):
            value = x_ref[r, :] + acc[r, :] + vec[0:1, :]
            out, normed, scale = norm_rows(value, vec[2:3, :], vec[3:4, :])
            mid[r, :] = out
            mid_low[r, :] = out.astype(jnp.bfloat16)
            hat[r, :] = normed
            inv[r, :] = jnp.broadcast_to(scale, (SLICE, 128))

        row_loop(rows)
        transpose_into(mid_t, mid_low)
        keep(mid_t, mid_out)
        keep(hat, hat_out)
        keep(inv, inv_out)

    def unit_up(u):
        ready(3 + u)
        def tile(i):
            at = columns(i)
            slot = i % 2

            @pl.when(i >= 2)
            def _():
                pltpu.make_async_copy(slope.at[slot], slope_out.at[u, :, at], store.at[12 + slot]).wait()

            value = dot(mid_low[...], w[3 + u, :, at]) + vec[8 + u : 9 + u, at]
            out, grad = gelu_both(value)
            act[u, :, at] = out.astype(jnp.bfloat16)
            slope[slot] = grad
            pltpu.make_async_copy(slope.at[slot], slope_out.at[u, :, at], store.at[12 + slot]).start()

        loop(WIDE // 256, tile)
        for slot in range(2):
            pltpu.make_async_copy(slope.at[slot], slope_out.at[u, :, columns(slot)], store.at[12 + slot]).wait()
        keep(act.at[u], act_out.at[u])

    def unit_down(u):
        ready(8 + u)

        def tile(i):
            at = columns(i, 1024)
            value = dot(act[u], w[8 + u, :, at])
            acc[:, at] = value if u == 0 else acc[:, at] + value

        loop(WIDE // 1024, tile)

    def unit_last():
        sums[...] = jnp.zeros_like(sums)

        def rows(r):
            value = mid[r, :] + acc[r, :] + vec[1:2, :]
            out, normed, scale = norm_rows(value, vec[4:5, :], vec[5:6, :])
            y_out[r, :] = out
            grad = cotangent[r, :].astype(jnp.float32)
            scaled = grad * vec[4:5, :]
            arg = scale * (scaled - mean_of(scaled) - normed * mean_of(scaled * normed))
            two[r, :] = arg
            sums[1:2, :] += jnp.sum(arg, 0, keepdims=True)
            sums[4:5, :] += jnp.sum(grad * normed, 0, keepdims=True)
            sums[5:6, :] += jnp.sum(grad, 0, keepdims=True)

        row_loop(rows)
        keep(y_out, layer_out)
        keep(two, two_out)
        keep(sums, sums_out)

    first(0, lambda copy: copy.start())
    first(1, lambda copy: copy.start())
    for kk in ORDER:
        pltpu.make_async_copy(whole_own(kk), spot_whole(z, kk), load.at[kk]).start()
    unit_embed()
    after = {
        4: lambda: (unit_qk(), unit_v()),
        5: lambda: unit_attend(0, 4),
        6: lambda: (unit_attend(4, 8), unit_context()),
        7: unit_mid,
        8: lambda: unit_up(0),
        9: lambda: (unit_up(1), unit_k_t()),
        10: lambda: unit_up(2),
        11: lambda: unit_up(3),
        12: lambda: unit_down(0),
        13: lambda: (unit_down(1), unit_down(2), unit_down(3), unit_last()),
    }
    for n in range(14):
        if n in (3, 6):
            first(n // 3 + 1, lambda copy: copy.start())
        for hop in range(3):
            if 0 <= n - hop < 12:
                stage(n - hop, hop, True)
        if n in after:
            after[n]()
    for n in range(12):
        for hop in range(3):
            stage(n, hop, False)
    for g in range(4):
        first(g, lambda copy: copy.wait_send())
    for kk in ORDER:
        pltpu.make_async_copy(w.at[kk], full_out.at[kk], store.at[kk]).wait()
    for copy in copies:
        copy.wait()


def forward(cols, outw, down, hidden, ids, boxes, cotangent, vec):
    anywhere = pl.BlockSpec(memory_space=pl.ANY)
    vmem = pl.BlockSpec(memory_space=pltpu.VMEM)
    dma = pltpu.SemaphoreType.DMA
    low, wide = jnp.bfloat16, jnp.float32
    page = (TOKENS, WIDE)
    outs = [
        ((12, WIDE, WIDE), low),
        (page, wide),
        ((WIDE, TOKENS), low),
        (page, low),
        (page, low),
        ((WIDE, TOKENS), low),
        (page, low),
        (page, low),
        ((H, 1, TOKENS), wide),
        ((WIDE, TOKENS), low),
        (page, wide),
        ((TOKENS, 128), wide),
        ((4,) + page, low),
        ((4,) + page, wide),
        (page, wide),
        ((16, WIDE), wide),
    ]
    return pl.pallas_call(
        forward_kernel,
        name="forward",
        out_shape=[jax.ShapeDtypeStruct(*o) for o in outs],
        in_specs=[anywhere] * 3 + [vmem] * 5,
        out_specs=[anywhere] * len(outs),
        scratch_shapes=[
            pltpu.VMEM((12, WIDE, WIDE), low),
            pltpu.VMEM((WIDE, TOKENS), low),
            pltpu.VMEM((WIDE, TOKENS), low),
            pltpu.VMEM((WIDE, TOKENS), low),
            pltpu.VMEM(page, wide),
            pltpu.VMEM(page, low),
            pltpu.VMEM(page, low),
            pltpu.VMEM(page, low),
            pltpu.VMEM(page, low),
            pltpu.VMEM((WIDE, TOKENS), low),
            pltpu.VMEM((WIDE, TOKENS), low),
            pltpu.VMEM(page, low),
            pltpu.VMEM((H, 1, TOKENS), wide),
            pltpu.VMEM(page, wide),
            pltpu.VMEM(page, wide),
            pltpu.VMEM(page, low),
            pltpu.VMEM(page, wide),
            pltpu.VMEM((TOKENS, 128), wide),
            pltpu.VMEM((4,) + page, low),
            pltpu.VMEM((2, TOKENS, 256), wide),
            pltpu.VMEM(page, wide),
            pltpu.VMEM(page, wide),
            pltpu.VMEM((16, WIDE), wide),
            dma((12,)),
            dma((12,)),
            dma((4, 4, 12)),
            dma((4, 12)),
            dma((4, 12)),
            dma((14,)),
            dma((20,)),
        ],
        compiler_params=pltpu.CompilerParams(
            collective_id=1, has_side_effects=True, vmem_limit_bytes=61 << 20
        ),
    )(cols, outw, down, hidden, ids, boxes, cotangent, vec)


KEPT = ((8, 5, 9, 0, 1, 4), (10, 3, 11, 2, 6, 7))
EARLY = (((0, 8), (0, 10), 0), ((1, 5), None, 0), (None, (1, 3), 0), ((2, 9), (2, 11), 8))
LATE = (((3, 0), (3, 2), 0), ((4, 1), None, 0), ((5, 4), (4, 6), 0), (None, (5, 7), 8))
UNIT_ORDER = (0, 2, 1, 3)
RING = 3


def attend_pair_back(t, q8, k, v, ctx_grad, k_t, stat, dq_t, dk, dv):
    at = columns(t, 128)
    keys, queries, values, grads = k[:, at], q8[:, at], v[:, at], ctx_grad[:, at]
    none = jnp.zeros_like(queries)
    key_sum = value_sum = None
    for e in range(2):
        mask = half_mask(e, queries.shape)
        own_q = jnp.where(mask, queries, none)
        own_g = jnp.where(mask, grads, none)
        probs = jnp.exp(dot_nt(keys, own_q) - stat[2 * t + e])
        prob_grad = dot_nt(values, own_g)
        carried = jnp.sum(probs * prob_grad, 0, keepdims=True)
        score_grad = (probs * (prob_grad - carried)).astype(jnp.bfloat16)
        rows = pl.ds(pl.multiple_of(t * 128 + e * 64, 64), 64)
        dq_t[rows, :] = (dot(k_t[rows, :], score_grad) * HD ** (-0.5)).astype(jnp.bfloat16)
        key_part = dot(score_grad, own_q)
        value_part = dot(probs.astype(jnp.bfloat16), own_g)
        key_sum = key_part if e == 0 else key_sum + key_part
        value_sum = value_part if e == 0 else value_sum + value_part
    dk[:, at] = key_sum.astype(jnp.bfloat16)
    dv[:, at] = value_sum.astype(jnp.bfloat16)


class Stream:
    def __init__(self, entries, chunk, lag, refs, ring, place):
        self.z, self.core, self.x, self.y, self.d = place
        self.p = 2 * self.y + self.x
        self.chunk, self.per, self.lag = chunk, WIDE // chunk, lag
        self.entries, self.refs, self.ring = entries, refs, ring
        self.base = min(item[0] for entry in entries for item in entry[:2] if item is not None)
        self.steps = max(entry[2] for entry in entries) + self.per + 6 * lag
        x, y = self.x, self.y
        self.corner = [(x if j % 2 == 0 else 1 - x, y if j // 2 == 0 else 1 - y) for j in range(3)]
        self.by_x, self.by_y = 2 - 4 * x, 4 - 8 * y

    def rows(self, r):
        return pl.ds(pl.multiple_of(r * self.chunk, self.chunk), self.chunk)

    def remote(self, source, dest, send_sem, recv_sem, device):
        return pltpu.make_async_remote_copy(
            src_ref=source, dst_ref=dest, send_sem=send_sem, recv_sem=recv_sem,
            device_id=device, device_id_type=MESH,
        )


    def forward(self, q, r, turn):
        R = self.refs
        at = self.rows(r)
        device = (self.d + self.by_y + turn * (self.by_x - self.by_y), self.z)
        return self.remote(R["mine"].at[q, at, :], R["land"].at[q, at, :], R["send"].at[q, r], R["recv"].at[q, r], device)

    def chained(self, i, r, way):
        R = self.refs
        at = self.rows(r)
        return R["chain"].at[way, i, at, :], R["chain_send"].at[way, i, r], R["chain_recv"].at[way, i, r]

    def pass_on(self, source, i, r, way):
        ref, ssem, rsem = self.chained(i, r, way)
        return self.remote(source, ref, ssem, rsem, (self.d, self.z + (1 if way == 0 else -1)))

    def total_out(self, source, i, r):
        R = self.refs
        return pltpu.make_async_copy(source, R["total"].at[i, self.rows(r), :], R["out"].at[i, r])

    def add_to_mine(self, q, r, ref):
        mine = self.refs["mine"]

        def part(g):
            at = pl.ds(pl.multiple_of(r * self.chunk + g * 32, 32), 32)
            here = pl.ds(pl.multiple_of(g * 32, 32), 32)
            mine[q, at, :] = (mine[q, at, :].astype(jnp.float32) + ref[here, :].astype(jnp.float32)).astype(jnp.bfloat16)

        loop(self.chunk // 32, part)

    def load(self, e, kind, q, r):
        source = self.refs["sib" if kind == 0 else "land"]
        return pltpu.make_async_copy(source.at[q, self.rows(r), :], self.ring.at[q - self.base, kind], self.refs["ring_sem"].at[q - self.base, kind])

    def begin_pair(self, e, q, j, i, r):
        R = self.refs
        quarter = 256 // self.chunk

        def arrival(f):
            at = pl.ds(pl.multiple_of(f * 256, 256), 256)
            ref = R["sib"].at[q, at, :]
            self.remote(ref, ref, R["give_send"].at[q, f], R["give_recv"].at[q, f], (self.d, self.z)).wait_recv()

        if quarter == 1:
            arrival(r)
        else:

            @pl.when(lax.rem(r, quarter) == 0)
            def _():
                arrival(lax.div(r, quarter))

        self.load(e, 0, q, r).start()

    def end_pair(self, e, q, j, i, r):
        self.load(e, 0, q, r).wait()
        self.add_to_mine(q, r, self.ring.at[q - self.base, 0])
        odd = lax.rem(r, 2)
        rx, ry = self.corner[j]

        @pl.when((rx + ry == 1) & (rx + odd == 1))
        def _():
            self.forward(q, r, odd).start()

    def path(self, hop, begin):
        def run(e, q, j, i, r):
            odd = lax.rem(r, 2)
            rx, ry = self.corner[j]
            here = {1: rx + ry == 2, 2: (rx + ry == 1) & (rx == odd), 3: rx + ry == 0}[hop]

            @pl.when(here)
            def _():
                copy = self.load(e, 1, q, r)
                if begin:
                    self.forward(q, r, odd).wait_recv()
                    copy.start()
                    return
                copy.wait()
                self.add_to_mine(q, r, self.ring.at[q - self.base, 1])
                if hop == 1:
                    self.forward(q, r, 1 - odd).start()
                if hop == 2:
                    self.forward(q, r, odd).start()
                if hop == 3:
                    mine = self.refs["mine"].at[q, self.rows(r), :]

                    @pl.when(self.z == 0)
                    def _():
                        self.pass_on(mine, i, r, 0).start()

                    @pl.when(self.z == 3)
                    def _():
                        self.pass_on(mine, i, r, 1).start()

        return run

    def link(self, q, i, r, way, last):
        R = self.refs
        at = self.rows(r)
        ref, ssem, rsem = self.chained(i, r, way)
        self.remote(ref, ref, ssem, rsem, (self.d, self.z)).wait_recv()
        mine, chain = R["mine"], R["chain"]

        def part(g):
            piece = pl.ds(pl.multiple_of(r * self.chunk + g * 32, 32), 32)
            came = chain[way, i, piece, :].astype(jnp.float32)
            chain[way, i, piece, :] = (mine[q, piece, :].astype(jnp.float32) + came).astype(jnp.bfloat16)
            if last:
                other = chain[1 - way, i, piece, :].astype(jnp.float32)
                mine[q, piece, :] = (other + came).astype(jnp.bfloat16)

        loop(self.chunk // 32, part)
        self.pass_on(ref, i, r, way).start()
        if last:
            self.total_out(mine.at[q, at, :], i, r).start()

    def links(self, last):
        def run(e, q, j, i, r):
            @pl.when(self.p == j)
            def _():
                for z, way in ((1, 1 if last else 0), (2, 0 if last else 1)):

                    @pl.when(self.z == z)
                    def _(way=way):
                        self.link(q, i, r, way, last)

        return run

    def ends(self, e, q, j, i, r):
        R = self.refs
        at = self.rows(r)

        @pl.when(self.p == j)
        def _():
            for z, way in ((0, 1), (3, 0)):

                @pl.when(self.z == z)
                def _(way=way):
                    ref, ssem, rsem = self.chained(i, r, way)
                    self.remote(ref, ref, ssem, rsem, (self.d, self.z)).wait_recv()
                    mine, chain = R["mine"], R["chain"]

                    def part(g):
                        piece = pl.ds(pl.multiple_of(r * self.chunk + g * 32, 32), 32)
                        chain[way, i, piece, :] = (
                            mine[q, piece, :].astype(jnp.float32) + chain[way, i, piece, :].astype(jnp.float32)
                        ).astype(jnp.bfloat16)

                    loop(self.chunk // 32, part)
                    self.total_out(ref, i, r).start()

    def each(self, function):
        for e, entry in enumerate(self.entries):
            here = [item for item in entry[:2] if item is not None]
            if len(here) == 2:
                (q, slot), (q_other, slot_other) = here
                assert slot // 4 == slot_other // 4
                if q != q_other:
                    q = q + self.core * (q_other - q)
                i = slot % 2
                if i != slot_other % 2:
                    i = i + self.core * (slot_other % 2 - i)
                function(e, entry[2], q, slot // 4, i)
            else:
                only = 0 if entry[1] is None else 1

                @pl.when(self.core == only)
                def _(e=e, entry=entry, item=here[0]):
                    function(e, entry[2], item[0], item[1] // 4, item[1] % 2)

    def begin(self, n):
        L = self.lag
        begins = ((0, self.begin_pair), (L, self.path(1, True)), (2 * L, self.path(2, True)), (3 * L, self.path(3, True)))
        self.visit(n, begins)

    def end(self, n):
        L = self.lag
        ends = (
            (6 * L, self.ends),
            (5 * L, self.links(True)),
            (4 * L, self.links(False)),
            (3 * L, self.path(3, False)),
            (2 * L, self.path(2, False)),
            (L, self.path(1, False)),
            (0, self.end_pair),
        )
        self.visit(n, ends)

    def visit(self, n, parts):
        L = self.lag

        def entry_parts(e, start, q, j, i):
            m = n - start

            @pl.when((m >= 0) & (m < self.per + 6 * L))
            def _():
                for lag, part in parts:
                    r = m - lag

                    @pl.when((r >= 0) & (r < self.per))
                    def _(r=r, part=part):
                        part(e, q, j, i, r)

        self.each(entry_parts)

    def finish(self):
        def chunk(e, start, q, j, i):
            rx, ry = self.corner[j]

            def body(r):
                @pl.when(rx + ry > 0)
                def _():
                    self.forward(q, r, 0).wait_send()

                mine = self.refs["mine"].at[q, self.rows(r), :]

                @pl.when((rx + ry == 0) & (self.z < 3))
                def _():
                    self.pass_on(mine, i, r, 0).wait_send()

                @pl.when((rx + ry == 0) & (self.z > 0))
                def _():
                    self.pass_on(mine, i, r, 1).wait_send()

                @pl.when(rx + ry == 0)
                def _():
                    self.total_out(mine, i, r).wait()

            loop(self.per, body)

        self.each(chunk)


def backward_kernel(
    full, x_in, q_in, k_in, kt_in, v_in, ctx_in, stat_in, mid_in, hat_in, inv_in, act_in, slope_in, two_in, sums_in, vec,
    input_out, total, sums, sib, land,
    w, pb, pt, pf, stat, inv, stage, mine, chain, ring_a, ring_b, vec_in,
    wsem, asem, ssem, isem, osem,
    give_send, give_recv, send_a, recv_a, chain_send_a, chain_recv_a, out_a, ring_sem_a,
    send_b, recv_b, chain_send_b, chain_recv_b, out_b, ring_sem_b, vec_send, vec_recv,
):
    z, core, x, y, near = position()
    p = 2 * y + x
    d = 2 * p + core
    z_one = (d, z + 1 - 2 * (z % 2))
    z_two = (d, z + 2 - 4 * (z // 2))
    shared = {"mine": mine, "land": land, "chain": chain, "sib": sib, "total": total, "give_send": give_send, "give_recv": give_recv}
    place = (z, core, x, y, d)
    early = Stream(EARLY, CHUNK_EARLY, LAG_EARLY, dict(
        shared, send=send_a, recv=recv_a, chain_send=chain_send_a, chain_recv=chain_recv_a, out=out_a, ring_sem=ring_sem_a,
    ), ring_a, place)
    late = Stream(LATE, CHUNK_LATE, LAG_LATE, dict(
        shared, send=send_b, recv=recv_b, chain_send=chain_send_b, chain_recv=chain_recv_b, out=out_b, ring_sem=ring_sem_b,
    ), ring_b, place)

    two_low, act_ring = pb.at[0], (pb.at[1], pb.at[2])
    up_grads = {0: pb.at[3], 2: pb.at[3], 1: pb.at[7], 3: pb.at[8]}
    k, q8, v = pb.at[4], pb.at[5], pb.at[6]
    one_low, ctx, ctx_grad, dq, dk, dv = pb.at[0], pb.at[1], pb.at[2], pb.at[0], pb.at[9], pb.at[3]
    two_t, mid_t, k_t = pt.at[0], pt.at[1], pt.at[2]
    one_t, x_t, dq_t = pt.at[0], pt.at[3], pt.at[4]
    two, back, slope_ring = pf.at[0], pf.at[1], (pf.at[2], pf.at[3])
    one, hat = pf.at[0], pf.at[2]
    uses = [slot for u in UNIT_ORDER for slot in (8 + u, 3 + u)] + [7, 0, 1, 2]

    def weight(n):
        return pltpu.make_async_copy(full.at[uses[n]], w.at[n % RING], wsem.at[n % RING])

    def act_load(n):
        return pltpu.make_async_copy(act_in.at[UNIT_ORDER[n]], act_ring[n % 2], asem.at[n % 2])

    def slope_load(n):
        return pltpu.make_async_copy(slope_in.at[UNIT_ORDER[n]], slope_ring[n % 2], ssem.at[n % 2])

    loads = {}

    def fetch(name, source, dest):
        loads[name] = pltpu.make_async_copy(source, dest, isem.at[len(loads)])
        loads[name].start()

    fetch("two", two_in, two)
    weight(0).start()
    slope_load(0).start()
    act_load(0).start()
    fetch("mid", mid_in, mid_t)
    weight(1).start()
    fetch("sums", sums_in, sums)
    weight(2).start()
    slope_load(1).start()
    act_load(1).start()
    for name, source, dest in (
        ("inv", inv_in, inv), ("k", k_in, k), ("q", q_in, q8), ("v", v_in, v), ("kt", kt_in, k_t), ("stat", stat_in, stat), ("x", x_in, x_t),
    ):
        fetch(name, source, dest)
    meet(z, near, (z_two,))

    counter = {"early": 0}
    produced = set()

    def run(count, body, at=()):
        base = counter["early"]
        for one_entry in EARLY:
            if at and one_entry[2] < base + len(at):
                assert all(item is None or item[1] in produced for item in one_entry[:2])

        def one_turn(i):
            if not at:
                body(i)
                return
            first, stride = at[0], (at[1] - at[0] if len(at) > 1 else count)
            now = (i >= first) & (lax.rem(i - first + stride, stride) == 0)

            @pl.when(now)
            def _():
                early.begin(base + lax.div(i - first, stride))

            body(i)

            @pl.when(now)
            def _():
                early.end(base + lax.div(i - first, stride))

        loop(count, one_turn)
        counter["early"] += len(at)

    def use(n):
        weight(n).wait()
        return w.at[n % RING]

    def done(n):
        if n + RING < 12:
            weight(n + RING).start()

    given = {0: [], 1: []}

    def give(slot, c, n, f):
        at = pl.ds(f * 256, 256)
        q = KEPT[1 - c].index(slot)
        return pltpu.make_async_remote_copy(
            src_ref=stage.at[n % 2, at, :], dst_ref=sib.at[q, at, :], send_sem=give_send.at[q, f],
            recv_sem=give_recv.at[q, f], device_id=near["c"], device_id_type=MESH,
        )

    def block(slot, left_t, right, after=()):
        owner = (slot // 2) % 2
        giver = 1 - owner
        q = KEPT[owner].index(slot)
        n = len(given[giver])
        if n >= 2:

            @pl.when(core == giver)
            def _():
                for f in range(4):
                    give(given[giver][n - 2], giver, n - 2, f).wait_send()

        def tile(i):
            at = columns(i, 512)
            value = dot(left_t[...], right[:, at]).astype(jnp.bfloat16)

            @pl.when(core == owner)
            def _():
                mine[q, :, at] = value

            @pl.when(core == giver)
            def _():
                stage[n % 2, :, at] = value

        run(WIDE // 512, tile, after)

        @pl.when(core == giver)
        def _():
            for f in range(4):
                give(slot, giver, n, f).start()

        given[giver].append(slot)
        produced.add(slot)

    def token_sum(row, ref):
        def tile(i):
            at = columns(i)
            sums[row : row + 1, at] = jnp.sum(ref[:, at].astype(jnp.float32), 0, keepdims=True)

        loop(WIDE // 256, tile)

    @pl.when(p == 3)
    def _():
        chain[0] = jnp.zeros(chain.shape[1:], chain.dtype)
        pltpu.make_async_copy(chain.at[0], total, osem.at[1]).start()

    loads["two"].wait()

    def to_low(r):
        two_low[r, :] = two[r, :].astype(jnp.bfloat16)

    row_loop(to_low)
    transpose_into(two_t, two_low)
    loads["mid"].wait()
    loads["sums"].wait()
    for n, u in enumerate(UNIT_ORDER):
        pace = PACE[n]
        weights = use(2 * n)
        slope_load(n).wait()
        act_load(n).wait()
        slope, up_grad = slope_ring[n % 2], up_grads[u]

        def tile(i):
            rows = columns(i, MOST if pace[0] else WIDE)
            grad = dot_nt(two_low[...], weights[rows, :]) * slope[:, rows]
            up_grad[:, rows] = grad.astype(jnp.bfloat16)

        run(WIDE // MOST if pace[0] else 1, tile, pace[0])
        done(2 * n)
        if n == 2:
            fetch("hat", hat_in, hat)
        token_sum(8 + u, up_grad)
        block(8 + u, two_t, act_ring[n % 2], pace[1])
        if n == 2:
            fetch("ctx", ctx_in, ctx)
        weights = use(2 * n + 1)

        def tile_back(i):
            at = columns(i, MOST if pace[2] else WIDE)
            value = dot_nt(up_grad[...], weights[at, :])
            back[:, at] = two[:, at] + value if n == 0 else back[:, at] + value

        run(WIDE // MOST if pace[2] else 1, tile_back, pace[2])
        done(2 * n + 1)
        if n < 2:
            block(3 + u, mid_t, up_grad, pace[3])
        if n + 2 < 4:
            slope_load(n + 2).start()
            act_load(n + 2).start()
    for name in ("hat", "inv"):
        loads[name].wait()
    sums[0:1, :] = jnp.zeros((1, WIDE), jnp.float32)
    sums[2:4, :] = jnp.zeros((2, WIDE), jnp.float32)

    def rows(i):
        r = pl.ds(pl.multiple_of(i * SLICE, SLICE), SLICE)
        grad, normed = back[r, :], hat[r, :]
        scaled = grad * vec[2:3, :]
        arg = inv[r, 0:1] * (scaled - mean_of(scaled) - normed * mean_of(scaled * normed))
        one[r, :] = arg
        one_low[r, :] = arg.astype(jnp.bfloat16)
        sums[0:1, :] += jnp.sum(arg, 0, keepdims=True)
        sums[2:3, :] += jnp.sum(grad * normed, 0, keepdims=True)
        sums[3:4, :] += jnp.sum(grad, 0, keepdims=True)

    run(TOKENS // SLICE, rows, PACE[4])
    transpose_into(one_t, one_low)
    weights = use(8)

    def tile_ctx(i):
        at = columns(i, MOST)
        ctx_grad[:, at] = dot_nt(one_low[...], weights[at, :]).astype(jnp.bfloat16)

    run(WIDE // MOST, tile_ctx, PACE[5])
    done(8)
    for name in ("k", "q", "v", "kt", "stat"):
        loads[name].wait()
    run(H // 2, lambda t: attend_pair_back(t, q8, k, v, ctx_grad, k_t, stat, dq_t, dk, dv), PACE[7])
    transpose_back(dq, dq_t)
    loads["x"].wait()
    block(0, x_t, dq, PACE[8])
    block(2, x_t, dv)
    block(1, x_t, dk)
    block(4, mid_t, up_grads[1], PACE[8])
    block(6, mid_t, up_grads[3])
    loads["ctx"].wait()
    block(7, one_t, ctx, PACE[8])

    def vec_hop(h):
        device = (near["c"], near["x"], near["y"], z_one, z_two)[h]
        return pltpu.make_async_remote_copy(
            src_ref=sums, dst_ref=vec_in.at[h], send_sem=vec_send.at[h], recv_sem=vec_recv.at[h],
            device_id=device, device_id_type=MESH,
        )

    token_sum(6, dq)
    token_sum(7, dv)
    vec_hop(0).start()
    hop = 0
    tail = {"early": counter["early"], "late": 0}

    def both(count, body=None, hops=False):
        base_late, base_early = tail["late"], tail["early"]

        def turn(i):
            now = lax.rem(i, LATE_TURNS) == LATE_TURNS - 1
            late.begin(base_late + i)

            @pl.when(now)
            def _():
                early.begin(base_early + lax.div(i, LATE_TURNS))

            if body is not None:
                body(i)
            late.end(base_late + i)

            @pl.when(now)
            def _():
                early.end(base_early + lax.div(i, LATE_TURNS))

            if hops:
                for h in range(5):

                    @pl.when(i == 1 + 2 * h)
                    def _(h=h):
                        vec_hop(h).wait()
                        sums[...] = sums[...] + vec_in[h]
                        if h < 4:
                            vec_hop(h + 1).start()

        loop(count, turn)
        tail["late"] += count
        tail["early"] += count // LATE_TURNS

    for kk, grad in ((0, dq), (1, dk), (2, dv)):
        weights = use(9 + kk)

        def tile_in(i):
            at = columns(i, 512)
            one[:, at] = one[:, at] + dot_nt(grad[...], weights[at, :])

        both(WIDE // 512, tile_in)
    out = pltpu.make_async_copy(one, input_out, osem.at[0])
    out.start()
    turns = max(late.steps - tail["late"], LATE_TURNS * (early.steps - tail["early"]))
    both(-(-turns // LATE_TURNS) * LATE_TURNS, hops=True)

    for c in range(2):

        @pl.when(core == c)
        def _(c=c):
            n = len(given[c])
            for back_by in (2, 1):
                for f in range(4):
                    give(given[c][n - back_by], c, n - back_by, f).wait_send()

    early.finish()
    late.finish()
    out.wait()

    @pl.when(p == 3)
    def _():
        pltpu.make_async_copy(chain.at[0], total, osem.at[1]).wait()


CHUNK_EARLY, CHUNK_LATE = 128, 32
LAG_EARLY, LAG_LATE = 2, 3
LATE_TURNS = 2
NO = ()
MOST = 512
PACE = (
    (NO, NO, NO, NO),
    (NO, NO, NO, NO),
    (NO, (1,), NO, NO),
    ((1,), NO, (1,), NO),
    NO,
    (1,),
    NO,
    (1, 3, 5, 7),
    (1,),
)


def backward(full, x, q, k, kt, v, ctx, stat, mid, hat, inv, act, slope, two, sums, vec):
    anywhere = pl.BlockSpec(memory_space=pl.ANY)
    vmem = pl.BlockSpec(memory_space=pltpu.VMEM)
    dma = pltpu.SemaphoreType.DMA
    low, wide = jnp.bfloat16, jnp.float32
    page = (TOKENS, WIDE)
    many_a, many_b = WIDE // CHUNK_EARLY, WIDE // CHUNK_LATE

    def stream_sems(many):
        return [dma((6, many)), dma((6, many)), dma((2, 2, many)), dma((2, 2, many)), dma((2, many)), dma((3, 2))]

    return pl.pallas_call(
        backward_kernel,
        name="backward",
        out_shape=[
            jax.ShapeDtypeStruct(page, wide),
            jax.ShapeDtypeStruct((2, WIDE, WIDE), low),
            jax.ShapeDtypeStruct((16, WIDE), wide),
            jax.ShapeDtypeStruct((6, WIDE, WIDE), low),
            jax.ShapeDtypeStruct((6, WIDE, WIDE), low),
        ],
        in_specs=[anywhere] * 15 + [vmem],
        out_specs=[anywhere, anywhere, vmem, anywhere, anywhere],
        scratch_shapes=[
            pltpu.VMEM((RING, WIDE, WIDE), low),
            pltpu.VMEM((10,) + page, low),
            pltpu.VMEM((5, WIDE, TOKENS), low),
            pltpu.VMEM((4,) + page, wide),
            pltpu.VMEM((H, 1, TOKENS), wide),
            pltpu.VMEM((TOKENS, 128), wide),
            pltpu.VMEM((2, WIDE, WIDE), low),
            pltpu.VMEM((6, WIDE, WIDE), low),
            pltpu.VMEM((2, 2, WIDE, WIDE), low),
            pltpu.VMEM((3, 2, CHUNK_EARLY, WIDE), low),
            pltpu.VMEM((3, 2, CHUNK_LATE, WIDE), low),
            pltpu.VMEM((5, 16, WIDE), wide),
            dma((RING,)), dma((2,)), dma((2,)), dma((12,)), dma((2,)),
            dma((6, 4)), dma((6, 4)),
            *stream_sems(many_a),
            *stream_sems(many_b),
            dma((5,)), dma((5,)),
        ],
        compiler_params=pltpu.CompilerParams(
            collective_id=2, has_side_effects=True, vmem_limit_bytes=62 << 20
        ),
    )(full, x, q, k, kt, v, ctx, stat, mid, hat, inv, act, slope, two, sums, vec)


STRIP = 256


def update_kernel(
    grads, left_stat, right_stat, left_root, right_root, master, averaged, sums, vectors, moment, page_one, page_two,
    block_out, left_out, right_out, master_out, copy_out, ema_out, vgrad_out, moment_out, vector_out, bias_out, one_out, two_out,
    b, ls, rs, lr, rr, ms, av, bt, pre, bo, cp, pages, isem, osem, psem,
):
    z, dp = lax.axis_index("tp"), lax.axis_index("dp")
    sources = (grads, left_root, right_root, left_stat, right_stat, master, averaged)
    places = (b, lr, rr, ls, rs, ms, av)

    def load(n, s):
        return pltpu.make_async_copy(sources[n].at[s], places[n].at[s], isem.at[n, s])

    for s in range(2):
        for n in range(7):
            load(n, s).start()

    def page(n, way):
        if way == 0:
            return pltpu.make_async_copy((page_one, page_two)[n], pages.at[n], psem.at[n, 0])
        return pltpu.make_async_copy(pages.at[n], (one_out, two_out)[n], psem.at[n, 1])

    page(0, 0).start()
    page(1, 0).start()
    own = pl.ds(pl.multiple_of(dp * 128, 128), 128)
    grad = sums[0:12, own]
    bias_out[...] = sums[0:1, own]
    vgrad_out[...] = grad
    fresh = MOMENTUM * moment[...] + grad
    moment_out[...] = fresh
    tokens = TOKENS * 32
    vector_out[...] = vectors[:, own] - (VEC_RATE / math.sqrt(tokens)) * fresh

    def store(n, s):
        dest = (block_out, left_out, right_out, master_out, copy_out, ema_out)[n].at[s]
        source = (bo, ls, rs, ms, cp, av)[n].at[s]
        return pltpu.make_async_copy(source, dest, osem.at[n, s])

    strip = pl.ds(pl.multiple_of(z * STRIP, STRIP), STRIP)
    for s in range(2):
        load(0, s).wait()
        load(1, s).wait()
        root_low = lr[s].astype(jnp.bfloat16)

        def first(i):
            at = columns(i)
            turned = b[s, columns(i), strip]
            bo[s, columns(i), :] = turned.astype(jnp.float32)
            bt[:, at] = turned.T

        pre[...] = dot(root_low, b[s]).astype(jnp.bfloat16)
        loop(WIDE // 256, first)
        store(0, s).start()
        load(3, s).wait()
        load(4, s).wait()

        def stats(i):
            at = columns(i, 1024)
            ls[s, :, at] = STAT_DECAY * ls[s, :, at] + (1.0 - STAT_DECAY) * dot_nt(b[s, strip, :], b[s, at, :])
            rs[s, :, at] = STAT_DECAY * rs[s, :, at] + (1.0 - STAT_DECAY) * dot(bt[...], b[s, :, at])

        loop(WIDE // 1024, stats)
        page(s, 0).wait()
        page(s, 1).start()
        store(1, s).start()
        store(2, s).start()
        load(2, s).wait()
        load(5, s).wait()
        load(6, s).wait()

        def second(i):
            at = columns(i, 1024)
            change = dot(pre[...], rr[s, :, at].astype(jnp.bfloat16))
            value = ms[s, :, at] - BLOCK_RATE * change
            ms[s, :, at] = value
            cp[s, :, at] = value.astype(jnp.bfloat16)
            av[s, :, at] = EMA_DECAY * av[s, :, at] + (1.0 - EMA_DECAY) * value

        loop(WIDE // 1024, second)
        for n in (3, 4, 5):
            store(n, s).start()
    for s in range(2):
        page(s, 1).wait()
        for n in range(6):
            store(n, s).wait()


def update(grads, left_stat, right_stat, left_root, right_root, master, averaged, sums, vectors, moment, page_one, page_two):
    anywhere = pl.BlockSpec(memory_space=pl.ANY)
    vmem = pl.BlockSpec(memory_space=pltpu.VMEM)
    dma = pltpu.SemaphoreType.DMA
    low, wide = jnp.bfloat16, jnp.float32
    rows = (2, STRIP, WIDE)
    shapes = [
        ((2, WIDE, STRIP), wide), (rows, wide), (rows, wide), (rows, wide), (rows, low), (rows, wide),
        ((12, 128), wide), ((12, 128), wide), ((12, 128), wide), ((1, 128), wide),
        ((TOKENS, WIDE), wide), ((TOKENS, WIDE), wide),
    ]
    return pl.pallas_call(
        update_kernel,
        name="update",
        out_shape=[jax.ShapeDtypeStruct(*shape) for shape in shapes],
        in_specs=[anywhere] * 7 + [vmem] * 3 + [anywhere] * 2,
        out_specs=[anywhere] * 6 + [vmem] * 4 + [anywhere] * 2,
        scratch_shapes=[
            pltpu.VMEM((2, WIDE, WIDE), low),
            pltpu.VMEM(rows, wide), pltpu.VMEM(rows, wide), pltpu.VMEM(rows, wide),
            pltpu.VMEM((2, WIDE, WIDE), wide),
            pltpu.VMEM(rows, wide), pltpu.VMEM(rows, wide),
            pltpu.VMEM((WIDE // 4, WIDE), low), pltpu.VMEM((STRIP, WIDE), low),
            pltpu.VMEM((2, WIDE, STRIP), wide),
            pltpu.VMEM(rows, low),
            pltpu.VMEM((2, TOKENS, WIDE), wide),
            dma((7, 2)), dma((6, 2)), dma((2, 2)),
        ],
        compiler_params=pltpu.CompilerParams(vmem_limit_bytes=56 << 20),
    )(grads, left_stat, right_stat, left_root, right_root, master, averaged, sums, vectors, moment, page_one, page_two)


def layout_embed(cell_boxes, cell_ids):
    cell_count = cell_boxes.shape[1]
    onehot = (
        cell_ids[:, :, None] == jnp.arange(cell_count, dtype=jnp.int32)[None, None, :]
    ).astype(jnp.float32)
    corners = jnp.einsum("psc,pck->psk", onehot, cell_boxes.astype(jnp.float32), precision=PRECISE)
    quarter = MODEL_WIDTH // 4
    half_width = quarter // 2
    frequency = jnp.exp(
        -jnp.arange(half_width, dtype=jnp.float32) * (math.log(1000.0) / half_width)
    )
    angle_grid = corners[..., None] * frequency
    wave_table = jnp.concatenate([jnp.sin(angle_grid), jnp.cos(angle_grid)], -1)
    return 0.5 * wave_table.reshape(corners.shape[0], corners.shape[1], MODEL_WIDTH)


def gelu_exact(values):
    return jax.nn.gelu(values, approximate=False)


def norm_forward(values, gain, shift):
    center = values - jnp.mean(values, -1, keepdims=True)
    inv_std = lax.rsqrt(jnp.mean(center * center, -1, keepdims=True) + EPS_NORM)
    normed = center * inv_std
    return (normed * gain + shift, normed, inv_std)


def norm_backward(grad_in, normed, inv_std, gain):
    scaled = grad_in * gain
    grad_arg = inv_std * (
        scaled
        - jnp.mean(scaled, -1, keepdims=True)
        - normed * jnp.mean(scaled * normed, -1, keepdims=True)
    )
    return (grad_arg, jnp.sum(grad_in * normed, (0, 1)), jnp.sum(grad_in, (0, 1)))


def attend(query_low, key_low, value_low, head_count):
    groups, seq_len = (query_low.shape[0], query_low.shape[1])
    shape_heads = (groups, seq_len, head_count, HD)
    scores = jnp.einsum(
        "gqhe,gkhe->ghqk",
        query_low.reshape(shape_heads),
        key_low.reshape(shape_heads),
        preferred_element_type=jnp.float32,
    ) * HD ** (-0.5)
    row_max = jnp.max(scores, -1, keepdims=True)
    log_total = row_max + jnp.log(jnp.sum(jnp.exp(scores - row_max), -1, keepdims=True))
    probs = jnp.exp(scores - log_total).astype(jnp.bfloat16)
    context = jnp.einsum(
        "ghqk,gkhe->gqhe", probs, value_low.reshape(shape_heads), preferred_element_type=jnp.float32
    )
    return (context.reshape(groups, seq_len, head_count * HD).astype(jnp.bfloat16), log_total)


def attend_back(query_low, key_low, value_low, log_total, ctx_grad, head_count):
    groups, seq_len = (query_low.shape[0], query_low.shape[1])
    shape_heads = (groups, seq_len, head_count, HD)
    query_heads = query_low.reshape(shape_heads)
    key_heads = key_low.reshape(shape_heads)
    value_heads = value_low.reshape(shape_heads)
    grad_heads = ctx_grad.reshape(shape_heads)
    scale = HD ** (-0.5)
    scores = (
        jnp.einsum("gqhe,gkhe->ghqk", query_heads, key_heads, preferred_element_type=jnp.float32)
        * scale
    )
    probs = jnp.exp(scores - log_total)
    value_grad = jnp.einsum(
        "ghqk,gqhe->gkhe",
        probs.astype(jnp.bfloat16),
        grad_heads,
        preferred_element_type=jnp.float32,
    )
    prob_grad = jnp.einsum(
        "gqhe,gkhe->ghqk", grad_heads, value_heads, preferred_element_type=jnp.float32
    )
    score_grad = (probs * (prob_grad - jnp.sum(probs * prob_grad, -1, keepdims=True))).astype(
        jnp.bfloat16
    )
    query_grad = (
        jnp.einsum("ghqk,gkhe->gqhe", score_grad, key_heads, preferred_element_type=jnp.float32)
        * scale
    )
    key_grad = (
        jnp.einsum("ghqk,gqhe->gkhe", score_grad, query_heads, preferred_element_type=jnp.float32)
        * scale
    )
    width = head_count * HD
    return (
        query_grad.reshape(groups, seq_len, width).astype(jnp.bfloat16),
        key_grad.reshape(groups, seq_len, width).astype(jnp.bfloat16),
        value_grad.reshape(groups, seq_len, width).astype(jnp.bfloat16),
    )


def by_collectives(
    hidden, cell_ids, cell_boxes, cotangent, weight_cols, weight_out, weight_down, vectors, slot_dev
):
    dp_count = lax.axis_size("dp")
    col_mats = lax.all_gather(weight_cols, "tp", axis=2, tiled=True)
    out_mat = lax.all_gather(weight_out, "tp", axis=0, tiled=True)
    down_mats = lax.all_gather(weight_down, "tp", axis=1, tiled=True)
    x_own = hidden.astype(jnp.float32) + layout_embed(cell_boxes, cell_ids)
    x_low = x_own.astype(jnp.bfloat16)
    projected = jnp.einsum(
        "gtd,kdc->kgtc", x_low, col_mats[0:3], preferred_element_type=jnp.float32
    )
    query_low = (projected[0] + vectors[:, 6]).astype(jnp.bfloat16)
    key_low = projected[1].astype(jnp.bfloat16)
    value_low = (projected[2] + vectors[:, 7]).astype(jnp.bfloat16)
    context, log_total = attend(query_low, key_low, value_low, H)
    attn_out = jnp.einsum("gtc,cd->gtd", context, out_mat, preferred_element_type=jnp.float32)
    mid_out, mid_hat, mid_inv = norm_forward(
        x_own + attn_out + vectors[:, 0], vectors[:, 2], vectors[:, 3]
    )
    mid_low = mid_out.astype(jnp.bfloat16)
    up_pre = jnp.einsum(
        "gtd,kdc->kgtc", mid_low, col_mats[3:7], preferred_element_type=jnp.float32
    )
    up_pre = up_pre + jnp.transpose(vectors[:, 8:12])[:, None, None, :]
    act_low = gelu_exact(up_pre).astype(jnp.bfloat16)
    ffn_out = jnp.einsum("kgtc,kcd->gtd", act_low, down_mats, preferred_element_type=jnp.float32)
    layer_out, out_hat, out_inv = norm_forward(
        mid_out + ffn_out + vectors[:, 1], vectors[:, 4], vectors[:, 5]
    )
    output_gradient = cotangent.astype(jnp.float32)
    grad_two, gain_two, shift_two = norm_backward(output_gradient, out_hat, out_inv, vectors[:, 4])
    two_low = grad_two.astype(jnp.bfloat16)
    act_grad = jnp.einsum("gtd,kcd->kgtc", two_low, down_mats, preferred_element_type=jnp.float32)
    gelu_pull = jax.vjp(gelu_exact, up_pre)[1]
    up_low = gelu_pull(act_grad)[0].astype(jnp.bfloat16)
    mid_back = jnp.einsum(
        "kgtc,kdc->gtd", up_low, col_mats[3:7], preferred_element_type=jnp.float32
    )
    grad_one, gain_one, shift_one = norm_backward(
        mid_back + grad_two, mid_hat, mid_inv, vectors[:, 2]
    )
    one_low = grad_one.astype(jnp.bfloat16)
    ctx_grad = jnp.einsum(
        "gtd,cd->gtc", one_low, out_mat, preferred_element_type=jnp.float32
    ).astype(jnp.bfloat16)
    query_grad, key_grad, value_grad = attend_back(
        query_low, key_low, value_low, log_total, ctx_grad, H
    )
    qkv_grad = jnp.stack([query_grad, key_grad, value_grad], 0)
    input_grad = grad_one + jnp.einsum(
        "kgtc,kdc->gtd", qkv_grad, col_mats[0:3], preferred_element_type=jnp.float32
    )

    def block(text, left, right):
        return jnp.einsum(text, left, right, preferred_element_type=jnp.float32).astype(
            jnp.bfloat16
        )

    qkv_blocks = block("gtd,kgtc->kdc", x_low, qkv_grad)
    up_blocks = block("gtd,kgtc->kdc", mid_low, up_low)
    out_block = block("gtd,gtc->dc", one_low, context)[None]
    down_blocks = block("gtd,kgtc->kdc", two_low, act_low)
    vector_part = jnp.stack(
        [
            jnp.sum(grad_one, (0, 1)),
            jnp.sum(grad_two, (0, 1)),
            gain_one,
            shift_one,
            gain_two,
            shift_two,
            jnp.sum(query_grad, (0, 1), dtype=jnp.float32),
            jnp.sum(value_grad, (0, 1), dtype=jnp.float32),
        ],
        0,
    )
    vector_part = jnp.concatenate(
        [vector_part, jnp.sum(up_low, (1, 2), dtype=jnp.float32)], 0
    )
    block_part = jnp.concatenate(
        [
            qkv_blocks,
            up_blocks,
            out_block,
            down_blocks,
            jnp.zeros((slot_dev * dp_count - 12, MODEL_WIDTH, MODEL_WIDTH), jnp.bfloat16),
        ],
        0,
    )
    block_owned = lax.psum_scatter(block_part, "dp", scatter_dimension=0, tiled=True)
    full_grad = lax.psum(block_owned, "tp")
    vector_all = lax.psum(vector_part, ("dp", "tp"))
    return layer_out, input_grad, full_grad, vector_all


def local(
    hidden,
    cell_ids,
    cell_boxes,
    cotangent,
    weight_cols,
    weight_out,
    weight_down,
    vectors,
    vector_moment,
    left_stat,
    right_stat,
    left_root,
    right_root,
    master,
    averaged_weight,
):
    tp_count = lax.axis_size("tp")
    dp_count = lax.axis_size("dp")
    tp_index = lax.axis_index("tp")
    dp_index = lax.axis_index("dp")
    strip_width = weight_cols.shape[2]
    page_rows, seq_len = (hidden.shape[0], hidden.shape[1])
    owned_rows = vector_moment.shape[0]
    slot_dev = left_stat.shape[0]
    if dp_count == 8 and tp_count == 4:
        vec = jnp.transpose(vectors)
        full, layer_out, *kept, sums = forward(
            weight_cols, weight_out, weight_down, hidden[0], cell_ids, jnp.transpose(cell_boxes[0]), cotangent[0], vec
        )
        input_grad, full_grad, vector_all, *_ = backward(full, *kept, sums, vec)
        outs = update(
            full_grad, left_stat, right_stat, left_root, right_root, master, averaged_weight, vector_all, vec,
            jnp.transpose(vector_moment), layer_out, input_grad
        )
        *blocks, vector_grad, moment_new, vector_new, bias_grad, layer_out, input_grad = outs
        thin = [jnp.transpose(array) for array in (vector_grad, moment_new, vector_new)]
        return (layer_out[None], input_grad[None], *blocks, *thin, bias_grad[0])
    else:
        layer_out, input_grad, full_grad, vector_all = by_collectives(
            hidden, cell_ids, cell_boxes, cotangent, weight_cols, weight_out, weight_down, vectors, slot_dev
        )
    vector_grad = jnp.transpose(
        lax.dynamic_slice_in_dim(vector_all[0:12], dp_index * owned_rows, owned_rows, 1)
    )
    own_rows = lax.dynamic_slice_in_dim(full_grad, tp_index * strip_width, strip_width, 1)
    own_cols = lax.dynamic_slice_in_dim(full_grad, tp_index * strip_width, strip_width, 2)
    block_grad = own_cols.astype(jnp.float32)
    left_new = STAT_DECAY * left_stat + (1.0 - STAT_DECAY) * jnp.einsum(
        "sic,sjc->sij", own_rows, full_grad, preferred_element_type=jnp.float32
    )
    right_new = STAT_DECAY * right_stat + (1.0 - STAT_DECAY) * jnp.einsum(
        "sic,sij->scj", own_cols, full_grad, preferred_element_type=jnp.float32
    )

    def parts(array):
        high = array.astype(jnp.bfloat16)
        return high, (array - high.astype(jnp.float32)).astype(jnp.bfloat16)

    def product(left, right):
        return jnp.einsum("sij,sjc->sic", left, right, preferred_element_type=jnp.float32)

    left_high, left_rest = parts(left_root)
    right_high, right_rest = parts(right_root)
    precond = product(left_high, full_grad) + product(left_rest, full_grad)
    pre_high, pre_rest = parts(precond)
    precond = (
        product(pre_high, right_high) + product(pre_rest, right_high) + product(pre_high, right_rest)
    )
    master_new = master - BLOCK_RATE * precond
    weight_copy = master_new.astype(jnp.bfloat16)
    ema_new = EMA_DECAY * averaged_weight + (1.0 - EMA_DECAY) * master_new
    vector_rows = lax.dynamic_slice_in_dim(vectors, dp_index * owned_rows, owned_rows, 0)
    moment_new = MOMENTUM * vector_moment + vector_grad
    total_tokens = page_rows * seq_len * dp_count * tp_count
    vector_new = vector_rows - VEC_RATE * lax.rsqrt(jnp.float32(total_tokens)) * moment_new
    bias_grad = vector_grad[:, 0]
    return (
        layer_out,
        input_grad,
        block_grad,
        left_new,
        right_new,
        master_new,
        weight_copy,
        ema_new,
        vector_grad,
        moment_new,
        vector_new,
        bias_grad,
    )


def solution(mesh):
    return jax.shard_map(
        local,
        mesh=mesh,
        in_specs=(
            P(("dp", "tp"), None, None),
            P(("dp", "tp"), None),
            P(("dp", "tp"), None, None),
            P(("dp", "tp"), None, None),
            P(None, None, "tp"),
            P("tp", None),
            P(None, "tp", None),
            P(),
            P("dp", None),
            P("dp", "tp", None),
            P("dp", "tp", None),
            P("dp", "tp", None),
            P("dp", None, None),
            P("dp", "tp", None),
            P("dp", "tp", None),
        ),
        out_specs=(
            P(("dp", "tp"), None, None),
            P(("dp", "tp"), None, None),
            P("dp", None, "tp"),
            P("dp", "tp", None),
            P("dp", "tp", None),
            P("dp", "tp", None),
            P("dp", "tp", None),
            P("dp", "tp", None),
            P("dp", None),
            P("dp", None),
            P("dp", None),
            P("dp"),
        ),
        check_vma=False,
    )
```

```python
import math

import jax
import jax.numpy as jnp
from jax import lax
from jax.experimental import pallas as pl
from jax.experimental.pallas import tpu as pltpu
from jax.sharding import PartitionSpec as P

MODEL_WIDTH = 1024
H = 16
HD = 64

PRECISE = lax.Precision.HIGHEST
EPS_NORM = 1e-06
STAT_DECAY = 0.5
BLOCK_RATE = 0.7
EMA_DECAY = 0.9
MOMENTUM = 0.9
VEC_RATE = 0.2

MESH = pl.DeviceIdType.MESH


def position():
    d, z = lax.axis_index("dp"), lax.axis_index("tp")
    core, x, y = d % 2, (d // 2) % 2, d // 4
    near = {
        "x": (d + 2 - 4 * x, z),
        "y": (d + 4 - 8 * y, z),
        "c": (d + 1 - 2 * core, z),
        "u": (d, z + 1),
        "v": (d, z - 1),
    }
    return z, core, x, y, near


def meet(z, near, extra=()):
    barrier = pltpu.get_barrier_semaphore()
    always = [near[name] for name in "xyc"] + list(extra)
    for device in always:
        pl.semaphore_signal(barrier, 1, device_id=device, device_id_type=MESH)

    @pl.when(z < 3)
    def _():
        pl.semaphore_signal(barrier, 1, device_id=near["u"], device_id_type=MESH)

    @pl.when(z > 0)
    def _():
        pl.semaphore_signal(barrier, 1, device_id=near["v"], device_id_type=MESH)

    pl.semaphore_wait(barrier, len(always) + (z + 2) // 3 + (5 - z) // 3)


ORDER = (0, 1, 2, 7, 3, 4, 5, 6, 8, 9, 10, 11)


NT = (((1,), (1,)), ((), ()))
TOKENS = 512
WIDE = MODEL_WIDTH


def dot(a, b):
    return jnp.dot(a, b, preferred_element_type=jnp.float32)


def dot_nt(a, b):
    return lax.dot_general(a, b, NT, preferred_element_type=jnp.float32)


def columns(i, width=256):
    return pl.ds(pl.multiple_of(i * width, width), width)


def loop(count, body):
    if count == 1:
        body(0)
        return

    def step(i, carry):
        body(i)
        return carry

    lax.fori_loop(0, count, step, 0)


def mean_of(rows):
    return jnp.sum(rows, -1, keepdims=True) * (1.0 / WIDE)


def transpose_into(dest, source):
    def body(i):
        dest[columns(i), :] = source[:, columns(i)].T

    loop(WIDE // 256, body)


def transpose_back(dest, source):
    def body(i):
        dest[:, columns(i)] = source[columns(i), :].T

    loop(WIDE // 256, body)


def embed_tokens(hidden, ids, boxes, x_ref, x_low):
    cells = boxes.shape[1]
    corners = boxes[...].astype(jnp.float32).T
    half = WIDE // 8
    place = lax.broadcasted_iota(jnp.int32, (1, half), 1).astype(jnp.float32)
    rate = jnp.exp(place * (-math.log(1000.0) / half))
    marks = lax.broadcasted_iota(jnp.int32, (cells, TOKENS), 0) == ids[...]
    chosen = jnp.where(marks, 1.0, 0.0).T.astype(jnp.bfloat16)
    for c in range(4):
        angle = corners[:, c : c + 1] * rate
        for kind, wave in enumerate((jnp.sin(angle), jnp.cos(angle))):
            wave = 0.5 * wave
            high = wave.astype(jnp.bfloat16)
            rest = wave - high.astype(jnp.float32)
            middle = rest.astype(jnp.bfloat16)
            low = (rest - middle.astype(jnp.float32)).astype(jnp.bfloat16)
            emb = dot(chosen, high) + (dot(chosen, middle) + dot(chosen, low))
            at = pl.ds(c * 2 * half + kind * half, half)
            value = hidden[:, at].astype(jnp.float32) + emb
            x_ref[:, at] = value
            x_low[:, at] = value.astype(jnp.bfloat16)


def project(x_low, weight, dest, bias, scale):
    def body(i):
        at = columns(i, 1024)
        value = dot(x_low[...], weight[:, at])
        if bias is not None:
            value = value + bias[:, at]
        value = value.astype(jnp.bfloat16)
        if scale:
            value = value * jnp.asarray(HD ** (-0.5), jnp.bfloat16)
        dest[:, at] = value

    loop(WIDE // 1024, body)


def half_mask(e, shape):
    lane = lax.broadcasted_iota(jnp.int32, shape, 1)
    return (lane < HD) if e == 0 else (lane >= HD)


def attend_pair(t, q8, k, v_t, ctx_t, stat):
    at = columns(t, 128)
    keys, queries = k[:, at], q8[:, at]
    for e in range(2):
        own = jnp.where(half_mask(e, queries.shape), queries, jnp.zeros_like(queries))
        scores = dot_nt(keys, own)
        top = jnp.max(scores, 0, keepdims=True)
        power = jnp.exp(scores - top)
        total = jnp.sum(power, 0, keepdims=True)
        probs = (power * (1.0 / total)).astype(jnp.bfloat16)
        rows = pl.ds(pl.multiple_of(t * 128 + e * 64, 64), 64)
        ctx_t[rows, :] = dot(v_t[rows, :], probs).astype(jnp.bfloat16)
        stat[2 * t + e, :, :] = top + jnp.log(total)


def norm_rows(values, gain, shift):
    center = values - mean_of(values)
    inv = lax.rsqrt(mean_of(center * center) + EPS_NORM)
    normed = center * inv
    return normed * gain + shift, normed, inv


SLICE = 64


def row_loop(body):
    loop(TOKENS // SLICE, lambda i: body(pl.ds(pl.multiple_of(i * SLICE, SLICE), SLICE)))


def gelu_both(value):
    phi = 0.5 * (1.0 + lax.erf(value * math.sqrt(0.5)))
    density = jnp.exp(-0.5 * value * value) * (1.0 / math.sqrt(2.0 * math.pi))
    return value * phi, phi + value * density


def forward_kernel(
    cols, outw, down, hidden, ids, boxes, cotangent, vec,
    full_out, layer_out, x_out, q_out, k_out, kt_out, v_out, ctx_out, stat_out, mid_out, hat_out, inv_out, act_out, slope_out,
    two_out, sums_out,
    w, x_t, mid_t, k_t, x_ref, x_low, q8, k, v, v_t, ctx_t, ctx, stat, acc, mid, mid_low, hat, inv, act, slope, y_out, two, sums,
    load, along, onward, arrived, beside, store, spill,
):
    z, core, x, y, near = position()
    p = 2 * y + x
    meet(z, near)

    def own(kk, h):
        if kk < 7:
            return cols.at[kk, pl.ds(h * 512, 512), :]
        if kk == 7:
            return outw.at[pl.ds(h * 128, 128), :]
        return down.at[kk - 8, pl.ds(h * 128, 128), :]

    def spot(s, kk, h):
        if kk < 7:
            return w.at[kk, pl.ds(h * 512, 512), pl.ds(pl.multiple_of(s * 256, 256), 256)]
        return w.at[kk, pl.ds(pl.multiple_of(s * 256 + h * 128, 128), 128), :]

    def spot_whole(s, kk):
        if kk < 7:
            return w.at[kk, :, pl.ds(pl.multiple_of(s * 256, 256), 256)]
        return w.at[kk, pl.ds(pl.multiple_of(s * 256, 256), 256), :]

    def whole_own(kk):
        if kk < 7:
            return cols.at[kk]
        return outw if kk == 7 else down.at[kk - 8]

    def to(source, s, kk, send_sem, recv_sem, name):
        return pltpu.make_async_remote_copy(
            src_ref=source,
            dst_ref=spot(s, kk, core),
            send_sem=send_sem,
            recv_sem=recv_sem.at[s, kk],
            device_id=near[name],
            device_id_type=MESH,
        )

    def first(g, act_on):
        for t in range(3):
            kk = ORDER[3 * g + t]
            mine = (p == t) | (p == 3) if t == 0 else p == t

            @pl.when(mine & (z < 3))
            def _(kk=kk):
                act_on(to(own(kk, core), z, kk, along.at[kk], arrived, "u"))

            @pl.when(mine & (z > 0))
            def _(kk=kk):
                act_on(to(own(kk, core), z, kk, onward.at[0, z, kk], arrived, "v"))

    far = 3 * (1 - z // 2)
    nearest = z + 1 - 2 * (z // 3)
    strips = (nearest, 6 - nearest - far - z, far)

    def item(n, t):
        return strips[n % 3], ORDER[3 * (n // 3) + t]

    def go(s, kk, kind, name, sems):
        return to(spot(s, kk, core), s, kk, onward.at[kind, s, kk], sems, name)

    def stage(n, hop, begin):
        for t in range(3):
            s, kk = item(n, t)
            who = {
                (0, 0): (p == 0) | (p == 3),
                (0, 1): p == 1,
                (0, 2): p == 2,
                (1, 0): (p == 1) | (p == 2),
                (1, 1): (p == 0) | (p == 3),
                (1, 2): (p == 0) | (p == 3),
                (2, 0): None,
                (2, 1): p == 2,
                (2, 2): p == 1,
            }[hop, t]
            if who is None:
                continue

            @pl.when(who)
            def _(s=s, kk=kk, t=t):
                if begin:
                    go(s, kk, 0, "x", arrived).wait_recv()

                def act_on(copy):
                    if begin:
                        copy.start()
                    else:
                        copy.wait_send()

                if hop == 0:

                    @pl.when((s > z) & (z > 0))
                    def _():
                        act_on(go(s, kk, 0, "v", arrived))

                    @pl.when((s < z) & (z < 3))
                    def _():
                        act_on(go(s, kk, 0, "u", arrived))

                    if t == 0:

                        @pl.when(p == 0)
                        def _():
                            act_on(go(s, kk, 1, "x", arrived))
                            act_on(go(s, kk, 2, "y", arrived))
                    else:
                        act_on(go(s, kk, 1, "x", arrived))
                        act_on(go(s, kk, 2, "y", arrived))
                if hop == 1 and t == 1:

                    @pl.when(p == 3)
                    def _():
                        act_on(go(s, kk, 1, "x", arrived))

                if hop == 1 and t == 2:

                    @pl.when(p == 3)
                    def _():
                        act_on(go(s, kk, 2, "y", arrived))

                act_on(go(s, kk, 3, "c", beside))

    copies = []

    def keep(source, dest):
        copy = pltpu.make_async_copy(source, dest, spill.at[len(copies)])
        copy.start()
        copies.append(copy)

    def ready(kk):
        pltpu.make_async_copy(whole_own(kk), spot_whole(z, kk), load.at[kk]).wait()
        for s in strips:
            pltpu.make_async_remote_copy(
                src_ref=spot(s, kk, 1 - core),
                dst_ref=spot(s, kk, 1 - core),
                send_sem=onward.at[3, s, kk],
                recv_sem=beside.at[s, kk],
                device_id=near["c"],
                device_id_type=MESH,
            ).wait_recv()
        copy = pltpu.make_async_copy(w.at[kk], full_out.at[kk], store.at[kk])
        copy.start()

    def unit_embed():
        embed_tokens(hidden, ids, boxes, x_ref, x_low)
        transpose_into(x_t, x_low)
        keep(x_t, x_out)

    def unit_qk():
        ready(0)
        project(x_low, w.at[0], q8, vec.at[6:7], True)
        keep(q8, q_out)
        ready(1)
        project(x_low, w.at[1], k, None, False)
        keep(k, k_out)

    def unit_v():
        ready(2)
        project(x_low, w.at[2], v, vec.at[7:8], False)
        transpose_into(v_t, v)
        keep(v, v_out)

    def unit_k_t():
        transpose_into(k_t, k)
        keep(k_t, kt_out)

    def unit_attend(lo, hi):
        loop(hi - lo, lambda i: attend_pair(lo + i, q8, k, v_t, ctx_t, stat))

    def unit_context():
        transpose_back(ctx, ctx_t)
        keep(ctx, ctx_out)
        keep(stat, stat_out)

    def unit_mid():
        ready(7)

        def tile(i):
            at = columns(i, 1024)
            acc[:, at] = dot(ctx[...], w[7, :, at])

        loop(WIDE // 1024, tile)

        def rows(r):
            value = x_ref[r, :] + acc[r, :] + vec[0:1, :]
            out, normed, scale = norm_rows(value, vec[2:3, :], vec[3:4, :])
            mid[r, :] = out
            mid_low[r, :] = out.astype(jnp.bfloat16)
            hat[r, :] = normed
            inv[r, :] = jnp.broadcast_to(scale, (SLICE, 128))

        row_loop(rows)
        transpose_into(mid_t, mid_low)
        keep(mid_t, mid_out)
        keep(hat, hat_out)
        keep(inv, inv_out)

    def unit_up(u):
        ready(3 + u)
        def tile(i):
            at = columns(i)
            slot = i % 2

            @pl.when(i >= 2)
            def _():
                pltpu.make_async_copy(slope.at[slot], slope_out.at[u, :, at], store.at[12 + slot]).wait()

            value = dot(mid_low[...], w[3 + u, :, at]) + vec[8 + u : 9 + u, at]
            out, grad = gelu_both(value)
            act[u, :, at] = out.astype(jnp.bfloat16)
            slope[slot] = grad
            pltpu.make_async_copy(slope.at[slot], slope_out.at[u, :, at], store.at[12 + slot]).start()

        loop(WIDE // 256, tile)
        for slot in range(2):
            pltpu.make_async_copy(slope.at[slot], slope_out.at[u, :, columns(slot)], store.at[12 + slot]).wait()
        keep(act.at[u], act_out.at[u])

    def unit_down(u):
        ready(8 + u)

        def tile(i):
            at = columns(i, 1024)
            value = dot(act[u], w[8 + u, :, at])
            acc[:, at] = value if u == 0 else acc[:, at] + value

        loop(WIDE // 1024, tile)

    def unit_last():
        sums[...] = jnp.zeros_like(sums)

        def rows(r):
            value = mid[r, :] + acc[r, :] + vec[1:2, :]
            out, normed, scale = norm_rows(value, vec[4:5, :], vec[5:6, :])
            y_out[r, :] = out
            grad = cotangent[r, :].astype(jnp.float32)
            scaled = grad * vec[4:5, :]
            arg = scale * (scaled - mean_of(scaled) - normed * mean_of(scaled * normed))
            two[r, :] = arg
            sums[1:2, :] += jnp.sum(arg, 0, keepdims=True)
            sums[4:5, :] += jnp.sum(grad * normed, 0, keepdims=True)
            sums[5:6, :] += jnp.sum(grad, 0, keepdims=True)

        row_loop(rows)
        keep(y_out, layer_out)
        keep(two, two_out)
        keep(sums, sums_out)

    first(0, lambda copy: copy.start())
    first(1, lambda copy: copy.start())
    for kk in ORDER:
        pltpu.make_async_copy(whole_own(kk), spot_whole(z, kk), load.at[kk]).start()
    unit_embed()
    after = {
        4: lambda: (unit_qk(), unit_v()),
        5: lambda: unit_attend(0, 4),
        6: lambda: (unit_attend(4, 8), unit_context()),
        7: unit_mid,
        8: lambda: unit_up(0),
        9: lambda: (unit_up(1), unit_k_t()),
        10: lambda: unit_up(2),
        11: lambda: unit_up(3),
        12: lambda: unit_down(0),
        13: lambda: (unit_down(1), unit_down(2), unit_down(3), unit_last()),
    }
    for n in range(14):
        if n in (3, 6):
            first(n // 3 + 1, lambda copy: copy.start())
        for hop in range(3):
            if 0 <= n - hop < 12:
                stage(n - hop, hop, True)
        if n in after:
            after[n]()
    for n in range(12):
        for hop in range(3):
            stage(n, hop, False)
    for g in range(4):
        first(g, lambda copy: copy.wait_send())
    for kk in ORDER:
        pltpu.make_async_copy(w.at[kk], full_out.at[kk], store.at[kk]).wait()
    for copy in copies:
        copy.wait()


def forward(cols, outw, down, hidden, ids, boxes, cotangent, vec):
    anywhere = pl.BlockSpec(memory_space=pl.ANY)
    vmem = pl.BlockSpec(memory_space=pltpu.VMEM)
    dma = pltpu.SemaphoreType.DMA
    low, wide = jnp.bfloat16, jnp.float32
    page = (TOKENS, WIDE)
    outs = [
        ((12, WIDE, WIDE), low),
        (page, wide),
        ((WIDE, TOKENS), low),
        (page, low),
        (page, low),
        ((WIDE, TOKENS), low),
        (page, low),
        (page, low),
        ((H, 1, TOKENS), wide),
        ((WIDE, TOKENS), low),
        (page, wide),
        ((TOKENS, 128), wide),
        ((4,) + page, low),
        ((4,) + page, wide),
        (page, wide),
        ((16, WIDE), wide),
    ]
    return pl.pallas_call(
        forward_kernel,
        name="forward",
        out_shape=[jax.ShapeDtypeStruct(*o) for o in outs],
        in_specs=[anywhere] * 3 + [vmem] * 5,
        out_specs=[anywhere] * len(outs),
        scratch_shapes=[
            pltpu.VMEM((12, WIDE, WIDE), low),
            pltpu.VMEM((WIDE, TOKENS), low),
            pltpu.VMEM((WIDE, TOKENS), low),
            pltpu.VMEM((WIDE, TOKENS), low),
            pltpu.VMEM(page, wide),
            pltpu.VMEM(page, low),
            pltpu.VMEM(page, low),
            pltpu.VMEM(page, low),
            pltpu.VMEM(page, low),
            pltpu.VMEM((WIDE, TOKENS), low),
            pltpu.VMEM((WIDE, TOKENS), low),
            pltpu.VMEM(page, low),
            pltpu.VMEM((H, 1, TOKENS), wide),
            pltpu.VMEM(page, wide),
            pltpu.VMEM(page, wide),
            pltpu.VMEM(page, low),
            pltpu.VMEM(page, wide),
            pltpu.VMEM((TOKENS, 128), wide),
            pltpu.VMEM((4,) + page, low),
            pltpu.VMEM((2, TOKENS, 256), wide),
            pltpu.VMEM(page, wide),
            pltpu.VMEM(page, wide),
            pltpu.VMEM((16, WIDE), wide),
            dma((12,)),
            dma((12,)),
            dma((4, 4, 12)),
            dma((4, 12)),
            dma((4, 12)),
            dma((14,)),
            dma((20,)),
        ],
        compiler_params=pltpu.CompilerParams(
            collective_id=1, has_side_effects=True, vmem_limit_bytes=61 << 20
        ),
    )(cols, outw, down, hidden, ids, boxes, cotangent, vec)


KEPT = ((8, 5, 9, 0, 1, 4), (10, 3, 11, 2, 6, 7))
EARLY = (((0, 8), (0, 10), 0), ((1, 5), None, 0), (None, (1, 3), 0), ((2, 9), (2, 11), 8))
LATE = (((3, 0), (3, 2), 0), ((4, 1), None, 8), ((5, 4), (4, 6), 0), (None, (5, 7), 8))
UNIT_ORDER = (0, 2, 1, 3)
RING = 3


def attend_pair_back(t, q8, k, v, ctx_grad, k_t, stat, dq_t, dk, dv):
    at = columns(t, 128)
    keys, queries, values, grads = k[:, at], q8[:, at], v[:, at], ctx_grad[:, at]
    none = jnp.zeros_like(queries)
    key_sum = value_sum = None
    for e in range(2):
        mask = half_mask(e, queries.shape)
        own_q = jnp.where(mask, queries, none)
        own_g = jnp.where(mask, grads, none)
        probs = jnp.exp(dot_nt(keys, own_q) - stat[2 * t + e])
        prob_grad = dot_nt(values, own_g)
        carried = jnp.sum(probs * prob_grad, 0, keepdims=True)
        score_grad = (probs * (prob_grad - carried)).astype(jnp.bfloat16)
        rows = pl.ds(pl.multiple_of(t * 128 + e * 64, 64), 64)
        dq_t[rows, :] = (dot(k_t[rows, :], score_grad) * HD ** (-0.5)).astype(jnp.bfloat16)
        key_part = dot(score_grad, own_q)
        value_part = dot(probs.astype(jnp.bfloat16), own_g)
        key_sum = key_part if e == 0 else key_sum + key_part
        value_sum = value_part if e == 0 else value_sum + value_part
    dk[:, at] = key_sum.astype(jnp.bfloat16)
    dv[:, at] = value_sum.astype(jnp.bfloat16)


class Stream:
    def __init__(self, entries, chunk, lag, refs, ring, place):
        self.z, self.core, self.x, self.y, self.d = place
        self.p = 2 * self.y + self.x
        self.chunk, self.per, self.lag = chunk, WIDE // chunk, lag
        self.entries, self.refs, self.ring = entries, refs, ring
        self.base = min(item[0] for entry in entries for item in entry[:2] if item is not None)
        self.steps = max(entry[2] for entry in entries) + self.per + 6 * lag
        x, y = self.x, self.y
        self.corner = [(x if j % 2 == 0 else 1 - x, y if j // 2 == 0 else 1 - y) for j in range(3)]
        self.by_x, self.by_y = 2 - 4 * x, 4 - 8 * y

    def rows(self, r):
        return pl.ds(pl.multiple_of(r * self.chunk, self.chunk), self.chunk)

    def remote(self, source, dest, send_sem, recv_sem, device):
        return pltpu.make_async_remote_copy(
            src_ref=source, dst_ref=dest, send_sem=send_sem, recv_sem=recv_sem,
            device_id=device, device_id_type=MESH,
        )


    def forward(self, q, r, turn):
        R = self.refs
        at = self.rows(r)
        device = (self.d + self.by_y + turn * (self.by_x - self.by_y), self.z)
        return self.remote(R["mine"].at[q, at, :], R["land"].at[q, at, :], R["send"].at[q, r], R["recv"].at[q, r], device)

    def chained(self, i, r, way):
        R = self.refs
        at = self.rows(r)
        return R["chain"].at[way, i, at, :], R["chain_send"].at[way, i, r], R["chain_recv"].at[way, i, r]

    def pass_on(self, source, i, r, way):
        ref, ssem, rsem = self.chained(i, r, way)
        return self.remote(source, ref, ssem, rsem, (self.d, self.z + (1 if way == 0 else -1)))

    def total_out(self, source, i, r):
        R = self.refs
        return pltpu.make_async_copy(source, R["total"].at[i, self.rows(r), :], R["out"].at[i, r])

    def add_to_mine(self, q, r, ref):
        mine = self.refs["mine"]

        def part(g):
            at = pl.ds(pl.multiple_of(r * self.chunk + g * 32, 32), 32)
            here = pl.ds(pl.multiple_of(g * 32, 32), 32)
            mine[q, at, :] = (mine[q, at, :].astype(jnp.float32) + ref[here, :].astype(jnp.float32)).astype(jnp.bfloat16)

        loop(self.chunk // 32, part)

    def load(self, e, kind, q, r):
        source = self.refs["sib" if kind == 0 else "land"]
        return pltpu.make_async_copy(source.at[q, self.rows(r), :], self.ring.at[q - self.base, kind], self.refs["ring_sem"].at[q - self.base, kind])

    def begin_pair(self, e, q, j, i, r):
        R = self.refs
        quarter = 256 // self.chunk

        def arrival(f):
            at = pl.ds(pl.multiple_of(f * 256, 256), 256)
            ref = R["sib"].at[q, at, :]
            self.remote(ref, ref, R["give_send"].at[q, f], R["give_recv"].at[q, f], (self.d, self.z)).wait_recv()

        if quarter == 1:
            arrival(r)
        else:

            @pl.when(lax.rem(r, quarter) == 0)
            def _():
                arrival(lax.div(r, quarter))

        self.load(e, 0, q, r).start()

    def end_pair(self, e, q, j, i, r):
        self.load(e, 0, q, r).wait()
        self.add_to_mine(q, r, self.ring.at[q - self.base, 0])
        odd = lax.rem(r, 2)
        rx, ry = self.corner[j]

        @pl.when((rx + ry == 1) & (rx + odd == 1))
        def _():
            self.forward(q, r, odd).start()

    def path(self, hop, begin):
        def run(e, q, j, i, r):
            odd = lax.rem(r, 2)
            rx, ry = self.corner[j]
            here = {1: rx + ry == 2, 2: (rx + ry == 1) & (rx == odd), 3: rx + ry == 0}[hop]

            @pl.when(here)
            def _():
                copy = self.load(e, 1, q, r)
                if begin:
                    self.forward(q, r, odd).wait_recv()
                    copy.start()
                    return
                copy.wait()
                self.add_to_mine(q, r, self.ring.at[q - self.base, 1])
                if hop == 1:
                    self.forward(q, r, 1 - odd).start()
                if hop == 2:
                    self.forward(q, r, odd).start()
                if hop == 3:
                    mine = self.refs["mine"].at[q, self.rows(r), :]

                    @pl.when(self.z == 0)
                    def _():
                        self.pass_on(mine, i, r, 0).start()

                    @pl.when(self.z == 3)
                    def _():
                        self.pass_on(mine, i, r, 1).start()

        return run

    def link(self, q, i, r, way, last):
        R = self.refs
        at = self.rows(r)
        ref, ssem, rsem = self.chained(i, r, way)
        self.remote(ref, ref, ssem, rsem, (self.d, self.z)).wait_recv()
        mine, chain = R["mine"], R["chain"]

        def part(g):
            piece = pl.ds(pl.multiple_of(r * self.chunk + g * 32, 32), 32)
            came = chain[way, i, piece, :].astype(jnp.float32)
            chain[way, i, piece, :] = (mine[q, piece, :].astype(jnp.float32) + came).astype(jnp.bfloat16)
            if last:
                other = chain[1 - way, i, piece, :].astype(jnp.float32)
                mine[q, piece, :] = (other + came).astype(jnp.bfloat16)

        loop(self.chunk // 32, part)
        self.pass_on(ref, i, r, way).start()
        if last:
            self.total_out(mine.at[q, at, :], i, r).start()

    def links(self, last):
        def run(e, q, j, i, r):
            @pl.when(self.p == j)
            def _():
                for z, way in ((1, 1 if last else 0), (2, 0 if last else 1)):

                    @pl.when(self.z == z)
                    def _(way=way):
                        self.link(q, i, r, way, last)

        return run

    def ends(self, e, q, j, i, r):
        R = self.refs
        at = self.rows(r)

        @pl.when(self.p == j)
        def _():
            for z, way in ((0, 1), (3, 0)):

                @pl.when(self.z == z)
                def _(way=way):
                    ref, ssem, rsem = self.chained(i, r, way)
                    self.remote(ref, ref, ssem, rsem, (self.d, self.z)).wait_recv()
                    mine, chain = R["mine"], R["chain"]

                    def part(g):
                        piece = pl.ds(pl.multiple_of(r * self.chunk + g * 32, 32), 32)
                        chain[way, i, piece, :] = (
                            mine[q, piece, :].astype(jnp.float32) + chain[way, i, piece, :].astype(jnp.float32)
                        ).astype(jnp.bfloat16)

                    loop(self.chunk // 32, part)
                    self.total_out(ref, i, r).start()

    def each(self, function):
        for e, entry in enumerate(self.entries):
            here = [item for item in entry[:2] if item is not None]
            if len(here) == 2:
                (q, slot), (q_other, slot_other) = here
                assert slot // 4 == slot_other // 4
                if q != q_other:
                    q = q + self.core * (q_other - q)
                i = slot % 2
                if i != slot_other % 2:
                    i = i + self.core * (slot_other % 2 - i)
                function(e, entry[2], q, slot // 4, i)
            else:
                only = 0 if entry[1] is None else 1

                @pl.when(self.core == only)
                def _(e=e, entry=entry, item=here[0]):
                    function(e, entry[2], item[0], item[1] // 4, item[1] % 2)

    def begin(self, n):
        L = self.lag
        begins = ((0, self.begin_pair), (L, self.path(1, True)), (2 * L, self.path(2, True)), (3 * L, self.path(3, True)))
        self.visit(n, begins)

    def end(self, n):
        L = self.lag
        ends = (
            (6 * L, self.ends),
            (5 * L, self.links(True)),
            (4 * L, self.links(False)),
            (3 * L, self.path(3, False)),
            (2 * L, self.path(2, False)),
            (L, self.path(1, False)),
            (0, self.end_pair),
        )
        self.visit(n, ends)

    def visit(self, n, parts):
        L = self.lag

        def entry_parts(e, start, q, j, i):
            m = n - start

            @pl.when((m >= 0) & (m < self.per + 6 * L))
            def _():
                for lag, part in parts:
                    r = m - lag

                    @pl.when((r >= 0) & (r < self.per))
                    def _(r=r, part=part):
                        part(e, q, j, i, r)

        self.each(entry_parts)

    def finish(self):
        def chunk(e, start, q, j, i):
            rx, ry = self.corner[j]

            def body(r):
                @pl.when(rx + ry > 0)
                def _():
                    self.forward(q, r, 0).wait_send()

                mine = self.refs["mine"].at[q, self.rows(r), :]

                @pl.when((rx + ry == 0) & (self.z < 3))
                def _():
                    self.pass_on(mine, i, r, 0).wait_send()

                @pl.when((rx + ry == 0) & (self.z > 0))
                def _():
                    self.pass_on(mine, i, r, 1).wait_send()

                @pl.when(rx + ry == 0)
                def _():
                    self.total_out(mine, i, r).wait()

            loop(self.per, body)

        self.each(chunk)


def backward_kernel(
    full, x_in, q_in, k_in, kt_in, v_in, ctx_in, stat_in, mid_in, hat_in, inv_in, act_in, slope_in, two_in, sums_in, vec,
    input_out, total, sums, sib, land,
    w, pb, pt, pf, stat, inv, stage, mine, chain, ring_a, ring_b, vec_in,
    wsem, asem, ssem, isem, osem,
    give_send, give_recv, send_a, recv_a, chain_send_a, chain_recv_a, out_a, ring_sem_a,
    send_b, recv_b, chain_send_b, chain_recv_b, out_b, ring_sem_b, vec_send, vec_recv,
):
    z, core, x, y, near = position()
    p = 2 * y + x
    d = 2 * p + core
    z_one = (d, z + 1 - 2 * (z % 2))
    z_two = (d, z + 2 - 4 * (z // 2))
    shared = {"mine": mine, "land": land, "chain": chain, "sib": sib, "total": total, "give_send": give_send, "give_recv": give_recv}
    place = (z, core, x, y, d)
    early = Stream(EARLY, CHUNK_EARLY, LAG_EARLY, dict(
        shared, send=send_a, recv=recv_a, chain_send=chain_send_a, chain_recv=chain_recv_a, out=out_a, ring_sem=ring_sem_a,
    ), ring_a, place)
    late = Stream(LATE, CHUNK_LATE, LAG_LATE, dict(
        shared, send=send_b, recv=recv_b, chain_send=chain_send_b, chain_recv=chain_recv_b, out=out_b, ring_sem=ring_sem_b,
    ), ring_b, place)

    two_low, act_ring = pb.at[0], (pb.at[1], pb.at[2])
    up_grads = {0: pb.at[3], 2: pb.at[3], 1: pb.at[7], 3: pb.at[8]}
    k, q8, v = pb.at[4], pb.at[5], pb.at[6]
    one_low, ctx, ctx_grad, dq, dk, dv = pb.at[0], pb.at[1], pb.at[2], pb.at[0], pb.at[9], pb.at[3]
    two_t, mid_t, k_t = pt.at[0], pt.at[1], pt.at[2]
    one_t, x_t, dq_t = pt.at[0], pt.at[3], pt.at[4]
    two, back, slope_ring = pf.at[0], pf.at[1], (pf.at[2], pf.at[3])
    one, hat = pf.at[0], pf.at[2]
    uses = [slot for u in UNIT_ORDER for slot in (8 + u, 3 + u)] + [7, 0, 1, 2]

    def weight(n):
        return pltpu.make_async_copy(full.at[uses[n]], w.at[n % RING], wsem.at[n % RING])

    def act_load(n):
        return pltpu.make_async_copy(act_in.at[UNIT_ORDER[n]], act_ring[n % 2], asem.at[n % 2])

    def slope_load(n):
        return pltpu.make_async_copy(slope_in.at[UNIT_ORDER[n]], slope_ring[n % 2], ssem.at[n % 2])

    loads = {}

    def fetch(name, source, dest):
        loads[name] = pltpu.make_async_copy(source, dest, isem.at[len(loads)])
        loads[name].start()

    fetch("two", two_in, two)
    weight(0).start()
    slope_load(0).start()
    act_load(0).start()
    fetch("mid", mid_in, mid_t)
    weight(1).start()
    fetch("sums", sums_in, sums)
    weight(2).start()
    slope_load(1).start()
    act_load(1).start()
    for name, source, dest in (
        ("inv", inv_in, inv), ("k", k_in, k), ("q", q_in, q8), ("v", v_in, v), ("kt", kt_in, k_t), ("stat", stat_in, stat), ("x", x_in, x_t),
    ):
        fetch(name, source, dest)
    meet(z, near, (z_two,))

    counter = {"early": 0}
    produced = set()

    def run(count, body, at=()):
        base = counter["early"]
        for one_entry in EARLY:
            if at and one_entry[2] < base + len(at):
                assert all(item is None or item[1] in produced for item in one_entry[:2])

        def one_turn(i):
            if not at:
                body(i)
                return
            first, stride = at[0], (at[1] - at[0] if len(at) > 1 else count)
            now = (i >= first) & (lax.rem(i - first + stride, stride) == 0)

            @pl.when(now)
            def _():
                early.begin(base + lax.div(i - first, stride))

            body(i)

            @pl.when(now)
            def _():
                early.end(base + lax.div(i - first, stride))

        loop(count, one_turn)
        counter["early"] += len(at)

    def use(n):
        weight(n).wait()
        return w.at[n % RING]

    def done(n):
        if n + RING < 12:
            weight(n + RING).start()

    given = {0: [], 1: []}

    def give(slot, c, n, f):
        at = pl.ds(f * 256, 256)
        q = KEPT[1 - c].index(slot)
        return pltpu.make_async_remote_copy(
            src_ref=stage.at[n % 2, at, :], dst_ref=sib.at[q, at, :], send_sem=give_send.at[q, f],
            recv_sem=give_recv.at[q, f], device_id=near["c"], device_id_type=MESH,
        )

    def block(slot, left_t, right, after=()):
        owner = (slot // 2) % 2
        giver = 1 - owner
        q = KEPT[owner].index(slot)
        n = len(given[giver])
        if n >= 2:

            @pl.when(core == giver)
            def _():
                for f in range(4):
                    give(given[giver][n - 2], giver, n - 2, f).wait_send()

        def tile(i):
            at = columns(i, 512)
            value = dot(left_t[...], right[:, at]).astype(jnp.bfloat16)

            @pl.when(core == owner)
            def _():
                mine[q, :, at] = value

            @pl.when(core == giver)
            def _():
                stage[n % 2, :, at] = value

        run(WIDE // 512, tile, after)

        @pl.when(core == giver)
        def _():
            for f in range(4):
                give(slot, giver, n, f).start()

        given[giver].append(slot)
        produced.add(slot)

    def token_sum(row, ref):
        def tile(i):
            at = columns(i)
            sums[row : row + 1, at] = jnp.sum(ref[:, at].astype(jnp.float32), 0, keepdims=True)

        loop(WIDE // 256, tile)

    @pl.when(p == 3)
    def _():
        chain[0] = jnp.zeros(chain.shape[1:], chain.dtype)
        pltpu.make_async_copy(chain.at[0], total, osem.at[1]).start()

    loads["two"].wait()

    def to_low(r):
        two_low[r, :] = two[r, :].astype(jnp.bfloat16)

    row_loop(to_low)
    transpose_into(two_t, two_low)
    loads["mid"].wait()
    loads["sums"].wait()
    for n, u in enumerate(UNIT_ORDER):
        pace = PACE[n]
        weights = use(2 * n)
        slope_load(n).wait()
        act_load(n).wait()
        slope, up_grad = slope_ring[n % 2], up_grads[u]

        def tile(i):
            rows = columns(i, MOST if pace[0] else WIDE)
            grad = dot_nt(two_low[...], weights[rows, :]) * slope[:, rows]
            up_grad[:, rows] = grad.astype(jnp.bfloat16)

        run(WIDE // MOST if pace[0] else 1, tile, pace[0])
        done(2 * n)
        if n == 2:
            fetch("hat", hat_in, hat)
        token_sum(8 + u, up_grad)
        block(8 + u, two_t, act_ring[n % 2], pace[1])
        if n == 2:
            fetch("ctx", ctx_in, ctx)
        weights = use(2 * n + 1)

        def tile_back(i):
            at = columns(i, MOST if pace[2] else WIDE)
            value = dot_nt(up_grad[...], weights[at, :])
            back[:, at] = two[:, at] + value if n == 0 else back[:, at] + value

        run(WIDE // MOST if pace[2] else 1, tile_back, pace[2])
        done(2 * n + 1)
        if n < 2:
            block(3 + u, mid_t, up_grad, pace[3])
        if n + 2 < 4:
            slope_load(n + 2).start()
            act_load(n + 2).start()
    for name in ("hat", "inv"):
        loads[name].wait()
    sums[0:1, :] = jnp.zeros((1, WIDE), jnp.float32)
    sums[2:4, :] = jnp.zeros((2, WIDE), jnp.float32)

    def rows(i):
        r = pl.ds(pl.multiple_of(i * SLICE, SLICE), SLICE)
        grad, normed = back[r, :], hat[r, :]
        scaled = grad * vec[2:3, :]
        arg = inv[r, 0:1] * (scaled - mean_of(scaled) - normed * mean_of(scaled * normed))
        one[r, :] = arg
        one_low[r, :] = arg.astype(jnp.bfloat16)
        sums[0:1, :] += jnp.sum(arg, 0, keepdims=True)
        sums[2:3, :] += jnp.sum(grad * normed, 0, keepdims=True)
        sums[3:4, :] += jnp.sum(grad, 0, keepdims=True)

    run(TOKENS // SLICE, rows, PACE[4])
    transpose_into(one_t, one_low)
    weights = use(8)

    def tile_ctx(i):
        at = columns(i, MOST)
        ctx_grad[:, at] = dot_nt(one_low[...], weights[at, :]).astype(jnp.bfloat16)

    run(WIDE // MOST, tile_ctx, PACE[5])
    done(8)
    for name in ("k", "q", "v", "kt", "stat"):
        loads[name].wait()
    run(H // 2, lambda t: attend_pair_back(t, q8, k, v, ctx_grad, k_t, stat, dq_t, dk, dv), PACE[7])
    transpose_back(dq, dq_t)
    loads["x"].wait()
    block(0, x_t, dq, PACE[8])
    block(2, x_t, dv)
    block(1, x_t, dk)
    block(4, mid_t, up_grads[1], PACE[8])
    block(6, mid_t, up_grads[3])
    loads["ctx"].wait()
    block(7, one_t, ctx, PACE[8])

    def vec_hop(h):
        device = (near["c"], near["x"], near["y"], z_one, z_two)[h]
        return pltpu.make_async_remote_copy(
            src_ref=sums, dst_ref=vec_in.at[h], send_sem=vec_send.at[h], recv_sem=vec_recv.at[h],
            device_id=device, device_id_type=MESH,
        )

    token_sum(6, dq)
    token_sum(7, dv)
    vec_hop(0).start()
    hop = 0
    tail = {"early": counter["early"], "late": 0}

    def both(count, body=None, hops=False):
        base_late, base_early = tail["late"], tail["early"]

        def turn(i):
            now = lax.rem(i, LATE_TURNS) == LATE_TURNS - 1
            late.begin(base_late + i)

            @pl.when(now)
            def _():
                early.begin(base_early + lax.div(i, LATE_TURNS))

            if body is not None:
                body(i)
            late.end(base_late + i)

            @pl.when(now)
            def _():
                early.end(base_early + lax.div(i, LATE_TURNS))

            if hops:
                for h in range(5):

                    @pl.when(i == 1 + 2 * h)
                    def _(h=h):
                        vec_hop(h).wait()
                        sums[...] = sums[...] + vec_in[h]
                        if h < 4:
                            vec_hop(h + 1).start()

        loop(count, turn)
        tail["late"] += count
        tail["early"] += count // LATE_TURNS

    for kk, grad in ((0, dq), (1, dk), (2, dv)):
        weights = use(9 + kk)

        def tile_in(i):
            at = columns(i, 512)
            one[:, at] = one[:, at] + dot_nt(grad[...], weights[at, :])

        both(WIDE // 512, tile_in)
    out = pltpu.make_async_copy(one, input_out, osem.at[0])
    out.start()
    turns = max(late.steps - tail["late"], LATE_TURNS * (early.steps - tail["early"]))
    both(-(-turns // LATE_TURNS) * LATE_TURNS, hops=True)

    for c in range(2):

        @pl.when(core == c)
        def _(c=c):
            n = len(given[c])
            for back_by in (2, 1):
                for f in range(4):
                    give(given[c][n - back_by], c, n - back_by, f).wait_send()

    early.finish()
    late.finish()
    out.wait()

    @pl.when(p == 3)
    def _():
        pltpu.make_async_copy(chain.at[0], total, osem.at[1]).wait()


CHUNK_EARLY, CHUNK_LATE = 128, 32
LAG_EARLY, LAG_LATE = 2, 3
LATE_TURNS = 2
NO = ()
MOST = 512
PACE = (
    (NO, NO, NO, NO),
    (NO, NO, NO, NO),
    (NO, (1,), NO, NO),
    ((1,), NO, (1,), NO),
    NO,
    (1,),
    NO,
    (1, 3, 5, 7),
    (1,),
)


def backward(full, x, q, k, kt, v, ctx, stat, mid, hat, inv, act, slope, two, sums, vec):
    anywhere = pl.BlockSpec(memory_space=pl.ANY)
    vmem = pl.BlockSpec(memory_space=pltpu.VMEM)
    dma = pltpu.SemaphoreType.DMA
    low, wide = jnp.bfloat16, jnp.float32
    page = (TOKENS, WIDE)
    many_a, many_b = WIDE // CHUNK_EARLY, WIDE // CHUNK_LATE

    def stream_sems(many):
        return [dma((6, many)), dma((6, many)), dma((2, 2, many)), dma((2, 2, many)), dma((2, many)), dma((3, 2))]

    return pl.pallas_call(
        backward_kernel,
        name="backward",
        out_shape=[
            jax.ShapeDtypeStruct(page, wide),
            jax.ShapeDtypeStruct((2, WIDE, WIDE), low),
            jax.ShapeDtypeStruct((16, WIDE), wide),
            jax.ShapeDtypeStruct((6, WIDE, WIDE), low),
            jax.ShapeDtypeStruct((6, WIDE, WIDE), low),
        ],
        in_specs=[anywhere] * 15 + [vmem],
        out_specs=[anywhere, anywhere, vmem, anywhere, anywhere],
        scratch_shapes=[
            pltpu.VMEM((RING, WIDE, WIDE), low),
            pltpu.VMEM((10,) + page, low),
            pltpu.VMEM((5, WIDE, TOKENS), low),
            pltpu.VMEM((4,) + page, wide),
            pltpu.VMEM((H, 1, TOKENS), wide),
            pltpu.VMEM((TOKENS, 128), wide),
            pltpu.VMEM((2, WIDE, WIDE), low),
            pltpu.VMEM((6, WIDE, WIDE), low),
            pltpu.VMEM((2, 2, WIDE, WIDE), low),
            pltpu.VMEM((3, 2, CHUNK_EARLY, WIDE), low),
            pltpu.VMEM((3, 2, CHUNK_LATE, WIDE), low),
            pltpu.VMEM((5, 16, WIDE), wide),
            dma((RING,)), dma((2,)), dma((2,)), dma((12,)), dma((2,)),
            dma((6, 4)), dma((6, 4)),
            *stream_sems(many_a),
            *stream_sems(many_b),
            dma((5,)), dma((5,)),
        ],
        compiler_params=pltpu.CompilerParams(
            collective_id=2, has_side_effects=True, vmem_limit_bytes=62 << 20
        ),
    )(full, x, q, k, kt, v, ctx, stat, mid, hat, inv, act, slope, two, sums, vec)


STRIP = 256


def update_kernel(
    grads, left_stat, right_stat, left_root, right_root, master, averaged, sums, vectors, moment, page_one, page_two,
    block_out, left_out, right_out, master_out, copy_out, ema_out, vgrad_out, moment_out, vector_out, bias_out, one_out, two_out,
    b, ls, rs, lr, rr, ms, av, bt, pre, bo, cp, pages, isem, osem, psem,
):
    z, dp = lax.axis_index("tp"), lax.axis_index("dp")
    sources = (grads, left_root, right_root, left_stat, right_stat, master, averaged)
    places = (b, lr, rr, ls, rs, ms, av)

    def load(n, s):
        return pltpu.make_async_copy(sources[n].at[s], places[n].at[s], isem.at[n, s])

    for s in range(2):
        for n in range(7):
            load(n, s).start()

    def page(n, way):
        if way == 0:
            return pltpu.make_async_copy((page_one, page_two)[n], pages.at[n], psem.at[n, 0])
        return pltpu.make_async_copy(pages.at[n], (one_out, two_out)[n], psem.at[n, 1])

    page(0, 0).start()
    page(1, 0).start()
    own = pl.ds(pl.multiple_of(dp * 128, 128), 128)
    grad = sums[0:12, own]
    bias_out[...] = sums[0:1, own]
    vgrad_out[...] = grad
    fresh = MOMENTUM * moment[...] + grad
    moment_out[...] = fresh
    tokens = TOKENS * 32
    vector_out[...] = vectors[:, own] - (VEC_RATE / math.sqrt(tokens)) * fresh

    def store(n, s):
        dest = (block_out, left_out, right_out, master_out, copy_out, ema_out)[n].at[s]
        source = (bo, ls, rs, ms, cp, av)[n].at[s]
        return pltpu.make_async_copy(source, dest, osem.at[n, s])

    strip = pl.ds(pl.multiple_of(z * STRIP, STRIP), STRIP)
    for s in range(2):
        load(0, s).wait()
        load(1, s).wait()
        root_low = lr[s].astype(jnp.bfloat16)

        def first(i):
            at = columns(i)
            turned = b[s, columns(i), strip]
            bo[s, columns(i), :] = turned.astype(jnp.float32)
            bt[:, at] = turned.T

        pre[...] = dot(root_low, b[s]).astype(jnp.bfloat16)
        loop(WIDE // 256, first)
        store(0, s).start()
        load(3, s).wait()
        load(4, s).wait()

        def stats(i):
            at = columns(i, 1024)
            ls[s, :, at] = STAT_DECAY * ls[s, :, at] + (1.0 - STAT_DECAY) * dot_nt(b[s, strip, :], b[s, at, :])
            rs[s, :, at] = STAT_DECAY * rs[s, :, at] + (1.0 - STAT_DECAY) * dot(bt[...], b[s, :, at])

        loop(WIDE // 1024, stats)
        page(s, 0).wait()
        page(s, 1).start()
        store(1, s).start()
        store(2, s).start()
        load(2, s).wait()
        load(5, s).wait()
        load(6, s).wait()

        def second(i):
            at = columns(i, 1024)
            change = dot(pre[...], rr[s, :, at].astype(jnp.bfloat16))
            value = ms[s, :, at] - BLOCK_RATE * change
            ms[s, :, at] = value
            cp[s, :, at] = value.astype(jnp.bfloat16)
            av[s, :, at] = EMA_DECAY * av[s, :, at] + (1.0 - EMA_DECAY) * value

        loop(WIDE // 1024, second)
        for n in (3, 4, 5):
            store(n, s).start()
    for s in range(2):
        page(s, 1).wait()
        for n in range(6):
            store(n, s).wait()


def update(grads, left_stat, right_stat, left_root, right_root, master, averaged, sums, vectors, moment, page_one, page_two):
    anywhere = pl.BlockSpec(memory_space=pl.ANY)
    vmem = pl.BlockSpec(memory_space=pltpu.VMEM)
    dma = pltpu.SemaphoreType.DMA
    low, wide = jnp.bfloat16, jnp.float32
    rows = (2, STRIP, WIDE)
    shapes = [
        ((2, WIDE, STRIP), wide), (rows, wide), (rows, wide), (rows, wide), (rows, low), (rows, wide),
        ((12, 128), wide), ((12, 128), wide), ((12, 128), wide), ((1, 128), wide),
        ((TOKENS, WIDE), wide), ((TOKENS, WIDE), wide),
    ]
    return pl.pallas_call(
        update_kernel,
        name="update",
        out_shape=[jax.ShapeDtypeStruct(*shape) for shape in shapes],
        in_specs=[anywhere] * 7 + [vmem] * 3 + [anywhere] * 2,
        out_specs=[anywhere] * 6 + [vmem] * 4 + [anywhere] * 2,
        scratch_shapes=[
            pltpu.VMEM((2, WIDE, WIDE), low),
            pltpu.VMEM(rows, wide), pltpu.VMEM(rows, wide), pltpu.VMEM(rows, wide),
            pltpu.VMEM((2, WIDE, WIDE), wide),
            pltpu.VMEM(rows, wide), pltpu.VMEM(rows, wide),
            pltpu.VMEM((WIDE // 4, WIDE), low), pltpu.VMEM((STRIP, WIDE), low),
            pltpu.VMEM((2, WIDE, STRIP), wide),
            pltpu.VMEM(rows, low),
            pltpu.VMEM((2, TOKENS, WIDE), wide),
            dma((7, 2)), dma((6, 2)), dma((2, 2)),
        ],
        compiler_params=pltpu.CompilerParams(vmem_limit_bytes=56 << 20),
    )(grads, left_stat, right_stat, left_root, right_root, master, averaged, sums, vectors, moment, page_one, page_two)


def layout_embed(cell_boxes, cell_ids):
    cell_count = cell_boxes.shape[1]
    onehot = (
        cell_ids[:, :, None] == jnp.arange(cell_count, dtype=jnp.int32)[None, None, :]
    ).astype(jnp.float32)
    corners = jnp.einsum("psc,pck->psk", onehot, cell_boxes.astype(jnp.float32), precision=PRECISE)
    quarter = MODEL_WIDTH // 4
    half_width = quarter // 2
    frequency = jnp.exp(
        -jnp.arange(half_width, dtype=jnp.float32) * (math.log(1000.0) / half_width)
    )
    angle_grid = corners[..., None] * frequency
    wave_table = jnp.concatenate([jnp.sin(angle_grid), jnp.cos(angle_grid)], -1)
    return 0.5 * wave_table.reshape(corners.shape[0], corners.shape[1], MODEL_WIDTH)


def gelu_exact(values):
    return jax.nn.gelu(values, approximate=False)


def norm_forward(values, gain, shift):
    center = values - jnp.mean(values, -1, keepdims=True)
    inv_std = lax.rsqrt(jnp.mean(center * center, -1, keepdims=True) + EPS_NORM)
    normed = center * inv_std
    return (normed * gain + shift, normed, inv_std)


def norm_backward(grad_in, normed, inv_std, gain):
    scaled = grad_in * gain
    grad_arg = inv_std * (
        scaled
        - jnp.mean(scaled, -1, keepdims=True)
        - normed * jnp.mean(scaled * normed, -1, keepdims=True)
    )
    return (grad_arg, jnp.sum(grad_in * normed, (0, 1)), jnp.sum(grad_in, (0, 1)))


def attend(query_low, key_low, value_low, head_count):
    groups, seq_len = (query_low.shape[0], query_low.shape[1])
    shape_heads = (groups, seq_len, head_count, HD)
    scores = jnp.einsum(
        "gqhe,gkhe->ghqk",
        query_low.reshape(shape_heads),
        key_low.reshape(shape_heads),
        preferred_element_type=jnp.float32,
    ) * HD ** (-0.5)
    row_max = jnp.max(scores, -1, keepdims=True)
    log_total = row_max + jnp.log(jnp.sum(jnp.exp(scores - row_max), -1, keepdims=True))
    probs = jnp.exp(scores - log_total).astype(jnp.bfloat16)
    context = jnp.einsum(
        "ghqk,gkhe->gqhe", probs, value_low.reshape(shape_heads), preferred_element_type=jnp.float32
    )
    return (context.reshape(groups, seq_len, head_count * HD).astype(jnp.bfloat16), log_total)


def attend_back(query_low, key_low, value_low, log_total, ctx_grad, head_count):
    groups, seq_len = (query_low.shape[0], query_low.shape[1])
    shape_heads = (groups, seq_len, head_count, HD)
    query_heads = query_low.reshape(shape_heads)
    key_heads = key_low.reshape(shape_heads)
    value_heads = value_low.reshape(shape_heads)
    grad_heads = ctx_grad.reshape(shape_heads)
    scale = HD ** (-0.5)
    scores = (
        jnp.einsum("gqhe,gkhe->ghqk", query_heads, key_heads, preferred_element_type=jnp.float32)
        * scale
    )
    probs = jnp.exp(scores - log_total)
    value_grad = jnp.einsum(
        "ghqk,gqhe->gkhe",
        probs.astype(jnp.bfloat16),
        grad_heads,
        preferred_element_type=jnp.float32,
    )
    prob_grad = jnp.einsum(
        "gqhe,gkhe->ghqk", grad_heads, value_heads, preferred_element_type=jnp.float32
    )
    score_grad = (probs * (prob_grad - jnp.sum(probs * prob_grad, -1, keepdims=True))).astype(
        jnp.bfloat16
    )
    query_grad = (
        jnp.einsum("ghqk,gkhe->gqhe", score_grad, key_heads, preferred_element_type=jnp.float32)
        * scale
    )
    key_grad = (
        jnp.einsum("ghqk,gqhe->gkhe", score_grad, query_heads, preferred_element_type=jnp.float32)
        * scale
    )
    width = head_count * HD
    return (
        query_grad.reshape(groups, seq_len, width).astype(jnp.bfloat16),
        key_grad.reshape(groups, seq_len, width).astype(jnp.bfloat16),
        value_grad.reshape(groups, seq_len, width).astype(jnp.bfloat16),
    )


def by_collectives(
    hidden, cell_ids, cell_boxes, cotangent, weight_cols, weight_out, weight_down, vectors, slot_dev
):
    dp_count = lax.axis_size("dp")
    col_mats = lax.all_gather(weight_cols, "tp", axis=2, tiled=True)
    out_mat = lax.all_gather(weight_out, "tp", axis=0, tiled=True)
    down_mats = lax.all_gather(weight_down, "tp", axis=1, tiled=True)
    x_own = hidden.astype(jnp.float32) + layout_embed(cell_boxes, cell_ids)
    x_low = x_own.astype(jnp.bfloat16)
    projected = jnp.einsum(
        "gtd,kdc->kgtc", x_low, col_mats[0:3], preferred_element_type=jnp.float32
    )
    query_low = (projected[0] + vectors[:, 6]).astype(jnp.bfloat16)
    key_low = projected[1].astype(jnp.bfloat16)
    value_low = (projected[2] + vectors[:, 7]).astype(jnp.bfloat16)
    context, log_total = attend(query_low, key_low, value_low, H)
    attn_out = jnp.einsum("gtc,cd->gtd", context, out_mat, preferred_element_type=jnp.float32)
    mid_out, mid_hat, mid_inv = norm_forward(
        x_own + attn_out + vectors[:, 0], vectors[:, 2], vectors[:, 3]
    )
    mid_low = mid_out.astype(jnp.bfloat16)
    up_pre = jnp.einsum(
        "gtd,kdc->kgtc", mid_low, col_mats[3:7], preferred_element_type=jnp.float32
    )
    up_pre = up_pre + jnp.transpose(vectors[:, 8:12])[:, None, None, :]
    act_low = gelu_exact(up_pre).astype(jnp.bfloat16)
    ffn_out = jnp.einsum("kgtc,kcd->gtd", act_low, down_mats, preferred_element_type=jnp.float32)
    layer_out, out_hat, out_inv = norm_forward(
        mid_out + ffn_out + vectors[:, 1], vectors[:, 4], vectors[:, 5]
    )
    output_gradient = cotangent.astype(jnp.float32)
    grad_two, gain_two, shift_two = norm_backward(output_gradient, out_hat, out_inv, vectors[:, 4])
    two_low = grad_two.astype(jnp.bfloat16)
    act_grad = jnp.einsum("gtd,kcd->kgtc", two_low, down_mats, preferred_element_type=jnp.float32)
    gelu_pull = jax.vjp(gelu_exact, up_pre)[1]
    up_low = gelu_pull(act_grad)[0].astype(jnp.bfloat16)
    mid_back = jnp.einsum(
        "kgtc,kdc->gtd", up_low, col_mats[3:7], preferred_element_type=jnp.float32
    )
    grad_one, gain_one, shift_one = norm_backward(
        mid_back + grad_two, mid_hat, mid_inv, vectors[:, 2]
    )
    one_low = grad_one.astype(jnp.bfloat16)
    ctx_grad = jnp.einsum(
        "gtd,cd->gtc", one_low, out_mat, preferred_element_type=jnp.float32
    ).astype(jnp.bfloat16)
    query_grad, key_grad, value_grad = attend_back(
        query_low, key_low, value_low, log_total, ctx_grad, H
    )
    qkv_grad = jnp.stack([query_grad, key_grad, value_grad], 0)
    input_grad = grad_one + jnp.einsum(
        "kgtc,kdc->gtd", qkv_grad, col_mats[0:3], preferred_element_type=jnp.float32
    )

    def block(text, left, right):
        return jnp.einsum(text, left, right, preferred_element_type=jnp.float32).astype(
            jnp.bfloat16
        )

    qkv_blocks = block("gtd,kgtc->kdc", x_low, qkv_grad)
    up_blocks = block("gtd,kgtc->kdc", mid_low, up_low)
    out_block = block("gtd,gtc->dc", one_low, context)[None]
    down_blocks = block("gtd,kgtc->kdc", two_low, act_low)
    vector_part = jnp.stack(
        [
            jnp.sum(grad_one, (0, 1)),
            jnp.sum(grad_two, (0, 1)),
            gain_one,
            shift_one,
            gain_two,
            shift_two,
            jnp.sum(query_grad, (0, 1), dtype=jnp.float32),
            jnp.sum(value_grad, (0, 1), dtype=jnp.float32),
        ],
        0,
    )
    vector_part = jnp.concatenate(
        [vector_part, jnp.sum(up_low, (1, 2), dtype=jnp.float32)], 0
    )
    block_part = jnp.concatenate(
        [
            qkv_blocks,
            up_blocks,
            out_block,
            down_blocks,
            jnp.zeros((slot_dev * dp_count - 12, MODEL_WIDTH, MODEL_WIDTH), jnp.bfloat16),
        ],
        0,
    )
    block_owned = lax.psum_scatter(block_part, "dp", scatter_dimension=0, tiled=True)
    full_grad = lax.psum(block_owned, "tp")
    vector_all = lax.psum(vector_part, ("dp", "tp"))
    return layer_out, input_grad, full_grad, vector_all


def local(
    hidden,
    cell_ids,
    cell_boxes,
    cotangent,
    weight_cols,
    weight_out,
    weight_down,
    vectors,
    vector_moment,
    left_stat,
    right_stat,
    left_root,
    right_root,
    master,
    averaged_weight,
):
    tp_count = lax.axis_size("tp")
    dp_count = lax.axis_size("dp")
    tp_index = lax.axis_index("tp")
    dp_index = lax.axis_index("dp")
    strip_width = weight_cols.shape[2]
    page_rows, seq_len = (hidden.shape[0], hidden.shape[1])
    owned_rows = vector_moment.shape[0]
    slot_dev = left_stat.shape[0]
    if dp_count == 8 and tp_count == 4:
        vec = jnp.transpose(vectors)
        full, layer_out, *kept, sums = forward(
            weight_cols, weight_out, weight_down, hidden[0], cell_ids, jnp.transpose(cell_boxes[0]), cotangent[0], vec
        )
        input_grad, full_grad, vector_all, *_ = backward(full, *kept, sums, vec)
        outs = update(
            full_grad, left_stat, right_stat, left_root, right_root, master, averaged_weight, vector_all, vec,
            jnp.transpose(vector_moment), layer_out, input_grad
        )
        *blocks, vector_grad, moment_new, vector_new, bias_grad, layer_out, input_grad = outs
        thin = [jnp.transpose(array) for array in (vector_grad, moment_new, vector_new)]
        return (layer_out[None], input_grad[None], *blocks, *thin, bias_grad[0])
    else:
        layer_out, input_grad, full_grad, vector_all = by_collectives(
            hidden, cell_ids, cell_boxes, cotangent, weight_cols, weight_out, weight_down, vectors, slot_dev
        )
    vector_grad = jnp.transpose(
        lax.dynamic_slice_in_dim(vector_all[0:12], dp_index * owned_rows, owned_rows, 1)
    )
    own_rows = lax.dynamic_slice_in_dim(full_grad, tp_index * strip_width, strip_width, 1)
    own_cols = lax.dynamic_slice_in_dim(full_grad, tp_index * strip_width, strip_width, 2)
    block_grad = own_cols.astype(jnp.float32)
    left_new = STAT_DECAY * left_stat + (1.0 - STAT_DECAY) * jnp.einsum(
        "sic,sjc->sij", own_rows, full_grad, preferred_element_type=jnp.float32
    )
    right_new = STAT_DECAY * right_stat + (1.0 - STAT_DECAY) * jnp.einsum(
        "sic,sij->scj", own_cols, full_grad, preferred_element_type=jnp.float32
    )

    def parts(array):
        high = array.astype(jnp.bfloat16)
        return high, (array - high.astype(jnp.float32)).astype(jnp.bfloat16)

    def product(left, right):
        return jnp.einsum("sij,sjc->sic", left, right, preferred_element_type=jnp.float32)

    left_high, left_rest = parts(left_root)
    right_high, right_rest = parts(right_root)
    precond = product(left_high, full_grad) + product(left_rest, full_grad)
    pre_high, pre_rest = parts(precond)
    precond = (
        product(pre_high, right_high) + product(pre_rest, right_high) + product(pre_high, right_rest)
    )
    master_new = master - BLOCK_RATE * precond
    weight_copy = master_new.astype(jnp.bfloat16)
    ema_new = EMA_DECAY * averaged_weight + (1.0 - EMA_DECAY) * master_new
    vector_rows = lax.dynamic_slice_in_dim(vectors, dp_index * owned_rows, owned_rows, 0)
    moment_new = MOMENTUM * vector_moment + vector_grad
    total_tokens = page_rows * seq_len * dp_count * tp_count
    vector_new = vector_rows - VEC_RATE * lax.rsqrt(jnp.float32(total_tokens)) * moment_new
    bias_grad = vector_grad[:, 0]
    return (
        layer_out,
        input_grad,
        block_grad,
        left_new,
        right_new,
        master_new,
        weight_copy,
        ema_new,
        vector_grad,
        moment_new,
        vector_new,
        bias_grad,
    )


def solution(mesh):
    return jax.shard_map(
        local,
        mesh=mesh,
        in_specs=(
            P(("dp", "tp"), None, None),
            P(("dp", "tp"), None),
            P(("dp", "tp"), None, None),
            P(("dp", "tp"), None, None),
            P(None, None, "tp"),
            P("tp", None),
            P(None, "tp", None),
            P(),
            P("dp", None),
            P("dp", "tp", None),
            P("dp", "tp", None),
            P("dp", "tp", None),
            P("dp", None, None),
            P("dp", "tp", None),
            P("dp", "tp", None),
        ),
        out_specs=(
            P(("dp", "tp"), None, None),
            P(("dp", "tp"), None, None),
            P("dp", None, "tp"),
            P("dp", "tp", None),
            P("dp", "tp", None),
            P("dp", "tp", None),
            P("dp", "tp", None),
            P("dp", "tp", None),
            P("dp", None),
            P("dp", None),
            P("dp", None),
            P("dp"),
        ),
        check_vma=False,
    )
```
